32 devices in a mesh: fsdp: 8 (over y, x, core), sp: 4 (over z).
Axes of the slice: x: 2, y: 2, z: 4, core: 2. Of those that a mesh axis runs over, the one named last changes fastest.
Arguments:
- hidden_in: bfloat16 [8, 1024, 2048], P('fsdp', 'sp'), may hold values from -6 to 6
- segments: int32 [8, 1024], P('fsdp'), may hold values from 0 to 3, never falling along the last dimension, each value on 1 to 640 neighbouring positions
- ln1_gain: float32 [2048], replicated, may hold values from 0.5 to 1.5
- ln1_bias: float32 [2048], replicated, may hold values from -1 to 1
- ln2_gain: float32 [2048], replicated, may hold values from 0.5 to 1.5
- ln2_bias: float32 [2048], replicated, may hold values from -1 to 1
- w_qkv: bfloat16 [6144, 2048], P('fsdp'), may hold values from -0.125 to 0.125
- b_qkv: float32 [6144], replicated, may hold values from -1 to 1
- w_dense: bfloat16 [2048, 2048], P('fsdp'), may hold values from -0.75 to 0.75
- b_dense: float32 [2048], replicated, may hold values from -1 to 1
- w_up: bfloat16 [8192, 2048], P('fsdp'), may hold values from -0.125 to 0.125
- b_up: float32 [8192], replicated, may hold values from -1 to 1
- w_down: bfloat16 [8192, 2048], P('fsdp'), may hold values from -0.0625 to 0.0625
- b_down: float32 [2048], replicated, may hold values from -1 to 1
- cotangent: bfloat16 [8, 1024, 2048], P('fsdp', 'sp'), may hold values from -6 to 6
Outputs:
- output: bfloat16 [8, 1024, 2048], P('fsdp', 'sp')
- input_grad: bfloat16 [8, 1024, 2048], P('fsdp', 'sp')
- grad_ln1_gain: float32 [2048], P('fsdp')
- grad_ln1_bias: float32 [2048], P('fsdp')
- grad_ln2_gain: float32 [2048], P('fsdp')
- grad_ln2_bias: float32 [2048], P('fsdp')
- grad_w_qkv: float32 [6144, 2048], P('fsdp')
- grad_b_qkv: float32 [6144], P('fsdp')
- grad_w_dense: float32 [2048, 2048], P('fsdp')
- grad_b_dense: float32 [2048], P('fsdp')
- grad_w_up: float32 [8192, 2048], P('fsdp')
- grad_b_up: float32 [8192], P('fsdp')
- grad_w_down: float32 [8192, 2048], P('fsdp')
- grad_b_down: float32 [2048], P('fsdp')
The draws below stay inside these ranges and needn't reach their ends.
Inputs may be any that keep to these rules, and one draw needn't show every extreme that they name: `segments`: along each sequence the segment numbers never fall; each document is one run of 1 to 640 positions, and some document has exactly 640.
All inputs are finite; a program needn't handle non-finite values.
Results may differ from the reference program's by a relative error of at most 0.011.
Values may be sent and summed in bfloat16 or wider, within the bound.
A program may use at most 704 MiB of HBM per device.

```python
import math
import jax
import jax.numpy as jnp
import numpy as np
from jax import lax

D = 2048
HEADS = 8
HEAD_DIM = 256
ROT = 64
FF = 8192
SEQ_LEN = 1024
SEQS = 8
DOC_MOST = 640


def raised(array, rng, source, target, shards_of, factor):
    owner, partner = [(jnp.arange(array.shape[dim]) // (array.shape[dim] // shards_of)).reshape([-1 if axis == dim else 1 for axis in range(array.ndim)]) for dim in (source, target)]
    chosen = jax.random.permutation(rng, shards_of)[partner]
    strong = (owner == chosen) | (owner == (partner + shards_of // 2) % shards_of)
    return jnp.where(strong, factor * array, array)


def block_levels(key, extent, pieces, low, top_value):
    def one(dim, shards_of):
        heights = jax.random.uniform(jax.random.fold_in(jax.random.fold_in(key, 6), dim), (shards_of,), jnp.float32, low / len(pieces), top_value / len(pieces))
        return jnp.repeat(jnp.exp(heights), extent[dim] // shards_of).reshape((-1,) + (1,) * (len(extent) - dim - 1))

    factor_of = one(*pieces[0])
    for cut in pieces[1:]:
        factor_of = factor_of * one(*cut)
    return factor_of


def length_profile(count, total, reach, slope):
    loads = [(1 << 20) // math.isqrt(rank ** slope) + 1 for rank in range(2, count + 1)]
    rest, given = total - reach - (count - 1), [1] * (count - 1)
    while rest > 0:
        movable = [i for i in range(count - 1) if given[i] < reach]
        whole, left = sum([loads[i] for i in movable]), rest
        for i in movable:
            extra = min(reach - given[i], max(1, left * loads[i] // whole), rest)
            given[i] = given[i] + extra
            rest = rest - extra
    return np.array([reach] + given)


def uneven_parts(own_key, number_of, total, reach, skew):
    if number_of == 2:
        one = jax.random.randint(own_key, (), max(1, total - reach), min(reach, total - 1) + 1)
        return jnp.stack([one, total - one])
    tallies = jnp.asarray(length_profile(number_of, total, reach, skew), jnp.int32)
    pairs = (number_of - 1) // 2
    source_of, sink = tallies[1:1 + 2 * pairs:2], tallies[2:2 + 2 * pairs:2]
    margin = jnp.minimum(source_of - 1, reach - sink)
    moved = jax.random.randint(jax.random.fold_in(own_key, 1), (pairs,), 0, 1 << 20) % (margin + 1)
    tallies = tallies.at[1:1 + 2 * pairs:2].set(source_of - moved).at[2:2 + 2 * pairs:2].set(sink + moved)
    return tallies[jax.random.permutation(jax.random.fold_in(own_key, 2), number_of)]


def gaussian(own_key, dims, spread, reach, shards=(), kind=jnp.bfloat16):
    drawn = jax.random.normal(own_key, dims, jnp.float32) * spread
    if len(shards) > 0:
        drawn = block_levels(own_key, dims, shards, -0.22, 0.18) * drawn
    return jnp.clip(drawn, min=-reach, max=reach).astype(kind)


def bell_draw_with(stream_key, extent, scale, limit, split, heavy, kind=jnp.bfloat16):
    entries = scale * jax.random.normal(stream_key, extent, jnp.float32)
    if split:
        entries = entries * block_levels(stream_key, extent, split, -0.22, 0.18)
    return jnp.clip(raised(entries, jax.random.fold_in(stream_key, 3), *heavy), -limit, limit).astype(kind)


def setup_inputs(seed: int = 0) -> dict:
    seeds = jax.random.split(jax.random.key(seed), 16)
    hidden_in = gaussian(seeds[0], (SEQS, SEQ_LEN, D), 1.0, 6.0, ((0, 8), (1, 4)))
    segments = jax.vmap(lambda own: jnp.searchsorted(jnp.cumsum(uneven_parts(own, 4, SEQ_LEN, DOC_MOST, 0)), jnp.arange(SEQ_LEN), side="right"))(jax.random.split(seeds[1], SEQS)).reshape((SEQS, SEQ_LEN)).astype(jnp.int32)
    ln1_gain = jnp.clip(1.0 + 0.1 * jax.random.normal(seeds[2], (D,), jnp.float32), 0.5, 1.5)
    ln1_bias = gaussian(seeds[3], (D,), 0.2, 1.0, (), jnp.float32)
    ln2_gain = jnp.clip(1.0 + 0.1 * jax.random.normal(seeds[4], (D,), jnp.float32), 0.5, 1.5)
    ln2_bias = gaussian(seeds[5], (D,), 0.2, 1.0, (), jnp.float32)
    w_qkv = gaussian(seeds[6], (3 * D, D), D ** -0.5, 0.125, ((0, 8),))
    b_qkv = gaussian(seeds[7], (3 * D,), 0.2, 1.0, (), jnp.float32)
    w_dense = gaussian(seeds[8], (D, D), (D // 32) ** -0.5, 0.75, ((0, 8),))
    b_dense = gaussian(seeds[9], (D,), 0.2, 1.0, (), jnp.float32)
    w_up = gaussian(seeds[10], (FF, D), D ** -0.5, 0.125, ((0, 8),))
    b_up = gaussian(seeds[11], (FF,), 0.2, 1.0, (), jnp.float32)
    w_down = gaussian(seeds[12], (FF, D), FF ** -0.5, 0.0625, ((0, 8),))
    b_down = gaussian(seeds[13], (D,), 0.2, 1.0, (), jnp.float32)
    cotangent = bell_draw_with(seeds[14], (SEQS, SEQ_LEN, D), 1.0, 6.0, ((0, 8), (1, 4)), (0, 2, 8, 2.0))
    return dict(hidden_in=hidden_in, segments=segments, ln1_gain=ln1_gain, ln1_bias=ln1_bias, ln2_gain=ln2_gain, ln2_bias=ln2_bias, w_qkv=w_qkv, b_qkv=b_qkv, w_dense=w_dense, b_dense=b_dense, w_up=w_up, b_up=b_up, w_down=w_down, b_down=b_down, cotangent=cotangent)


HIGHEST = lax.Precision.HIGHEST
EPSILON = 1e-05
NEGATIVE = -1e+30
ROOT_HALF = 0.7071067811865476

@jax.custom_vjp
def low(v):
    return lax.optimization_barrier(v.astype(jnp.bfloat16)).astype(jnp.float32)

@jax.custom_vjp
def low_back(v):
    return v

def low_keep(v):
    return (low(v), None)

def low_pass(kept, grad):
    return (grad,)

def back_keep(v):
    return (v, None)

def back_low(kept, grad):
    return (low(grad),)
low.defvjp(low_keep, low_pass)
low_back.defvjp(back_keep, back_low)

def rotary_tables(segment_rows):
    length = segment_rows.shape[-1]
    places = jnp.arange(length, dtype=jnp.int32)
    changes = jnp.concatenate([jnp.ones_like(segment_rows[..., :1]), (segment_rows[..., 1:] != segment_rows[..., :-1]).astype(jnp.int32)], axis=-1)
    first_place = lax.cummax(changes * places, axis=segment_rows.ndim - 1)
    position = (places - first_place).astype(jnp.float32)
    exponent = jnp.arange(0, ROT, 2).astype(jnp.float32) / ROT
    frequency = 1.0 / jnp.power(10000.0, exponent)
    angles = position[..., None] * frequency
    angles = jnp.concatenate([angles, angles], axis=-1)
    return (jnp.cos(angles), jnp.sin(angles))

def rotate(heads_part, cos_table, sin_table):
    half_rot = ROT // 2
    turned = heads_part[..., :ROT]
    swapped = jnp.concatenate([-turned[..., half_rot:], turned[..., :half_rot]], axis=-1)
    turned = turned * cos_table[..., None, :] + swapped * sin_table[..., None, :]
    return jnp.concatenate([turned, heads_part[..., ROT:]], axis=-1)

def build_mask(segment_row):
    places = jnp.arange(segment_row.shape[0], dtype=jnp.int32)
    return (segment_row[:, None] == segment_row[None, :]) & (places[None, :] <= places[:, None])

def layer_norm(inputs, norm_gain, norm_shift):
    average = lax.optimization_barrier(jnp.mean(inputs, axis=-1, keepdims=True))
    centred = inputs - average
    variance = lax.optimization_barrier(jnp.mean(centred * centred, axis=-1, keepdims=True))
    return centred * lax.rsqrt(variance + EPSILON) * norm_gain + norm_shift

def attend_sequence(scanned):
    packed_seq, segment_row = scanned
    cos_table, sin_table = rotary_tables(segment_row)
    queries = low(rotate(packed_seq[..., :HEAD_DIM], cos_table, sin_table))
    keys_rot = low(rotate(packed_seq[..., HEAD_DIM:2 * HEAD_DIM], cos_table, sin_table))
    values = packed_seq[..., 2 * HEAD_DIM:]
    scores = jnp.einsum('qhd,khd->hqk', queries, keys_rot, precision=HIGHEST) * (1.0 / math.sqrt(HEAD_DIM))
    scores = jnp.where(build_mask(segment_row)[None], low_back(scores), NEGATIVE)
    row_top = lax.optimization_barrier(jnp.max(scores, axis=-1, keepdims=True))
    exponent = jnp.exp(scores - row_top)
    attention = exponent / lax.optimization_barrier(jnp.sum(exponent, axis=-1, keepdims=True))
    return jnp.einsum('hqk,khd->qhd', low(attention), values, precision=HIGHEST)

def layer(inputs, segment_rows, params):
    ln1_gain, ln1_bias, ln2_gain, ln2_bias, w_qkv, b_qkv, w_dense, b_dense, w_up, b_up, w_down, b_down = params
    seq_total = inputs.shape[0]
    length = inputs.shape[1]
    normed = low(layer_norm(inputs, ln1_gain, ln1_bias))
    packed = jnp.einsum('gtd,ed->gte', normed, w_qkv, precision=HIGHEST) + b_qkv
    packed = low_back(low(packed)).reshape(seq_total, length, HEADS, 3 * HEAD_DIM)
    context = lax.map(jax.checkpoint(attend_sequence), (packed, segment_rows))
    context = low_back(low(context.reshape(seq_total, length, D)))
    attended = jnp.einsum('gtd,ed->gte', context, w_dense, precision=HIGHEST) + b_dense
    normed_mlp = low(layer_norm(inputs, ln2_gain, ln2_bias))
    hidden = low_back(jnp.einsum('gtd,fd->gtf', normed_mlp, w_up, precision=HIGHEST) + b_up)
    activated = low(0.5 * hidden * (1.0 + jax.scipy.special.erf(hidden * ROOT_HALF)))
    mlp_out = jnp.einsum('gtf,fd->gtd', activated, w_down, precision=HIGHEST) + b_down
    return inputs + attended + mlp_out

def reference(hidden_in, segments, ln1_gain, ln1_bias, ln2_gain, ln2_bias, w_qkv, b_qkv, w_dense, b_dense, w_up, b_up, w_down, b_down, cotangent):
    group_size = math.gcd(SEQS, 4)
    group_count = SEQS // group_size
    params = tuple((param_array.astype(jnp.float32) for param_array in (ln1_gain, ln1_bias, ln2_gain, ln2_bias, w_qkv, b_qkv, w_dense, b_dense, w_up, b_up, w_down, b_down)))
    inputs = hidden_in.astype(jnp.float32).reshape(group_count, group_size, SEQ_LEN, D)
    upstream = cotangent.astype(jnp.float32).reshape(group_count, group_size, SEQ_LEN, D)
    segment_groups = segments.reshape(group_count, group_size, SEQ_LEN)

    def one_group(totals, scanned):
        group_inputs, group_segments, group_upstream = scanned

        def forward(layer_inputs, layer_params):
            return layer(layer_inputs, group_segments, layer_params)
        result, pullback = jax.vjp(forward, group_inputs, params)
        input_part, param_grads = pullback(group_upstream)
        totals = jax.tree.map(jnp.add, totals, param_grads)
        return (totals, (result, input_part))
    initial = jax.tree.map(jnp.zeros_like, params)
    totals, (results, input_parts) = lax.scan(one_group, initial, (inputs, segment_groups, upstream))
    output = results.reshape(SEQS, SEQ_LEN, D).astype(jnp.bfloat16)
    input_grad = input_parts.reshape(SEQS, SEQ_LEN, D).astype(jnp.bfloat16)
    return (output, input_grad, totals[0], totals[1], totals[2], totals[3], totals[4], totals[5], totals[6], totals[7], totals[8], totals[9], totals[10], totals[11])
```

```python
import math

import jax
import jax.numpy as jnp
from jax import lax
from jax.sharding import PartitionSpec as P

HEADS = 8
HEAD_DIM = 256
ROT = 64


EPSILON = 1e-05
NEGATIVE = -1e30
ROOT_HALF = 0.7071067811865476
ROOT_TWO_PI = 2.5066282746310002
SCALE = 1.0 / math.sqrt(HEAD_DIM)


def rounded(array):
    return lax.reduce_precision(array.astype(jnp.float32), 8, 7).astype(jnp.bfloat16)


def contract_rows(former, latter):
    return lax.dot_general(
        former, latter, (((0,), (0,)), ((), ())), preferred_element_type=jnp.float32
    )


def times_transposed(former, latter):
    return lax.dot_general(
        former, latter, (((1,), (1,)), ((), ())), preferred_element_type=jnp.float32
    )


def times(former, latter):
    return jnp.dot(former, latter, preferred_element_type=jnp.float32)


def norm_scaled(inputs):
    average = jnp.mean(inputs, axis=-1, keepdims=True)
    centred = inputs - average
    variance = jnp.mean(centred * centred, axis=-1, keepdims=True)
    inverse = lax.rsqrt(variance + EPSILON)
    return centred * inverse, inverse


def gelu_pair(hidden):
    cumulative = 0.5 * (1.0 + jax.scipy.special.erf(hidden * ROOT_HALF))
    return (
        hidden * cumulative,
        cumulative + hidden * jnp.exp(-0.5 * hidden * hidden) / ROOT_TWO_PI,
    )


def rotary_tables(segment_rows):
    length = segment_rows.shape[-1]
    places = jnp.arange(length, dtype=jnp.int32)
    changes = jnp.concatenate(
        [
            jnp.ones_like(segment_rows[..., :1]),
            (segment_rows[..., 1:] != segment_rows[..., :-1]).astype(jnp.int32),
        ],
        axis=-1,
    )
    first_place = lax.cummax(changes * places, axis=segment_rows.ndim - 1)
    position = (places - first_place).astype(jnp.float32)
    exponent = jnp.arange(0, ROT, 2).astype(jnp.float32) / ROT
    frequency = 1.0 / jnp.power(10000.0, exponent)
    angles = position[..., None] * frequency
    angles = jnp.concatenate([angles, angles], axis=-1)
    return (jnp.cos(angles), jnp.sin(angles))


def rotate(heads_part, cos_table, sin_table):
    half_rot = ROT // 2
    turned = heads_part[..., :ROT]
    swapped = jnp.concatenate([-turned[..., half_rot:], turned[..., :half_rot]], axis=-1)
    turned = turned * cos_table[..., None, :] + swapped * sin_table[..., None, :]
    return jnp.concatenate([turned, heads_part[..., ROT:]], axis=-1)


def unrotate(grads_part, cos_table, sin_table):
    half_rot = ROT // 2
    turned = grads_part[..., :ROT]
    along_sin = turned * sin_table[..., None, :]
    back_turn = jnp.concatenate([along_sin[..., half_rot:], -along_sin[..., :half_rot]], axis=-1)
    turned = turned * cos_table[..., None, :] + back_turn
    return jnp.concatenate([turned, grads_part[..., ROT:]], axis=-1)


def build_mask(segment_rows):
    places = jnp.arange(segment_rows.shape[-1], dtype=jnp.int32)
    return (segment_rows[:, :, None] == segment_rows[:, None, :]) & (
        places[None, :] <= places[:, None]
    )


def attention_scores(queries, keys_rot):
    return (
        jnp.einsum("bqhd,bkhd->bhqk", queries, keys_rot, preferred_element_type=jnp.float32) * SCALE
    )


def attend_forward(queries, keys_rot, values, mask):
    scores = jnp.where(mask[:, None], attention_scores(queries, keys_rot), NEGATIVE)
    row_top = jnp.max(scores, axis=-1, keepdims=True)
    exponent = jnp.exp(scores - row_top)
    row_total = jnp.sum(exponent, axis=-1, keepdims=True)
    attention = (exponent / row_total).astype(jnp.bfloat16)
    context = jnp.einsum("bhqk,bkhd->bqhd", attention, values, preferred_element_type=jnp.float32)
    return (context.astype(jnp.bfloat16), row_top + jnp.log(row_total))


def attend_backward(queries, keys_rot, values, mask, log_total, context_grad):
    scores = attention_scores(queries, keys_rot)
    attention = jnp.where(mask[:, None], jnp.exp(scores - log_total), 0.0)
    value_grad = jnp.einsum(
        "bhqk,bqhd->bkhd",
        attention.astype(jnp.bfloat16),
        context_grad,
        preferred_element_type=jnp.float32,
    )
    attention_grad = jnp.einsum(
        "bqhd,bkhd->bhqk", context_grad, values, preferred_element_type=jnp.float32
    )
    row_centre = jnp.sum(attention * attention_grad, axis=-1, keepdims=True)
    score_grad = (attention * (attention_grad - row_centre)).astype(jnp.bfloat16)
    query_grad = (
        jnp.einsum("bhqk,bkhd->bqhd", score_grad, keys_rot, preferred_element_type=jnp.float32)
        * SCALE
    )
    key_grad = (
        jnp.einsum("bhqk,bqhd->bkhd", score_grad, queries, preferred_element_type=jnp.float32)
        * SCALE
    )
    return (query_grad, key_grad, value_grad)


def sum_over_line(partial):
    inward = lax.ppermute(partial, "sp", [(0, 1), (3, 2)])
    half = rounded(partial.astype(jnp.float32) + inward.astype(jnp.float32))
    other = lax.ppermute(half, "sp", [(1, 2), (2, 1)])
    whole = rounded(half.astype(jnp.float32) + other.astype(jnp.float32))
    outward = lax.ppermute(whole, "sp", [(1, 0), (2, 3)])
    place = lax.axis_index("sp")
    inner = (place == 1) | (place == 2)
    return jnp.where(inner, whole, outward).astype(jnp.float32)


def sum_over_sp(partial):
    partial = rounded(partial)
    if lax.axis_size("sp") == 4:
        return sum_over_line(partial)
    return lax.psum(partial, "sp").astype(jnp.float32)


def per_device(
    hidden_in,
    segments,
    ln1_gain,
    ln1_bias,
    ln2_gain,
    ln2_bias,
    w_qkv,
    b_qkv,
    w_dense,
    b_dense,
    w_up,
    b_up,
    w_down,
    b_down,
    cotangent,
):
    seq_local, shard_len, width = hidden_in.shape
    seq_len = segments.shape[1]
    nf, ns = lax.axis_size("fsdp"), lax.axis_size("sp")
    f_place, s_place = lax.axis_index("fsdp"), lax.axis_index("sp")
    seqs = seq_local * nf
    group = seqs // ns
    piece = shard_len // nf
    tokens = group * seq_len
    per_head = max(1, nf // HEADS)
    head_count = max(1, HEADS // nf)
    head_sets = [[head * per_head + k for k in range(per_head)] for head in range(nf // per_head)]

    def gather_tokens(block):
        part = lax.all_to_all(block, "fsdp", split_axis=1, concat_axis=0, tiled=True)
        part = lax.all_to_all(part, "sp", split_axis=0, concat_axis=1, tiled=True)
        return lax.all_gather(part, "fsdp", axis=0, tiled=True).reshape(tokens, width)

    def scatter_tokens(partial):
        part = partial.reshape(nf * group, ns * piece, width)
        part = lax.psum_scatter(part, "fsdp", scatter_dimension=0, tiled=True)
        part = lax.all_to_all(part, "sp", split_axis=1, concat_axis=0, tiled=True)
        return lax.all_to_all(part, "fsdp", split_axis=0, concat_axis=1, tiled=True)

    def in_order(array):
        array = array.reshape(nf, group, ns, piece, -1)
        return array.transpose(1, 2, 0, 3, 4).reshape(group, seq_len, -1)

    def out_of_order(array):
        array = array.reshape(group, ns, nf, piece, -1)
        return array.transpose(2, 0, 1, 3, 4).reshape(tokens, -1)

    def over_head(array, axis):
        if per_head == 1:
            return array
        return lax.all_gather(
            array, "fsdp", axis=axis, tiled=True, axis_index_groups=head_sets
        )

    def own_columns(array):
        if per_head == 1:
            return array
        share = array.shape[-1] // per_head
        return lax.dynamic_slice_in_dim(array, (f_place % per_head) * share, share, array.ndim - 1)

    def own_part(vector):
        share = vector.shape[0] // nf
        return lax.dynamic_slice_in_dim(vector, f_place * share, share, 0)

    gathered = gather_tokens(hidden_in)
    upstream = gather_tokens(cotangent)
    rows = lax.all_gather(segments, "fsdp", axis=0, tiled=True)
    rows = lax.dynamic_slice_in_dim(rows, s_place * group, group, 0)

    dense_in = lax.all_to_all(w_dense, "fsdp", split_axis=1, concat_axis=0, tiled=True)
    head_qkv = over_head(w_qkv, 0)
    head_dense = over_head(dense_in, 1)
    head_bias = lax.dynamic_slice_in_dim(
        b_qkv, (f_place // per_head) * head_qkv.shape[0], head_qkv.shape[0], 0
    )

    scaled, _ = norm_scaled(gathered.astype(jnp.float32))
    normed = (scaled * ln1_gain + ln1_bias).astype(jnp.bfloat16)
    normed_mlp = (scaled * ln2_gain + ln2_bias).astype(jnp.bfloat16)

    hidden = times_transposed(normed_mlp, w_up) + own_part(b_up)
    activated, slope = gelu_pair(hidden)
    activated = activated.astype(jnp.bfloat16)
    hidden_grad = (times_transposed(upstream, w_down) * slope).astype(jnp.bfloat16)
    down_term = contract_rows(activated, upstream)
    up_term = contract_rows(hidden_grad, normed_mlp)
    mlp_norm_grad = times(hidden_grad, w_up)

    packed = (times_transposed(normed, head_qkv) + head_bias).astype(jnp.bfloat16)
    packed = in_order(packed).reshape(group, seq_len, head_count, 3 * HEAD_DIM)
    cos_table, sin_table = rotary_tables(rows)
    queries = rotate(packed[..., :HEAD_DIM].astype(jnp.float32), cos_table, sin_table).astype(
        jnp.bfloat16
    )
    keys_rot = rotate(
        packed[..., HEAD_DIM : 2 * HEAD_DIM].astype(jnp.float32), cos_table, sin_table
    ).astype(jnp.bfloat16)
    values = packed[..., 2 * HEAD_DIM :]
    mask = build_mask(rows)
    context, log_total = attend_forward(queries, keys_rot, values, mask)
    context = own_columns(out_of_order(context))
    partial_out = times_transposed(context, dense_in) + times(activated, w_down)
    context_grad = in_order(times(upstream, head_dense).astype(jnp.bfloat16)).reshape(
        group, seq_len, head_count, HEAD_DIM
    )
    query_grad, key_grad, value_grad = attend_backward(
        queries, keys_rot, values, mask, log_total, context_grad
    )
    packed_grad = jnp.concatenate(
        [
            unrotate(query_grad, cos_table, sin_table),
            unrotate(key_grad, cos_table, sin_table),
            value_grad,
        ],
        axis=-1,
    ).astype(jnp.bfloat16)
    packed_grad = own_columns(out_of_order(packed_grad))
    attn_norm_grad = times(packed_grad, w_qkv)
    qkv_term = contract_rows(packed_grad, normed)
    dense_term = contract_rows(upstream, context).astype(jnp.bfloat16)
    dense_term = lax.all_to_all(dense_term, "fsdp", split_axis=0, concat_axis=1, tiled=True)

    vectors = jnp.stack(
        [
            jnp.sum(attn_norm_grad * scaled, axis=0),
            jnp.sum(attn_norm_grad, axis=0),
            jnp.sum(mlp_norm_grad * scaled, axis=0),
            jnp.sum(mlp_norm_grad, axis=0),
        ],
        axis=1,
    )
    vectors = lax.psum_scatter(vectors, "fsdp", scatter_dimension=0, tiled=True)
    bias_out = own_part(jnp.sum(upstream.astype(jnp.float32), axis=0))
    bias_qkv = jnp.sum(packed_grad.astype(jnp.float32), axis=0)
    bias_up = jnp.sum(hidden_grad.astype(jnp.float32), axis=0)
    vectors, bias_out, bias_qkv, bias_up = lax.psum((vectors, bias_out, bias_qkv, bias_up), "sp")

    output = scatter_tokens(rounded(partial_out))
    weighted = scatter_tokens(rounded(attn_norm_grad * ln1_gain + mlp_norm_grad * ln2_gain))
    inputs = hidden_in.astype(jnp.float32)
    output = (inputs + (output.astype(jnp.float32) + (b_dense + b_down))).astype(jnp.bfloat16)
    own_scaled, own_inverse = norm_scaled(inputs)
    weighted = weighted.astype(jnp.float32)
    first_mean = jnp.mean(weighted, axis=-1, keepdims=True)
    second_mean = jnp.mean(weighted * own_scaled, axis=-1, keepdims=True)
    input_grad = (
        cotangent.astype(jnp.float32)
        + own_inverse * (weighted - first_mean - own_scaled * second_mean)
    ).astype(jnp.bfloat16)

    grad_down_w = sum_over_sp(down_term)
    grad_up_w = sum_over_sp(up_term)
    grad_qkv_w = sum_over_sp(qkv_term)
    grad_dense_w = sum_over_sp(dense_term)
    return (
        output,
        input_grad,
        vectors[:, 0],
        vectors[:, 1],
        vectors[:, 2],
        vectors[:, 3],
        grad_qkv_w,
        bias_qkv,
        grad_dense_w,
        bias_out,
        grad_up_w,
        bias_up,
        grad_down_w,
        bias_out,
    )


def solution(mesh):
    rows = P("fsdp", "sp", None)
    first = P("fsdp", None)
    return jax.shard_map(
        per_device,
        mesh=mesh,
        in_specs=(
            rows,
            first,
            P(),
            P(),
            P(),
            P(),
            first,
            P(),
            first,
            P(),
            first,
            P(),
            first,
            P(),
            rows,
        ),
        out_specs=(
            rows,
            rows,
            P("fsdp"),
            P("fsdp"),
            P("fsdp"),
            P("fsdp"),
            first,
            P("fsdp"),
            first,
            P("fsdp"),
            first,
            P("fsdp"),
            first,
            P("fsdp"),
        ),
        check_vma=False,
    )
```

```python
import math

import jax
import jax.numpy as jnp
from jax import lax
from jax.experimental import pallas as pl
from jax.experimental.pallas import tpu as pltpu
from jax.sharding import PartitionSpec as P

MESH = pl.DeviceIdType.MESH

HEADS = 8
HEAD_DIM = 256
ROT = 64


EPSILON = 1e-05
NEGATIVE = -1e30
ROOT_HALF = 0.7071067811865476
ROOT_TWO_PI = 2.5066282746310002
SCALE = 1.0 / math.sqrt(HEAD_DIM)


def rounded(array):
    return lax.reduce_precision(array.astype(jnp.float32), 8, 7).astype(jnp.bfloat16)


def contract_rows(former, latter):
    return lax.dot_general(
        former, latter, (((0,), (0,)), ((), ())), preferred_element_type=jnp.float32
    )


def times_transposed(former, latter):
    return lax.dot_general(
        former, latter, (((1,), (1,)), ((), ())), preferred_element_type=jnp.float32
    )


def times(former, latter):
    return jnp.dot(former, latter, preferred_element_type=jnp.float32)


def norm_scaled(inputs):
    average = jnp.mean(inputs, axis=-1, keepdims=True)
    centred = inputs - average
    variance = jnp.mean(centred * centred, axis=-1, keepdims=True)
    inverse = lax.rsqrt(variance + EPSILON)
    return centred * inverse, inverse


def gelu_pair(hidden):
    cumulative = 0.5 * (1.0 + jax.scipy.special.erf(hidden * ROOT_HALF))
    return (
        hidden * cumulative,
        cumulative + hidden * jnp.exp(-0.5 * hidden * hidden) / ROOT_TWO_PI,
    )


def rotary_tables(segment_rows):
    length = segment_rows.shape[-1]
    places = jnp.arange(length, dtype=jnp.int32)
    changes = jnp.concatenate(
        [
            jnp.ones_like(segment_rows[..., :1]),
            (segment_rows[..., 1:] != segment_rows[..., :-1]).astype(jnp.int32),
        ],
        axis=-1,
    )
    first_place = lax.cummax(changes * places, axis=segment_rows.ndim - 1)
    position = (places - first_place).astype(jnp.float32)
    exponent = jnp.arange(0, ROT, 2).astype(jnp.float32) / ROT
    frequency = 1.0 / jnp.power(10000.0, exponent)
    angles = position[..., None] * frequency
    angles = jnp.concatenate([angles, angles], axis=-1)
    return (jnp.cos(angles), jnp.sin(angles))


def rotate(heads_part, cos_table, sin_table):
    half_rot = ROT // 2
    turned = heads_part[..., :ROT]
    swapped = jnp.concatenate([-turned[..., half_rot:], turned[..., :half_rot]], axis=-1)
    turned = turned * cos_table[..., None, :] + swapped * sin_table[..., None, :]
    return jnp.concatenate([turned, heads_part[..., ROT:]], axis=-1)


def unrotate(grads_part, cos_table, sin_table):
    half_rot = ROT // 2
    turned = grads_part[..., :ROT]
    along_sin = turned * sin_table[..., None, :]
    back_turn = jnp.concatenate([along_sin[..., half_rot:], -along_sin[..., :half_rot]], axis=-1)
    turned = turned * cos_table[..., None, :] + back_turn
    return jnp.concatenate([turned, grads_part[..., ROT:]], axis=-1)


def build_mask(segment_rows):
    places = jnp.arange(segment_rows.shape[-1], dtype=jnp.int32)
    return (segment_rows[:, :, None] == segment_rows[:, None, :]) & (
        places[None, :] <= places[:, None]
    )


def attention_scores(queries, keys_rot):
    return (
        jnp.einsum("bqhd,bkhd->bhqk", queries, keys_rot, preferred_element_type=jnp.float32) * SCALE
    )


def attend_forward(queries, keys_rot, values, mask):
    scores = jnp.where(mask[:, None], attention_scores(queries, keys_rot), NEGATIVE)
    row_top = jnp.max(scores, axis=-1, keepdims=True)
    exponent = jnp.exp(scores - row_top)
    row_total = jnp.sum(exponent, axis=-1, keepdims=True)
    attention = (exponent / row_total).astype(jnp.bfloat16)
    context = jnp.einsum("bhqk,bkhd->bqhd", attention, values, preferred_element_type=jnp.float32)
    return (context.astype(jnp.bfloat16), row_top + jnp.log(row_total))


def attend_backward(queries, keys_rot, values, mask, log_total, context_grad):
    scores = attention_scores(queries, keys_rot)
    attention = jnp.where(mask[:, None], jnp.exp(scores - log_total), 0.0)
    value_grad = jnp.einsum(
        "bhqk,bqhd->bkhd",
        attention.astype(jnp.bfloat16),
        context_grad,
        preferred_element_type=jnp.float32,
    )
    attention_grad = jnp.einsum(
        "bqhd,bkhd->bhqk", context_grad, values, preferred_element_type=jnp.float32
    )
    row_centre = jnp.sum(attention * attention_grad, axis=-1, keepdims=True)
    score_grad = (attention * (attention_grad - row_centre)).astype(jnp.bfloat16)
    query_grad = (
        jnp.einsum("bhqk,bkhd->bqhd", score_grad, keys_rot, preferred_element_type=jnp.float32)
        * SCALE
    )
    key_grad = (
        jnp.einsum("bhqk,bqhd->bkhd", score_grad, queries, preferred_element_type=jnp.float32)
        * SCALE
    )
    return (query_grad, key_grad, value_grad)


def sum_over_line(partial):
    inward = lax.ppermute(partial, "sp", [(0, 1), (3, 2)])
    half = rounded(partial.astype(jnp.float32) + inward.astype(jnp.float32))
    other = lax.ppermute(half, "sp", [(1, 2), (2, 1)])
    whole = rounded(half.astype(jnp.float32) + other.astype(jnp.float32))
    outward = lax.ppermute(whole, "sp", [(1, 0), (2, 3)])
    place = lax.axis_index("sp")
    inner = (place == 1) | (place == 2)
    return jnp.where(inner, whole, outward).astype(jnp.float32)


def sum_over_sp(partial):
    partial = rounded(partial)
    if lax.axis_size("sp") == 4:
        return sum_over_line(partial)
    return lax.psum(partial, "sp").astype(jnp.float32)


def gather_kernel(x_ref, c_ref, xg_ref, cg_ref, held, s1, r1, s2, r2, s3, r3, local):
    f, s = lax.axis_index("fsdp"), lax.axis_index("sp")
    core, col, row = f % 2, (f // 2) % 2, f // 4
    f_x, f_y, f_c = f + 2 - 4 * col, f + 4 - 8 * row, f + 1 - 2 * core
    f_d = f_x + 4 - 8 * row
    piece = xg_ref.shape[3]
    barrier = pltpu.get_barrier_semaphore()
    for k in range(1, 8):
        pl.semaphore_signal(barrier, inc=1, device_id=((f + k) % 8, s), device_id_type=MESH)
    for k in range(1, 4):
        pl.semaphore_signal(barrier, inc=1, device_id=(f, (s + k) % 4), device_id_type=MESH)
    pl.semaphore_wait(barrier, 10)
    pairs = ((x_ref, xg_ref), (c_ref, cg_ref))
    sent = []

    def send(src, dst, send_sem, recv_sem, device):
        copy = pltpu.make_async_remote_copy(
            src_ref=src, dst_ref=dst, send_sem=send_sem, recv_sem=recv_sem,
            device_id=device, device_id_type=MESH,
        )
        copy.start()
        sent.append(copy)

    def arrived(ref, recv_sem):
        pltpu.make_async_remote_copy(
            src_ref=ref, dst_ref=ref, send_sem=s1.at[0, 0], recv_sem=recv_sem,
            device_id=(f_c, s), device_id_type=MESH,
        ).wait_recv()

    kept = []
    for a, (src, _) in enumerate(pairs):
        own = pltpu.make_async_copy(src.at[pl.ds(f * piece, piece)], held.at[a, f], local.at[a, 0])
        own.start()
        kept.append(own)
        for k in range(1, 8):
            j = (f + k) % 8
            send(src.at[pl.ds(j * piece, piece)], held.at[a, f], s1.at[a, k], r1.at[a, k], (j, s))

    def to_planes(a):
        out = pairs[a][1]
        kept[a].wait()
        for k in range(1, 8):
            arrived(held.at[a, (f + 8 - k) % 8], r1.at[a, k])
        for k in range(1, 4):
            plane = (s + k) % 4
            send(held.at[a, pl.ds(2 * plane, 2)], out.at[:, s, f], s2.at[a, k], r2.at[a, k], (f, plane))
        own = pltpu.make_async_copy(held.at[a, pl.ds(2 * s, 2)], out.at[:, s, f], local.at[a, 1])
        own.start()
        return own

    def spread(a, k):
        out = pairs[a][1]
        z = (s + 4 - k) % 4
        if k:
            arrived(out.at[:, z, f], r2.at[a, k])
        ref = out.at[:, z, f]
        send(ref, ref, s3.at[a, 0, k], r3.at[a, 0, k], (f_x, s))
        send(ref, ref, s3.at[a, 1, k], r3.at[a, 1, k], (f_y, s))
        send(ref, ref, s3.at[a, 2, k], r3.at[a, 2, k], (f_c, s))

    def pass_on(a, k):
        out = pairs[a][1]
        z = (s + 4 - k) % 4
        ref = out.at[:, z, f_x]
        arrived(ref, r3.at[a, 0, k])
        send(out.at[0, z, f_x], out.at[0, z, f_x], s3.at[a, 5, k], r3.at[a, 5, k], (f_y, s))
        send(ref, ref, s3.at[a, 3, k], r3.at[a, 3, k], (f_c, s))
        ref = out.at[:, z, f_y]
        arrived(ref, r3.at[a, 1, k])
        send(out.at[1, z, f_y], out.at[1, z, f_y], s3.at[a, 6, k], r3.at[a, 6, k], (f_x, s))
        send(ref, ref, s3.at[a, 4, k], r3.at[a, 4, k], (f_c, s))

    def pass_corner(a, k):
        out = pairs[a][1]
        z = (s + 4 - k) % 4
        for half in range(2):
            ref = out.at[half, z, f_d]
            arrived(ref, r3.at[a, 5 + half, k])
            send(ref, ref, s3.at[a, 7 + half, k], r3.at[a, 7 + half, k], (f_c, s))

    def from_core(a, k):
        out = pairs[a][1]
        z = (s + 4 - k) % 4
        g_x, g_y = f_c + 2 - 4 * col, f_c + 4 - 8 * row
        g_d = g_x + 4 - 8 * row
        arrived(out.at[:, z, f_c], r3.at[a, 2, k])
        arrived(out.at[:, z, g_x], r3.at[a, 3, k])
        arrived(out.at[:, z, g_y], r3.at[a, 4, k])
        for half in range(2):
            arrived(out.at[half, z, g_d], r3.at[a, 7 + half, k])

    own0 = to_planes(0)
    own1 = to_planes(1)
    steps = [(a, k) for a in range(2) for k in range(4)]
    for i in range(len(steps) + 2):
        if i < len(steps):
            a, k = steps[i]
            if k == 0:
                (own0 if a == 0 else own1).wait()
            spread(a, k)
        if 0 <= i - 1 < len(steps):
            pass_on(*steps[i - 1])
        if 0 <= i - 2 < len(steps):
            pass_corner(*steps[i - 2])
    for a, k in steps:
        from_core(a, k)
    for copy in sent:
        copy.wait_send()


def gather_both(x, c):
    rows, width = x.shape
    piece = rows // 8
    shape = jax.ShapeDtypeStruct((2, 4, 8, piece, width), x.dtype)
    dma = pltpu.SemaphoreType.DMA
    return pl.pallas_call(
        gather_kernel,
        out_shape=(shape, shape),
        in_specs=[pl.BlockSpec(memory_space=pl.ANY)] * 2,
        out_specs=[pl.BlockSpec(memory_space=pl.ANY)] * 2,
        scratch_shapes=[
            pltpu.VMEM((2, 8, piece, width), x.dtype),
            dma((2, 8)), dma((2, 8)), dma((2, 4)), dma((2, 4)), dma((2, 9, 4)), dma((2, 9, 4)), dma((2, 2)),
        ],
        compiler_params=pltpu.CompilerParams(collective_id=1, has_side_effects=True),
        name="gather_tokens",
    )(x, c)


def per_device(
    hidden_in,
    segments,
    ln1_gain,
    ln1_bias,
    ln2_gain,
    ln2_bias,
    w_qkv,
    b_qkv,
    w_dense,
    b_dense,
    w_up,
    b_up,
    w_down,
    b_down,
    cotangent,
):
    seq_local, shard_len, width = hidden_in.shape
    seq_len = segments.shape[1]
    nf, ns = lax.axis_size("fsdp"), lax.axis_size("sp")
    f_place, s_place = lax.axis_index("fsdp"), lax.axis_index("sp")
    seqs = seq_local * nf
    group = seqs // ns
    piece = shard_len // nf
    tokens = group * seq_len
    per_head = max(1, nf // HEADS)
    head_count = max(1, HEADS // nf)
    head_sets = [[head * per_head + k for k in range(per_head)] for head in range(nf // per_head)]

    def gather_tokens(block):
        part = lax.all_to_all(block, "fsdp", split_axis=1, concat_axis=0, tiled=True)
        part = lax.all_to_all(part, "sp", split_axis=0, concat_axis=1, tiled=True)
        return in_order(lax.all_gather(part, "fsdp", axis=0, tiled=True)).reshape(tokens, width)

    def scatter_tokens(partial):
        part = out_of_order(partial).reshape(nf * group, ns * piece, width)
        part = lax.psum_scatter(part, "fsdp", scatter_dimension=0, tiled=True)
        part = lax.all_to_all(part, "sp", split_axis=1, concat_axis=0, tiled=True)
        return lax.all_to_all(part, "fsdp", split_axis=0, concat_axis=1, tiled=True)

    def in_order(array):
        array = array.reshape(nf, group, ns, piece, -1)
        return array.transpose(1, 2, 0, 3, 4).reshape(group, seq_len, -1)

    def out_of_order(array):
        array = array.reshape(group, ns, nf, piece, -1)
        return array.transpose(2, 0, 1, 3, 4).reshape(tokens, -1)

    def over_head(array, axis):
        if per_head == 1:
            return array
        return lax.all_gather(
            array, "fsdp", axis=axis, tiled=True, axis_index_groups=head_sets
        )

    def own_columns(array):
        if per_head == 1:
            return array
        share = array.shape[-1] // per_head
        return lax.dynamic_slice_in_dim(array, (f_place % per_head) * share, share, array.ndim - 1)

    def own_part(vector):
        share = vector.shape[0] // nf
        return lax.dynamic_slice_in_dim(vector, f_place * share, share, 0)

    if (nf, ns, seq_local) == (8, 4, 1):
        gathered, upstream = (
            array.reshape(tokens, width) for array in gather_both(hidden_in[0], cotangent[0])
        )
    else:
        gathered, upstream = gather_tokens(hidden_in), gather_tokens(cotangent)
    rows = lax.all_gather(segments, "fsdp", axis=0, tiled=True)
    rows = lax.dynamic_slice_in_dim(rows, s_place * group, group, 0)

    dense_in = lax.all_to_all(w_dense, "fsdp", split_axis=1, concat_axis=0, tiled=True)
    head_qkv = over_head(w_qkv, 0)
    head_dense = over_head(dense_in, 1)
    head_bias = lax.dynamic_slice_in_dim(
        b_qkv, (f_place // per_head) * head_qkv.shape[0], head_qkv.shape[0], 0
    )

    scaled, _ = norm_scaled(gathered.astype(jnp.float32))
    normed = (scaled * ln1_gain + ln1_bias).astype(jnp.bfloat16)
    normed_mlp = (scaled * ln2_gain + ln2_bias).astype(jnp.bfloat16)

    hidden = times_transposed(normed_mlp, w_up) + own_part(b_up)
    activated, slope = gelu_pair(hidden)
    activated = activated.astype(jnp.bfloat16)
    hidden_grad = (times_transposed(upstream, w_down) * slope).astype(jnp.bfloat16)
    down_term = contract_rows(activated, upstream)
    up_term = contract_rows(hidden_grad, normed_mlp)
    mlp_norm_grad = times(hidden_grad, w_up)

    packed = (times_transposed(normed, head_qkv) + head_bias).astype(jnp.bfloat16)
    packed = packed.reshape(group, seq_len, head_count, 3 * HEAD_DIM)
    cos_table, sin_table = rotary_tables(rows)
    queries = rotate(packed[..., :HEAD_DIM].astype(jnp.float32), cos_table, sin_table).astype(
        jnp.bfloat16
    )
    keys_rot = rotate(
        packed[..., HEAD_DIM : 2 * HEAD_DIM].astype(jnp.float32), cos_table, sin_table
    ).astype(jnp.bfloat16)
    values = packed[..., 2 * HEAD_DIM :]
    mask = build_mask(rows)
    context, log_total = attend_forward(queries, keys_rot, values, mask)
    context = own_columns(context.reshape(tokens, -1))
    partial_out = times_transposed(context, dense_in) + times(activated, w_down)
    context_grad = times(upstream, head_dense).astype(jnp.bfloat16).reshape(
        group, seq_len, head_count, HEAD_DIM
    )
    query_grad, key_grad, value_grad = attend_backward(
        queries, keys_rot, values, mask, log_total, context_grad
    )
    packed_grad = jnp.concatenate(
        [
            unrotate(query_grad, cos_table, sin_table),
            unrotate(key_grad, cos_table, sin_table),
            value_grad,
        ],
        axis=-1,
    ).astype(jnp.bfloat16)
    packed_grad = own_columns(packed_grad.reshape(tokens, -1))
    attn_norm_grad = times(packed_grad, w_qkv)
    qkv_term = contract_rows(packed_grad, normed)
    dense_term = contract_rows(upstream, context).astype(jnp.bfloat16)
    dense_term = lax.all_to_all(dense_term, "fsdp", split_axis=0, concat_axis=1, tiled=True)

    vectors = jnp.stack(
        [
            jnp.sum(attn_norm_grad * scaled, axis=0),
            jnp.sum(attn_norm_grad, axis=0),
            jnp.sum(mlp_norm_grad * scaled, axis=0),
            jnp.sum(mlp_norm_grad, axis=0),
        ],
        axis=1,
    )
    vectors = lax.psum_scatter(vectors, "fsdp", scatter_dimension=0, tiled=True)
    bias_out = own_part(jnp.sum(upstream.astype(jnp.float32), axis=0))
    bias_qkv = jnp.sum(packed_grad.astype(jnp.float32), axis=0)
    bias_up = jnp.sum(hidden_grad.astype(jnp.float32), axis=0)
    vectors, bias_out, bias_qkv, bias_up = lax.psum((vectors, bias_out, bias_qkv, bias_up), "sp")

    output = scatter_tokens(rounded(partial_out))
    weighted = scatter_tokens(rounded(attn_norm_grad * ln1_gain + mlp_norm_grad * ln2_gain))
    inputs = hidden_in.astype(jnp.float32)
    output = (inputs + (output.astype(jnp.float32) + (b_dense + b_down))).astype(jnp.bfloat16)
    own_scaled, own_inverse = norm_scaled(inputs)
    weighted = weighted.astype(jnp.float32)
    first_mean = jnp.mean(weighted, axis=-1, keepdims=True)
    second_mean = jnp.mean(weighted * own_scaled, axis=-1, keepdims=True)
    input_grad = (
        cotangent.astype(jnp.float32)
        + own_inverse * (weighted - first_mean - own_scaled * second_mean)
    ).astype(jnp.bfloat16)

    grad_down_w = sum_over_sp(down_term)
    grad_up_w = sum_over_sp(up_term)
    grad_qkv_w = sum_over_sp(qkv_term)
    grad_dense_w = sum_over_sp(dense_term)
    return (
        output,
        input_grad,
        vectors[:, 0],
        vectors[:, 1],
        vectors[:, 2],
        vectors[:, 3],
        grad_qkv_w,
        bias_qkv,
        grad_dense_w,
        bias_out,
        grad_up_w,
        bias_up,
        grad_down_w,
        bias_out,
    )


def solution(mesh):
    rows = P("fsdp", "sp", None)
    first = P("fsdp", None)
    return jax.shard_map(
        per_device,
        mesh=mesh,
        in_specs=(
            rows,
            first,
            P(),
            P(),
            P(),
            P(),
            first,
            P(),
            first,
            P(),
            first,
            P(),
            first,
            P(),
            rows,
        ),
        out_specs=(
            rows,
            rows,
            P("fsdp"),
            P("fsdp"),
            P("fsdp"),
            P("fsdp"),
            first,
            P("fsdp"),
            first,
            P("fsdp"),
            first,
            P("fsdp"),
            first,
            P("fsdp"),
        ),
        check_vma=False,
    )
```

```python
import functools
import math

import jax
import jax.numpy as jnp
from jax import lax
from jax.experimental import pallas as pl
from jax.experimental.pallas import tpu as pltpu
from jax.sharding import PartitionSpec as P

MESH = pl.DeviceIdType.MESH

HEADS = 8
HEAD_DIM = 256
ROT = 64


EPSILON = 1e-05
NEGATIVE = -1e30
ROOT_HALF = 0.7071067811865476
ROOT_TWO_PI = 2.5066282746310002
SCALE = 1.0 / math.sqrt(HEAD_DIM)


def rounded(array):
    return lax.reduce_precision(array.astype(jnp.float32), 8, 7).astype(jnp.bfloat16)


def contract_rows(former, latter):
    return lax.dot_general(
        former, latter, (((0,), (0,)), ((), ())), preferred_element_type=jnp.float32
    )


def times_transposed(former, latter):
    return lax.dot_general(
        former, latter, (((1,), (1,)), ((), ())), preferred_element_type=jnp.float32
    )


def times(former, latter):
    return jnp.dot(former, latter, preferred_element_type=jnp.float32)


def norm_scaled(inputs):
    average = jnp.mean(inputs, axis=-1, keepdims=True)
    centred = inputs - average
    variance = jnp.mean(centred * centred, axis=-1, keepdims=True)
    inverse = lax.rsqrt(variance + EPSILON)
    return centred * inverse, inverse


def gelu_pair(hidden):
    cumulative = 0.5 * (1.0 + jax.scipy.special.erf(hidden * ROOT_HALF))
    return (
        hidden * cumulative,
        cumulative + hidden * jnp.exp(-0.5 * hidden * hidden) / ROOT_TWO_PI,
    )


def rotary_tables(segment_rows):
    length = segment_rows.shape[-1]
    places = jnp.arange(length, dtype=jnp.int32)
    changes = jnp.concatenate(
        [
            jnp.ones_like(segment_rows[..., :1]),
            (segment_rows[..., 1:] != segment_rows[..., :-1]).astype(jnp.int32),
        ],
        axis=-1,
    )
    first_place = lax.cummax(changes * places, axis=segment_rows.ndim - 1)
    position = (places - first_place).astype(jnp.float32)
    exponent = jnp.arange(0, ROT, 2).astype(jnp.float32) / ROT
    frequency = 1.0 / jnp.power(10000.0, exponent)
    angles = position[..., None] * frequency
    angles = jnp.concatenate([angles, angles], axis=-1)
    return (jnp.cos(angles), jnp.sin(angles))


def rotate(heads_part, cos_table, sin_table):
    half_rot = ROT // 2
    turned = heads_part[..., :ROT]
    swapped = jnp.concatenate([-turned[..., half_rot:], turned[..., :half_rot]], axis=-1)
    turned = turned * cos_table[..., None, :] + swapped * sin_table[..., None, :]
    return jnp.concatenate([turned, heads_part[..., ROT:]], axis=-1)


def unrotate(grads_part, cos_table, sin_table):
    half_rot = ROT // 2
    turned = grads_part[..., :ROT]
    along_sin = turned * sin_table[..., None, :]
    back_turn = jnp.concatenate([along_sin[..., half_rot:], -along_sin[..., :half_rot]], axis=-1)
    turned = turned * cos_table[..., None, :] + back_turn
    return jnp.concatenate([turned, grads_part[..., ROT:]], axis=-1)


def build_mask(segment_rows):
    places = jnp.arange(segment_rows.shape[-1], dtype=jnp.int32)
    return (segment_rows[:, :, None] == segment_rows[:, None, :]) & (
        places[None, :] <= places[:, None]
    )


def attention_scores(queries, keys_rot):
    return (
        jnp.einsum("bqhd,bkhd->bhqk", queries, keys_rot, preferred_element_type=jnp.float32) * SCALE
    )


def attend_forward(queries, keys_rot, values, mask):
    scores = jnp.where(mask[:, None], attention_scores(queries, keys_rot), NEGATIVE)
    row_top = jnp.max(scores, axis=-1, keepdims=True)
    exponent = jnp.exp(scores - row_top)
    row_total = jnp.sum(exponent, axis=-1, keepdims=True)
    attention = (exponent / row_total).astype(jnp.bfloat16)
    context = jnp.einsum("bhqk,bkhd->bqhd", attention, values, preferred_element_type=jnp.float32)
    return (context.astype(jnp.bfloat16), row_top + jnp.log(row_total))


def attend_backward(queries, keys_rot, values, mask, log_total, context_grad):
    scores = attention_scores(queries, keys_rot)
    attention = jnp.where(mask[:, None], jnp.exp(scores - log_total), 0.0)
    value_grad = jnp.einsum(
        "bhqk,bqhd->bkhd",
        attention.astype(jnp.bfloat16),
        context_grad,
        preferred_element_type=jnp.float32,
    )
    attention_grad = jnp.einsum(
        "bqhd,bkhd->bhqk", context_grad, values, preferred_element_type=jnp.float32
    )
    row_centre = jnp.sum(attention * attention_grad, axis=-1, keepdims=True)
    score_grad = (attention * (attention_grad - row_centre)).astype(jnp.bfloat16)
    query_grad = (
        jnp.einsum("bhqk,bkhd->bqhd", score_grad, keys_rot, preferred_element_type=jnp.float32)
        * SCALE
    )
    key_grad = (
        jnp.einsum("bhqk,bqhd->bkhd", score_grad, queries, preferred_element_type=jnp.float32)
        * SCALE
    )
    return (query_grad, key_grad, value_grad)


def gather_kernel(x_ref, c_ref, xg_ref, cg_ref, held, s1, r1, s2, r2, s3, r3, local):
    f, s = lax.axis_index("fsdp"), lax.axis_index("sp")
    core, col, row = f % 2, (f // 2) % 2, f // 4
    f_x, f_y, f_c = f + 2 - 4 * col, f + 4 - 8 * row, f + 1 - 2 * core
    f_d = f_x + 4 - 8 * row
    piece = xg_ref.shape[3]
    barrier = pltpu.get_barrier_semaphore()
    for k in range(1, 8):
        pl.semaphore_signal(barrier, inc=1, device_id=((f + k) % 8, s), device_id_type=MESH)
    for k in range(1, 4):
        pl.semaphore_signal(barrier, inc=1, device_id=(f, (s + k) % 4), device_id_type=MESH)
    pl.semaphore_wait(barrier, 10)
    pairs = ((x_ref, xg_ref), (c_ref, cg_ref))
    sent = []

    def send(src, dst, send_sem, recv_sem, device):
        copy = pltpu.make_async_remote_copy(
            src_ref=src, dst_ref=dst, send_sem=send_sem, recv_sem=recv_sem,
            device_id=device, device_id_type=MESH,
        )
        copy.start()
        sent.append(copy)

    def arrived(ref, recv_sem):
        pltpu.make_async_remote_copy(
            src_ref=ref, dst_ref=ref, send_sem=s1.at[0, 0], recv_sem=recv_sem,
            device_id=(f_c, s), device_id_type=MESH,
        ).wait_recv()

    kept = []
    for a, (src, _) in enumerate(pairs):
        own = pltpu.make_async_copy(src.at[pl.ds(f * piece, piece)], held.at[a, f], local.at[a, 0])
        own.start()
        kept.append(own)
        for k in range(1, 8):
            j = (f + k) % 8
            send(src.at[pl.ds(j * piece, piece)], held.at[a, f], s1.at[a, k], r1.at[a, k], (j, s))

    def to_planes(a):
        out = pairs[a][1]
        kept[a].wait()
        for k in range(1, 8):
            arrived(held.at[a, (f + 8 - k) % 8], r1.at[a, k])
        for k in range(1, 4):
            plane = (s + k) % 4
            send(held.at[a, pl.ds(2 * plane, 2)], out.at[:, s, f], s2.at[a, k], r2.at[a, k], (f, plane))
        own = pltpu.make_async_copy(held.at[a, pl.ds(2 * s, 2)], out.at[:, s, f], local.at[a, 1])
        own.start()
        return own

    def spread(a, k):
        out = pairs[a][1]
        z = (s + 4 - k) % 4
        if k:
            arrived(out.at[:, z, f], r2.at[a, k])
        ref = out.at[:, z, f]
        send(ref, ref, s3.at[a, 0, k], r3.at[a, 0, k], (f_x, s))
        send(ref, ref, s3.at[a, 1, k], r3.at[a, 1, k], (f_y, s))
        send(ref, ref, s3.at[a, 2, k], r3.at[a, 2, k], (f_c, s))

    def pass_on(a, k):
        out = pairs[a][1]
        z = (s + 4 - k) % 4
        ref = out.at[:, z, f_x]
        arrived(ref, r3.at[a, 0, k])
        send(out.at[0, z, f_x], out.at[0, z, f_x], s3.at[a, 5, k], r3.at[a, 5, k], (f_y, s))
        send(ref, ref, s3.at[a, 3, k], r3.at[a, 3, k], (f_c, s))
        ref = out.at[:, z, f_y]
        arrived(ref, r3.at[a, 1, k])
        send(out.at[1, z, f_y], out.at[1, z, f_y], s3.at[a, 6, k], r3.at[a, 6, k], (f_x, s))
        send(ref, ref, s3.at[a, 4, k], r3.at[a, 4, k], (f_c, s))

    def pass_corner(a, k):
        out = pairs[a][1]
        z = (s + 4 - k) % 4
        for half in range(2):
            ref = out.at[half, z, f_d]
            arrived(ref, r3.at[a, 5 + half, k])
            send(ref, ref, s3.at[a, 7 + half, k], r3.at[a, 7 + half, k], (f_c, s))

    def from_core(a, k):
        out = pairs[a][1]
        z = (s + 4 - k) % 4
        g_x, g_y = f_c + 2 - 4 * col, f_c + 4 - 8 * row
        g_d = g_x + 4 - 8 * row
        arrived(out.at[:, z, f_c], r3.at[a, 2, k])
        arrived(out.at[:, z, g_x], r3.at[a, 3, k])
        arrived(out.at[:, z, g_y], r3.at[a, 4, k])
        for half in range(2):
            arrived(out.at[half, z, g_d], r3.at[a, 7 + half, k])

    own0 = to_planes(0)
    own1 = to_planes(1)
    steps = [(a, k) for a in range(2) for k in range(4)]
    for i in range(len(steps) + 2):
        if i < len(steps):
            a, k = steps[i]
            if k == 0:
                (own0 if a == 0 else own1).wait()
            spread(a, k)
        if 0 <= i - 1 < len(steps):
            pass_on(*steps[i - 1])
        if 0 <= i - 2 < len(steps):
            pass_corner(*steps[i - 2])
    for a, k in steps:
        from_core(a, k)
    for copy in sent:
        copy.wait_send()


def gather_both(x, c):
    rows, width = x.shape
    piece = rows // 8
    shape = jax.ShapeDtypeStruct((2, 4, 8, piece, width), x.dtype)
    dma = pltpu.SemaphoreType.DMA
    return pl.pallas_call(
        gather_kernel,
        out_shape=(shape, shape),
        in_specs=[pl.BlockSpec(memory_space=pl.ANY)] * 2,
        out_specs=[pl.BlockSpec(memory_space=pl.ANY)] * 2,
        scratch_shapes=[
            pltpu.VMEM((2, 8, piece, width), x.dtype),
            dma((2, 8)), dma((2, 8)), dma((2, 4)), dma((2, 4)), dma((2, 9, 4)), dma((2, 9, 4)), dma((2, 2)),
        ],
        compiler_params=pltpu.CompilerParams(collective_id=1, has_side_effects=True),
        name="gather_tokens",
    )(x, c)


def reduce_kernel(
    sizes, steps,
    down_ref, up_ref, qkv_ref, dense_ref, out_ref, back_ref, vec_ref, bias_ref,
    g_down, g_up, g_qkv, g_dense, o_out, o_back, o_small,
    line_a, line_b, turned, own, paired, block, crossed, reduced, homed, vec_in, small, small_in,
    in_s, in_r, mid_s, mid_r, end_s, end_r, own_l, keep_l,
    turn_s, turn_r, pair_s, pair_r, block_l, cross_s, cross_r, home_s, home_r, back_s, back_r, local,
    vec_s, vec_r, small_s, small_r,
):
    f, s = lax.axis_index("fsdp"), lax.axis_index("sp")
    core, col, row = f % 2, (f // 2) % 2, f // 4
    f_x, f_y, f_c = f + 2 - 4 * col, f + 4 - 8 * row, f + 1 - 2 * core
    f_d = f_x + 4 - 8 * row
    is_end = (s == 0) | (s == 3)
    is_mid = (s == 1) | (s == 2)
    inner = 1 + s // 3
    outer = 3 * (s // 2)
    facing = 3 - s
    barrier = pltpu.get_barrier_semaphore()
    for k in range(1, 8):
        pl.semaphore_signal(barrier, inc=1, device_id=((f + k) % 8, s), device_id_type=MESH)
    for k in range(1, 4):
        pl.semaphore_signal(barrier, inc=1, device_id=(f, (s + k) % 4), device_id_type=MESH)
    pl.semaphore_wait(barrier, 10)
    sent = []

    def send(src, dst, send_sem, recv_sem, device, track=True):
        copy = pltpu.make_async_remote_copy(
            src_ref=src, dst_ref=dst, send_sem=send_sem, recv_sem=recv_sem,
            device_id=device, device_id_type=MESH,
        )
        copy.start()
        if track:
            sent.append(copy)
        return copy

    def arrived(ref, recv_sem):
        pltpu.make_async_remote_copy(
            src_ref=ref, dst_ref=ref, send_sem=vec_s.at[0], recv_sem=recv_sem,
            device_id=(f_c, s), device_id_type=MESH,
        ).wait_recv()

    def copied(src, dst, sem):
        copy = pltpu.make_async_copy(src, dst, sem)
        copy.start()
        return copy

    part = turned.shape[0]
    span = dense_ref.shape[1]
    columns = pl.ds(pl.multiple_of(f * span, span), span)
    vec_own = copied(vec_ref.at[f], vec_in.at[f], local.at[0])
    turn_own = copied(dense_ref.at[pl.ds(f * part, part)], turned.at[:, columns], local.at[1])
    bias_own = copied(bias_ref, small.at[pl.ds(8, 8)], local.at[2])
    for k in range(1, 8):
        j = (f + k) % 8
        send(vec_ref.at[j], vec_in.at[f], vec_s.at[k], vec_r.at[k], (j, s))

    chunks = []
    offset = 0
    for ref, result, rows_of in (
        (down_ref, g_down, sizes[0]), (up_ref, g_up, sizes[1]), (qkv_ref, g_qkv, sizes[2]), (turned, g_dense, sizes[3]),
    ):
        first = 0
        for rows in rows_of:
            chunks.append((ref, result, first, rows, offset))
            first += rows
            offset += rows
    count = len(chunks)
    ahead = 5

    def from_end(k):
        ref, _, first, rows, at = chunks[k]
        return pltpu.make_async_remote_copy(
            src_ref=ref.at[pl.ds(first, rows)], dst_ref=line_a.at[pl.ds(at, rows)],
            send_sem=in_s.at[k], recv_sem=in_r.at[k], device_id=(f, inner), device_id_type=MESH,
        )

    def across(k):
        _, _, _, rows, at = chunks[k]
        return pltpu.make_async_remote_copy(
            src_ref=line_a.at[pl.ds(at, rows)], dst_ref=line_b.at[pl.ds(at, rows)],
            send_sem=mid_s.at[k], recv_sem=mid_r.at[k], device_id=(f, facing), device_id_type=MESH,
        )

    def to_end(k):
        _, result, first, rows, at = chunks[k]
        return pltpu.make_async_remote_copy(
            src_ref=line_b.at[pl.ds(at, rows)], dst_ref=result.at[pl.ds(first, rows)],
            send_sem=end_s.at[k], recv_sem=end_r.at[k], device_id=(f, outer), device_id_type=MESH,
        )

    def load_own(k):
        ref, _, first, rows, _ = chunks[k]
        return pltpu.make_async_copy(
            ref.at[pl.ds(first, rows)], own.at[k % 3, pl.ds(0, rows)], own_l.at[k % 3]
        )

    def keep(k):
        _, result, first, rows, at = chunks[k]
        return pltpu.make_async_copy(
            line_b.at[pl.ds(at, rows)], result.at[pl.ds(first, rows)], keep_l.at[k]
        )

    tile = 16

    def add_rows(target, target_at, left, left_at, right, rows):
        @pl.loop(0, rows // tile)
        def _(i):
            at = pl.multiple_of(i * tile, tile)
            total = (
                left[pl.ds(left_at + at, tile), :].astype(jnp.float32)
                + right[pl.ds(at, tile), :].astype(jnp.float32)
            )
            target[pl.ds(target_at + at, tile), :] = total.astype(target.dtype)

    def mid_in(k):
        _, _, _, rows, at = chunks[k]
        load_own(k).wait()
        from_end(k).wait_recv()
        add_rows(line_a, at, line_a, at, own.at[k % 3], rows)
        across(k).start()
        if k + 3 < count:
            load_own(k + 3).start()

    def mid_out(k):
        _, _, _, rows, at = chunks[k]
        across(k).wait_recv()
        add_rows(line_b, at, line_b, at, line_a.at[pl.ds(at, rows)], rows)
        to_end(k).start()
        keep(k).start()

    pairs = ((out_ref, o_out), (back_ref, o_back))
    order = (f_d // 2, f_x // 2, f_y // 2, f // 2)
    for a, (ref, _) in enumerate(pairs):
        for n, q in enumerate(order):
            send(ref.at[:, :, q, 1 - core], paired.at[a, n], pair_s.at[a, n], pair_r.at[a, n], (f_c, s))
    for k in range(1, 8):
        j = (f + k) % 8
        send(dense_ref.at[pl.ds(j * part, part)], turned.at[:, columns], turn_s.at[k], turn_r.at[k], (j, s))

    def load_block(i):
        a, n = i // 4, i % 4
        return pltpu.make_async_copy(
            pairs[a][0].at[:, :, order[n], core], block.at[i % 2], block_l.at[i % 2]
        )

    load_block(0).start()
    load_block(1).start()

    def add_pair(i):
        a, n = i // 4, i % 4
        load_block(i).wait()
        arrived(paired.at[a, n], pair_r.at[a, n])

        @pl.loop(0, 8)
        def _(m):
            b, z = m // 4, m % 4
            total = paired[a, n, b, z].astype(jnp.float32) + block[i % 2, b, z].astype(jnp.float32)
            paired[a, n, b, z] = total.astype(paired.dtype)

        if n < 3:
            send(paired.at[a, n], crossed.at[a, n], cross_s.at[a, n], cross_r.at[a, n], ((f_d, f_x, f_y)[n], s))
        if i + 2 < 8:
            load_block(i + 2).start()

    placed = {}

    def add_chips(a):
        for n in range(3):
            arrived(crossed.at[a, n], cross_r.at[a, n])

        @pl.loop(0, 8)
        def _(m):
            b, z = m // 4, m % 4
            total = paired[a, 3, b, z].astype(jnp.float32)
            for n in range(3):
                total = total + crossed[a, n, b, z].astype(jnp.float32)
            reduced[a, b, z] = total.astype(reduced.dtype)

        for k in range(1, 4):
            z = (s + k) % 4
            send(reduced.at[a, :, z], homed.at[a, s], home_s.at[a, k], home_r.at[a, k], (f, z))
        placed["along", a] = copied(reduced.at[a, :, s], homed.at[a, s], local.at[3 + a])

    def go_home(a):
        result = pairs[a][1]
        placed["along", a].wait()
        for k in range(1, 4):
            arrived(homed.at[a, (s + 4 - k) % 4], home_r.at[a, k])
        for k in range(1, 8):
            j = (f + k) % 8
            send(homed.at[a, j // 2, j % 2], result.at[f], back_s.at[a, k], back_r.at[a, k], (j, s))
        placed["home", a] = copied(homed.at[a, f // 2, core], result.at[f], local.at[5 + a])

    def add_vectors():
        vec_own.wait()
        bias_own.wait()
        for k in range(1, 8):
            arrived(vec_in.at[(f + 8 - k) % 8], vec_r.at[k])
        total = vec_in[0]
        for j in range(1, 8):
            total = total + vec_in[j]
        small[0:8, :] = total
        for k in range(1, 4):
            send(small, small_in.at[s], small_s.at[k], small_r.at[k], (f, (s + k) % 4))
        placed["small"] = copied(small, small_in.at[s], local.at[7])

    def add_small():
        placed["small"].wait()
        for k in range(1, 4):
            arrived(small_in.at[(s + 4 - k) % 4], small_r.at[k])
        total = small_in[0]
        for z in range(1, 4):
            total = total + small_in[z]
        o_small[...] = total

    def turn_done():
        turn_own.wait()
        for k in range(1, 8):
            j = (f + 8 - k) % 8
            at = pl.ds(pl.multiple_of(j * span, span), span)
            arrived(turned.at[:, at], turn_r.at[k])

    def tasks(name):
        if name == "vec":
            add_vectors()
        elif name == "small":
            add_small()
        elif name == "turn":
            turn_done()
        elif name[0] == "p":
            add_pair(int(name[1:]))
        elif name[0] == "c":
            add_chips(int(name[1:]))
        elif name[0] == "h":
            go_home(int(name[1:]))

    @pl.when(is_end)
    def _():
        for k in range(ahead):
            from_end(k).start()

    @pl.when(is_mid)
    def _():
        for k in range(3):
            load_own(k).start()

    for k in range(count + 1):
        for name in steps.get(k, ()):
            tasks(name)

        @pl.when(is_mid)
        def _():
            if k < count:
                mid_in(k)
            if k >= 1:
                mid_out(k - 1)

        @pl.when(is_end)
        def _():
            if k >= 1:
                to_end(k - 1).wait_recv()
                if k - 1 + ahead < count:
                    from_end(k - 1 + ahead).start()

    for name in steps.get(count + 1, ()):
        tasks(name)
    for a in range(2):
        placed["home", a].wait()
        for k in range(1, 8):
            arrived(pairs[a][1].at[(f + 8 - k) % 8], back_r.at[a, k])
    for copy in sent:
        copy.wait_send()

    @pl.when(is_end)
    def _():
        for k in range(count):
            from_end(k).wait_send()

    @pl.when(is_mid)
    def _():
        for k in range(count):
            across(k).wait_send()
            to_end(k).wait_send()
            keep(k).wait()


STEPS = {
    0: ("p0", "p1", "p2", "p3", "vec"),
    1: ("p4", "p5"),
    2: ("p6", "p7"),
    3: ("small",),
    5: ("c0",),
    7: ("h0",),
    8: ("c1", "turn"),
    10: ("h1",),
}


def reduce_all(down, up, qkv, dense, out_part, back_part, vec, bias, sizes, steps=STEPS):
    width = down.shape[1]
    dtype = down.dtype
    total = sum(sum(rows) for rows in sizes)
    count = sum(len(rows) for rows in sizes)
    largest = max(max(rows) for rows in sizes)
    piece = out_part.shape[4]
    dma = pltpu.SemaphoreType.DMA
    grads = [jax.ShapeDtypeStruct((sum(rows), width), dtype) for rows in sizes]
    token = jax.ShapeDtypeStruct((8, piece, width), dtype)
    span = dense.shape[1]
    anywhere = pl.BlockSpec(memory_space=pl.ANY)
    vmem = pltpu.VMEM
    return pl.pallas_call(
        functools.partial(reduce_kernel, sizes, steps),
        out_shape=(*grads, token, token, jax.ShapeDtypeStruct((16, vec.shape[2]), jnp.float32)),
        in_specs=[anywhere] * 8,
        out_specs=[anywhere] * 6 + [pl.BlockSpec(memory_space=pltpu.VMEM)],
        scratch_shapes=[
            vmem((total, width), dtype), vmem((total, width), dtype), vmem((sum(sizes[3]), width), dtype),
            vmem((3, largest, width), dtype),
            vmem((2, 4, 2, 4, piece, width), dtype), vmem((2, 2, 4, piece, width), dtype),
            vmem((2, 3, 2, 4, piece, width), dtype), vmem((2, 2, 4, piece, width), dtype),
            vmem((2, 4, 2, piece, width), dtype),
            vmem((8, 8, vec.shape[2]), jnp.float32), vmem((16, vec.shape[2]), jnp.float32),
            vmem((4, 16, vec.shape[2]), jnp.float32),
            dma((count,)), dma((count,)), dma((count,)), dma((count,)), dma((count,)), dma((count,)),
            dma((3,)), dma((count,)),
            dma((8,)), dma((8,)), dma((2, 4)), dma((2, 4)), dma((2,)), dma((2, 3)), dma((2, 3)),
            dma((2, 4)), dma((2, 4)), dma((2, 8)), dma((2, 8)), dma((8,)),
            dma((8,)), dma((8,)), dma((4,)), dma((4,)),
        ],
        compiler_params=pltpu.CompilerParams(
            collective_id=2, has_side_effects=True, vmem_limit_bytes=60 * 1024 * 1024
        ),
        name="reduce_all",
    )(down, up, qkv, dense, out_part, back_part, vec, bias)


def cut(rows, unit, first=False, last=False):
    sizes = [4 * unit] * (rows // (4 * unit))
    if first:
        sizes[:1] = [unit, unit, 2 * unit]
    if last:
        sizes[-1:] = [2 * unit, unit, unit]
    return tuple(sizes)


def reduce_tokens(terms, partial_out, partial_back, vectors, biases):
    down, up, qkv, dense = (term.astype(jnp.bfloat16) for term in terms)
    sizes = (
        cut(down.shape[0], 64, first=True),
        cut(up.shape[0], 64),
        cut(qkv.shape[0], 64),
        cut(dense.shape[0] // 8, 64, last=True),
    )
    *grads, output, weighted, sums = reduce_all(
        down,
        up,
        qkv,
        dense,
        partial_out.astype(jnp.bfloat16),
        partial_back.astype(jnp.bfloat16),
        vectors,
        biases,
        sizes,
    )
    return [grad.astype(jnp.float32) for grad in grads], output, weighted, sums


def per_device(
    hidden_in,
    segments,
    ln1_gain,
    ln1_bias,
    ln2_gain,
    ln2_bias,
    w_qkv,
    b_qkv,
    w_dense,
    b_dense,
    w_up,
    b_up,
    w_down,
    b_down,
    cotangent,
):
    seq_local, shard_len, width = hidden_in.shape
    seq_len = segments.shape[1]
    nf, ns = lax.axis_size("fsdp"), lax.axis_size("sp")
    f_place, s_place = lax.axis_index("fsdp"), lax.axis_index("sp")
    seqs = seq_local * nf
    group = seqs // ns
    piece = shard_len // nf
    tokens = group * seq_len
    per_head = max(1, nf // HEADS)
    head_count = max(1, HEADS // nf)
    head_sets = [[head * per_head + k for k in range(per_head)] for head in range(nf // per_head)]

    def gather_tokens(block):
        part = lax.all_to_all(block, "fsdp", split_axis=1, concat_axis=0, tiled=True)
        part = lax.all_to_all(part, "sp", split_axis=0, concat_axis=1, tiled=True)
        return in_order(lax.all_gather(part, "fsdp", axis=0, tiled=True)).reshape(tokens, width)

    def scatter_tokens(partial):
        part = out_of_order(partial).reshape(nf * group, ns * piece, width)
        part = lax.psum_scatter(part, "fsdp", scatter_dimension=0, tiled=True)
        part = lax.all_to_all(part, "sp", split_axis=1, concat_axis=0, tiled=True)
        return lax.all_to_all(part, "fsdp", split_axis=0, concat_axis=1, tiled=True)

    def in_order(array):
        array = array.reshape(nf, group, ns, piece, -1)
        return array.transpose(1, 2, 0, 3, 4).reshape(group, seq_len, -1)

    def out_of_order(array):
        array = array.reshape(group, ns, nf, piece, -1)
        return array.transpose(2, 0, 1, 3, 4).reshape(tokens, -1)

    def over_head(array, axis):
        if per_head == 1:
            return array
        return lax.all_gather(
            array, "fsdp", axis=axis, tiled=True, axis_index_groups=head_sets
        )

    def own_columns(array):
        if per_head == 1:
            return array
        share = array.shape[-1] // per_head
        return lax.dynamic_slice_in_dim(array, (f_place % per_head) * share, share, array.ndim - 1)

    def own_part(vector):
        share = vector.shape[0] // nf
        return lax.dynamic_slice_in_dim(vector, f_place * share, share, 0)

    fast = (nf, ns, seq_local, HEADS) == (8, 4, 1, 8)
    if fast:
        gathered, upstream = (
            array.reshape(tokens, width) for array in gather_both(hidden_in[0], cotangent[0])
        )
    else:
        gathered, upstream = gather_tokens(hidden_in), gather_tokens(cotangent)
    rows = lax.all_gather(segments, "fsdp", axis=0, tiled=True)
    rows = lax.dynamic_slice_in_dim(rows, s_place * group, group, 0)

    dense_in = lax.all_to_all(w_dense, "fsdp", split_axis=1, concat_axis=0, tiled=True)
    head_qkv = over_head(w_qkv, 0)
    head_dense = over_head(dense_in, 1)
    head_bias = lax.dynamic_slice_in_dim(
        b_qkv, (f_place // per_head) * head_qkv.shape[0], head_qkv.shape[0], 0
    )

    scaled, _ = norm_scaled(gathered.astype(jnp.float32))
    normed = (scaled * ln1_gain + ln1_bias).astype(jnp.bfloat16)
    normed_mlp = (scaled * ln2_gain + ln2_bias).astype(jnp.bfloat16)

    hidden = times_transposed(normed_mlp, w_up) + own_part(b_up)
    activated, slope = gelu_pair(hidden)
    activated = activated.astype(jnp.bfloat16)
    hidden_grad = (times_transposed(upstream, w_down) * slope).astype(jnp.bfloat16)
    down_term = contract_rows(activated, upstream)
    up_term = contract_rows(hidden_grad, normed_mlp)
    mlp_norm_grad = times(hidden_grad, w_up)

    packed = (times_transposed(normed, head_qkv) + head_bias).astype(jnp.bfloat16)
    packed = packed.reshape(group, seq_len, head_count, 3 * HEAD_DIM)
    cos_table, sin_table = rotary_tables(rows)
    queries = rotate(packed[..., :HEAD_DIM].astype(jnp.float32), cos_table, sin_table).astype(
        jnp.bfloat16
    )
    keys_rot = rotate(
        packed[..., HEAD_DIM : 2 * HEAD_DIM].astype(jnp.float32), cos_table, sin_table
    ).astype(jnp.bfloat16)
    values = packed[..., 2 * HEAD_DIM :]
    mask = build_mask(rows)
    context, log_total = attend_forward(queries, keys_rot, values, mask)
    context = own_columns(context.reshape(tokens, -1))
    partial_out = times_transposed(context, dense_in) + times(activated, w_down)
    context_grad = times(upstream, head_dense).astype(jnp.bfloat16).reshape(
        group, seq_len, head_count, HEAD_DIM
    )
    query_grad, key_grad, value_grad = attend_backward(
        queries, keys_rot, values, mask, log_total, context_grad
    )
    packed_grad = jnp.concatenate(
        [
            unrotate(query_grad, cos_table, sin_table),
            unrotate(key_grad, cos_table, sin_table),
            value_grad,
        ],
        axis=-1,
    ).astype(jnp.bfloat16)
    packed_grad = own_columns(packed_grad.reshape(tokens, -1))
    attn_norm_grad = times(packed_grad, w_qkv)
    qkv_term = contract_rows(packed_grad, normed)
    dense_term = contract_rows(upstream, context).astype(jnp.bfloat16)

    partial_back = attn_norm_grad * ln1_gain + mlp_norm_grad * ln2_gain
    vectors = jnp.stack(
        [
            jnp.sum(attn_norm_grad * scaled, axis=0),
            jnp.sum(attn_norm_grad, axis=0),
            jnp.sum(mlp_norm_grad * scaled, axis=0),
            jnp.sum(mlp_norm_grad, axis=0),
        ]
    )
    bias_out = own_part(jnp.sum(upstream.astype(jnp.float32), axis=0))
    bias_qkv = jnp.sum(packed_grad.astype(jnp.float32), axis=0)
    bias_up = jnp.sum(hidden_grad.astype(jnp.float32), axis=0)
    if fast:
        share = width // nf
        vectors = jnp.pad(vectors.reshape(4, nf, share).transpose(1, 0, 2), ((0, 0), (0, 4), (0, 0)))
        biases = jnp.concatenate([bias_out, bias_qkv, bias_up]).reshape(8, share)
        token_shape = (group, ns, 4, 2, piece, width)
        grads, output, weighted, sums = reduce_tokens(
            (down_term, up_term, qkv_term, dense_term),
            partial_out.reshape(token_shape),
            partial_back.reshape(token_shape),
            vectors,
            biases,
        )
        grad_down_w, grad_up_w, grad_qkv_w, grad_dense_w = grads
        output = output.reshape(hidden_in.shape)
        weighted = weighted.reshape(hidden_in.shape)
        vectors = sums[:4]
        bias_out, bias_qkv, bias_up = sums[8], sums[9:12].reshape(-1), sums[12:16].reshape(-1)
    else:
        vectors = lax.psum_scatter(vectors, "fsdp", scatter_dimension=1, tiled=True)
        vectors, bias_out, bias_qkv, bias_up = lax.psum((vectors, bias_out, bias_qkv, bias_up), "sp")
        output = scatter_tokens(rounded(partial_out))
        weighted = scatter_tokens(rounded(partial_back))
        dense_term = lax.all_to_all(dense_term, "fsdp", split_axis=0, concat_axis=1, tiled=True)
        grad_down_w, grad_up_w, grad_qkv_w, grad_dense_w = (
            lax.psum(term.astype(jnp.bfloat16), "sp").astype(jnp.float32)
            for term in (down_term, up_term, qkv_term, dense_term)
        )
    inputs = hidden_in.astype(jnp.float32)
    output = (inputs + (output.astype(jnp.float32) + (b_dense + b_down))).astype(jnp.bfloat16)
    own_scaled, own_inverse = norm_scaled(inputs)
    weighted = weighted.astype(jnp.float32)
    first_mean = jnp.mean(weighted, axis=-1, keepdims=True)
    second_mean = jnp.mean(weighted * own_scaled, axis=-1, keepdims=True)
    input_grad = (
        cotangent.astype(jnp.float32)
        + own_inverse * (weighted - first_mean - own_scaled * second_mean)
    ).astype(jnp.bfloat16)

    return (
        output,
        input_grad,
        vectors[0],
        vectors[1],
        vectors[2],
        vectors[3],
        grad_qkv_w,
        bias_qkv,
        grad_dense_w,
        bias_out,
        grad_up_w,
        bias_up,
        grad_down_w,
        bias_out,
    )


def solution(mesh):
    rows = P("fsdp", "sp", None)
    first = P("fsdp", None)
    return jax.shard_map(
        per_device,
        mesh=mesh,
        in_specs=(
            rows,
            first,
            P(),
            P(),
            P(),
            P(),
            first,
            P(),
            first,
            P(),
            first,
            P(),
            first,
            P(),
            rows,
        ),
        out_specs=(
            rows,
            rows,
            P("fsdp"),
            P("fsdp"),
            P("fsdp"),
            P("fsdp"),
            first,
            P("fsdp"),
            first,
            P("fsdp"),
            first,
            P("fsdp"),
            first,
            P("fsdp"),
        ),
        check_vma=False,
    )
```

```python
import functools
import math

import jax
import jax.numpy as jnp
from jax import lax
from jax.experimental import pallas as pl
from jax.experimental.pallas import tpu as pltpu
from jax.sharding import PartitionSpec as P

MESH = pl.DeviceIdType.MESH

HEADS = 8
HEAD_DIM = 256
ROT = 64


EPSILON = 1e-05
NEGATIVE = -1e30
ROOT_HALF = 0.7071067811865476
ROOT_TWO_PI = 2.5066282746310002
SCALE = 1.0 / math.sqrt(HEAD_DIM)


def rounded(array):
    return lax.reduce_precision(array.astype(jnp.float32), 8, 7).astype(jnp.bfloat16)


def contract_rows(former, latter):
    return lax.dot_general(
        former, latter, (((0,), (0,)), ((), ())), preferred_element_type=jnp.float32
    )


def times_transposed(former, latter):
    return lax.dot_general(
        former, latter, (((1,), (1,)), ((), ())), preferred_element_type=jnp.float32
    )


def times(former, latter):
    return jnp.dot(former, latter, preferred_element_type=jnp.float32)


def norm_scaled(inputs):
    average = jnp.mean(inputs, axis=-1, keepdims=True)
    centred = inputs - average
    variance = jnp.mean(centred * centred, axis=-1, keepdims=True)
    inverse = lax.rsqrt(variance + EPSILON)
    return centred * inverse, inverse


def gelu_pair(hidden):
    cumulative = 0.5 * (1.0 + jax.scipy.special.erf(hidden * ROOT_HALF))
    return (
        hidden * cumulative,
        cumulative + hidden * jnp.exp(-0.5 * hidden * hidden) / ROOT_TWO_PI,
    )


def rotary_tables(segment_rows):
    length = segment_rows.shape[-1]
    places = jnp.arange(length, dtype=jnp.int32)
    changes = jnp.concatenate(
        [
            jnp.ones_like(segment_rows[..., :1]),
            (segment_rows[..., 1:] != segment_rows[..., :-1]).astype(jnp.int32),
        ],
        axis=-1,
    )
    first_place = lax.cummax(changes * places, axis=segment_rows.ndim - 1)
    position = (places - first_place).astype(jnp.float32)
    exponent = jnp.arange(0, ROT, 2).astype(jnp.float32) / ROT
    frequency = 1.0 / jnp.power(10000.0, exponent)
    angles = position[..., None] * frequency
    angles = jnp.concatenate([angles, angles], axis=-1)
    return (jnp.cos(angles), jnp.sin(angles))


def rotate(heads_part, cos_table, sin_table):
    half_rot = ROT // 2
    turned = heads_part[..., :ROT]
    swapped = jnp.concatenate([-turned[..., half_rot:], turned[..., :half_rot]], axis=-1)
    turned = turned * cos_table[..., None, :] + swapped * sin_table[..., None, :]
    return jnp.concatenate([turned, heads_part[..., ROT:]], axis=-1)


def unrotate(grads_part, cos_table, sin_table):
    half_rot = ROT // 2
    turned = grads_part[..., :ROT]
    along_sin = turned * sin_table[..., None, :]
    back_turn = jnp.concatenate([along_sin[..., half_rot:], -along_sin[..., :half_rot]], axis=-1)
    turned = turned * cos_table[..., None, :] + back_turn
    return jnp.concatenate([turned, grads_part[..., ROT:]], axis=-1)


def build_mask(segment_rows):
    places = jnp.arange(segment_rows.shape[-1], dtype=jnp.int32)
    return (segment_rows[:, :, None] == segment_rows[:, None, :]) & (
        places[None, :] <= places[:, None]
    )


def attention_scores(queries, keys_rot):
    return (
        jnp.einsum("bqhd,bkhd->bhqk", queries, keys_rot, preferred_element_type=jnp.float32) * SCALE
    )


def attend_forward(queries, keys_rot, values, mask):
    scores = jnp.where(mask[:, None], attention_scores(queries, keys_rot), NEGATIVE)
    row_top = jnp.max(scores, axis=-1, keepdims=True)
    exponent = jnp.exp(scores - row_top)
    row_total = jnp.sum(exponent, axis=-1, keepdims=True)
    attention = (exponent / row_total).astype(jnp.bfloat16)
    context = jnp.einsum("bhqk,bkhd->bqhd", attention, values, preferred_element_type=jnp.float32)
    return (context.astype(jnp.bfloat16), row_top + jnp.log(row_total))


def attend_backward(queries, keys_rot, values, mask, log_total, context_grad):
    scores = attention_scores(queries, keys_rot)
    attention = jnp.where(mask[:, None], jnp.exp(scores - log_total), 0.0)
    value_grad = jnp.einsum(
        "bhqk,bqhd->bkhd",
        attention.astype(jnp.bfloat16),
        context_grad,
        preferred_element_type=jnp.float32,
    )
    attention_grad = jnp.einsum(
        "bqhd,bkhd->bhqk", context_grad, values, preferred_element_type=jnp.float32
    )
    row_centre = jnp.sum(attention * attention_grad, axis=-1, keepdims=True)
    score_grad = (attention * (attention_grad - row_centre)).astype(jnp.bfloat16)
    query_grad = (
        jnp.einsum("bhqk,bkhd->bqhd", score_grad, keys_rot, preferred_element_type=jnp.float32)
        * SCALE
    )
    key_grad = (
        jnp.einsum("bhqk,bqhd->bkhd", score_grad, queries, preferred_element_type=jnp.float32)
        * SCALE
    )
    return (query_grad, key_grad, value_grad)


def gather_kernel(x_ref, c_ref, seg_ref, xg_ref, cg_ref, segs_ref, held, seg_s, seg_r, seg_l, s1, r1, s2, r2, s3, r3, local):
    f, s = lax.axis_index("fsdp"), lax.axis_index("sp")
    core, col, row = f % 2, (f // 2) % 2, f // 4
    f_x, f_y, f_c = f + 2 - 4 * col, f + 4 - 8 * row, f + 1 - 2 * core
    f_d = f_x + 4 - 8 * row
    piece = xg_ref.shape[3]
    barrier = pltpu.get_barrier_semaphore()
    for k in range(1, 8):
        pl.semaphore_signal(barrier, inc=1, device_id=((f + k) % 8, s), device_id_type=MESH)
    for k in range(1, 4):
        pl.semaphore_signal(barrier, inc=1, device_id=(f, (s + k) % 4), device_id_type=MESH)
    pl.semaphore_wait(barrier, 10)
    pairs = ((x_ref, xg_ref), (c_ref, cg_ref))
    sent = []

    def send(src, dst, send_sem, recv_sem, device):
        copy = pltpu.make_async_remote_copy(
            src_ref=src, dst_ref=dst, send_sem=send_sem, recv_sem=recv_sem,
            device_id=device, device_id_type=MESH,
        )
        copy.start()
        sent.append(copy)

    def arrived(ref, recv_sem):
        pltpu.make_async_remote_copy(
            src_ref=ref, dst_ref=ref, send_sem=s1.at[0, 0], recv_sem=recv_sem,
            device_id=(f_c, s), device_id_type=MESH,
        ).wait_recv()

    holds = f // 2 == s
    keep_seg = pltpu.make_async_copy(seg_ref, segs_ref.at[core], seg_l.at[0])
    give_seg = [
        pltpu.make_async_remote_copy(
            src_ref=seg_ref, dst_ref=segs_ref.at[core], send_sem=seg_s.at[k], recv_sem=seg_r.at[core],
            device_id=((f + k) % 8, s), device_id_type=MESH,
        )
        for k in range(1, 8)
    ]

    @pl.when(holds)
    def _():
        keep_seg.start()
        for copy in give_seg:
            copy.start()

    kept = []
    for a, (src, _) in enumerate(pairs):
        own = pltpu.make_async_copy(src.at[pl.ds(f * piece, piece)], held.at[a, f], local.at[a, 0])
        own.start()
        kept.append(own)
        for k in range(1, 8):
            j = (f + k) % 8
            send(src.at[pl.ds(j * piece, piece)], held.at[a, f], s1.at[a, k], r1.at[a, k], (j, s))

    def to_planes(a):
        out = pairs[a][1]
        kept[a].wait()
        for k in range(1, 8):
            arrived(held.at[a, (f + 8 - k) % 8], r1.at[a, k])
        for k in range(1, 4):
            plane = (s + k) % 4
            send(held.at[a, pl.ds(2 * plane, 2)], out.at[:, s, f], s2.at[a, k], r2.at[a, k], (f, plane))
        own = pltpu.make_async_copy(held.at[a, pl.ds(2 * s, 2)], out.at[:, s, f], local.at[a, 1])
        own.start()
        return own

    def spread(a, k):
        out = pairs[a][1]
        z = (s + 4 - k) % 4
        if k:
            arrived(out.at[:, z, f], r2.at[a, k])
        ref = out.at[:, z, f]
        send(ref, ref, s3.at[a, 0, k], r3.at[a, 0, k], (f_x, s))
        send(ref, ref, s3.at[a, 1, k], r3.at[a, 1, k], (f_y, s))
        send(ref, ref, s3.at[a, 2, k], r3.at[a, 2, k], (f_c, s))

    def pass_on(a, k):
        out = pairs[a][1]
        z = (s + 4 - k) % 4
        ref = out.at[:, z, f_x]
        arrived(ref, r3.at[a, 0, k])
        send(out.at[0, z, f_x], out.at[0, z, f_x], s3.at[a, 5, k], r3.at[a, 5, k], (f_y, s))
        send(ref, ref, s3.at[a, 3, k], r3.at[a, 3, k], (f_c, s))
        ref = out.at[:, z, f_y]
        arrived(ref, r3.at[a, 1, k])
        send(out.at[1, z, f_y], out.at[1, z, f_y], s3.at[a, 6, k], r3.at[a, 6, k], (f_x, s))
        send(ref, ref, s3.at[a, 4, k], r3.at[a, 4, k], (f_c, s))

    def pass_corner(a, k):
        out = pairs[a][1]
        z = (s + 4 - k) % 4
        for half in range(2):
            ref = out.at[half, z, f_d]
            arrived(ref, r3.at[a, 5 + half, k])
            send(ref, ref, s3.at[a, 7 + half, k], r3.at[a, 7 + half, k], (f_c, s))

    def from_core(a, k):
        out = pairs[a][1]
        z = (s + 4 - k) % 4
        g_x, g_y = f_c + 2 - 4 * col, f_c + 4 - 8 * row
        g_d = g_x + 4 - 8 * row
        arrived(out.at[:, z, f_c], r3.at[a, 2, k])
        arrived(out.at[:, z, g_x], r3.at[a, 3, k])
        arrived(out.at[:, z, g_y], r3.at[a, 4, k])
        for half in range(2):
            arrived(out.at[half, z, g_d], r3.at[a, 7 + half, k])

    own0 = to_planes(0)
    own1 = to_planes(1)
    steps = [(a, k) for a in range(2) for k in range(4)]
    for i in range(len(steps) + 2):
        if i < len(steps):
            a, k = steps[i]
            if k == 0:
                (own0 if a == 0 else own1).wait()
            spread(a, k)
        if 0 <= i - 1 < len(steps):
            pass_on(*steps[i - 1])
        if 0 <= i - 2 < len(steps):
            pass_corner(*steps[i - 2])
    for a, k in steps:
        from_core(a, k)
    for b in range(2):

        @pl.when(f != 2 * s + b)
        def _():
            arrived(segs_ref.at[b], seg_r.at[b])

    @pl.when(holds)
    def _():
        keep_seg.wait()
        for copy in give_seg:
            copy.wait_send()

    for copy in sent:
        copy.wait_send()


def gather_both(x, c, segments):
    rows, width = x.shape
    piece = rows // 8
    shape = jax.ShapeDtypeStruct((2, 4, 8, piece, width), x.dtype)
    dma = pltpu.SemaphoreType.DMA
    return pl.pallas_call(
        gather_kernel,
        out_shape=(shape, shape, jax.ShapeDtypeStruct((2, *segments.shape), segments.dtype)),
        in_specs=[pl.BlockSpec(memory_space=pl.ANY)] * 3,
        out_specs=[pl.BlockSpec(memory_space=pl.ANY)] * 3,
        scratch_shapes=[
            pltpu.VMEM((2, 8, piece, width), x.dtype),
            dma((8,)), dma((2,)), dma((1,)),
            dma((2, 8)), dma((2, 8)), dma((2, 4)), dma((2, 4)), dma((2, 9, 4)), dma((2, 9, 4)), dma((2, 2)),
        ],
        compiler_params=pltpu.CompilerParams(collective_id=1, has_side_effects=True),
        name="gather_tokens",
    )(x, c, segments)


def reduce_kernel(
    sizes, steps,
    up_ref, qkv_ref, dense_ref, out_ref, back_ref, vec_ref, bias_ref,
    g_up, g_qkv, g_dense, o_out, o_back, o_small,
    line_a, line_b, turned, own, paired, block, crossed, reduced, homed, vec_in, small, small_in,
    in_s, in_r, mid_s, mid_r, end_s, end_r, own_l, keep_l,
    turn_s, turn_r, pair_s, pair_r, block_l, cross_s, cross_r, home_s, home_r, back_s, back_r, local,
    vec_s, vec_r, small_s, small_r,
):
    f, s = lax.axis_index("fsdp"), lax.axis_index("sp")
    core, col, row = f % 2, (f // 2) % 2, f // 4
    f_x, f_y, f_c = f + 2 - 4 * col, f + 4 - 8 * row, f + 1 - 2 * core
    f_d = f_x + 4 - 8 * row
    is_end = (s == 0) | (s == 3)
    is_mid = (s == 1) | (s == 2)
    inner = 1 + s // 3
    outer = 3 * (s // 2)
    facing = 3 - s
    barrier = pltpu.get_barrier_semaphore()
    for k in range(1, 8):
        pl.semaphore_signal(barrier, inc=1, device_id=((f + k) % 8, s), device_id_type=MESH)
    for k in range(1, 4):
        pl.semaphore_signal(barrier, inc=1, device_id=(f, (s + k) % 4), device_id_type=MESH)
    pl.semaphore_wait(barrier, 10)
    sent = []

    def send(src, dst, send_sem, recv_sem, device, track=True):
        copy = pltpu.make_async_remote_copy(
            src_ref=src, dst_ref=dst, send_sem=send_sem, recv_sem=recv_sem,
            device_id=device, device_id_type=MESH,
        )
        copy.start()
        if track:
            sent.append(copy)
        return copy

    def arrived(ref, recv_sem):
        pltpu.make_async_remote_copy(
            src_ref=ref, dst_ref=ref, send_sem=vec_s.at[0], recv_sem=recv_sem,
            device_id=(f_c, s), device_id_type=MESH,
        ).wait_recv()

    def copied(src, dst, sem):
        copy = pltpu.make_async_copy(src, dst, sem)
        copy.start()
        return copy

    part = turned.shape[0]
    span = dense_ref.shape[1]
    columns = pl.ds(pl.multiple_of(f * span, span), span)
    vec_own = copied(vec_ref.at[f], vec_in.at[f], local.at[0])
    turn_own = copied(dense_ref.at[pl.ds(f * part, part)], turned.at[:, columns], local.at[1])
    bias_own = copied(bias_ref, small.at[pl.ds(8, 8)], local.at[2])
    for k in range(1, 8):
        j = (f + k) % 8
        send(vec_ref.at[j], vec_in.at[f], vec_s.at[k], vec_r.at[k], (j, s))

    chunks = []
    offset = 0
    for ref, result, rows_of in (
        (up_ref, g_up, sizes[0]), (qkv_ref, g_qkv, sizes[1]), (turned, g_dense, sizes[2]),
    ):
        first = 0
        for rows in rows_of:
            chunks.append((ref, result, first, rows, offset))
            first += rows
            offset += rows
    count = len(chunks)
    ahead = 4

    def from_end(k):
        ref, _, first, rows, at = chunks[k]
        return pltpu.make_async_remote_copy(
            src_ref=ref.at[pl.ds(first, rows)], dst_ref=line_a.at[pl.ds(at, rows)],
            send_sem=in_s.at[k], recv_sem=in_r.at[k], device_id=(f, inner), device_id_type=MESH,
        )

    def across(k):
        _, _, _, rows, at = chunks[k]
        return pltpu.make_async_remote_copy(
            src_ref=line_a.at[pl.ds(at, rows)], dst_ref=line_b.at[pl.ds(at, rows)],
            send_sem=mid_s.at[k], recv_sem=mid_r.at[k], device_id=(f, facing), device_id_type=MESH,
        )

    def to_end(k):
        _, result, first, rows, at = chunks[k]
        return pltpu.make_async_remote_copy(
            src_ref=line_b.at[pl.ds(at, rows)], dst_ref=result.at[pl.ds(first, rows)],
            send_sem=end_s.at[k], recv_sem=end_r.at[k], device_id=(f, outer), device_id_type=MESH,
        )

    def load_own(k):
        ref, _, first, rows, _ = chunks[k]
        return pltpu.make_async_copy(
            ref.at[pl.ds(first, rows)], own.at[k % 3, pl.ds(0, rows)], own_l.at[k % 3]
        )

    def keep(k):
        _, result, first, rows, at = chunks[k]
        return pltpu.make_async_copy(
            line_b.at[pl.ds(at, rows)], result.at[pl.ds(first, rows)], keep_l.at[k]
        )

    tile = 16

    def add_rows(target, target_at, left, left_at, right, rows):
        @pl.loop(0, rows // tile)
        def _(i):
            at = pl.multiple_of(i * tile, tile)
            total = (
                left[pl.ds(left_at + at, tile), :].astype(jnp.float32)
                + right[pl.ds(at, tile), :].astype(jnp.float32)
            )
            target[pl.ds(target_at + at, tile), :] = total.astype(target.dtype)

    def mid_in(k):
        _, _, _, rows, at = chunks[k]
        load_own(k).wait()
        from_end(k).wait_recv()
        add_rows(line_a, at, line_a, at, own.at[k % 3], rows)
        across(k).start()
        if k + 3 < count:
            load_own(k + 3).start()

    def mid_out(k):
        _, _, _, rows, at = chunks[k]
        across(k).wait_recv()
        add_rows(line_b, at, line_b, at, line_a.at[pl.ds(at, rows)], rows)
        to_end(k).start()
        keep(k).start()

    pairs = ((out_ref, o_out), (back_ref, o_back))
    order = (f_d // 2, f_x // 2, f_y // 2, f // 2)
    for a, (ref, _) in enumerate(pairs):
        for n, q in enumerate(order):
            send(ref.at[:, :, q, 1 - core], paired.at[a, n], pair_s.at[a, n], pair_r.at[a, n], (f_c, s))
    for k in range(1, 8):
        j = (f + k) % 8
        send(dense_ref.at[pl.ds(j * part, part)], turned.at[:, columns], turn_s.at[k], turn_r.at[k], (j, s))

    def load_block(i):
        a, n = i // 4, i % 4
        return pltpu.make_async_copy(
            pairs[a][0].at[:, :, order[n], core], block.at[i % 2], block_l.at[i % 2]
        )

    load_block(0).start()
    load_block(1).start()

    def add_pair(i):
        a, n = i // 4, i % 4
        load_block(i).wait()
        arrived(paired.at[a, n], pair_r.at[a, n])

        @pl.loop(0, 8)
        def _(m):
            b, z = m // 4, m % 4
            total = paired[a, n, b, z].astype(jnp.float32) + block[i % 2, b, z].astype(jnp.float32)
            paired[a, n, b, z] = total.astype(paired.dtype)

        if n < 3:
            send(paired.at[a, n], crossed.at[a, n], cross_s.at[a, n], cross_r.at[a, n], ((f_d, f_x, f_y)[n], s))
        if i + 2 < 8:
            load_block(i + 2).start()

    placed = {}

    def add_chips(a):
        for n in range(3):
            arrived(crossed.at[a, n], cross_r.at[a, n])

        @pl.loop(0, 8)
        def _(m):
            b, z = m // 4, m % 4
            total = paired[a, 3, b, z].astype(jnp.float32)
            for n in range(3):
                total = total + crossed[a, n, b, z].astype(jnp.float32)
            reduced[a, b, z] = total.astype(reduced.dtype)

        for k in range(1, 4):
            z = (s + k) % 4
            send(reduced.at[a, :, z], homed.at[a, s], home_s.at[a, k], home_r.at[a, k], (f, z))
        placed["along", a] = copied(reduced.at[a, :, s], homed.at[a, s], local.at[3 + a])

    def go_home(a):
        result = pairs[a][1]
        placed["along", a].wait()
        for k in range(1, 4):
            arrived(homed.at[a, (s + 4 - k) % 4], home_r.at[a, k])
        for k in range(1, 8):
            j = (f + k) % 8
            send(homed.at[a, j // 2, j % 2], result.at[f], back_s.at[a, k], back_r.at[a, k], (j, s))
        placed["home", a] = copied(homed.at[a, f // 2, core], result.at[f], local.at[5 + a])

    def add_vectors():
        vec_own.wait()
        bias_own.wait()
        for k in range(1, 8):
            arrived(vec_in.at[(f + 8 - k) % 8], vec_r.at[k])
        total = vec_in[0]
        for j in range(1, 8):
            total = total + vec_in[j]
        small[0:8, :] = total
        for k in range(1, 4):
            send(small, small_in.at[s], small_s.at[k], small_r.at[k], (f, (s + k) % 4))
        placed["small"] = copied(small, small_in.at[s], local.at[7])

    def add_small():
        placed["small"].wait()
        for k in range(1, 4):
            arrived(small_in.at[(s + 4 - k) % 4], small_r.at[k])
        total = small_in[0]
        for z in range(1, 4):
            total = total + small_in[z]
        o_small[...] = total

    def turn_done():
        turn_own.wait()
        for k in range(1, 8):
            j = (f + 8 - k) % 8
            at = pl.ds(pl.multiple_of(j * span, span), span)
            arrived(turned.at[:, at], turn_r.at[k])

    def tasks(name):
        if name == "vec":
            add_vectors()
        elif name == "small":
            add_small()
        elif name == "turn":
            turn_done()
        elif name[0] == "p":
            add_pair(int(name[1:]))
        elif name[0] == "c":
            add_chips(int(name[1:]))
        elif name[0] == "h":
            go_home(int(name[1:]))

    @pl.when(is_end)
    def _():
        for k in range(ahead):
            from_end(k).start()

    @pl.when(is_mid)
    def _():
        for k in range(3):
            load_own(k).start()

    for k in range(count + 1):
        for name in steps.get(k, ()):
            tasks(name)

        @pl.when(is_mid)
        def _():
            if k < count:
                mid_in(k)
            if k >= 1:
                mid_out(k - 1)

        @pl.when(is_end)
        def _():
            if k >= 1:
                to_end(k - 1).wait_recv()
                if k - 1 + ahead < count:
                    from_end(k - 1 + ahead).start()

    for name in steps.get(count + 1, ()):
        tasks(name)
    for a in range(2):
        placed["home", a].wait()
        for k in range(1, 8):
            arrived(pairs[a][1].at[(f + 8 - k) % 8], back_r.at[a, k])
    for copy in sent:
        copy.wait_send()

    @pl.when(is_end)
    def _():
        for k in range(count):
            from_end(k).wait_send()

    @pl.when(is_mid)
    def _():
        for k in range(count):
            across(k).wait_send()
            to_end(k).wait_send()
            keep(k).wait()


STEPS = {
    0: ("p0", "p1", "p2", "p3", "vec"),
    1: ("p4", "p5"),
    2: ("p6", "p7"),
    3: ("turn", "small"),
    5: ("c0",),
    7: ("h0", "c1"),
    9: ("h1",),
}


def reduce_all(up, qkv, dense, out_part, back_part, vec, bias, sizes, steps=STEPS):
    width = up.shape[1]
    dtype = up.dtype
    total = sum(sum(rows) for rows in sizes)
    count = sum(len(rows) for rows in sizes)
    largest = max(max(rows) for rows in sizes)
    piece = out_part.shape[4]
    dma = pltpu.SemaphoreType.DMA
    grads = [jax.ShapeDtypeStruct((sum(rows), width), dtype) for rows in sizes]
    token = jax.ShapeDtypeStruct((8, piece, width), dtype)
    span = dense.shape[1]
    anywhere = pl.BlockSpec(memory_space=pl.ANY)
    vmem = pltpu.VMEM
    return pl.pallas_call(
        functools.partial(reduce_kernel, sizes, steps),
        out_shape=(*grads, token, token, jax.ShapeDtypeStruct((16, vec.shape[2]), jnp.float32)),
        in_specs=[anywhere] * 7,
        out_specs=[anywhere] * 5 + [pl.BlockSpec(memory_space=pltpu.VMEM)],
        scratch_shapes=[
            vmem((total, width), dtype), vmem((total, width), dtype), vmem((sum(sizes[-1]), width), dtype),
            vmem((3, largest, width), dtype),
            vmem((2, 4, 2, 4, piece, width), dtype), vmem((2, 2, 4, piece, width), dtype),
            vmem((2, 3, 2, 4, piece, width), dtype), vmem((2, 2, 4, piece, width), dtype),
            vmem((2, 4, 2, piece, width), dtype),
            vmem((8, 8, vec.shape[2]), jnp.float32), vmem((16, vec.shape[2]), jnp.float32),
            vmem((4, 16, vec.shape[2]), jnp.float32),
            dma((count,)), dma((count,)), dma((count,)), dma((count,)), dma((count,)), dma((count,)),
            dma((3,)), dma((count,)),
            dma((8,)), dma((8,)), dma((2, 4)), dma((2, 4)), dma((2,)), dma((2, 3)), dma((2, 3)),
            dma((2, 4)), dma((2, 4)), dma((2, 8)), dma((2, 8)), dma((8,)),
            dma((8,)), dma((8,)), dma((4,)), dma((4,)),
        ],
        compiler_params=pltpu.CompilerParams(
            collective_id=2, has_side_effects=True, vmem_limit_bytes=60 * 1024 * 1024
        ),
        name="reduce_all",
    )(up, qkv, dense, out_part, back_part, vec, bias)


def cut(rows, unit, first=False, last=False):
    sizes = [4 * unit] * (rows // (4 * unit))
    if first:
        sizes[:1] = [unit, unit, 2 * unit]
    if last:
        sizes[-1:] = [2 * unit, unit, unit]
    return tuple(sizes)


def reduce_tokens(terms, partial_out, partial_back, vectors, biases):
    up, qkv, dense = (term.astype(jnp.bfloat16) for term in terms)
    sizes = (
        cut(up.shape[0], 64, first=True),
        cut(qkv.shape[0], 64),
        cut(dense.shape[0] // 8, 64, last=True),
    )
    *grads, output, weighted, sums = reduce_all(
        up,
        qkv,
        dense,
        partial_out.astype(jnp.bfloat16),
        partial_back.astype(jnp.bfloat16),
        vectors,
        biases,
        sizes,
    )
    return [grad.astype(jnp.float32) for grad in grads], output, weighted, sums


def per_device(
    hidden_in,
    segments,
    ln1_gain,
    ln1_bias,
    ln2_gain,
    ln2_bias,
    w_qkv,
    b_qkv,
    w_dense,
    b_dense,
    w_up,
    b_up,
    w_down,
    b_down,
    cotangent,
):
    seq_local, shard_len, width = hidden_in.shape
    seq_len = segments.shape[1]
    nf, ns = lax.axis_size("fsdp"), lax.axis_size("sp")
    f_place, s_place = lax.axis_index("fsdp"), lax.axis_index("sp")
    seqs = seq_local * nf
    group = seqs // ns
    piece = shard_len // nf
    tokens = group * seq_len
    per_head = max(1, nf // HEADS)
    head_count = max(1, HEADS // nf)
    head_sets = [[head * per_head + k for k in range(per_head)] for head in range(nf // per_head)]

    def gather_tokens(block):
        part = lax.all_to_all(block, "fsdp", split_axis=1, concat_axis=0, tiled=True)
        part = lax.all_to_all(part, "sp", split_axis=0, concat_axis=1, tiled=True)
        return in_order(lax.all_gather(part, "fsdp", axis=0, tiled=True)).reshape(tokens, width)

    def scatter_tokens(partial):
        part = out_of_order(partial).reshape(nf * group, ns * piece, width)
        part = lax.psum_scatter(part, "fsdp", scatter_dimension=0, tiled=True)
        part = lax.all_to_all(part, "sp", split_axis=1, concat_axis=0, tiled=True)
        return lax.all_to_all(part, "fsdp", split_axis=0, concat_axis=1, tiled=True)

    def in_order(array):
        array = array.reshape(nf, group, ns, piece, -1)
        return array.transpose(1, 2, 0, 3, 4).reshape(group, seq_len, -1)

    def out_of_order(array):
        array = array.reshape(group, ns, nf, piece, -1)
        return array.transpose(2, 0, 1, 3, 4).reshape(tokens, -1)

    def over_head(array, axis):
        if per_head == 1:
            return array
        return lax.all_gather(
            array, "fsdp", axis=axis, tiled=True, axis_index_groups=head_sets
        )

    def own_columns(array):
        if per_head == 1:
            return array
        share = array.shape[-1] // per_head
        return lax.dynamic_slice_in_dim(array, (f_place % per_head) * share, share, array.ndim - 1)

    def own_part(vector):
        share = vector.shape[0] // nf
        return lax.dynamic_slice_in_dim(vector, f_place * share, share, 0)

    fast = (nf, ns, seq_local, HEADS) == (8, 4, 1, 8)
    if fast:
        gathered, upstream, rows = gather_both(
            hidden_in[0], cotangent[0], segments.reshape(8, seq_len // 8)
        )
        gathered, upstream = (array.reshape(tokens, width) for array in (gathered, upstream))
        rows = rows.reshape(group, seq_len)
        w_dense, gathered = lax.optimization_barrier((w_dense, gathered))
    else:
        gathered, upstream = gather_tokens(hidden_in), gather_tokens(cotangent)
        rows = lax.all_gather(segments, "fsdp", axis=0, tiled=True)
        rows = lax.dynamic_slice_in_dim(rows, s_place * group, group, 0)

    dense_in = lax.all_to_all(w_dense, "fsdp", split_axis=1, concat_axis=0, tiled=True)
    head_qkv = over_head(w_qkv, 0)
    head_dense = over_head(dense_in, 1)
    head_bias = lax.dynamic_slice_in_dim(
        b_qkv, (f_place // per_head) * head_qkv.shape[0], head_qkv.shape[0], 0
    )

    scaled, _ = norm_scaled(gathered.astype(jnp.float32))
    normed = (scaled * ln1_gain + ln1_bias).astype(jnp.bfloat16)
    normed_mlp = (scaled * ln2_gain + ln2_bias).astype(jnp.bfloat16)

    hidden = times_transposed(normed_mlp, w_up) + own_part(b_up)
    activated, slope = gelu_pair(hidden)
    activated = activated.astype(jnp.bfloat16)
    down_term = contract_rows(activated, upstream).astype(jnp.bfloat16)
    grad_down_w = lax.psum(down_term, "sp").astype(jnp.float32)
    normed, down_term = lax.optimization_barrier((normed, down_term))
    hidden_grad = (times_transposed(upstream, w_down) * slope).astype(jnp.bfloat16)
    up_term = contract_rows(hidden_grad, normed_mlp)
    mlp_norm_grad = times(hidden_grad, w_up)

    packed = (times_transposed(normed, head_qkv) + head_bias).astype(jnp.bfloat16)
    packed = packed.reshape(group, seq_len, head_count, 3 * HEAD_DIM)
    cos_table, sin_table = rotary_tables(rows)
    queries = rotate(packed[..., :HEAD_DIM].astype(jnp.float32), cos_table, sin_table).astype(
        jnp.bfloat16
    )
    keys_rot = rotate(
        packed[..., HEAD_DIM : 2 * HEAD_DIM].astype(jnp.float32), cos_table, sin_table
    ).astype(jnp.bfloat16)
    values = packed[..., 2 * HEAD_DIM :]
    mask = build_mask(rows)
    context, log_total = attend_forward(queries, keys_rot, values, mask)
    context = own_columns(context.reshape(tokens, -1))
    partial_out = times_transposed(context, dense_in) + times(activated, w_down)
    context_grad = times(upstream, head_dense).astype(jnp.bfloat16).reshape(
        group, seq_len, head_count, HEAD_DIM
    )
    query_grad, key_grad, value_grad = attend_backward(
        queries, keys_rot, values, mask, log_total, context_grad
    )
    packed_grad = jnp.concatenate(
        [
            unrotate(query_grad, cos_table, sin_table),
            unrotate(key_grad, cos_table, sin_table),
            value_grad,
        ],
        axis=-1,
    ).astype(jnp.bfloat16)
    packed_grad = own_columns(packed_grad.reshape(tokens, -1))
    attn_norm_grad = times(packed_grad, w_qkv)
    qkv_term = contract_rows(packed_grad, normed)
    dense_term = contract_rows(upstream, context).astype(jnp.bfloat16)

    partial_back = attn_norm_grad * ln1_gain + mlp_norm_grad * ln2_gain
    vectors = jnp.stack(
        [
            jnp.sum(attn_norm_grad * scaled, axis=0),
            jnp.sum(attn_norm_grad, axis=0),
            jnp.sum(mlp_norm_grad * scaled, axis=0),
            jnp.sum(mlp_norm_grad, axis=0),
        ]
    )
    bias_out = own_part(jnp.sum(upstream.astype(jnp.float32), axis=0))
    bias_qkv = jnp.sum(packed_grad.astype(jnp.float32), axis=0)
    bias_up = jnp.sum(hidden_grad.astype(jnp.float32), axis=0)
    if fast:
        share = width // nf
        vectors = jnp.pad(vectors.reshape(4, nf, share).transpose(1, 0, 2), ((0, 0), (0, 4), (0, 0)))
        biases = jnp.concatenate([bias_out, bias_qkv, bias_up]).reshape(8, share)
        token_shape = (group, ns, 4, 2, piece, width)
        grads, output, weighted, sums = reduce_tokens(
            (up_term, qkv_term, dense_term),
            partial_out.reshape(token_shape),
            partial_back.reshape(token_shape),
            vectors,
            biases,
        )
        grad_up_w, grad_qkv_w, grad_dense_w = grads
        output = output.reshape(hidden_in.shape)
        weighted = weighted.reshape(hidden_in.shape)
        vectors = sums[:4]
        bias_out, bias_qkv, bias_up = sums[8], sums[9:12].reshape(-1), sums[12:16].reshape(-1)
    else:
        vectors = lax.psum_scatter(vectors, "fsdp", scatter_dimension=1, tiled=True)
        vectors, bias_out, bias_qkv, bias_up = lax.psum((vectors, bias_out, bias_qkv, bias_up), "sp")
        output = scatter_tokens(rounded(partial_out))
        weighted = scatter_tokens(rounded(partial_back))
        dense_term = lax.all_to_all(dense_term, "fsdp", split_axis=0, concat_axis=1, tiled=True)
        grad_up_w, grad_qkv_w, grad_dense_w = (
            lax.psum(term.astype(jnp.bfloat16), "sp").astype(jnp.float32)
            for term in (up_term, qkv_term, dense_term)
        )
    inputs = hidden_in.astype(jnp.float32)
    output = (inputs + (output.astype(jnp.float32) + (b_dense + b_down))).astype(jnp.bfloat16)
    own_scaled, own_inverse = norm_scaled(inputs)
    weighted = weighted.astype(jnp.float32)
    first_mean = jnp.mean(weighted, axis=-1, keepdims=True)
    second_mean = jnp.mean(weighted * own_scaled, axis=-1, keepdims=True)
    input_grad = (
        cotangent.astype(jnp.float32)
        + own_inverse * (weighted - first_mean - own_scaled * second_mean)
    ).astype(jnp.bfloat16)

    return (
        output,
        input_grad,
        vectors[0],
        vectors[1],
        vectors[2],
        vectors[3],
        grad_qkv_w,
        bias_qkv,
        grad_dense_w,
        bias_out,
        grad_up_w,
        bias_up,
        grad_down_w,
        bias_out,
    )


def solution(mesh):
    rows = P("fsdp", "sp", None)
    first = P("fsdp", None)
    return jax.shard_map(
        per_device,
        mesh=mesh,
        in_specs=(
            rows,
            first,
            P(),
            P(),
            P(),
            P(),
            first,
            P(),
            first,
            P(),
            first,
            P(),
            first,
            P(),
            rows,
        ),
        out_specs=(
            rows,
            rows,
            P("fsdp"),
            P("fsdp"),
            P("fsdp"),
            P("fsdp"),
            first,
            P("fsdp"),
            first,
            P("fsdp"),
            first,
            P("fsdp"),
            first,
            P("fsdp"),
        ),
        check_vma=False,
    )
```

```python
import functools
import math

import jax
import jax.numpy as jnp
from jax import lax
from jax.experimental import pallas as pl
from jax.experimental.pallas import tpu as pltpu
from jax.sharding import PartitionSpec as P

MESH = pl.DeviceIdType.MESH

HEADS = 8
HEAD_DIM = 256
ROT = 64


EPSILON = 1e-05
NEGATIVE = -1e30
ROOT_HALF = 0.7071067811865476
ROOT_TWO_PI = 2.5066282746310002
SCALE = 1.0 / math.sqrt(HEAD_DIM)


def rounded(array):
    return lax.reduce_precision(array.astype(jnp.float32), 8, 7).astype(jnp.bfloat16)


def contract_rows(former, latter):
    return lax.dot_general(
        former, latter, (((0,), (0,)), ((), ())), preferred_element_type=jnp.float32
    )


def times_transposed(former, latter):
    return lax.dot_general(
        former, latter, (((1,), (1,)), ((), ())), preferred_element_type=jnp.float32
    )


def times(former, latter):
    return jnp.dot(former, latter, preferred_element_type=jnp.float32)


def norm_scaled(inputs):
    average = jnp.mean(inputs, axis=-1, keepdims=True)
    centred = inputs - average
    variance = jnp.mean(centred * centred, axis=-1, keepdims=True)
    inverse = lax.rsqrt(variance + EPSILON)
    return centred * inverse, inverse


def gelu_pair(hidden):
    cumulative = 0.5 * (1.0 + lax.erf(hidden * ROOT_HALF))
    return (
        hidden * cumulative,
        cumulative + hidden * (jnp.exp(-0.5 * hidden * hidden) * (1.0 / ROOT_TWO_PI)),
    )


def document_starts(segment_rows):
    places = jnp.arange(segment_rows.shape[-1], dtype=jnp.int32)
    changes = jnp.concatenate(
        [
            jnp.ones_like(segment_rows[..., :1]),
            (segment_rows[..., 1:] != segment_rows[..., :-1]).astype(jnp.int32),
        ],
        axis=-1,
    )
    return places, lax.cummax(changes * places, axis=segment_rows.ndim - 1)


def frequencies():
    return 1.0 / jnp.power(10000.0, jnp.arange(0, ROT, 2).astype(jnp.float32) / ROT)


def rotary_tables(segment_rows):
    places, starts = document_starts(segment_rows)
    angles = (places - starts).astype(jnp.float32)[..., None] * frequencies()
    angles = jnp.concatenate([angles, angles], axis=-1)
    return (jnp.cos(angles), jnp.sin(angles))


def head_tables(segment_rows):
    places, starts = document_starts(segment_rows)
    angles = (places - starts).astype(jnp.float32)[:, None, :] * frequencies()[None, :, None]
    starts = jnp.broadcast_to(
        starts.astype(jnp.float32)[:, None, :], (starts.shape[0], ROT, starts.shape[1])
    )
    return jnp.concatenate([jnp.cos(angles), jnp.sin(angles), starts], axis=1)


def rotate(heads_part, cos_table, sin_table):
    half_rot = ROT // 2
    turned = heads_part[..., :ROT]
    swapped = jnp.concatenate([-turned[..., half_rot:], turned[..., :half_rot]], axis=-1)
    turned = turned * cos_table[..., None, :] + swapped * sin_table[..., None, :]
    return jnp.concatenate([turned, heads_part[..., ROT:]], axis=-1)


def unrotate(grads_part, cos_table, sin_table):
    half_rot = ROT // 2
    turned = grads_part[..., :ROT]
    along_sin = turned * sin_table[..., None, :]
    back_turn = jnp.concatenate([along_sin[..., half_rot:], -along_sin[..., :half_rot]], axis=-1)
    turned = turned * cos_table[..., None, :] + back_turn
    return jnp.concatenate([turned, grads_part[..., ROT:]], axis=-1)


def build_mask(segment_rows):
    places = jnp.arange(segment_rows.shape[-1], dtype=jnp.int32)
    return (segment_rows[:, :, None] == segment_rows[:, None, :]) & (
        places[None, :] <= places[:, None]
    )


def attention_scores(queries, keys_rot):
    return (
        jnp.einsum("bqhd,bkhd->bhqk", queries, keys_rot, preferred_element_type=jnp.float32) * SCALE
    )


def attend_forward(queries, keys_rot, values, mask):
    scores = jnp.where(mask[:, None], attention_scores(queries, keys_rot), NEGATIVE)
    row_top = jnp.max(scores, axis=-1, keepdims=True)
    exponent = jnp.exp(scores - row_top)
    row_total = jnp.sum(exponent, axis=-1, keepdims=True)
    attention = (exponent / row_total).astype(jnp.bfloat16)
    context = jnp.einsum("bhqk,bkhd->bqhd", attention, values, preferred_element_type=jnp.float32)
    return (context.astype(jnp.bfloat16), row_top + jnp.log(row_total))


def attend_backward(queries, keys_rot, values, mask, log_total, context_grad):
    scores = attention_scores(queries, keys_rot)
    attention = jnp.where(mask[:, None], jnp.exp(scores - log_total), 0.0)
    value_grad = jnp.einsum(
        "bhqk,bqhd->bkhd",
        attention.astype(jnp.bfloat16),
        context_grad,
        preferred_element_type=jnp.float32,
    )
    attention_grad = jnp.einsum(
        "bqhd,bkhd->bhqk", context_grad, values, preferred_element_type=jnp.float32
    )
    row_centre = jnp.sum(attention * attention_grad, axis=-1, keepdims=True)
    score_grad = (attention * (attention_grad - row_centre)).astype(jnp.bfloat16)
    query_grad = (
        jnp.einsum("bhqk,bkhd->bqhd", score_grad, keys_rot, preferred_element_type=jnp.float32)
        * SCALE
    )
    key_grad = (
        jnp.einsum("bhqk,bqhd->bkhd", score_grad, queries, preferred_element_type=jnp.float32)
        * SCALE
    )
    return (query_grad, key_grad, value_grad)


def whole_block(array):
    return pl.BlockSpec(array.shape, lambda *_: (0,) * array.ndim, pipeline_mode=pl.Buffered(1))


def eight_rows(array):
    return jnp.sum(array.reshape(array.shape[0] // 8, 8, array.shape[1]), axis=0)


def upstream_kernel(c_ref, slope_ref, down_ref, dense_ref, grad_ref, context_ref, c_sum_ref, h_sum_ref):
    @pl.when(pl.program_id(0) == 0)
    def _():
        c_sum_ref[...] = jnp.zeros_like(c_sum_ref)
        h_sum_ref[...] = jnp.zeros_like(h_sum_ref)

    hidden_grad = (times_transposed(c_ref[...], down_ref[...]) * slope_ref[...]).astype(grad_ref.dtype)
    grad_ref[...] = hidden_grad
    context_ref[...] = times(c_ref[...], dense_ref[...]).astype(context_ref.dtype)
    c_sum_ref[...] += eight_rows(c_ref[...].astype(jnp.float32))
    h_sum_ref[...] += eight_rows(hidden_grad.astype(jnp.float32))


def upstream_parts(c, slope, w_down, dense, rows=256):
    tokens, width = c.shape
    units, columns = w_down.shape[0], dense.shape[1]

    def tile(size):
        return pl.BlockSpec((rows, size), lambda i: (i, 0))

    def total(size):
        return pl.BlockSpec((8, size), lambda i: (0, 0))

    return pl.pallas_call(
        upstream_kernel,
        grid=(tokens // rows,),
        out_shape=(
            jax.ShapeDtypeStruct((tokens, units), c.dtype), jax.ShapeDtypeStruct((tokens, columns), c.dtype),
            jax.ShapeDtypeStruct((8, width), jnp.float32), jax.ShapeDtypeStruct((8, units), jnp.float32),
        ),
        in_specs=[tile(width), tile(units), whole_block(w_down), whole_block(dense)],
        out_specs=[tile(units), tile(columns), total(width), total(units)],
        compiler_params=pltpu.CompilerParams(vmem_limit_bytes=48 * 1024 * 1024),
        cost_estimate=pl.CostEstimate(
            flops=2 * tokens * width * (units + columns), transcendentals=0,
            bytes_accessed=2 * tokens * (width + 3 * units + columns) + 2 * width * (units + columns),
        ),
        name="upstream_parts",
    )(c, slope, w_down, dense)


def attention_kernel(packed_ref, grad_ref, table_ref, context_ref, back_ref, sum_ref, q_ref, k_ref, low_ref, score_ref, turned_ref):
    length = packed_ref.shape[0]
    size = 256
    lanes = 128
    lane = lax.broadcasted_iota(jnp.int32, (size, lanes), 1)
    half = ROT // 2

    def tables(rows):
        table = turned_ref[rows, :]
        cosine = jnp.where(lane < half, table, jnp.where(lane < ROT, pltpu.roll(table, half, 1), 1.0))
        sine = jnp.where(lane < half, pltpu.roll(table, lanes - half, 1), jnp.where(lane < ROT, table, 0.0))
        return cosine, jnp.where(lane < half, -sine, sine)

    def swapped(array):
        return jnp.where(lane < half, pltpu.roll(array, lanes - half, 1), pltpu.roll(array, half, 1))

    def turn(array, cosine, sine):
        front = array[:, :lanes]
        return jnp.concatenate([front * cosine + swapped(front) * sine, array[:, lanes:]], axis=1)

    blocks = length // size
    for i in range(blocks):
        rows = pl.ds(i * size, size)
        turned_ref[rows, :] = jnp.transpose(table_ref[0, :, rows])
        cosine, sine = tables(rows)
        for part, ref in enumerate((q_ref, k_ref)):
            array = packed_ref[rows, part * HEAD_DIM : (part + 1) * HEAD_DIM].astype(jnp.float32)
            ref[rows, :] = turn(array, cosine, sine).astype(ref.dtype)

    values = pl.ds(2 * HEAD_DIM, HEAD_DIM)
    for i in range(blocks):
        rows = pl.ds(i * size, size)
        reach = (i + 1) * size
        keys = pl.ds(0, reach)
        scores = times_transposed(q_ref[rows, :], k_ref[keys, :]) * SCALE
        gradient = times_transposed(grad_ref[rows, :], packed_ref[keys, values])
        place = lax.broadcasted_iota(jnp.int32, (size, reach), 1)
        query = lax.broadcasted_iota(jnp.int32, (size, reach), 0) + i * size
        start = turned_ref[rows, ROT : ROT + 1].astype(jnp.int32)
        allowed = (place >= start) & (place <= query)
        scores = jnp.where(allowed, scores, NEGATIVE)
        exponent = jnp.exp(scores - jnp.max(scores, axis=-1, keepdims=True))
        attention = exponent / jnp.sum(exponent, axis=-1, keepdims=True)
        low = attention.astype(low_ref.dtype)
        low_ref[rows, keys] = low
        context_ref[rows, :] = times(low, packed_ref[keys, values]).astype(context_ref.dtype)
        centre = jnp.sum(attention * gradient, axis=-1, keepdims=True)
        score_grad = (attention * (gradient - centre)).astype(score_ref.dtype)
        score_ref[rows, keys] = score_grad
        query_grad = times(score_grad, k_ref[keys, :]) * SCALE
        cosine, sine = tables(rows)
        back_ref[rows, :HEAD_DIM] = turn(query_grad, cosine, -sine).astype(back_ref.dtype)

    for j in range(blocks):
        keys = pl.ds(j * size, size)
        rows = pl.ds(j * size, length - j * size)
        key_grad = contract_rows(score_ref[rows, keys], q_ref[rows, :]) * SCALE
        cosine, sine = tables(keys)
        back_ref[keys, HEAD_DIM : 2 * HEAD_DIM] = turn(key_grad, cosine, -sine).astype(back_ref.dtype)
        value_grad = contract_rows(low_ref[rows, keys], grad_ref[rows, :])
        back_ref[keys, values] = value_grad.astype(back_ref.dtype)

    @pl.when(pl.program_id(0) == 0)
    def _():
        sum_ref[...] = jnp.zeros_like(sum_ref)

    for i in range(blocks):
        sum_ref[...] += eight_rows(back_ref[pl.ds(i * size, size), :].astype(jnp.float32))


def attend(packed, context_grad, table, length):
    tokens, columns = packed.shape
    low = packed.dtype

    def tile(size):
        return pl.BlockSpec((length, size), lambda i: (i, 0))

    pairs = tokens * (length + 256) // 2
    return pl.pallas_call(
        attention_kernel,
        grid=(tokens // length,),
        out_shape=(
            jax.ShapeDtypeStruct((tokens, HEAD_DIM), low), jax.ShapeDtypeStruct((tokens, columns), low),
            jax.ShapeDtypeStruct((8, columns), jnp.float32),
        ),
        in_specs=[tile(columns), tile(HEAD_DIM), pl.BlockSpec((1, *table.shape[1:]), lambda i: (i, 0, 0))],
        out_specs=[tile(HEAD_DIM), tile(columns), pl.BlockSpec((8, columns), lambda i: (0, 0))],
        scratch_shapes=[
            pltpu.VMEM((length, HEAD_DIM), low), pltpu.VMEM((length, HEAD_DIM), low),
            pltpu.VMEM((length, length), low), pltpu.VMEM((length, length), low),
            pltpu.VMEM((length, table.shape[1]), jnp.float32),
        ],
        compiler_params=pltpu.CompilerParams(vmem_limit_bytes=48 * 1024 * 1024),
        cost_estimate=pl.CostEstimate(
            flops=14 * pairs * HEAD_DIM, transcendentals=pairs, bytes_accessed=tokens * (4 * columns + 4 * HEAD_DIM + 512)
        ),
        name="attend",
    )(packed, context_grad, table)


def output_kernel(context_ref, act_ref, dense_ref, down_ref, out_ref):
    total = times_transposed(context_ref[...], dense_ref[...]) + times(act_ref[...], down_ref[...])
    out_ref[...] = total.astype(out_ref.dtype)


def input_kernel(packed_ref, hidden_ref, qkv_ref, up_ref, norm_ref, out_ref):
    total = times(packed_ref[...], qkv_ref[...]) * norm_ref[0:1, :]
    total = total + times(hidden_ref[...], up_ref[...]) * norm_ref[2:3, :]
    out_ref[...] = total.astype(out_ref.dtype)


def two_products(kernel, name, former, latter, weights, rows=256):
    tokens = former.shape[0]
    width = weights[1].shape[1]
    depth = former.shape[1] + latter.shape[1]

    def tile(size):
        return pl.BlockSpec((rows, size), lambda i: (i, 0))

    return pl.pallas_call(
        kernel,
        grid=(tokens // rows,),
        out_shape=jax.ShapeDtypeStruct((tokens, width), former.dtype),
        in_specs=[tile(former.shape[1]), tile(latter.shape[1])] + [whole_block(a) for a in weights],
        out_specs=tile(width),
        compiler_params=pltpu.CompilerParams(vmem_limit_bytes=48 * 1024 * 1024),
        cost_estimate=pl.CostEstimate(
            flops=2 * tokens * depth * width, transcendentals=0,
            bytes_accessed=2 * (tokens * (depth + width) + depth * width),
        ),
        name=name,
    )(former, latter, *weights)


def gather_kernel(
    x_ref, c_ref, seg_ref, up_ref, qkv_ref, b_up_ref, b_qkv_ref, norm_ref,
    xg_ref, cg_ref, segs_ref, normed_out, normed_mlp_out, packed_out, act_out, slope_out,
    held, tile, w_up, w_qkv, normed, normed_mlp, packed, act, slope,
    seg_s, seg_r, seg_l, s1, r1, s2, r2, s3, r3, local, w_l, tile_l, keep_l,
):
    f, s = lax.axis_index("fsdp"), lax.axis_index("sp")
    core, col, row = f % 2, (f // 2) % 2, f // 4
    f_x, f_y, f_c = f + 2 - 4 * col, f + 4 - 8 * row, f + 1 - 2 * core
    f_d = f_x + 4 - 8 * row
    piece = xg_ref.shape[3]
    barrier = pltpu.get_barrier_semaphore()
    for k in range(1, 8):
        pl.semaphore_signal(barrier, inc=1, device_id=((f + k) % 8, s), device_id_type=MESH)
    for k in range(1, 4):
        pl.semaphore_signal(barrier, inc=1, device_id=(f, (s + k) % 4), device_id_type=MESH)
    pl.semaphore_wait(barrier, 10)
    pairs = ((x_ref, xg_ref), (c_ref, cg_ref))
    sent = []

    def send(src, dst, send_sem, recv_sem, device):
        copy = pltpu.make_async_remote_copy(
            src_ref=src, dst_ref=dst, send_sem=send_sem, recv_sem=recv_sem,
            device_id=device, device_id_type=MESH,
        )
        copy.start()
        sent.append(copy)

    def arrived(ref, recv_sem):
        pltpu.make_async_remote_copy(
            src_ref=ref, dst_ref=ref, send_sem=s1.at[0, 0], recv_sem=recv_sem,
            device_id=(f_c, s), device_id_type=MESH,
        ).wait_recv()

    holds = f // 2 == s
    keep_seg = pltpu.make_async_copy(seg_ref, segs_ref.at[core], seg_l.at[0])
    give_seg = [
        pltpu.make_async_remote_copy(
            src_ref=seg_ref, dst_ref=segs_ref.at[core], send_sem=seg_s.at[k], recv_sem=seg_r.at[core],
            device_id=((f + k) % 8, s), device_id_type=MESH,
        )
        for k in range(1, 8)
    ]

    @pl.when(holds)
    def _():
        keep_seg.start()
        for copy in give_seg:
            copy.start()

    weights = [
        pltpu.make_async_copy(up_ref, w_up, w_l.at[0]), pltpu.make_async_copy(qkv_ref, w_qkv, w_l.at[1])
    ]
    for copy in weights:
        copy.start()
    kept = []
    for a, (src, _) in enumerate(pairs):
        own = pltpu.make_async_copy(src.at[pl.ds(f * piece, piece)], held.at[a, f], local.at[a, 0])
        own.start()
        kept.append(own)
        for k in range(1, 8):
            j = (f + k) % 8
            send(src.at[pl.ds(j * piece, piece)], held.at[a, f], s1.at[a, k], r1.at[a, k], (j, s))

    def to_planes(a):
        out = pairs[a][1]
        kept[a].wait()
        for k in range(1, 8):
            arrived(held.at[a, (f + 8 - k) % 8], r1.at[a, k])
        for k in range(1, 4):
            plane = (s + k) % 4
            send(held.at[a, pl.ds(2 * plane, 2)], out.at[:, s, f], s2.at[a, k], r2.at[a, k], (f, plane))
        own = pltpu.make_async_copy(held.at[a, pl.ds(2 * s, 2)], out.at[:, s, f], local.at[a, 1])
        own.start()
        return own

    def spread(a, k):
        out = pairs[a][1]
        z = (s + 4 - k) % 4
        if k:
            arrived(out.at[:, z, f], r2.at[a, k])
        ref = out.at[:, z, f]
        send(ref, ref, s3.at[a, 0, k], r3.at[a, 0, k], (f_x, s))
        send(ref, ref, s3.at[a, 1, k], r3.at[a, 1, k], (f_y, s))
        send(ref, ref, s3.at[a, 2, k], r3.at[a, 2, k], (f_c, s))

    def pass_on(a, k):
        out = pairs[a][1]
        z = (s + 4 - k) % 4
        ref = out.at[:, z, f_x]
        arrived(ref, r3.at[a, 0, k])
        send(out.at[0, z, f_x], out.at[0, z, f_x], s3.at[a, 5, k], r3.at[a, 5, k], (f_y, s))
        send(ref, ref, s3.at[a, 3, k], r3.at[a, 3, k], (f_c, s))
        ref = out.at[:, z, f_y]
        arrived(ref, r3.at[a, 1, k])
        send(out.at[1, z, f_y], out.at[1, z, f_y], s3.at[a, 6, k], r3.at[a, 6, k], (f_x, s))
        send(ref, ref, s3.at[a, 4, k], r3.at[a, 4, k], (f_c, s))

    def pass_corner(a, k):
        out = pairs[a][1]
        z = (s + 4 - k) % 4
        for half in range(2):
            ref = out.at[half, z, f_d]
            arrived(ref, r3.at[a, 5 + half, k])
            send(ref, ref, s3.at[a, 7 + half, k], r3.at[a, 7 + half, k], (f_c, s))

    def from_core(a, k):
        out = pairs[a][1]
        z = (s + 4 - k) % 4
        g_x, g_y = f_c + 2 - 4 * col, f_c + 4 - 8 * row
        g_d = g_x + 4 - 8 * row
        arrived(out.at[:, z, f_c], r3.at[a, 2, k])
        arrived(out.at[:, z, g_x], r3.at[a, 3, k])
        arrived(out.at[:, z, g_y], r3.at[a, 4, k])
        for half in range(2):
            arrived(out.at[half, z, g_d], r3.at[a, 7 + half, k])

    results = ((normed, normed_out), (normed_mlp, normed_mlp_out), (packed, packed_out), (act, act_out), (slope, slope_out))
    size = 8 * piece

    def keep(b, z, n):
        rows = pl.ds(pl.multiple_of((b * 4 + z) * size, size), size)
        return pltpu.make_async_copy(results[n][0].at[b], results[n][1].at[rows], keep_l.at[b, n])

    def work(k):
        z = (s + 4 - k) % 4
        loads = [pltpu.make_async_copy(xg_ref.at[b, z], tile.at[b], tile_l.at[b]) for b in range(2)]
        for copy in loads:
            copy.start()
        if k == 0:
            for copy in weights:
                copy.wait()
        for b in range(2):
            loads[b].wait()
            if k:
                for n in range(5):
                    keep(b, (s + 5 - k) % 4, n).wait()

            @pl.loop(0, 8)
            def _(i):
                inputs = tile[b, i].astype(jnp.float32)
                centred = inputs - jnp.mean(inputs, axis=-1, keepdims=True)
                variance = jnp.mean(centred * centred, axis=-1, keepdims=True)
                scaled = centred * lax.rsqrt(variance + EPSILON)
                rows = pl.ds(pl.multiple_of(i * piece, piece), piece)
                low = normed.dtype
                normed[b, rows, :] = (scaled * norm_ref[0:1, :] + norm_ref[1:2, :]).astype(low)
                normed_mlp[b, rows, :] = (scaled * norm_ref[2:3, :] + norm_ref[3:4, :]).astype(low)

            hidden = times_transposed(normed_mlp[b], w_up[...]) + b_up_ref[...]
            packed[b] = (times_transposed(normed[b], w_qkv[...]) + b_qkv_ref[...]).astype(packed.dtype)
            activated, grown = gelu_pair(hidden)
            act[b] = activated.astype(act.dtype)
            slope[b] = grown
            for n in range(5):
                keep(b, z, n).start()

    own0 = to_planes(0)
    own1 = to_planes(1)
    steps = [(a, k) for a in range(2) for k in range(4)]
    for i in range(len(steps) + 2):
        if i < len(steps):
            a, k = steps[i]
            if k == 0:
                (own0 if a == 0 else own1).wait()
            spread(a, k)
        if 0 <= i - 1 < len(steps):
            pass_on(*steps[i - 1])
        if 0 <= i - 2 < len(steps):
            pass_corner(*steps[i - 2])
        if 5 <= i < 9:
            from_core(0, i - 5)
            work(i - 5)
    for k in range(4):
        from_core(1, k)
    for b in range(2):
        for n in range(5):
            keep(b, (s + 1) % 4, n).wait()
    for b in range(2):

        @pl.when(f != 2 * s + b)
        def _():
            arrived(segs_ref.at[b], seg_r.at[b])

    @pl.when(holds)
    def _():
        keep_seg.wait()
        for copy in give_seg:
            copy.wait_send()

    for copy in sent:
        copy.wait_send()


def gather_both(x, c, segments, w_up, w_qkv, b_up, b_qkv, norms):
    rows, width = x.shape
    piece = rows // 8
    tokens = 8 * rows
    units, columns = w_up.shape[0], w_qkv.shape[0]
    shape = jax.ShapeDtypeStruct((2, 4, 8, piece, width), x.dtype)
    dma = pltpu.SemaphoreType.DMA
    vmem = pltpu.VMEM
    anywhere = pl.BlockSpec(memory_space=pl.ANY)
    inside = pl.BlockSpec(memory_space=pltpu.VMEM)
    sizes = ((width, x.dtype), (width, x.dtype), (columns, x.dtype), (units, x.dtype), (units, jnp.float32))
    return pl.pallas_call(
        gather_kernel,
        out_shape=(
            shape, shape, jax.ShapeDtypeStruct((2, *segments.shape), segments.dtype),
            *(jax.ShapeDtypeStruct((tokens, size), kind) for size, kind in sizes),
        ),
        in_specs=[anywhere] * 5 + [inside] * 3,
        out_specs=[anywhere] * 8,
        scratch_shapes=[
            vmem((2, 8, piece, width), x.dtype), vmem((2, 8, piece, width), x.dtype),
            vmem(w_up.shape, w_up.dtype), vmem(w_qkv.shape, w_qkv.dtype),
            *(vmem((2, 8 * piece, size), kind) for size, kind in sizes),
            dma((8,)), dma((2,)), dma((1,)),
            dma((2, 8)), dma((2, 8)), dma((2, 4)), dma((2, 4)), dma((2, 9, 4)), dma((2, 9, 4)), dma((2, 2)),
            dma((2,)), dma((2,)), dma((2, 5)),
        ],
        compiler_params=pltpu.CompilerParams(
            collective_id=1, has_side_effects=True, vmem_limit_bytes=48 * 1024 * 1024
        ),
        name="gather_tokens",
    )(x, c, segments, w_up, w_qkv, b_up.reshape(1, units), b_qkv.reshape(1, columns), norms)


def reduce_kernel(
    sizes, steps,
    up_ref, qkv_ref, dense_ref, out_ref, back_ref, vec_ref, bias_ref,
    g_up, g_qkv, g_dense, o_out, o_back, o_small,
    line_a, line_b, turned, own, paired, block, crossed, reduced, homed, vec_in, small, small_in,
    in_s, in_r, mid_s, mid_r, end_s, end_r, own_l, keep_l,
    turn_s, turn_r, pair_s, pair_r, block_l, cross_s, cross_r, home_s, home_r, back_s, back_r, local,
    vec_s, vec_r, small_s, small_r,
):
    f, s = lax.axis_index("fsdp"), lax.axis_index("sp")
    core, col, row = f % 2, (f // 2) % 2, f // 4
    f_x, f_y, f_c = f + 2 - 4 * col, f + 4 - 8 * row, f + 1 - 2 * core
    f_d = f_x + 4 - 8 * row
    is_end = (s == 0) | (s == 3)
    is_mid = (s == 1) | (s == 2)
    inner = 1 + s // 3
    outer = 3 * (s // 2)
    facing = 3 - s
    barrier = pltpu.get_barrier_semaphore()
    for k in range(1, 8):
        pl.semaphore_signal(barrier, inc=1, device_id=((f + k) % 8, s), device_id_type=MESH)
    for k in range(1, 4):
        pl.semaphore_signal(barrier, inc=1, device_id=(f, (s + k) % 4), device_id_type=MESH)
    pl.semaphore_wait(barrier, 10)
    sent = []

    def send(src, dst, send_sem, recv_sem, device, track=True):
        copy = pltpu.make_async_remote_copy(
            src_ref=src, dst_ref=dst, send_sem=send_sem, recv_sem=recv_sem,
            device_id=device, device_id_type=MESH,
        )
        copy.start()
        if track:
            sent.append(copy)
        return copy

    def arrived(ref, recv_sem):
        pltpu.make_async_remote_copy(
            src_ref=ref, dst_ref=ref, send_sem=vec_s.at[0], recv_sem=recv_sem,
            device_id=(f_c, s), device_id_type=MESH,
        ).wait_recv()

    def copied(src, dst, sem):
        copy = pltpu.make_async_copy(src, dst, sem)
        copy.start()
        return copy

    part = turned.shape[0]
    span = dense_ref.shape[1]
    columns = pl.ds(pl.multiple_of(f * span, span), span)
    vec_own = copied(vec_ref.at[f], vec_in.at[f], local.at[0])
    turn_own = copied(dense_ref.at[pl.ds(f * part, part)], turned.at[:, columns], local.at[1])
    bias_own = copied(bias_ref, small.at[pl.ds(8, 8)], local.at[2])
    for k in range(1, 8):
        j = (f + k) % 8
        send(vec_ref.at[j], vec_in.at[f], vec_s.at[k], vec_r.at[k], (j, s))

    chunks = []
    offset = 0
    for ref, result, rows_of in (
        (up_ref, g_up, sizes[0]), (qkv_ref, g_qkv, sizes[1]), (turned, g_dense, sizes[2]),
    ):
        first = 0
        for rows in rows_of:
            chunks.append((ref, result, first, rows, offset))
            first += rows
            offset += rows
    count = len(chunks)
    ahead = 4

    def from_end(k):
        ref, _, first, rows, at = chunks[k]
        return pltpu.make_async_remote_copy(
            src_ref=ref.at[pl.ds(first, rows)], dst_ref=line_a.at[pl.ds(at, rows)],
            send_sem=in_s.at[k], recv_sem=in_r.at[k], device_id=(f, inner), device_id_type=MESH,
        )

    def across(k):
        _, _, _, rows, at = chunks[k]
        return pltpu.make_async_remote_copy(
            src_ref=line_a.at[pl.ds(at, rows)], dst_ref=line_b.at[pl.ds(at, rows)],
            send_sem=mid_s.at[k], recv_sem=mid_r.at[k], device_id=(f, facing), device_id_type=MESH,
        )

    def to_end(k):
        _, result, first, rows, at = chunks[k]
        return pltpu.make_async_remote_copy(
            src_ref=line_b.at[pl.ds(at, rows)], dst_ref=result.at[pl.ds(first, rows)],
            send_sem=end_s.at[k], recv_sem=end_r.at[k], device_id=(f, outer), device_id_type=MESH,
        )

    def load_own(k):
        ref, _, first, rows, _ = chunks[k]
        return pltpu.make_async_copy(
            ref.at[pl.ds(first, rows)], own.at[k % 3, pl.ds(0, rows)], own_l.at[k % 3]
        )

    def keep(k):
        _, result, first, rows, at = chunks[k]
        return pltpu.make_async_copy(
            line_b.at[pl.ds(at, rows)], result.at[pl.ds(first, rows)], keep_l.at[k]
        )

    tile = 16

    def add_rows(target, target_at, left, left_at, right, rows):
        @pl.loop(0, rows // tile)
        def _(i):
            at = pl.multiple_of(i * tile, tile)
            total = (
                left[pl.ds(left_at + at, tile), :].astype(jnp.float32)
                + right[pl.ds(at, tile), :].astype(jnp.float32)
            )
            target[pl.ds(target_at + at, tile), :] = total.astype(target.dtype)

    def mid_in(k):
        _, _, _, rows, at = chunks[k]
        load_own(k).wait()
        from_end(k).wait_recv()
        add_rows(line_a, at, line_a, at, own.at[k % 3], rows)
        across(k).start()
        if k + 3 < count:
            load_own(k + 3).start()

    def mid_out(k):
        _, _, _, rows, at = chunks[k]
        across(k).wait_recv()
        add_rows(line_b, at, line_b, at, line_a.at[pl.ds(at, rows)], rows)
        to_end(k).start()
        keep(k).start()

    pairs = ((out_ref, o_out), (back_ref, o_back))
    order = (f_d // 2, f_x // 2, f_y // 2, f // 2)
    for a, (ref, _) in enumerate(pairs):
        for n, q in enumerate(order):
            send(ref.at[:, :, q, 1 - core], paired.at[a, n], pair_s.at[a, n], pair_r.at[a, n], (f_c, s))
    for k in range(1, 8):
        j = (f + k) % 8
        send(dense_ref.at[pl.ds(j * part, part)], turned.at[:, columns], turn_s.at[k], turn_r.at[k], (j, s))

    def load_block(i):
        a, n = i // 4, i % 4
        return pltpu.make_async_copy(
            pairs[a][0].at[:, :, order[n], core], block.at[i % 2], block_l.at[i % 2]
        )

    load_block(0).start()
    load_block(1).start()

    def add_pair(i):
        a, n = i // 4, i % 4
        load_block(i).wait()
        arrived(paired.at[a, n], pair_r.at[a, n])

        @pl.loop(0, 8)
        def _(m):
            b, z = m // 4, m % 4
            total = paired[a, n, b, z].astype(jnp.float32) + block[i % 2, b, z].astype(jnp.float32)
            paired[a, n, b, z] = total.astype(paired.dtype)

        if n < 3:
            send(paired.at[a, n], crossed.at[a, n], cross_s.at[a, n], cross_r.at[a, n], ((f_d, f_x, f_y)[n], s))
        if i + 2 < 8:
            load_block(i + 2).start()

    placed = {}

    def add_chips(a):
        for n in range(3):
            arrived(crossed.at[a, n], cross_r.at[a, n])

        @pl.loop(0, 8)
        def _(m):
            b, z = m // 4, m % 4
            total = paired[a, 3, b, z].astype(jnp.float32)
            for n in range(3):
                total = total + crossed[a, n, b, z].astype(jnp.float32)
            reduced[a, b, z] = total.astype(reduced.dtype)

        for k in range(1, 4):
            z = (s + k) % 4
            send(reduced.at[a, :, z], homed.at[a, s], home_s.at[a, k], home_r.at[a, k], (f, z))
        placed["along", a] = copied(reduced.at[a, :, s], homed.at[a, s], local.at[3 + a])

    def go_home(a):
        result = pairs[a][1]
        placed["along", a].wait()
        for k in range(1, 4):
            arrived(homed.at[a, (s + 4 - k) % 4], home_r.at[a, k])
        for k in range(1, 8):
            j = (f + k) % 8
            send(homed.at[a, j // 2, j % 2], result.at[f], back_s.at[a, k], back_r.at[a, k], (j, s))
        placed["home", a] = copied(homed.at[a, f // 2, core], result.at[f], local.at[5 + a])

    def add_vectors():
        vec_own.wait()
        bias_own.wait()
        for k in range(1, 8):
            arrived(vec_in.at[(f + 8 - k) % 8], vec_r.at[k])
        total = vec_in[0]
        for j in range(1, 8):
            total = total + vec_in[j]
        small[0:8, :] = total
        for k in range(1, 4):
            send(small, small_in.at[s], small_s.at[k], small_r.at[k], (f, (s + k) % 4))
        placed["small"] = copied(small, small_in.at[s], local.at[7])

    def add_small():
        placed["small"].wait()
        for k in range(1, 4):
            arrived(small_in.at[(s + 4 - k) % 4], small_r.at[k])
        total = small_in[0]
        for z in range(1, 4):
            total = total + small_in[z]
        o_small[...] = total

    def turn_done():
        turn_own.wait()
        for k in range(1, 8):
            j = (f + 8 - k) % 8
            at = pl.ds(pl.multiple_of(j * span, span), span)
            arrived(turned.at[:, at], turn_r.at[k])

    def tasks(name):
        if name == "vec":
            add_vectors()
        elif name == "small":
            add_small()
        elif name == "turn":
            turn_done()
        elif name[0] == "p":
            add_pair(int(name[1:]))
        elif name[0] == "c":
            add_chips(int(name[1:]))
        elif name[0] == "h":
            go_home(int(name[1:]))

    @pl.when(is_end)
    def _():
        for k in range(ahead):
            from_end(k).start()

    @pl.when(is_mid)
    def _():
        for k in range(3):
            load_own(k).start()

    for k in range(count + 1):
        for name in steps.get(k, ()):
            tasks(name)

        @pl.when(is_mid)
        def _():
            if k < count:
                mid_in(k)
            if k >= 1:
                mid_out(k - 1)

        @pl.when(is_end)
        def _():
            if k >= 1:
                to_end(k - 1).wait_recv()
                if k - 1 + ahead < count:
                    from_end(k - 1 + ahead).start()

    for name in steps.get(count + 1, ()):
        tasks(name)
    for a in range(2):
        placed["home", a].wait()
        for k in range(1, 8):
            arrived(pairs[a][1].at[(f + 8 - k) % 8], back_r.at[a, k])
    for copy in sent:
        copy.wait_send()

    @pl.when(is_end)
    def _():
        for k in range(count):
            from_end(k).wait_send()

    @pl.when(is_mid)
    def _():
        for k in range(count):
            across(k).wait_send()
            to_end(k).wait_send()
            keep(k).wait()


STEPS = {
    0: ("p0", "p1", "p2", "p3", "vec"),
    1: ("p4", "p5"),
    2: ("p6", "p7"),
    3: ("turn", "small"),
    5: ("c0",),
    7: ("h0", "c1"),
    9: ("h1",),
}


def reduce_all(up, qkv, dense, out_part, back_part, vec, bias, sizes, steps=STEPS):
    width = up.shape[1]
    dtype = up.dtype
    total = sum(sum(rows) for rows in sizes)
    count = sum(len(rows) for rows in sizes)
    largest = max(max(rows) for rows in sizes)
    piece = out_part.shape[4]
    dma = pltpu.SemaphoreType.DMA
    grads = [jax.ShapeDtypeStruct((sum(rows), width), dtype) for rows in sizes]
    token = jax.ShapeDtypeStruct((8, piece, width), dtype)
    span = dense.shape[1]
    anywhere = pl.BlockSpec(memory_space=pl.ANY)
    vmem = pltpu.VMEM
    return pl.pallas_call(
        functools.partial(reduce_kernel, sizes, steps),
        out_shape=(*grads, token, token, jax.ShapeDtypeStruct((16, vec.shape[2]), jnp.float32)),
        in_specs=[anywhere] * 7,
        out_specs=[anywhere] * 5 + [pl.BlockSpec(memory_space=pltpu.VMEM)],
        scratch_shapes=[
            vmem((total, width), dtype), vmem((total, width), dtype), vmem((sum(sizes[-1]), width), dtype),
            vmem((3, largest, width), dtype),
            vmem((2, 4, 2, 4, piece, width), dtype), vmem((2, 2, 4, piece, width), dtype),
            vmem((2, 3, 2, 4, piece, width), dtype), vmem((2, 2, 4, piece, width), dtype),
            vmem((2, 4, 2, piece, width), dtype),
            vmem((8, 8, vec.shape[2]), jnp.float32), vmem((16, vec.shape[2]), jnp.float32),
            vmem((4, 16, vec.shape[2]), jnp.float32),
            dma((count,)), dma((count,)), dma((count,)), dma((count,)), dma((count,)), dma((count,)),
            dma((3,)), dma((count,)),
            dma((8,)), dma((8,)), dma((2, 4)), dma((2, 4)), dma((2,)), dma((2, 3)), dma((2, 3)),
            dma((2, 4)), dma((2, 4)), dma((2, 8)), dma((2, 8)), dma((8,)),
            dma((8,)), dma((8,)), dma((4,)), dma((4,)),
        ],
        compiler_params=pltpu.CompilerParams(
            collective_id=2, has_side_effects=True, vmem_limit_bytes=60 * 1024 * 1024
        ),
        name="reduce_all",
    )(up, qkv, dense, out_part, back_part, vec, bias)


def cut(rows, unit, first=False, last=False):
    sizes = [4 * unit] * (rows // (4 * unit))
    if first:
        sizes[:1] = [unit, unit, 2 * unit]
    if last:
        sizes[-1:] = [2 * unit, unit, unit]
    return tuple(sizes)


def reduce_tokens(terms, partial_out, partial_back, vectors, biases):
    up, qkv, dense = (term.astype(jnp.bfloat16) for term in terms)
    sizes = (
        cut(up.shape[0], 64, first=True),
        cut(qkv.shape[0], 64),
        cut(dense.shape[0] // 8, 64, last=True),
    )
    *grads, output, weighted, sums = reduce_all(
        up,
        qkv,
        dense,
        partial_out.astype(jnp.bfloat16),
        partial_back.astype(jnp.bfloat16),
        vectors,
        biases,
        sizes,
    )
    return [grad.astype(jnp.float32) for grad in grads], output, weighted, sums


def own_tokens(hidden_in, cotangent, output, weighted, shift):
    inputs = hidden_in.astype(jnp.float32)
    output = (inputs + (output.astype(jnp.float32) + shift)).astype(jnp.bfloat16)
    scaled, inverse = norm_scaled(inputs)
    weighted = weighted.astype(jnp.float32)
    first_mean = jnp.mean(weighted, axis=-1, keepdims=True)
    second_mean = jnp.mean(weighted * scaled, axis=-1, keepdims=True)
    input_grad = (
        cotangent.astype(jnp.float32) + inverse * (weighted - first_mean - scaled * second_mean)
    ).astype(jnp.bfloat16)
    return output, input_grad


def by_collectives(
    hidden_in,
    segments,
    ln1_gain,
    ln1_bias,
    ln2_gain,
    ln2_bias,
    w_qkv,
    b_qkv,
    w_dense,
    b_dense,
    w_up,
    b_up,
    w_down,
    b_down,
    cotangent,
):
    seq_local, shard_len, width = hidden_in.shape
    seq_len = segments.shape[1]
    nf, ns = lax.axis_size("fsdp"), lax.axis_size("sp")
    f_place, s_place = lax.axis_index("fsdp"), lax.axis_index("sp")
    seqs = seq_local * nf
    group = seqs // ns
    piece = shard_len // nf
    tokens = group * seq_len
    per_head = max(1, nf // HEADS)
    head_count = max(1, HEADS // nf)
    head_sets = [[head * per_head + k for k in range(per_head)] for head in range(nf // per_head)]

    def gather_tokens(block):
        part = lax.all_to_all(block, "fsdp", split_axis=1, concat_axis=0, tiled=True)
        part = lax.all_to_all(part, "sp", split_axis=0, concat_axis=1, tiled=True)
        return in_order(lax.all_gather(part, "fsdp", axis=0, tiled=True)).reshape(tokens, width)

    def scatter_tokens(partial):
        part = out_of_order(partial).reshape(nf * group, ns * piece, width)
        part = lax.psum_scatter(part, "fsdp", scatter_dimension=0, tiled=True)
        part = lax.all_to_all(part, "sp", split_axis=1, concat_axis=0, tiled=True)
        return lax.all_to_all(part, "fsdp", split_axis=0, concat_axis=1, tiled=True)

    def in_order(array):
        array = array.reshape(nf, group, ns, piece, -1)
        return array.transpose(1, 2, 0, 3, 4).reshape(group, seq_len, -1)

    def out_of_order(array):
        array = array.reshape(group, ns, nf, piece, -1)
        return array.transpose(2, 0, 1, 3, 4).reshape(tokens, -1)

    def over_head(array, axis):
        if per_head == 1:
            return array
        return lax.all_gather(
            array, "fsdp", axis=axis, tiled=True, axis_index_groups=head_sets
        )

    def own_columns(array):
        if per_head == 1:
            return array
        share = array.shape[-1] // per_head
        return lax.dynamic_slice_in_dim(array, (f_place % per_head) * share, share, array.ndim - 1)

    def own_part(vector):
        share = vector.shape[0] // nf
        return lax.dynamic_slice_in_dim(vector, f_place * share, share, 0)

    gathered, upstream = gather_tokens(hidden_in), gather_tokens(cotangent)
    rows = lax.all_gather(segments, "fsdp", axis=0, tiled=True)
    rows = lax.dynamic_slice_in_dim(rows, s_place * group, group, 0)

    dense_in = lax.all_to_all(w_dense, "fsdp", split_axis=1, concat_axis=0, tiled=True)
    head_qkv = over_head(w_qkv, 0)
    head_dense = over_head(dense_in, 1)
    head_bias = lax.dynamic_slice_in_dim(
        b_qkv, (f_place // per_head) * head_qkv.shape[0], head_qkv.shape[0], 0
    )

    scaled, _ = norm_scaled(gathered.astype(jnp.float32))
    normed = (scaled * ln1_gain + ln1_bias).astype(jnp.bfloat16)
    normed_mlp = (scaled * ln2_gain + ln2_bias).astype(jnp.bfloat16)

    hidden = times_transposed(normed_mlp, w_up) + own_part(b_up)
    activated, slope = gelu_pair(hidden)
    activated = activated.astype(jnp.bfloat16)
    down_term = contract_rows(activated, upstream).astype(jnp.bfloat16)
    grad_down_w = lax.psum(down_term, "sp").astype(jnp.float32)
    hidden_grad = (times_transposed(upstream, w_down) * slope).astype(jnp.bfloat16)
    up_term = contract_rows(hidden_grad, normed_mlp)
    mlp_norm_grad = times(hidden_grad, w_up)

    packed = (times_transposed(normed, head_qkv) + head_bias).astype(jnp.bfloat16)
    packed = packed.reshape(group, seq_len, head_count, 3 * HEAD_DIM)
    cos_table, sin_table = rotary_tables(rows)
    queries = rotate(packed[..., :HEAD_DIM].astype(jnp.float32), cos_table, sin_table).astype(
        jnp.bfloat16
    )
    keys_rot = rotate(
        packed[..., HEAD_DIM : 2 * HEAD_DIM].astype(jnp.float32), cos_table, sin_table
    ).astype(jnp.bfloat16)
    values = packed[..., 2 * HEAD_DIM :]
    mask = build_mask(rows)
    context, log_total = attend_forward(queries, keys_rot, values, mask)
    context = own_columns(context.reshape(tokens, -1))
    partial_out = times_transposed(context, dense_in) + times(activated, w_down)
    context_grad = times(upstream, head_dense).astype(jnp.bfloat16).reshape(
        group, seq_len, head_count, HEAD_DIM
    )
    query_grad, key_grad, value_grad = attend_backward(
        queries, keys_rot, values, mask, log_total, context_grad
    )
    packed_grad = jnp.concatenate(
        [
            unrotate(query_grad, cos_table, sin_table),
            unrotate(key_grad, cos_table, sin_table),
            value_grad,
        ],
        axis=-1,
    ).astype(jnp.bfloat16)
    packed_grad = own_columns(packed_grad.reshape(tokens, -1))
    attn_norm_grad = times(packed_grad, w_qkv)
    qkv_term = contract_rows(packed_grad, normed)
    dense_term = contract_rows(upstream, context).astype(jnp.bfloat16)

    partial_back = attn_norm_grad * ln1_gain + mlp_norm_grad * ln2_gain
    vectors = jnp.stack(
        [
            jnp.sum(attn_norm_grad * scaled, axis=0),
            jnp.sum(attn_norm_grad, axis=0),
            jnp.sum(mlp_norm_grad * scaled, axis=0),
            jnp.sum(mlp_norm_grad, axis=0),
        ]
    )
    bias_out = own_part(jnp.sum(upstream.astype(jnp.float32), axis=0))
    bias_qkv = jnp.sum(packed_grad.astype(jnp.float32), axis=0)
    bias_up = jnp.sum(hidden_grad.astype(jnp.float32), axis=0)
    vectors = lax.psum_scatter(vectors, "fsdp", scatter_dimension=1, tiled=True)
    vectors, bias_out, bias_qkv, bias_up = lax.psum((vectors, bias_out, bias_qkv, bias_up), "sp")
    output = scatter_tokens(rounded(partial_out))
    weighted = scatter_tokens(rounded(partial_back))
    dense_term = lax.all_to_all(dense_term, "fsdp", split_axis=0, concat_axis=1, tiled=True)
    grad_up_w, grad_qkv_w, grad_dense_w = (
        lax.psum(term.astype(jnp.bfloat16), "sp").astype(jnp.float32)
        for term in (up_term, qkv_term, dense_term)
    )
    output, input_grad = own_tokens(hidden_in, cotangent, output, weighted, b_dense + b_down)
    return (
        output,
        input_grad,
        vectors[0],
        vectors[1],
        vectors[2],
        vectors[3],
        grad_qkv_w,
        bias_qkv,
        grad_dense_w,
        bias_out,
        grad_up_w,
        bias_up,
        grad_down_w,
        bias_out,
    )


def norm_sums(weights, term, column_sums, gain, shift):
    weights = weights.astype(jnp.float32)
    column_sums = column_sums[:, None]
    scaled = jnp.sum(weights * (term.astype(jnp.float32) - column_sums * shift), axis=0) / gain
    return scaled, jnp.sum(weights * column_sums, axis=0)


def by_kernels(
    hidden_in,
    segments,
    ln1_gain,
    ln1_bias,
    ln2_gain,
    ln2_bias,
    w_qkv,
    b_qkv,
    w_dense,
    b_dense,
    w_up,
    b_up,
    w_down,
    b_down,
    cotangent,
):
    width = hidden_in.shape[2]
    seq_len = segments.shape[1]
    nf, ns = lax.axis_size("fsdp"), lax.axis_size("sp")
    group = nf // ns
    tokens = group * seq_len
    share = width // nf
    f_place = lax.axis_index("fsdp")

    def own_part(vector):
        size = vector.shape[0] // nf
        return lax.dynamic_slice_in_dim(vector, f_place * size, size, 0)

    norms = jnp.stack([ln1_gain, ln1_bias, ln2_gain, ln2_bias])
    _, upstream, rows, normed, normed_mlp, packed, activated, slope = gather_both(
        hidden_in[0],
        cotangent[0],
        segments.reshape(8, seq_len // 8),
        w_up,
        w_qkv,
        own_part(b_up),
        own_part(b_qkv),
        norms,
    )
    upstream = upstream.reshape(tokens, width)
    w_dense, upstream = lax.optimization_barrier((w_dense, upstream))
    dense_in = lax.all_to_all(w_dense, "fsdp", split_axis=1, concat_axis=0, tiled=True)
    down_term = contract_rows(activated, upstream).astype(jnp.bfloat16)
    grad_down_w = lax.psum(down_term, "sp").astype(jnp.float32)
    slope, down_term = lax.optimization_barrier((slope, down_term))
    hidden_grad, context_grad, c_sums, h_sums = upstream_parts(upstream, slope, w_down, dense_in)
    context, packed_grad, p_sums = attend(
        packed, context_grad, head_tables(rows.reshape(group, seq_len)), seq_len
    )
    partial_out = two_products(
        output_kernel, "partial_out", context, activated, (dense_in, w_down)
    )
    partial_back = two_products(
        input_kernel, "partial_back", packed_grad, hidden_grad, (w_qkv, w_up, norms)
    )
    up_term = contract_rows(hidden_grad, normed_mlp).astype(jnp.bfloat16)
    qkv_term = contract_rows(packed_grad, normed).astype(jnp.bfloat16)
    dense_term = contract_rows(upstream, context).astype(jnp.bfloat16)
    bias_up, bias_qkv = jnp.sum(h_sums, axis=0), jnp.sum(p_sums, axis=0)
    bias_out = own_part(jnp.sum(c_sums, axis=0))
    vectors = jnp.stack(
        norm_sums(w_qkv, qkv_term, bias_qkv, ln1_gain, ln1_bias)
        + norm_sums(w_up, up_term, bias_up, ln2_gain, ln2_bias)
    )
    vectors = jnp.pad(vectors.reshape(4, nf, share).transpose(1, 0, 2), ((0, 0), (0, 4), (0, 0)))
    biases = jnp.concatenate([bias_out, bias_qkv, bias_up]).reshape(8, share)
    token_shape = (group, ns, 4, 2, seq_len // (ns * nf), width)
    grads, output, weighted, sums = reduce_tokens(
        (up_term, qkv_term, dense_term),
        partial_out.reshape(token_shape),
        partial_back.reshape(token_shape),
        vectors,
        biases,
    )
    grad_up_w, grad_qkv_w, grad_dense_w = grads
    bias_out = sums[8]
    output, input_grad = own_tokens(
        hidden_in,
        cotangent,
        output.reshape(hidden_in.shape),
        weighted.reshape(hidden_in.shape),
        b_dense + b_down,
    )
    return (
        output,
        input_grad,
        sums[0],
        sums[1],
        sums[2],
        sums[3],
        grad_qkv_w,
        sums[9:12].reshape(-1),
        grad_dense_w,
        bias_out,
        grad_up_w,
        sums[12:16].reshape(-1),
        grad_down_w,
        bias_out,
    )


def per_device(hidden_in, *rest):
    sizes = (lax.axis_size("fsdp"), lax.axis_size("sp"), hidden_in.shape[0])
    shapes = (hidden_in.shape[1] % 256, hidden_in.shape[2] % (8 * HEAD_DIM), rest[9].shape[0] % 256)
    if sizes == (8, 4, 1) and HEADS == 8 and not any(shapes):
        return by_kernels(hidden_in, *rest)
    return by_collectives(hidden_in, *rest)


def solution(mesh):
    rows = P("fsdp", "sp", None)
    first = P("fsdp", None)
    return jax.shard_map(
        per_device,
        mesh=mesh,
        in_specs=(
            rows,
            first,
            P(),
            P(),
            P(),
            P(),
            first,
            P(),
            first,
            P(),
            first,
            P(),
            first,
            P(),
            rows,
        ),
        out_specs=(
            rows,
            rows,
            P("fsdp"),
            P("fsdp"),
            P("fsdp"),
            P("fsdp"),
            first,
            P("fsdp"),
            first,
            P("fsdp"),
            first,
            P("fsdp"),
            first,
            P("fsdp"),
        ),
        check_vma=False,
    )
```

```python
import functools
import math

import jax
import jax.numpy as jnp
from jax import lax
from jax.experimental import pallas as pl
from jax.experimental.pallas import tpu as pltpu
from jax.sharding import PartitionSpec as P

MESH = pl.DeviceIdType.MESH

HEADS = 8
HEAD_DIM = 256
ROT = 64


EPSILON = 1e-05
NEGATIVE = -1e30
ROOT_HALF = 0.7071067811865476
ROOT_TWO_PI = 2.5066282746310002
SCALE = 1.0 / math.sqrt(HEAD_DIM)


def rounded(array):
    return lax.reduce_precision(array.astype(jnp.float32), 8, 7).astype(jnp.bfloat16)


def contract_rows(former, latter):
    return lax.dot_general(former, latter, (((0,), (0,)), ((), ())), preferred_element_type=jnp.float32)


def times_transposed(former, latter):
    return lax.dot_general(former, latter, (((1,), (1,)), ((), ())), preferred_element_type=jnp.float32)


def times(former, latter):
    return jnp.dot(former, latter, preferred_element_type=jnp.float32)


def norm_scaled(inputs):
    average = jnp.mean(inputs, axis=-1, keepdims=True)
    centred = inputs - average
    variance = jnp.mean(centred * centred, axis=-1, keepdims=True)
    inverse = lax.rsqrt(variance + EPSILON)
    return (centred * inverse, inverse)


def gelu_pair(hidden):
    cumulative = 0.5 * (1.0 + lax.erf(hidden * ROOT_HALF))
    return (hidden * cumulative, cumulative + hidden * (jnp.exp(-0.5 * hidden * hidden) * (1.0 / ROOT_TWO_PI)))


def document_starts(segment_rows):
    places = jnp.arange(segment_rows.shape[-1], dtype=jnp.int32)
    changes = jnp.concatenate([jnp.ones_like(segment_rows[..., :1]), (segment_rows[..., 1:] != segment_rows[..., :-1]).astype(jnp.int32)], axis=-1)
    return (places, lax.cummax(changes * places, axis=segment_rows.ndim - 1))


def frequencies():
    return 1.0 / jnp.power(10000.0, jnp.arange(0, ROT, 2).astype(jnp.float32) / ROT)


def rotary_tables(segment_rows):
    places, starts = document_starts(segment_rows)
    angles = (places - starts).astype(jnp.float32)[..., None] * frequencies()
    angles = jnp.concatenate([angles, angles], axis=-1)
    return (jnp.cos(angles), jnp.sin(angles))


def head_tables(segment_rows):
    places, starts = document_starts(segment_rows)
    angles = (places - starts).astype(jnp.float32)[:, None, :] * frequencies()[None, :, None]
    starts = jnp.broadcast_to(starts.astype(jnp.float32)[:, None, :], (starts.shape[0], ROT, starts.shape[1]))
    return jnp.concatenate([jnp.cos(angles), jnp.sin(angles), starts], axis=1)


def rotate(heads_part, cos_table, sin_table):
    half_rot = ROT // 2
    turned = heads_part[..., :ROT]
    swapped = jnp.concatenate([-turned[..., half_rot:], turned[..., :half_rot]], axis=-1)
    turned = turned * cos_table[..., None, :] + swapped * sin_table[..., None, :]
    return jnp.concatenate([turned, heads_part[..., ROT:]], axis=-1)


def unrotate(grads_part, cos_table, sin_table):
    half_rot = ROT // 2
    turned = grads_part[..., :ROT]
    along_sin = turned * sin_table[..., None, :]
    back_turn = jnp.concatenate([along_sin[..., half_rot:], -along_sin[..., :half_rot]], axis=-1)
    turned = turned * cos_table[..., None, :] + back_turn
    return jnp.concatenate([turned, grads_part[..., ROT:]], axis=-1)


def build_mask(segment_rows):
    places = jnp.arange(segment_rows.shape[-1], dtype=jnp.int32)
    return (segment_rows[:, :, None] == segment_rows[:, None, :]) & (places[None, :] <= places[:, None])


def attention_scores(queries, keys_rot):
    return jnp.einsum('bqhd,bkhd->bhqk', queries, keys_rot, preferred_element_type=jnp.float32) * SCALE


def attend_forward(queries, keys_rot, values, mask):
    scores = jnp.where(mask[:, None], attention_scores(queries, keys_rot), NEGATIVE)
    row_top = jnp.max(scores, axis=-1, keepdims=True)
    exponent = jnp.exp(scores - row_top)
    row_total = jnp.sum(exponent, axis=-1, keepdims=True)
    attention = (exponent / row_total).astype(jnp.bfloat16)
    context = jnp.einsum('bhqk,bkhd->bqhd', attention, values, preferred_element_type=jnp.float32)
    return (context.astype(jnp.bfloat16), row_top + jnp.log(row_total))


def attend_backward(queries, keys_rot, values, mask, log_total, context_grad):
    scores = attention_scores(queries, keys_rot)
    attention = jnp.where(mask[:, None], jnp.exp(scores - log_total), 0.0)
    value_grad = jnp.einsum('bhqk,bqhd->bkhd', attention.astype(jnp.bfloat16), context_grad, preferred_element_type=jnp.float32)
    attention_grad = jnp.einsum('bqhd,bkhd->bhqk', context_grad, values, preferred_element_type=jnp.float32)
    row_centre = jnp.sum(attention * attention_grad, axis=-1, keepdims=True)
    score_grad = (attention * (attention_grad - row_centre)).astype(jnp.bfloat16)
    query_grad = jnp.einsum('bhqk,bkhd->bqhd', score_grad, keys_rot, preferred_element_type=jnp.float32) * SCALE
    key_grad = jnp.einsum('bhqk,bqhd->bkhd', score_grad, queries, preferred_element_type=jnp.float32) * SCALE
    return (query_grad, key_grad, value_grad)


def whole_block(array):
    return pl.BlockSpec(array.shape, lambda *_: (0,) * array.ndim, pipeline_mode=pl.Buffered(1))


def eight_rows(array):
    return jnp.sum(array.reshape(array.shape[0] // 8, 8, array.shape[1]), axis=0)


def upstream_kernel(c_ref, slope_ref, down_ref, dense_ref, grad_ref, context_ref, c_sum_ref, h_sum_ref):
    @pl.when(pl.program_id(0) == 0)
    def _():
        c_sum_ref[...] = jnp.zeros_like(c_sum_ref)
        h_sum_ref[...] = jnp.zeros_like(h_sum_ref)
    hidden_grad = (times_transposed(c_ref[...], down_ref[...]) * slope_ref[...]).astype(grad_ref.dtype)
    grad_ref[...] = hidden_grad
    context_ref[...] = times(c_ref[...], dense_ref[...]).astype(context_ref.dtype)
    c_sum_ref[...] += eight_rows(c_ref[...].astype(jnp.float32))
    h_sum_ref[...] += eight_rows(hidden_grad.astype(jnp.float32))


def upstream_parts(c, slope, w_down, dense, rows=256):
    tokens, width = c.shape
    units, columns = (w_down.shape[0], dense.shape[1])

    def tile(size):
        return pl.BlockSpec((rows, size), lambda i: (i, 0))

    def total(size):
        return pl.BlockSpec((8, size), lambda i: (0, 0))
    return pl.pallas_call(upstream_kernel, grid=(tokens // rows,), out_shape=(jax.ShapeDtypeStruct((tokens, units), c.dtype),
        jax.ShapeDtypeStruct((tokens, columns), c.dtype), jax.ShapeDtypeStruct((8, width), jnp.float32), jax.ShapeDtypeStruct((8, units),
        jnp.float32)), in_specs=[tile(width), tile(units), whole_block(w_down), whole_block(dense)], out_specs=[tile(units), tile(columns),
        total(width), total(units)], compiler_params=pltpu.CompilerParams(vmem_limit_bytes=48 * 1024 * 1024),
        cost_estimate=pl.CostEstimate(flops=2 * tokens * width * (units + columns), transcendentals=0,
        bytes_accessed=2 * tokens * (width + 3 * units + columns) + 2 * width * (units + columns)), name='upstream_parts')(c, slope, w_down, dense)


def attention_kernel(packed_ref, grad_ref, table_ref, context_ref, back_ref, sum_ref, q_ref, k_ref, low_ref, score_ref, turned_ref):
    length = packed_ref.shape[0]
    size = 256
    lanes = 128
    lane = lax.broadcasted_iota(jnp.int32, (size, lanes), 1)
    half = ROT // 2

    def tables(rows):
        table = turned_ref[rows, :]
        cosine = jnp.where(lane < half, table, jnp.where(lane < ROT, pltpu.roll(table, half, 1), 1.0))
        sine = jnp.where(lane < half, pltpu.roll(table, lanes - half, 1), jnp.where(lane < ROT, table, 0.0))
        return (cosine, jnp.where(lane < half, -sine, sine))

    def swapped(array):
        return jnp.where(lane < half, pltpu.roll(array, lanes - half, 1), pltpu.roll(array, half, 1))

    def turn(array, cosine, sine):
        front = array[:, :lanes]
        return jnp.concatenate([front * cosine + swapped(front) * sine, array[:, lanes:]], axis=1)
    blocks = length // size
    for i in range(blocks):
        rows = pl.ds(i * size, size)
        turned_ref[rows, :] = jnp.transpose(table_ref[0, :, rows])
        cosine, sine = tables(rows)
        for part, ref in enumerate((q_ref, k_ref)):
            array = packed_ref[rows, part * HEAD_DIM:(part + 1) * HEAD_DIM].astype(jnp.float32)
            ref[rows, :] = turn(array, cosine, sine).astype(ref.dtype)
    values = pl.ds(2 * HEAD_DIM, HEAD_DIM)
    for i in range(blocks):
        rows = pl.ds(i * size, size)
        reach = (i + 1) * size
        keys = pl.ds(0, reach)
        scores = times_transposed(q_ref[rows, :], k_ref[keys, :]) * SCALE
        gradient = times_transposed(grad_ref[rows, :], packed_ref[keys, values])
        place = lax.broadcasted_iota(jnp.int32, (size, reach), 1)
        query = lax.broadcasted_iota(jnp.int32, (size, reach), 0) + i * size
        start = turned_ref[rows, ROT:ROT + 1].astype(jnp.int32)
        allowed = (place >= start) & (place <= query)
        scores = jnp.where(allowed, scores, NEGATIVE)
        exponent = jnp.exp(scores - jnp.max(scores, axis=-1, keepdims=True))
        attention = exponent / jnp.sum(exponent, axis=-1, keepdims=True)
        low = attention.astype(low_ref.dtype)
        low_ref[rows, keys] = low
        context_ref[rows, :] = times(low, packed_ref[keys, values]).astype(context_ref.dtype)
        centre = jnp.sum(attention * gradient, axis=-1, keepdims=True)
        score_grad = (attention * (gradient - centre)).astype(score_ref.dtype)
        score_ref[rows, keys] = score_grad
        query_grad = times(score_grad, k_ref[keys, :]) * SCALE
        cosine, sine = tables(rows)
        back_ref[rows, :HEAD_DIM] = turn(query_grad, cosine, -sine).astype(back_ref.dtype)
    for j in range(blocks):
        keys = pl.ds(j * size, size)
        rows = pl.ds(j * size, length - j * size)
        key_grad = contract_rows(score_ref[rows, keys], q_ref[rows, :]) * SCALE
        cosine, sine = tables(keys)
        back_ref[keys, HEAD_DIM:2 * HEAD_DIM] = turn(key_grad, cosine, -sine).astype(back_ref.dtype)
        value_grad = contract_rows(low_ref[rows, keys], grad_ref[rows, :])
        back_ref[keys, values] = value_grad.astype(back_ref.dtype)

    @pl.when(pl.program_id(0) == 0)
    def _():
        sum_ref[...] = jnp.zeros_like(sum_ref)
    for i in range(blocks):
        sum_ref[...] += eight_rows(back_ref[pl.ds(i * size, size), :].astype(jnp.float32))


def attend(packed, context_grad, table, length):
    tokens, columns = packed.shape
    low = packed.dtype

    def tile(size):
        return pl.BlockSpec((length, size), lambda i: (i, 0))
    pairs = tokens * (length + 256) // 2
    return pl.pallas_call(attention_kernel, grid=(tokens // length,), out_shape=(jax.ShapeDtypeStruct((tokens, HEAD_DIM), low),
        jax.ShapeDtypeStruct((tokens, columns), low), jax.ShapeDtypeStruct((8, columns), jnp.float32)), in_specs=[tile(columns), tile(HEAD_DIM),
        pl.BlockSpec((1, *table.shape[1:]), lambda i: (i, 0, 0))], out_specs=[tile(HEAD_DIM), tile(columns), pl.BlockSpec((8, columns), lambda i: (0,
        0))], scratch_shapes=[pltpu.VMEM((length, HEAD_DIM), low), pltpu.VMEM((length, HEAD_DIM), low), pltpu.VMEM((length, length), low),
        pltpu.VMEM((length, length), low), pltpu.VMEM((length, table.shape[1]), jnp.float32)],
        compiler_params=pltpu.CompilerParams(vmem_limit_bytes=48 * 1024 * 1024), cost_estimate=pl.CostEstimate(flops=14 * pairs * HEAD_DIM,
        transcendentals=pairs, bytes_accessed=tokens * (4 * columns + 4 * HEAD_DIM + 512)), name='attend')(packed, context_grad, table)


def remote(src, dst, send_sem, recv_sem, device):
    return pltpu.make_async_remote_copy(src_ref=src, dst_ref=dst, send_sem=send_sem, recv_sem=recv_sem, device_id=device, device_id_type=MESH)


def copied(src, dst, sem):
    copy = pltpu.make_async_copy(src, dst, sem)
    copy.start()
    return copy


def meet(f, s):
    barrier = pltpu.get_barrier_semaphore()
    for k in range(1, 8):
        pl.semaphore_signal(barrier, inc=1, device_id=((f + k) % 8, s), device_id_type=MESH)
    for k in range(1, 4):
        pl.semaphore_signal(barrier, inc=1, device_id=(f, (s + k) % 4), device_id_type=MESH)
    pl.semaphore_wait(barrier, 10)


def neighbours(f):
    f_x, f_y = (f + 2 - 4 * (f // 2 % 2), f + 4 - 8 * (f // 4))
    return (f_x, f_y, f + 1 - 2 * (f % 2), f_x + f_y - f)


def gather_kernel(x_ref, c_ref, seg_ref, up_ref, qkv_ref, b_up_ref, b_qkv_ref, norm_ref, xg_ref, cg_ref, segs_ref, normed_out, normed_mlp_out,
    packed_out, act_out, slope_out, held, tile, w_up, w_qkv, normed, normed_mlp, packed, act, slope, seg_s, seg_r, seg_l, s1, r1, s2, r2, s3, r3,
    local, w_l, tile_l, keep_l):
    f, s = (lax.axis_index('fsdp'), lax.axis_index('sp'))
    core = f % 2
    f_x, f_y, f_c, f_d = neighbours(f)
    piece = xg_ref.shape[3]
    meet(f, s)
    pairs = ((x_ref, xg_ref), (c_ref, cg_ref))
    sent = []

    def send(src, dst, send_sem, recv_sem, device):
        copy = remote(src, dst, send_sem, recv_sem, device)
        copy.start()
        sent.append(copy)

    def arrived(ref, recv_sem):
        remote(ref, ref, s1.at[0, 0], recv_sem, (f_c, s)).wait_recv()
    holds = f // 2 == s
    keep_seg = pltpu.make_async_copy(seg_ref, segs_ref.at[core], seg_l.at[0])
    give_seg = [remote(seg_ref, segs_ref.at[core], seg_s.at[k], seg_r.at[core], ((f + k) % 8, s)) for k in range(1, 8)]

    @pl.when(holds)
    def _():
        keep_seg.start()
        for copy in give_seg:
            copy.start()
    weights = [pltpu.make_async_copy(up_ref, w_up, w_l.at[0]), pltpu.make_async_copy(qkv_ref, w_qkv, w_l.at[1])]
    for copy in weights:
        copy.start()
    kept = []
    for a, (src, _) in enumerate(pairs):
        own = pltpu.make_async_copy(src.at[pl.ds(f * piece, piece)], held.at[a, f], local.at[a, 0])
        own.start()
        kept.append(own)
        for k in range(1, 8):
            j = (f + k) % 8
            send(src.at[pl.ds(j * piece, piece)], held.at[a, f], s1.at[a, k], r1.at[a, k], (j, s))

    def to_planes(a):
        out = pairs[a][1]
        kept[a].wait()
        for k in range(1, 8):
            arrived(held.at[a, (f + 8 - k) % 8], r1.at[a, k])
        for k in range(1, 4):
            plane = (s + k) % 4
            send(held.at[a, pl.ds(2 * plane, 2)], out.at[:, s, f], s2.at[a, k], r2.at[a, k], (f, plane))
        own = pltpu.make_async_copy(held.at[a, pl.ds(2 * s, 2)], out.at[:, s, f], local.at[a, 1])
        own.start()
        return own

    def spread(a, k):
        out = pairs[a][1]
        z = (s + 4 - k) % 4
        if k:
            arrived(out.at[:, z, f], r2.at[a, k])
        ref = out.at[:, z, f]
        send(ref, ref, s3.at[a, 0, k], r3.at[a, 0, k], (f_x, s))
        send(ref, ref, s3.at[a, 1, k], r3.at[a, 1, k], (f_y, s))
        send(ref, ref, s3.at[a, 2, k], r3.at[a, 2, k], (f_c, s))

    def pass_on(a, k):
        out = pairs[a][1]
        z = (s + 4 - k) % 4
        ref = out.at[:, z, f_x]
        arrived(ref, r3.at[a, 0, k])
        send(out.at[0, z, f_x], out.at[0, z, f_x], s3.at[a, 5, k], r3.at[a, 5, k], (f_y, s))
        send(ref, ref, s3.at[a, 3, k], r3.at[a, 3, k], (f_c, s))
        ref = out.at[:, z, f_y]
        arrived(ref, r3.at[a, 1, k])
        send(out.at[1, z, f_y], out.at[1, z, f_y], s3.at[a, 6, k], r3.at[a, 6, k], (f_x, s))
        send(ref, ref, s3.at[a, 4, k], r3.at[a, 4, k], (f_c, s))

    def pass_corner(a, k):
        out = pairs[a][1]
        z = (s + 4 - k) % 4
        for half in range(2):
            ref = out.at[half, z, f_d]
            arrived(ref, r3.at[a, 5 + half, k])
            send(ref, ref, s3.at[a, 7 + half, k], r3.at[a, 7 + half, k], (f_c, s))

    def from_core(a, k):
        out = pairs[a][1]
        z = (s + 4 - k) % 4
        g_x, g_y, _, g_d = neighbours(f_c)
        arrived(out.at[:, z, f_c], r3.at[a, 2, k])
        arrived(out.at[:, z, g_x], r3.at[a, 3, k])
        arrived(out.at[:, z, g_y], r3.at[a, 4, k])
        for half in range(2):
            arrived(out.at[half, z, g_d], r3.at[a, 7 + half, k])
    results = ((normed, normed_out), (normed_mlp, normed_mlp_out), (packed, packed_out), (act, act_out), (slope, slope_out))
    size = 8 * piece

    def keep(b, z, n):
        rows = pl.ds(pl.multiple_of((b * 4 + z) * size, size), size)
        return pltpu.make_async_copy(results[n][0].at[b], results[n][1].at[rows], keep_l.at[b, n])

    def work(k):
        z = (s + 4 - k) % 4
        loads = [pltpu.make_async_copy(xg_ref.at[b, z], tile.at[b], tile_l.at[b]) for b in range(2)]
        for copy in loads:
            copy.start()
        if k == 0:
            for copy in weights:
                copy.wait()
        for b in range(2):
            loads[b].wait()
            if k:
                for n in range(5):
                    keep(b, (s + 5 - k) % 4, n).wait()

            @pl.loop(0, 8)
            def _(i):
                inputs = tile[b, i].astype(jnp.float32)
                centred = inputs - jnp.mean(inputs, axis=-1, keepdims=True)
                variance = jnp.mean(centred * centred, axis=-1, keepdims=True)
                scaled = centred * lax.rsqrt(variance + EPSILON)
                rows = pl.ds(pl.multiple_of(i * piece, piece), piece)
                low = normed.dtype
                normed[b, rows, :] = (scaled * norm_ref[0:1, :] + norm_ref[1:2, :]).astype(low)
                normed_mlp[b, rows, :] = (scaled * norm_ref[2:3, :] + norm_ref[3:4, :]).astype(low)
            hidden = times_transposed(normed_mlp[b], w_up[...]) + b_up_ref[...]
            packed[b] = (times_transposed(normed[b], w_qkv[...]) + b_qkv_ref[...]).astype(packed.dtype)
            activated, grown = gelu_pair(hidden)
            act[b] = activated.astype(act.dtype)
            slope[b] = grown
            for n in range(5):
                keep(b, z, n).start()
    own0 = to_planes(0)
    own1 = to_planes(1)
    steps = [(a, k) for a in range(2) for k in range(4)]
    for i in range(len(steps) + 2):
        if i < len(steps):
            a, k = steps[i]
            if k == 0:
                (own0 if a == 0 else own1).wait()
            spread(a, k)
        if 0 <= i - 1 < len(steps):
            pass_on(*steps[i - 1])
        if 0 <= i - 2 < len(steps):
            pass_corner(*steps[i - 2])
        if 5 <= i < 9:
            from_core(0, i - 5)
            work(i - 5)
    for k in range(4):
        from_core(1, k)
    for b in range(2):
        for n in range(5):
            keep(b, (s + 1) % 4, n).wait()
    for b in range(2):

        @pl.when(f != 2 * s + b)
        def _():
            arrived(segs_ref.at[b], seg_r.at[b])

    @pl.when(holds)
    def _():
        keep_seg.wait()
        for copy in give_seg:
            copy.wait_send()
    for copy in sent:
        copy.wait_send()


def gather_both(x, c, segments, w_up, w_qkv, b_up, b_qkv, norms):
    rows, width = x.shape
    piece = rows // 8
    tokens = 8 * rows
    units, columns = (w_up.shape[0], w_qkv.shape[0])
    shape = jax.ShapeDtypeStruct((2, 4, 8, piece, width), x.dtype)
    dma = pltpu.SemaphoreType.DMA
    vmem = pltpu.VMEM
    anywhere = pl.BlockSpec(memory_space=pl.ANY)
    inside = pl.BlockSpec(memory_space=pltpu.VMEM)
    sizes = ((width, x.dtype), (width, x.dtype), (columns, x.dtype), (units, x.dtype), (units, jnp.float32))
    return pl.pallas_call(gather_kernel, out_shape=(shape, shape, jax.ShapeDtypeStruct((2, *segments.shape), segments.dtype),
        *(jax.ShapeDtypeStruct((tokens, size), kind) for size, kind in sizes)), in_specs=[anywhere] * 5 + [inside] * 3, out_specs=[anywhere] * 8,
        scratch_shapes=[vmem((2, 8, piece, width), x.dtype), vmem((2, 8, piece, width), x.dtype), vmem(w_up.shape, w_up.dtype), vmem(w_qkv.shape,
        w_qkv.dtype), *(vmem((2, 8 * piece, size), kind) for size, kind in sizes), dma((8,)), dma((2,)), dma((1,)), dma((2, 8)), dma((2, 8)), dma((2,
        4)), dma((2, 4)), dma((2, 9, 4)), dma((2, 9, 4)), dma((2, 2)), dma((2,)), dma((2,)), dma((2, 5))],
        compiler_params=pltpu.CompilerParams(collective_id=1, has_side_effects=True, vmem_limit_bytes=48 * 1024 * 1024), name='gather_tokens')(x, c,
        segments, w_up, w_qkv, b_up.reshape(1, units), b_qkv.reshape(1, columns), norms)


def finish_kernel(down_ref, dense_ref, hidden_ref, normed_mlp_ref, packed_ref, normed_ref, act_ref, context_ref, up_w_ref, down_w_ref, qkv_w_ref,
    dense_w_ref, norm_ref, h_col_ref, p_col_ref, bias_ref, g_down, g_up, g_qkv, g_dense, o_out, o_back, part, paired, kept, crossed, homed, o_small,
    line_a, line_b, turned, big, hidden, packed, weight, qkv_w, dense_w, context, act, total, made, own, right, vecs, vec_out, vec_in, small,
    small_in, load_l, act_l, part_l, tile_s, tile_r, tile_l, left_l, right_l, in_s, in_r, mid_s, mid_r, end_s, end_r, own_l, keep_l, turn_s, turn_r,
    cross_s, cross_r, home_s, home_r, back_s, back_r, local, vec_s, vec_r, small_s, small_r):
    f, s = (lax.axis_index('fsdp'), lax.axis_index('sp'))
    core = f % 2
    f_x, f_y, f_c, f_d = neighbours(f)
    is_end = (s == 0) | (s == 3)
    is_mid = (s == 1) | (s == 2)
    inner, outer, facing = (1 + s // 3, 3 * (s // 2), 3 - s)
    unit = made.shape[3]
    size = 8 * unit
    low = made.dtype
    meet(f, s)
    sent = []

    def send(src, dst, send_sem, recv_sem, device):
        copy = remote(src, dst, send_sem, recv_sem, device)
        copy.start()
        return copy

    def arrived(ref, recv_sem):
        remote(ref, ref, vec_s.at[0], recv_sem, (f_c, s)).wait_recv()
    chunks = []
    at = 0
    groups = {}
    for name, ref, first, result in (('down', down_ref, 0, g_down), ('up', part, 0, g_up), ('qkv', part, g_up.shape[0], g_qkv), ('dense', turned, 0,
        g_dense)):
        for g in range(result.shape[0]):
            cuts = (4,)
            if not chunks:
                cuts = (1, 1, 2)
            if name == 'dense':
                cuts = (2, 1, 1)
            start = 0
            for pairs_of in cuts:
                chunks.append((ref, first + g, result, g, start, pairs_of, at))
                groups[len(chunks) - 1] = (name, first + g)
                start += pairs_of
            at += 1
    count = len(chunks)
    ahead = 4

    def cut(ref, g, k):
        _, _, _, _, start, pairs_of, _ = chunks[k]
        return ref.at[g, pl.ds(start, pairs_of)]

    def source(k):
        return cut(chunks[k][0], chunks[k][1], k)

    def goal(k):
        return cut(chunks[k][2], chunks[k][3], k)

    def from_end(k):
        return remote(source(k), cut(line_a, chunks[k][6], k), in_s.at[k], in_r.at[k], (f, inner))

    def across(k):
        return remote(cut(line_a, chunks[k][6], k), cut(line_b, chunks[k][6], k), mid_s.at[k], mid_r.at[k], (f, facing))

    def to_end(k):
        return remote(cut(line_b, chunks[k][6], k), goal(k), end_s.at[k], end_r.at[k], (f, outer))

    def load_own(k):
        return pltpu.make_async_copy(source(k), cut(own, k % 2, k), own_l.at[k % 2])

    def keep(k):
        return pltpu.make_async_copy(cut(line_b, chunks[k][6], k), goal(k), keep_l.at[k])

    def add_units(target, others, number):
        @pl.loop(0, number)
        def _(i):
            for half in range(2):
                rows = pl.ds(half * (unit // 2), unit // 2)
                value = target[i // 2, i % 2, rows, :].astype(jnp.float32)
                for other in others:
                    value = value + other[i // 2, i % 2, rows, :].astype(jnp.float32)
                target[i // 2, i % 2, rows, :] = value.astype(low)

    def mid_in(k):
        load_own(k).wait()
        from_end(k).wait_recv()
        add_units(cut(line_a, chunks[k][6], k), [cut(own, k % 2, k)], 2 * chunks[k][5])
        across(k).start()
        if k + 2 < count:
            load_own(k + 2).start()

    def mid_out(k):
        across(k).wait_recv()
        add_units(cut(line_b, chunks[k][6], k), [cut(line_a, chunks[k][6], k)], 2 * chunks[k][5])
        to_end(k).start()
        keep(k).start()
    coming = {'big': copied(normed_mlp_ref, big, load_l.at[0]), 'hidden': copied(hidden_ref, hidden, load_l.at[1]), 'weight': copied(up_w_ref,
        weight, load_l.at[2]), 'packed': copied(packed_ref, packed, load_l.at[3]), 'qkv': copied(qkv_w_ref, qkv_w, load_l.at[4]),
        'dense': copied(dense_w_ref, dense_w, load_l.at[5]), 'context': copied(context_ref, context, load_l.at[6])}

    def ready(*names):
        for name in names:
            if coming[name] is not None:
                coming[name].wait()
                coming[name] = None
    span = dense_ref.shape[4]
    columns = pl.ds(pl.multiple_of(f * span, span), span)
    turn_own = copied(dense_ref.at[f], turned.at[0, :, :, :, columns], local.at[0])
    bias_own = copied(bias_ref, small.at[pl.ds(8, 8)], local.at[1])
    vecs[...] = jnp.zeros_like(vecs)
    vec_out[...] = jnp.zeros_like(vec_out)
    busy = {0: [], 1: []}
    turns = [0]

    def next_made():
        slot = turns[0] % 2
        turns[0] += 1
        for wait in busy[slot]:
            wait()
        busy[slot] = []
        return slot
    stores = {}

    def finish_group(g, weights, first, column_ref, which):
        slot = next_made()

        @pl.loop(0, 8)
        def _(i):
            rows = pl.ds(pl.multiple_of(i * unit, unit), unit)
            wide = pl.ds(pl.multiple_of(first + i * unit, unit), unit)
            value = total[rows, :]
            made[slot, i // 2, i % 2] = value.astype(low)
            line = weights[wide, :].astype(jnp.float32)
            sums = column_ref[wide, 0:1]
            scaled = line * (value - sums * norm_ref[2 * which + 1:2 * which + 2, :])
            vecs[2 * which] += eight_rows(scaled)
            vecs[2 * which + 1] += eight_rows(line * sums)
        stores[g] = copied(made.at[slot], part.at[g], part_l.at[g])
        busy[slot] = [functools.partial(stored, g)]

    def stored(g):
        if stores[g] is not None:
            stores[g].wait()
            stores[g] = None

    def up_group(g):
        ready('big', 'hidden', 'weight')
        total[...] = contract_rows(hidden[:, g * size:(g + 1) * size], big[...])
        finish_group(g, weight, g * size, h_col_ref, 1)
        if g == g_up.shape[0] - 1:
            coming['big'] = copied(normed_ref, big, load_l.at[7])
            coming['weight'] = copied(down_w_ref, weight, load_l.at[8])
            load_act(0)

    def qkv_group(g):
        ready('big', 'packed', 'qkv')
        total[...] = contract_rows(packed[:, g * size:(g + 1) * size], big[...])
        finish_group(g_up.shape[0] + g, qkv_w, g * size, p_col_ref, 0)

    def load_act(t):
        coming['act', t] = copied(act_ref.at[pl.ds(t * size, size)], act.at[t % 2], act_l.at[t % 2])

    def give_tile(a, t, value):
        b, z = (t // 4, t % 4)
        slot = next_made()
        made[slot] = value.astype(low).reshape(4, 2, unit, value.shape[1])
        give = send(made.at[slot, :, 1 - core], paired.at[a, :, z, b], tile_s.at[a, t], tile_r.at[a, t], (f_c, s))
        hold = copied(made.at[slot, :, core], kept.at[a, :, z, b], tile_l.at[a, t])
        busy[slot] = [give.wait_send, hold.wait]

    def out_tile(t):
        ready('weight', 'context', 'dense', ('act', t))
        if t < 7:
            load_act(t + 1)
        rows = slice(t * size, (t + 1) * size)
        value = times_transposed(context[rows, :], dense_w[...]) + times(act[t % 2], weight[...])
        give_tile(0, t, value)
        if t == 7:
            coming['weight'] = copied(up_w_ref, weight, load_l.at[9])

    def back_tile(t):
        ready('weight', 'packed', 'qkv', 'hidden')
        rows = slice(t * size, (t + 1) * size)
        value = times(packed[rows, :], qkv_w[...]) * norm_ref[0:1, :]
        value = value + times(hidden[rows, :], weight[...]) * norm_ref[2:3, :]
        give_tile(1, t, value)
    results = (o_out, o_back)
    order = (f_d // 2, f_x // 2, f_y // 2, f // 2)
    def free(slot):
        for wait in busy[slot]:
            wait()
        busy[slot] = []

    def tiles_here(a):
        for slot in range(2):
            free(slot)
        for t in range(8):
            arrived(paired.at[a, :, t % 4, t // 4], tile_r.at[a, t])

    def add_pair(a, n):
        if n == 0:
            tiles_here(a)
        slot = next_made()
        first = copied(paired.at[a, order[n]], made.at[slot], left_l.at[slot])
        second = copied(kept.at[a, order[n]], right.at[slot], right_l.at[slot])
        first.wait()
        second.wait()
        add_units(made.at[slot], [right.at[slot]], 8)
        give = send(made.at[slot], crossed.at[a, n], cross_s.at[a, n], cross_r.at[a, n], ((f_d, f_x, f_y)[n], s))
        busy[slot] = [give.wait_send]

    def add_chips(a):
        one, two = next_made(), next_made()
        first = copied(paired.at[a, order[3]], made.at[one], left_l.at[one])
        second = copied(kept.at[a, order[3]], right.at[0], right_l.at[0])
        arrived(crossed.at[a, 0], cross_r.at[a, 0])
        third = copied(crossed.at[a, 0], made.at[two], left_l.at[two])
        arrived(crossed.at[a, 1], cross_r.at[a, 1])
        fourth = copied(crossed.at[a, 1], right.at[1], right_l.at[1])
        first.wait()
        second.wait()
        add_units(made.at[one], [right.at[0]], 8)
        arrived(crossed.at[a, 2], cross_r.at[a, 2])
        fifth = copied(crossed.at[a, 2], right.at[0], right_l.at[0])
        third.wait()
        fourth.wait()
        fifth.wait()
        add_units(made.at[one], [made.at[two], right.at[1], right.at[0]], 8)
        for k in range(1, 4):
            z = (s + k) % 4
            give = send(made.at[one, z], homed.at[a, s], home_s.at[a, k], home_r.at[a, k], (f, z))
            busy[one].append(give.wait_send)
        hold = copied(made.at[one, s], homed.at[a, s], local.at[2 + a])
        busy[one].append(hold.wait)
        home_slot[a] = one
    homes, home_slot = {}, {}

    def go_home(a):
        free(home_slot[a])
        for k in range(1, 4):
            arrived(homed.at[a, (s + 4 - k) % 4], home_r.at[a, k])
        for k in range(1, 8):
            j = (f + k) % 8
            sent.append(send(homed.at[a, j // 2, j % 2], results[a].at[f], back_s.at[a, k], back_r.at[a, k], (j, s)))
        homes[a] = copied(homed.at[a, f // 2, core], results[a].at[f], local.at[4 + a])

    def give_vectors():
        for which in range(2):
            gain = norm_ref[2 * which:2 * which + 1, :]
            scaled = jnp.sum(vecs[2 * which], axis=0, keepdims=True) / gain
            plain = jnp.sum(vecs[2 * which + 1], axis=0, keepdims=True)
            for j in range(8):
                part_of = slice(j * span, (j + 1) * span)
                vec_out[j, 2 * which:2 * which + 1, :] = scaled[:, part_of]
                vec_out[j, 2 * which + 1:2 * which + 2, :] = plain[:, part_of]
        for k in range(1, 8):
            j = (f + k) % 8
            sent.append(send(vec_out.at[j], vec_in.at[f], vec_s.at[k], vec_r.at[k], (j, s)))
        homes['vec'] = copied(vec_out.at[f], vec_in.at[f], local.at[6])

    def add_vectors():
        homes['vec'].wait()
        bias_own.wait()
        for k in range(1, 8):
            arrived(vec_in.at[(f + 8 - k) % 8], vec_r.at[k])
        value = vec_in[0]
        for j in range(1, 8):
            value = value + vec_in[j]
        small[0:8, :] = value
        for k in range(1, 4):
            sent.append(send(small, small_in.at[s], small_s.at[k], small_r.at[k], (f, (s + k) % 4)))
        homes['small'] = copied(small, small_in.at[s], local.at[7])

    def add_small():
        homes['small'].wait()
        for k in range(1, 4):
            arrived(small_in.at[(s + 4 - k) % 4], small_r.at[k])
        value = small_in[0]
        for z in range(1, 4):
            value = value + small_in[z]
        o_small[...] = value

    def turn_start():
        for k in range(1, 8):
            j = (f + k) % 8
            sent.append(send(dense_ref.at[j], turned.at[0, :, :, :, columns], turn_s.at[k], turn_r.at[k], (j, s)))

    def turn_done():
        turn_own.wait()
        for k in range(1, 8):
            j = (f + 8 - k) % 8
            there = pl.ds(pl.multiple_of(j * span, span), span)
            arrived(turned.at[0, :, :, :, there], turn_r.at[k])

    def task(name, i):
        if name == 'turn':
            turn_start()
        elif name == 'turned':
            turn_done()
        elif name == 'up':
            up_group(i)
        elif name == 'qkv':
            qkv_group(i)
        elif name == 'out':
            out_tile(i)
        elif name == 'back':
            back_tile(i)
        elif name == 'pair':
            add_pair(i // 3, i % 3)
        elif name == 'chips':
            add_chips(i)
        elif name == 'home':
            go_home(i)
        elif name == 'vectors':
            give_vectors()
        elif name == 'sums':
            add_vectors()
        else:
            add_small()

    @pl.when(is_end)
    def _():
        for k in range(ahead):
            from_end(k).start()

    @pl.when(is_mid)
    def _():
        for k in range(2):
            load_own(k).start()
    for k in range(count + 2):
        for name, first, last in FINISH_STEPS[k] if k in FINISH_STEPS else ():
            for i in range(first, last):
                task(name, i)
        if k + ahead - 1 in groups and groups[k + ahead - 1][0] in ('up', 'qkv'):
            stored(groups[k + ahead - 1][1])

        @pl.when(is_mid)
        def _():
            if k < count:
                mid_in(k)
            if 1 <= k <= count:
                mid_out(k - 1)

        @pl.when(is_end)
        def _():
            if 1 <= k <= count:
                to_end(k - 1).wait_recv()
                if k - 1 + ahead < count:
                    from_end(k - 1 + ahead).start()
    for a in range(2):
        homes[a].wait()
        for k in range(1, 8):
            arrived(results[a].at[(f + 8 - k) % 8], back_r.at[a, k])
    for slot in range(2):
        free(slot)
    for copy in sent:
        copy.wait_send()

    @pl.when(is_end)
    def _():
        for k in range(count):
            from_end(k).wait_send()

    @pl.when(is_mid)
    def _():
        for k in range(count):
            across(k).wait_send()
            to_end(k).wait_send()
            keep(k).wait()


FINISH_STEPS = {
    0: (("turn", 0, 1), ("up", 0, 2)),
    1: (("up", 2, 3),),
    2: (("up", 3, 4),),
    3: (("qkv", 0, 3), ("out", 0, 2)),
    4: (("out", 2, 8),),
    5: (("back", 0, 4), ("pair", 0, 3)),
    6: (("back", 4, 8), ("vectors", 0, 1)),
    7: (("pair", 3, 6), ("turned", 0, 1)),
    8: (("chips", 0, 1), ("sums", 0, 1)),
    9: (("home", 0, 1),),
    10: (("chips", 1, 2), ("small", 0, 1)),
    12: (("home", 1, 2),),
}


def finish(down, dense, hidden_grad, normed_mlp, packed_grad, normed, act, context, w_up, w_down, w_qkv, dense_in, norms, h_sums, p_sums, bias):
    width = down.shape[1]
    tokens = hidden_grad.shape[0]
    low = down.dtype
    unit = tokens // 64
    size = 8 * unit
    span = width // 8

    def grouped(rows):
        return (rows // size, 4, 2, unit, width)

    def columns(sums):
        return jnp.broadcast_to(sums[:, None], (sums.shape[0], 128))
    sets = [w.shape[0] // size for w in (down, w_up, w_qkv)]
    number = sum(sets) + 1
    count = sum(sets) + 5
    sums = [jax.ShapeDtypeStruct(grouped(n * size), low) for n in (*sets, 1)]
    token = jax.ShapeDtypeStruct((8, unit, width), low)
    halves = jax.ShapeDtypeStruct((2, 4, 4, 2, unit, width), low)
    others = [jax.ShapeDtypeStruct(grouped((sets[1] + sets[2]) * size), low), halves, halves, jax.ShapeDtypeStruct((2, 3, 4, 2, unit, width), low),
        jax.ShapeDtypeStruct((2, 4, 2, unit, width), low)]
    dma = pltpu.SemaphoreType.DMA
    vmem = pltpu.VMEM
    anywhere = pl.BlockSpec(memory_space=pl.ANY)
    inside = pl.BlockSpec(memory_space=pltpu.VMEM)
    result = pl.pallas_call(finish_kernel, out_shape=(*sums, token, token, *others, jax.ShapeDtypeStruct((16, span), jnp.float32)),
        in_specs=[anywhere] * 12 + [inside] * 3 + [anywhere], out_specs=[anywhere] * 11 + [inside], scratch_shapes=[vmem((number, 4, 2, unit, width),
        low), vmem((number, 4, 2, unit, width), low), vmem((1, 4, 2, unit, width), low), vmem((tokens, width), low), vmem(hidden_grad.shape, low),
        vmem(packed_grad.shape, low), vmem(w_up.shape, low), vmem(w_qkv.shape, low), vmem(dense_in.shape, low), vmem(context.shape, low), vmem((2,
        size, act.shape[1]), low), vmem((size, width), jnp.float32), *(vmem((2, 4, 2, unit, width), low) for _ in range(3)), vmem((4, 8, width),
        jnp.float32), vmem((8, 8, span), jnp.float32), vmem((8, 8, span), jnp.float32), vmem((16, span), jnp.float32), vmem((4, 16, span),
        jnp.float32), dma((10,)), dma((2,)), dma((sets[1] + sets[2],)), dma((2, 8)), dma((2, 8)), dma((2, 8)), dma((2,)), dma((2,)), dma((count,)),
        dma((count,)), dma((count,)), dma((count,)), dma((count,)), dma((count,)), dma((2,)), dma((count,)), dma((8,)), dma((8,)), dma((2, 3)),
        dma((2, 3)), dma((2, 4)), dma((2, 4)), dma((2, 8)), dma((2, 8)), dma((8,)), dma((8,)), dma((8,)), dma((4,)), dma((4,))],
        compiler_params=pltpu.CompilerParams(collective_id=2, has_side_effects=True, vmem_limit_bytes=60 * 1024 * 1024),
        name='finish')(down.reshape(grouped(down.shape[0])), dense.reshape(8, 4, 2, unit, span), hidden_grad, normed_mlp, packed_grad, normed, act,
        context, w_up, w_down, w_qkv, dense_in, norms, columns(h_sums), columns(p_sums), bias)
    grads = [grad.reshape(-1, width) for grad in result[:4]]
    return (grads, result[4], result[5], result[11])


def own_tokens(hidden_in, cotangent, output, weighted, shift):
    inputs = hidden_in.astype(jnp.float32)
    output = (inputs + (output.astype(jnp.float32) + shift)).astype(jnp.bfloat16)
    scaled, inverse = norm_scaled(inputs)
    weighted = weighted.astype(jnp.float32)
    first_mean = jnp.mean(weighted, axis=-1, keepdims=True)
    second_mean = jnp.mean(weighted * scaled, axis=-1, keepdims=True)
    input_grad = (cotangent.astype(jnp.float32) + inverse * (weighted - first_mean - scaled * second_mean)).astype(jnp.bfloat16)
    return (output, input_grad)


def by_collectives(hidden_in, segments, ln1_gain, ln1_bias, ln2_gain, ln2_bias, w_qkv, b_qkv, w_dense, b_dense, w_up, b_up, w_down, b_down,
    cotangent):
    seq_local, shard_len, width = hidden_in.shape
    seq_len = segments.shape[1]
    nf, ns = (lax.axis_size('fsdp'), lax.axis_size('sp'))
    f_place, s_place = (lax.axis_index('fsdp'), lax.axis_index('sp'))
    seqs = seq_local * nf
    group = seqs // ns
    piece = shard_len // nf
    tokens = group * seq_len
    per_head = max(1, nf // HEADS)
    head_count = max(1, HEADS // nf)
    head_sets = [[head * per_head + k for k in range(per_head)] for head in range(nf // per_head)]

    def gather_tokens(block):
        part = lax.all_to_all(block, 'fsdp', split_axis=1, concat_axis=0, tiled=True)
        part = lax.all_to_all(part, 'sp', split_axis=0, concat_axis=1, tiled=True)
        return in_order(lax.all_gather(part, 'fsdp', axis=0, tiled=True)).reshape(tokens, width)

    def scatter_tokens(partial):
        part = out_of_order(partial).reshape(nf * group, ns * piece, width)
        part = lax.psum_scatter(part, 'fsdp', scatter_dimension=0, tiled=True)
        part = lax.all_to_all(part, 'sp', split_axis=1, concat_axis=0, tiled=True)
        return lax.all_to_all(part, 'fsdp', split_axis=0, concat_axis=1, tiled=True)

    def in_order(array):
        array = array.reshape(nf, group, ns, piece, -1)
        return array.transpose(1, 2, 0, 3, 4).reshape(group, seq_len, -1)

    def out_of_order(array):
        array = array.reshape(group, ns, nf, piece, -1)
        return array.transpose(2, 0, 1, 3, 4).reshape(tokens, -1)

    def over_head(array, axis):
        if per_head == 1:
            return array
        return lax.all_gather(array, 'fsdp', axis=axis, tiled=True, axis_index_groups=head_sets)

    def own_columns(array):
        if per_head == 1:
            return array
        share = array.shape[-1] // per_head
        return lax.dynamic_slice_in_dim(array, f_place % per_head * share, share, array.ndim - 1)

    def own_part(vector):
        share = vector.shape[0] // nf
        return lax.dynamic_slice_in_dim(vector, f_place * share, share, 0)
    gathered, upstream = (gather_tokens(hidden_in), gather_tokens(cotangent))
    rows = lax.all_gather(segments, 'fsdp', axis=0, tiled=True)
    rows = lax.dynamic_slice_in_dim(rows, s_place * group, group, 0)
    dense_in = lax.all_to_all(w_dense, 'fsdp', split_axis=1, concat_axis=0, tiled=True)
    head_qkv = over_head(w_qkv, 0)
    head_dense = over_head(dense_in, 1)
    head_bias = lax.dynamic_slice_in_dim(b_qkv, f_place // per_head * head_qkv.shape[0], head_qkv.shape[0], 0)
    scaled, _ = norm_scaled(gathered.astype(jnp.float32))
    normed = (scaled * ln1_gain + ln1_bias).astype(jnp.bfloat16)
    normed_mlp = (scaled * ln2_gain + ln2_bias).astype(jnp.bfloat16)
    hidden = times_transposed(normed_mlp, w_up) + own_part(b_up)
    activated, slope = gelu_pair(hidden)
    activated = activated.astype(jnp.bfloat16)
    down_term = contract_rows(activated, upstream).astype(jnp.bfloat16)
    grad_down_w = lax.psum(down_term, 'sp').astype(jnp.float32)
    hidden_grad = (times_transposed(upstream, w_down) * slope).astype(jnp.bfloat16)
    up_term = contract_rows(hidden_grad, normed_mlp)
    mlp_norm_grad = times(hidden_grad, w_up)
    packed = (times_transposed(normed, head_qkv) + head_bias).astype(jnp.bfloat16)
    packed = packed.reshape(group, seq_len, head_count, 3 * HEAD_DIM)
    cos_table, sin_table = rotary_tables(rows)
    queries = rotate(packed[..., :HEAD_DIM].astype(jnp.float32), cos_table, sin_table).astype(jnp.bfloat16)
    keys_rot = rotate(packed[..., HEAD_DIM:2 * HEAD_DIM].astype(jnp.float32), cos_table, sin_table).astype(jnp.bfloat16)
    values = packed[..., 2 * HEAD_DIM:]
    mask = build_mask(rows)
    context, log_total = attend_forward(queries, keys_rot, values, mask)
    context = own_columns(context.reshape(tokens, -1))
    partial_out = times_transposed(context, dense_in) + times(activated, w_down)
    context_grad = times(upstream, head_dense).astype(jnp.bfloat16).reshape(group, seq_len, head_count, HEAD_DIM)
    query_grad, key_grad, value_grad = attend_backward(queries, keys_rot, values, mask, log_total, context_grad)
    packed_grad = jnp.concatenate([unrotate(query_grad, cos_table, sin_table), unrotate(key_grad, cos_table, sin_table), value_grad],
        axis=-1).astype(jnp.bfloat16)
    packed_grad = own_columns(packed_grad.reshape(tokens, -1))
    attn_norm_grad = times(packed_grad, w_qkv)
    qkv_term = contract_rows(packed_grad, normed)
    dense_term = contract_rows(upstream, context).astype(jnp.bfloat16)
    partial_back = attn_norm_grad * ln1_gain + mlp_norm_grad * ln2_gain
    vectors = jnp.stack([jnp.sum(attn_norm_grad * scaled, axis=0), jnp.sum(attn_norm_grad, axis=0), jnp.sum(mlp_norm_grad * scaled, axis=0),
        jnp.sum(mlp_norm_grad, axis=0)])
    bias_out = own_part(jnp.sum(upstream.astype(jnp.float32), axis=0))
    bias_qkv = jnp.sum(packed_grad.astype(jnp.float32), axis=0)
    bias_up = jnp.sum(hidden_grad.astype(jnp.float32), axis=0)
    vectors = lax.psum_scatter(vectors, 'fsdp', scatter_dimension=1, tiled=True)
    vectors, bias_out, bias_qkv, bias_up = lax.psum((vectors, bias_out, bias_qkv, bias_up), 'sp')
    output = scatter_tokens(rounded(partial_out))
    weighted = scatter_tokens(rounded(partial_back))
    dense_term = lax.all_to_all(dense_term, 'fsdp', split_axis=0, concat_axis=1, tiled=True)
    grad_up_w, grad_qkv_w, grad_dense_w = (lax.psum(term.astype(jnp.bfloat16), 'sp').astype(jnp.float32) for term in (up_term, qkv_term, dense_term))
    output, input_grad = own_tokens(hidden_in, cotangent, output, weighted, b_dense + b_down)
    return (output, input_grad, vectors[0], vectors[1], vectors[2], vectors[3], grad_qkv_w, bias_qkv, grad_dense_w, bias_out, grad_up_w, bias_up,
        grad_down_w, bias_out)


def by_kernels(hidden_in, segments, ln1_gain, ln1_bias, ln2_gain, ln2_bias, w_qkv, b_qkv, w_dense, b_dense, w_up, b_up, w_down, b_down, cotangent):
    width = hidden_in.shape[2]
    seq_len = segments.shape[1]
    nf, ns = (lax.axis_size('fsdp'), lax.axis_size('sp'))
    group = nf // ns
    tokens = group * seq_len
    share = width // nf
    f_place = lax.axis_index('fsdp')

    def own_part(vector):
        size = vector.shape[0] // nf
        return lax.dynamic_slice_in_dim(vector, f_place * size, size, 0)
    norms = jnp.stack([ln1_gain, ln1_bias, ln2_gain, ln2_bias])
    _, upstream, rows, normed, normed_mlp, packed, activated, slope = gather_both(hidden_in[0], cotangent[0], segments.reshape(8, seq_len // 8),
        w_up, w_qkv, own_part(b_up), own_part(b_qkv), norms)
    upstream = upstream.reshape(tokens, width)
    w_dense, upstream = lax.optimization_barrier((w_dense, upstream))
    dense_in = lax.all_to_all(w_dense, 'fsdp', split_axis=1, concat_axis=0, tiled=True)
    early = activated.shape[1] // 2
    down_term = contract_rows(activated[:, :early], upstream).astype(jnp.bfloat16)
    early_down_w = lax.psum(down_term, 'sp').astype(jnp.float32)
    slope, activated, down_term = lax.optimization_barrier((slope, activated, down_term))
    hidden_grad, context_grad, c_sums, h_sums = upstream_parts(upstream, slope, w_down, dense_in)
    context, packed_grad, p_sums = attend(packed, context_grad, head_tables(rows.reshape(group, seq_len)), seq_len)
    late_down_term = contract_rows(activated[:, early:], upstream).astype(jnp.bfloat16)
    dense_term = contract_rows(upstream, context).astype(jnp.bfloat16)
    bias_up, bias_qkv = (jnp.sum(h_sums, axis=0), jnp.sum(p_sums, axis=0))
    bias_out = own_part(jnp.sum(c_sums, axis=0))
    grads, output, weighted, sums = finish(late_down_term, dense_term, hidden_grad, normed_mlp, packed_grad, normed, activated, context, w_up,
        w_down, w_qkv, dense_in, norms, bias_up, bias_qkv, jnp.concatenate([bias_out, bias_qkv, bias_up]).reshape(8, share))
    late_down_w, grad_up_w, grad_qkv_w, grad_dense_w = (grad.astype(jnp.float32) for grad in grads)
    grad_down_w = jnp.concatenate([early_down_w, late_down_w])
    bias_out = sums[8]
    output, input_grad = own_tokens(hidden_in, cotangent, output.reshape(hidden_in.shape), weighted.reshape(hidden_in.shape), b_dense + b_down)
    return (output, input_grad, sums[0], sums[1], sums[2], sums[3], grad_qkv_w, sums[9:12].reshape(-1), grad_dense_w, bias_out, grad_up_w,
        sums[12:16].reshape(-1), grad_down_w, bias_out)


def per_device(hidden_in, *rest):
    sizes = (lax.axis_size('fsdp'), lax.axis_size('sp'), hidden_in.shape[0])
    shapes = (hidden_in.shape[1] % 256, hidden_in.shape[2] % (8 * HEAD_DIM), rest[9].shape[0] % 256)
    if sizes == (8, 4, 1) and HEADS == 8 and (not any(shapes)):
        return by_kernels(hidden_in, *rest)
    return by_collectives(hidden_in, *rest)


def solution(mesh):
    rows = P('fsdp', 'sp', None)
    first = P('fsdp', None)
    return jax.shard_map(per_device, mesh=mesh, in_specs=(rows, first, P(), P(), P(), P(), first, P(), first, P(), first, P(), first, P(), rows),
        out_specs=(rows, rows, P('fsdp'), P('fsdp'), P('fsdp'), P('fsdp'), first, P('fsdp'), first, P('fsdp'), first, P('fsdp'), first, P('fsdp')),
        check_vma=False)
```

```python
import functools
import math

import jax
import jax.numpy as jnp
from jax import lax
from jax.experimental import pallas as pl
from jax.experimental.pallas import tpu as pltpu
from jax.sharding import PartitionSpec as P

MESH = pl.DeviceIdType.MESH

HEADS = 8
HEAD_DIM = 256
ROT = 64


EPSILON = 1e-05
NEGATIVE = -1e30
ROOT_HALF = 0.7071067811865476
ROOT_TWO_PI = 2.5066282746310002
SCALE = 1.0 / math.sqrt(HEAD_DIM)


def rounded(array):
    return lax.reduce_precision(array.astype(jnp.float32), 8, 7).astype(jnp.bfloat16)


def contract_rows(former, latter):
    return lax.dot_general(former, latter, (((0,), (0,)), ((), ())), preferred_element_type=jnp.float32)


def times_transposed(former, latter):
    return lax.dot_general(former, latter, (((1,), (1,)), ((), ())), preferred_element_type=jnp.float32)


def times(former, latter):
    return jnp.dot(former, latter, preferred_element_type=jnp.float32)


def norm_scaled(inputs):
    average = jnp.mean(inputs, axis=-1, keepdims=True)
    centred = inputs - average
    variance = jnp.mean(centred * centred, axis=-1, keepdims=True)
    inverse = lax.rsqrt(variance + EPSILON)
    return (centred * inverse, inverse)


def gelu_pair(hidden):
    cumulative = 0.5 * (1.0 + lax.erf(hidden * ROOT_HALF))
    return (hidden * cumulative, cumulative + hidden * (jnp.exp(-0.5 * hidden * hidden) * (1.0 / ROOT_TWO_PI)))


def document_starts(segment_rows):
    places = jnp.arange(segment_rows.shape[-1], dtype=jnp.int32)
    changes = jnp.concatenate([jnp.ones_like(segment_rows[..., :1]), (segment_rows[..., 1:] != segment_rows[..., :-1]).astype(jnp.int32)], axis=-1)
    return (places, lax.cummax(changes * places, axis=segment_rows.ndim - 1))


def frequencies():
    return 1.0 / jnp.power(10000.0, jnp.arange(0, ROT, 2).astype(jnp.float32) / ROT)


def rotary_tables(segment_rows):
    places, starts = document_starts(segment_rows)
    angles = (places - starts).astype(jnp.float32)[..., None] * frequencies()
    angles = jnp.concatenate([angles, angles], axis=-1)
    return (jnp.cos(angles), jnp.sin(angles))


def head_tables(segment_rows):
    places, starts = document_starts(segment_rows)
    angles = (places - starts).astype(jnp.float32)[:, None, :] * frequencies()[None, :, None]
    starts = jnp.broadcast_to(starts.astype(jnp.float32)[:, None, :], (starts.shape[0], ROT, starts.shape[1]))
    return jnp.concatenate([jnp.cos(angles), jnp.sin(angles), starts], axis=1)


def rotate(heads_part, cos_table, sin_table):
    half_rot = ROT // 2
    turned = heads_part[..., :ROT]
    swapped = jnp.concatenate([-turned[..., half_rot:], turned[..., :half_rot]], axis=-1)
    turned = turned * cos_table[..., None, :] + swapped * sin_table[..., None, :]
    return jnp.concatenate([turned, heads_part[..., ROT:]], axis=-1)


def unrotate(grads_part, cos_table, sin_table):
    half_rot = ROT // 2
    turned = grads_part[..., :ROT]
    along_sin = turned * sin_table[..., None, :]
    back_turn = jnp.concatenate([along_sin[..., half_rot:], -along_sin[..., :half_rot]], axis=-1)
    turned = turned * cos_table[..., None, :] + back_turn
    return jnp.concatenate([turned, grads_part[..., ROT:]], axis=-1)


def build_mask(segment_rows):
    places = jnp.arange(segment_rows.shape[-1], dtype=jnp.int32)
    return (segment_rows[:, :, None] == segment_rows[:, None, :]) & (places[None, :] <= places[:, None])


def attention_scores(queries, keys_rot):
    return jnp.einsum('bqhd,bkhd->bhqk', queries, keys_rot, preferred_element_type=jnp.float32) * SCALE


def attend_forward(queries, keys_rot, values, mask):
    scores = jnp.where(mask[:, None], attention_scores(queries, keys_rot), NEGATIVE)
    row_top = jnp.max(scores, axis=-1, keepdims=True)
    exponent = jnp.exp(scores - row_top)
    row_total = jnp.sum(exponent, axis=-1, keepdims=True)
    attention = (exponent / row_total).astype(jnp.bfloat16)
    context = jnp.einsum('bhqk,bkhd->bqhd', attention, values, preferred_element_type=jnp.float32)
    return (context.astype(jnp.bfloat16), row_top + jnp.log(row_total))


def attend_backward(queries, keys_rot, values, mask, log_total, context_grad):
    scores = attention_scores(queries, keys_rot)
    attention = jnp.where(mask[:, None], jnp.exp(scores - log_total), 0.0)
    value_grad = jnp.einsum('bhqk,bqhd->bkhd', attention.astype(jnp.bfloat16), context_grad, preferred_element_type=jnp.float32)
    attention_grad = jnp.einsum('bqhd,bkhd->bhqk', context_grad, values, preferred_element_type=jnp.float32)
    row_centre = jnp.sum(attention * attention_grad, axis=-1, keepdims=True)
    score_grad = (attention * (attention_grad - row_centre)).astype(jnp.bfloat16)
    query_grad = jnp.einsum('bhqk,bkhd->bqhd', score_grad, keys_rot, preferred_element_type=jnp.float32) * SCALE
    key_grad = jnp.einsum('bhqk,bqhd->bkhd', score_grad, queries, preferred_element_type=jnp.float32) * SCALE
    return (query_grad, key_grad, value_grad)


def whole_block(array):
    return pl.BlockSpec(array.shape, lambda *_: (0,) * array.ndim, pipeline_mode=pl.Buffered(1))


def eight_rows(array):
    return jnp.sum(array.reshape(array.shape[0] // 8, 8, array.shape[1]), axis=0)


def upstream_kernel(c_ref, slope_ref, down_ref, dense_ref, grad_ref, context_ref, c_sum_ref, h_sum_ref):
    @pl.when(pl.program_id(0) == 0)
    def _():
        c_sum_ref[...] = jnp.zeros_like(c_sum_ref)
        h_sum_ref[...] = jnp.zeros_like(h_sum_ref)
    hidden_grad = (times_transposed(c_ref[...], down_ref[...]) * slope_ref[...]).astype(grad_ref.dtype)
    grad_ref[...] = hidden_grad
    context_ref[...] = times(c_ref[...], dense_ref[...]).astype(context_ref.dtype)
    c_sum_ref[...] += eight_rows(c_ref[...].astype(jnp.float32))
    h_sum_ref[...] += eight_rows(hidden_grad.astype(jnp.float32))


def upstream_parts(c, slope, w_down, dense, rows=256):
    tokens, width = c.shape
    units, columns = (w_down.shape[0], dense.shape[1])

    def tile(size):
        return pl.BlockSpec((rows, size), lambda i: (i, 0))

    def total(size):
        return pl.BlockSpec((8, size), lambda i: (0, 0))
    return pl.pallas_call(upstream_kernel, grid=(tokens // rows,), out_shape=(jax.ShapeDtypeStruct((tokens, units), c.dtype),
        jax.ShapeDtypeStruct((tokens, columns), c.dtype), jax.ShapeDtypeStruct((8, width), jnp.float32), jax.ShapeDtypeStruct((8, units),
        jnp.float32)), in_specs=[tile(width), tile(units), whole_block(w_down), whole_block(dense)], out_specs=[tile(units), tile(columns),
        total(width), total(units)], compiler_params=pltpu.CompilerParams(vmem_limit_bytes=48 * 1024 * 1024),
        cost_estimate=pl.CostEstimate(flops=2 * tokens * width * (units + columns), transcendentals=0,
        bytes_accessed=2 * tokens * (width + 3 * units + columns) + 2 * width * (units + columns)), name='upstream_parts')(c, slope, w_down, dense)


def attention_kernel(packed_ref, grad_ref, table_ref, context_ref, back_ref, sum_ref, q_ref, k_ref, low_ref, score_ref, turned_ref):
    length = packed_ref.shape[0]
    size = 256
    lanes = 128
    lane = lax.broadcasted_iota(jnp.int32, (size, lanes), 1)
    half = ROT // 2

    def tables(rows):
        table = turned_ref[rows, :]
        cosine = jnp.where(lane < half, table, jnp.where(lane < ROT, pltpu.roll(table, half, 1), 1.0))
        sine = jnp.where(lane < half, pltpu.roll(table, lanes - half, 1), jnp.where(lane < ROT, table, 0.0))
        return (cosine, jnp.where(lane < half, -sine, sine))

    def swapped(array):
        return jnp.where(lane < half, pltpu.roll(array, lanes - half, 1), pltpu.roll(array, half, 1))

    def turn(array, cosine, sine):
        front = array[:, :lanes]
        return jnp.concatenate([front * cosine + swapped(front) * sine, array[:, lanes:]], axis=1)
    blocks = length // size
    for i in range(blocks):
        rows = pl.ds(i * size, size)
        turned_ref[rows, :] = jnp.transpose(table_ref[0, :, rows])
        cosine, sine = tables(rows)
        for part, ref in enumerate((q_ref, k_ref)):
            array = packed_ref[rows, part * HEAD_DIM:(part + 1) * HEAD_DIM].astype(jnp.float32)
            ref[rows, :] = turn(array, cosine, sine).astype(ref.dtype)
    values = pl.ds(2 * HEAD_DIM, HEAD_DIM)
    for i in range(blocks):
        rows = pl.ds(i * size, size)
        reach = (i + 1) * size
        keys = pl.ds(0, reach)
        scores = times_transposed(q_ref[rows, :], k_ref[keys, :]) * SCALE
        gradient = times_transposed(grad_ref[rows, :], packed_ref[keys, values])
        place = lax.broadcasted_iota(jnp.int32, (size, reach), 1)
        query = lax.broadcasted_iota(jnp.int32, (size, reach), 0) + i * size
        start = turned_ref[rows, ROT:ROT + 1].astype(jnp.int32)
        allowed = (place >= start) & (place <= query)
        scores = jnp.where(allowed, scores, NEGATIVE)
        exponent = jnp.exp(scores - jnp.max(scores, axis=-1, keepdims=True))
        attention = exponent / jnp.sum(exponent, axis=-1, keepdims=True)
        low = attention.astype(low_ref.dtype)
        low_ref[rows, keys] = low
        context_ref[rows, :] = times(low, packed_ref[keys, values]).astype(context_ref.dtype)
        centre = jnp.sum(attention * gradient, axis=-1, keepdims=True)
        score_grad = (attention * (gradient - centre)).astype(score_ref.dtype)
        score_ref[rows, keys] = score_grad
        query_grad = times(score_grad, k_ref[keys, :]) * SCALE
        cosine, sine = tables(rows)
        back_ref[rows, :HEAD_DIM] = turn(query_grad, cosine, -sine).astype(back_ref.dtype)
    for j in range(blocks):
        keys = pl.ds(j * size, size)
        rows = pl.ds(j * size, length - j * size)
        key_grad = contract_rows(score_ref[rows, keys], q_ref[rows, :]) * SCALE
        cosine, sine = tables(keys)
        back_ref[keys, HEAD_DIM:2 * HEAD_DIM] = turn(key_grad, cosine, -sine).astype(back_ref.dtype)
        value_grad = contract_rows(low_ref[rows, keys], grad_ref[rows, :])
        back_ref[keys, values] = value_grad.astype(back_ref.dtype)

    @pl.when(pl.program_id(0) == 0)
    def _():
        sum_ref[...] = jnp.zeros_like(sum_ref)
    for i in range(blocks):
        sum_ref[...] += eight_rows(back_ref[pl.ds(i * size, size), :].astype(jnp.float32))


def attend(packed, context_grad, table, length):
    tokens, columns = packed.shape
    low = packed.dtype

    def tile(size):
        return pl.BlockSpec((length, size), lambda i: (i, 0))
    pairs = tokens * (length + 256) // 2
    return pl.pallas_call(attention_kernel, grid=(tokens // length,), out_shape=(jax.ShapeDtypeStruct((tokens, HEAD_DIM), low),
        jax.ShapeDtypeStruct((tokens, columns), low), jax.ShapeDtypeStruct((8, columns), jnp.float32)), in_specs=[tile(columns), tile(HEAD_DIM),
        pl.BlockSpec((1, *table.shape[1:]), lambda i: (i, 0, 0))], out_specs=[tile(HEAD_DIM), tile(columns), pl.BlockSpec((8, columns), lambda i: (0,
        0))], scratch_shapes=[pltpu.VMEM((length, HEAD_DIM), low), pltpu.VMEM((length, HEAD_DIM), low), pltpu.VMEM((length, length), low),
        pltpu.VMEM((length, length), low), pltpu.VMEM((length, table.shape[1]), jnp.float32)],
        compiler_params=pltpu.CompilerParams(vmem_limit_bytes=48 * 1024 * 1024), cost_estimate=pl.CostEstimate(flops=14 * pairs * HEAD_DIM,
        transcendentals=pairs, bytes_accessed=tokens * (4 * columns + 4 * HEAD_DIM + 512)), name='attend')(packed, context_grad, table)


def remote(src, dst, send_sem, recv_sem, device):
    return pltpu.make_async_remote_copy(src_ref=src, dst_ref=dst, send_sem=send_sem, recv_sem=recv_sem, device_id=device, device_id_type=MESH)


def copied(src, dst, sem):
    copy = pltpu.make_async_copy(src, dst, sem)
    copy.start()
    return copy


def meet(f, s):
    barrier = pltpu.get_barrier_semaphore()
    for k in range(1, 8):
        pl.semaphore_signal(barrier, inc=1, device_id=((f + k) % 8, s), device_id_type=MESH)
    for k in range(1, 4):
        pl.semaphore_signal(barrier, inc=1, device_id=(f, (s + k) % 4), device_id_type=MESH)
    pl.semaphore_wait(barrier, 10)


def neighbours(f):
    f_x, f_y = (f + 2 - 4 * (f // 2 % 2), f + 4 - 8 * (f // 4))
    return (f_x, f_y, f + 1 - 2 * (f % 2), f_x + f_y - f)


def gather_kernel(x_ref, c_ref, seg_ref, up_ref, qkv_ref, b_up_ref, b_qkv_ref, norm_ref, xg_ref, cg_ref, segs_ref, normed_out, normed_mlp_out,
    packed_out, act_out, slope_out, held, tile, w_up, w_qkv, normed, normed_mlp, packed, act, slope, seg_s, seg_r, seg_l, s1, r1, s2, r2, s3, r3,
    local, w_l, tile_l, keep_l):
    f, s = (lax.axis_index('fsdp'), lax.axis_index('sp'))
    core = f % 2
    f_x, f_y, f_c, f_d = neighbours(f)
    piece = xg_ref.shape[3]
    meet(f, s)
    pairs = ((x_ref, xg_ref), (c_ref, cg_ref))
    sent = []

    def send(src, dst, send_sem, recv_sem, device):
        copy = remote(src, dst, send_sem, recv_sem, device)
        copy.start()
        sent.append(copy)

    def arrived(ref, recv_sem):
        remote(ref, ref, s1.at[0, 0], recv_sem, (f_c, s)).wait_recv()
    holds = f // 2 == s
    keep_seg = pltpu.make_async_copy(seg_ref, segs_ref.at[core], seg_l.at[0])
    give_seg = [remote(seg_ref, segs_ref.at[core], seg_s.at[k], seg_r.at[core], ((f + k) % 8, s)) for k in range(1, 8)]

    @pl.when(holds)
    def _():
        keep_seg.start()
        for copy in give_seg:
            copy.start()
    weights = [pltpu.make_async_copy(up_ref, w_up, w_l.at[0]), pltpu.make_async_copy(qkv_ref, w_qkv, w_l.at[1])]
    for copy in weights:
        copy.start()
    kept = []
    for a, (src, _) in enumerate(pairs):
        own = pltpu.make_async_copy(src.at[pl.ds(f * piece, piece)], held.at[a, f], local.at[a, 0])
        own.start()
        kept.append(own)
        for k in range(1, 8):
            j = (f + k) % 8
            send(src.at[pl.ds(j * piece, piece)], held.at[a, f], s1.at[a, k], r1.at[a, k], (j, s))

    def to_planes(a):
        out = pairs[a][1]
        kept[a].wait()
        for k in range(1, 8):
            arrived(held.at[a, (f + 8 - k) % 8], r1.at[a, k])
        for k in range(1, 4):
            plane = (s + k) % 4
            send(held.at[a, pl.ds(2 * plane, 2)], out.at[:, s, f], s2.at[a, k], r2.at[a, k], (f, plane))
        own = pltpu.make_async_copy(held.at[a, pl.ds(2 * s, 2)], out.at[:, s, f], local.at[a, 1])
        own.start()
        return own

    def spread(a, k):
        out = pairs[a][1]
        z = (s + 4 - k) % 4
        if k:
            arrived(out.at[:, z, f], r2.at[a, k])
        ref = out.at[:, z, f]
        send(ref, ref, s3.at[a, 0, k], r3.at[a, 0, k], (f_x, s))
        send(ref, ref, s3.at[a, 1, k], r3.at[a, 1, k], (f_y, s))
        send(ref, ref, s3.at[a, 2, k], r3.at[a, 2, k], (f_c, s))

    def pass_on(a, k):
        out = pairs[a][1]
        z = (s + 4 - k) % 4
        ref = out.at[:, z, f_x]
        arrived(ref, r3.at[a, 0, k])
        send(out.at[0, z, f_x], out.at[0, z, f_x], s3.at[a, 5, k], r3.at[a, 5, k], (f_y, s))
        send(ref, ref, s3.at[a, 3, k], r3.at[a, 3, k], (f_c, s))
        ref = out.at[:, z, f_y]
        arrived(ref, r3.at[a, 1, k])
        send(out.at[1, z, f_y], out.at[1, z, f_y], s3.at[a, 6, k], r3.at[a, 6, k], (f_x, s))
        send(ref, ref, s3.at[a, 4, k], r3.at[a, 4, k], (f_c, s))

    def pass_corner(a, k):
        out = pairs[a][1]
        z = (s + 4 - k) % 4
        for half in range(2):
            ref = out.at[half, z, f_d]
            arrived(ref, r3.at[a, 5 + half, k])
            send(ref, ref, s3.at[a, 7 + half, k], r3.at[a, 7 + half, k], (f_c, s))

    def from_core(a, k):
        out = pairs[a][1]
        z = (s + 4 - k) % 4
        g_x, g_y, _, g_d = neighbours(f_c)
        arrived(out.at[:, z, f_c], r3.at[a, 2, k])
        arrived(out.at[:, z, g_x], r3.at[a, 3, k])
        arrived(out.at[:, z, g_y], r3.at[a, 4, k])
        for half in range(2):
            arrived(out.at[half, z, g_d], r3.at[a, 7 + half, k])
    results = ((normed, normed_out), (normed_mlp, normed_mlp_out), (packed, packed_out), (act, act_out), (slope, slope_out))
    size = 8 * piece

    def keep(b, z, n):
        rows = pl.ds(pl.multiple_of((b * 4 + z) * size, size), size)
        return pltpu.make_async_copy(results[n][0].at[b], results[n][1].at[rows], keep_l.at[b, n])

    def work(k):
        z = (s + 4 - k) % 4
        loads = [pltpu.make_async_copy(xg_ref.at[b, z], tile.at[b], tile_l.at[b]) for b in range(2)]
        for copy in loads:
            copy.start()
        if k == 0:
            for copy in weights:
                copy.wait()
        for b in range(2):
            loads[b].wait()
            if k:
                for n in range(5):
                    keep(b, (s + 5 - k) % 4, n).wait()

            @pl.loop(0, 8)
            def _(i):
                inputs = tile[b, i].astype(jnp.float32)
                centred = inputs - jnp.mean(inputs, axis=-1, keepdims=True)
                variance = jnp.mean(centred * centred, axis=-1, keepdims=True)
                scaled = centred * lax.rsqrt(variance + EPSILON)
                rows = pl.ds(pl.multiple_of(i * piece, piece), piece)
                low = normed.dtype
                normed[b, rows, :] = (scaled * norm_ref[0:1, :] + norm_ref[1:2, :]).astype(low)
                normed_mlp[b, rows, :] = (scaled * norm_ref[2:3, :] + norm_ref[3:4, :]).astype(low)
            hidden = times_transposed(normed_mlp[b], w_up[...]) + b_up_ref[...]
            packed[b] = (times_transposed(normed[b], w_qkv[...]) + b_qkv_ref[...]).astype(packed.dtype)
            activated, grown = gelu_pair(hidden)
            act[b] = activated.astype(act.dtype)
            slope[b] = grown
            for n in range(5):
                keep(b, z, n).start()
    own0 = to_planes(0)
    own1 = to_planes(1)
    steps = [(a, k) for a in range(2) for k in range(4)]
    for i in range(len(steps) + 2):
        if i < len(steps):
            a, k = steps[i]
            if k == 0:
                (own0 if a == 0 else own1).wait()
            spread(a, k)
        if 0 <= i - 1 < len(steps):
            pass_on(*steps[i - 1])
        if 0 <= i - 2 < len(steps):
            pass_corner(*steps[i - 2])
        if 5 <= i < 9:
            from_core(0, i - 5)
            work(i - 5)
    for k in range(4):
        from_core(1, k)
    for b in range(2):
        for n in range(5):
            keep(b, (s + 1) % 4, n).wait()
    for b in range(2):

        @pl.when(f != 2 * s + b)
        def _():
            arrived(segs_ref.at[b], seg_r.at[b])

    @pl.when(holds)
    def _():
        keep_seg.wait()
        for copy in give_seg:
            copy.wait_send()
    for copy in sent:
        copy.wait_send()


def gather_both(x, c, segments, w_up, w_qkv, b_up, b_qkv, norms):
    rows, width = x.shape
    piece = rows // 8
    tokens = 8 * rows
    units, columns = (w_up.shape[0], w_qkv.shape[0])
    shape = jax.ShapeDtypeStruct((2, 4, 8, piece, width), x.dtype)
    dma = pltpu.SemaphoreType.DMA
    vmem = pltpu.VMEM
    anywhere = pl.BlockSpec(memory_space=pl.ANY)
    inside = pl.BlockSpec(memory_space=pltpu.VMEM)
    sizes = ((width, x.dtype), (width, x.dtype), (columns, x.dtype), (units, x.dtype), (units, jnp.float32))
    return pl.pallas_call(gather_kernel, out_shape=(shape, shape, jax.ShapeDtypeStruct((2, *segments.shape), segments.dtype),
        *(jax.ShapeDtypeStruct((tokens, size), kind) for size, kind in sizes)), in_specs=[anywhere] * 5 + [inside] * 3, out_specs=[anywhere] * 8,
        scratch_shapes=[vmem((2, 8, piece, width), x.dtype), vmem((2, 8, piece, width), x.dtype), vmem(w_up.shape, w_up.dtype), vmem(w_qkv.shape,
        w_qkv.dtype), *(vmem((2, 8 * piece, size), kind) for size, kind in sizes), dma((8,)), dma((2,)), dma((1,)), dma((2, 8)), dma((2, 8)), dma((2,
        4)), dma((2, 4)), dma((2, 9, 4)), dma((2, 9, 4)), dma((2, 2)), dma((2,)), dma((2,)), dma((2, 5))],
        compiler_params=pltpu.CompilerParams(collective_id=1, has_side_effects=True, vmem_limit_bytes=48 * 1024 * 1024), name='gather_tokens')(x, c,
        segments, w_up, w_qkv, b_up.reshape(1, units), b_qkv.reshape(1, columns), norms)


def finish_kernel(down_ref, dense_ref, hidden_ref, normed_mlp_ref, packed_ref, normed_ref, act_ref, context_ref, up_w_ref, down_w_ref, qkv_w_ref,
    dense_w_ref, norm_ref, h_col_ref, p_col_ref, bias_ref, g_down, g_up, g_qkv, g_dense, o_out, o_back, part, paired, kept, crossed, homed, o_small,
    line_a, line_b, turned, big, hidden, packed, weight, qkv_w, dense_w, context, act, total, made, own, right, vecs, vec_out, vec_in, small,
    small_in, load_l, act_l, part_l, tile_s, tile_r, tile_l, left_l, right_l, in_s, in_r, mid_s, mid_r, end_s, end_r, own_l, keep_l, turn_s, turn_r,
    cross_s, cross_r, home_s, home_r, back_s, back_r, local, vec_s, vec_r, small_s, small_r):
    f, s = (lax.axis_index('fsdp'), lax.axis_index('sp'))
    core = f % 2
    f_x, f_y, f_c, f_d = neighbours(f)
    is_end = (s == 0) | (s == 3)
    is_mid = (s == 1) | (s == 2)
    inner, outer, facing = (1 + s // 3, 3 * (s // 2), 3 - s)
    unit = made.shape[3]
    size = 8 * unit
    low = made.dtype
    meet(f, s)
    sent = []

    def send(src, dst, send_sem, recv_sem, device):
        copy = remote(src, dst, send_sem, recv_sem, device)
        copy.start()
        return copy

    def arrived(ref, recv_sem):
        remote(ref, ref, vec_s.at[0], recv_sem, (f_c, s)).wait_recv()
    chunks = []
    at = 0
    groups = {}
    for name, ref, first, result in (('down', down_ref, 0, g_down), ('up', part, 0, g_up), ('qkv', part, g_up.shape[0], g_qkv), ('dense', turned, 0,
        g_dense)):
        for g in range(result.shape[0]):
            cuts = (4,)
            if not chunks:
                cuts = (1, 1, 2)
            if name == 'dense':
                cuts = (2, 1, 1)
            start = 0
            for pairs_of in cuts:
                chunks.append((ref, first + g, result, g, start, pairs_of, at))
                groups[len(chunks) - 1] = (name, first + g)
                start += pairs_of
            at += 1
    count = len(chunks)
    ahead = 4

    def cut(ref, g, k):
        _, _, _, _, start, pairs_of, _ = chunks[k]
        return ref.at[g, pl.ds(start, pairs_of)]

    def source(k):
        return cut(chunks[k][0], chunks[k][1], k)

    def goal(k):
        return cut(chunks[k][2], chunks[k][3], k)

    def from_end(k):
        return remote(source(k), cut(line_a, chunks[k][6], k), in_s.at[k], in_r.at[k], (f, inner))

    def across(k):
        return remote(cut(line_a, chunks[k][6], k), cut(line_b, chunks[k][6], k), mid_s.at[k], mid_r.at[k], (f, facing))

    def to_end(k):
        return remote(cut(line_b, chunks[k][6], k), goal(k), end_s.at[k], end_r.at[k], (f, outer))

    def load_own(k):
        return pltpu.make_async_copy(source(k), cut(own, k % 2, k), own_l.at[k % 2])

    def keep(k):
        return pltpu.make_async_copy(cut(line_b, chunks[k][6], k), goal(k), keep_l.at[k])

    def add_units(target, others, number):
        @pl.loop(0, number)
        def _(i):
            for half in range(2):
                rows = pl.ds(half * (unit // 2), unit // 2)
                value = target[i // 2, i % 2, rows, :].astype(jnp.float32)
                for other in others:
                    value = value + other[i // 2, i % 2, rows, :].astype(jnp.float32)
                target[i // 2, i % 2, rows, :] = value.astype(low)

    def mid_in(k):
        load_own(k).wait()
        from_end(k).wait_recv()
        add_units(cut(line_a, chunks[k][6], k), [cut(own, k % 2, k)], 2 * chunks[k][5])
        across(k).start()
        if k + 2 < count:
            load_own(k + 2).start()

    def mid_out(k):
        across(k).wait_recv()
        add_units(cut(line_b, chunks[k][6], k), [cut(line_a, chunks[k][6], k)], 2 * chunks[k][5])
        to_end(k).start()
        keep(k).start()
    coming = {'big': copied(normed_mlp_ref, big, load_l.at[0]), 'hidden': copied(hidden_ref, hidden, load_l.at[1]), 'weight': copied(up_w_ref,
        weight, load_l.at[2]), 'packed': copied(packed_ref, packed, load_l.at[3]), 'qkv': copied(qkv_w_ref, qkv_w, load_l.at[4]),
        'dense': copied(dense_w_ref, dense_w, load_l.at[5]), 'context': copied(context_ref, context, load_l.at[6])}

    def ready(*names):
        for name in names:
            if coming[name] is not None:
                coming[name].wait()
                coming[name] = None
    span = dense_ref.shape[4]
    columns = pl.ds(pl.multiple_of(f * span, span), span)
    turn_own = copied(dense_ref.at[f], turned.at[0, :, :, :, columns], local.at[0])
    bias_own = copied(bias_ref, small.at[pl.ds(8, 8)], local.at[1])
    vecs[...] = jnp.zeros_like(vecs)
    vec_out[...] = jnp.zeros_like(vec_out)
    busy = {0: [], 1: []}
    turns = [0]

    def next_made():
        slot = turns[0] % 2
        turns[0] += 1
        for wait in busy[slot]:
            wait()
        busy[slot] = []
        return slot
    stores = {}

    def finish_group(g, weights, first, column_ref, which):
        slot = next_made()

        @pl.loop(0, 8)
        def _(i):
            rows = pl.ds(pl.multiple_of(i * unit, unit), unit)
            wide = pl.ds(pl.multiple_of(first + i * unit, unit), unit)
            value = total[rows, :]
            made[slot, i // 2, i % 2] = value.astype(low)
            line = weights[wide, :].astype(jnp.float32)
            sums = column_ref[wide, 0:1]
            scaled = line * (value - sums * norm_ref[2 * which + 1:2 * which + 2, :])
            vecs[2 * which] += eight_rows(scaled)
            vecs[2 * which + 1] += eight_rows(line * sums)
        stores[g] = copied(made.at[slot], part.at[g], part_l.at[g])
        busy[slot] = [functools.partial(stored, g)]

    def stored(g):
        if stores[g] is not None:
            stores[g].wait()
            stores[g] = None

    def up_group(g):
        ready('big', 'hidden', 'weight')
        total[...] = contract_rows(hidden[:, g * size:(g + 1) * size], big[...].reshape(hidden.shape[0], -1))
        finish_group(g, weight, g * size, h_col_ref, 1)
        if g == g_up.shape[0] - 1:
            coming['big'] = copied(normed_ref, big, load_l.at[7])
            coming['weight'] = copied(down_w_ref, weight, load_l.at[8])
            load_act(0)

    def qkv_group(g):
        ready('big', 'packed', 'qkv')
        total[...] = contract_rows(packed[:, g * size:(g + 1) * size], big[...].reshape(hidden.shape[0], -1))
        finish_group(g_up.shape[0] + g, qkv_w, g * size, p_col_ref, 0)

    def load_act(t):
        coming['act', t] = copied(act_ref.at[pl.ds(t * size, size)], act.at[t % 2], act_l.at[t % 2])

    def give_tile(a, t, value):
        b, z = (t // 4, t % 4)
        slot = next_made()
        made[slot] = value.astype(low).reshape(4, 2, unit, value.shape[1])
        give = send(made.at[slot, :, 1 - core], paired.at[a, :, z, b], tile_s.at[a, t], tile_r.at[a, t], (f_c, s))
        hold = copied(made.at[slot, :, core], kept.at[a, :, z, b], tile_l.at[a, t])
        busy[slot] = [give.wait_send, hold.wait]

    def out_tile(t):
        ready('weight', 'context', 'dense', ('act', t))
        if t < 7:
            load_act(t + 1)
        rows = slice(t * size, (t + 1) * size)
        value = times_transposed(context[rows, :], dense_w[...]) + times(act[t % 2], weight[...])
        give_tile(0, t, value)
        if t == 7:
            coming['weight'] = copied(up_w_ref, weight, load_l.at[9])

    def back_tile(t):
        ready('weight', 'packed', 'qkv', 'hidden')
        rows = slice(t * size, (t + 1) * size)
        value = times(packed[rows, :], qkv_w[...]) * norm_ref[0:1, :]
        value = value + times(hidden[rows, :], weight[...]) * norm_ref[2:3, :]
        give_tile(1, t, value)
    results = (o_out, o_back)
    order = (f_d // 2, f_x // 2, f_y // 2, f // 2)
    homes = {}

    def free(slot):
        for wait in busy[slot]:
            wait()
        busy[slot] = []

    def tiles_here(a):
        for slot in range(2):
            free(slot)
        for t in range(8):
            arrived(paired.at[a, :, t % 4, t // 4], tile_r.at[a, t])

    def add_pair(a, n):
        if n == 0:
            tiles_here(a)
        left = big.at[3 * a + n]
        slot = n % 2
        first = copied(paired.at[a, order[n]], left, left_l.at[slot])
        second = copied(kept.at[a, order[n]], right.at[slot], right_l.at[slot])
        first.wait()
        second.wait()
        add_units(left, [right.at[slot]], 8)
        sent.append(send(left, crossed.at[a, n], cross_s.at[a, n], cross_r.at[a, n], ((f_d, f_x, f_y)[n], s)))

    def add_chips(a):
        left = big.at[6 + a]
        copies = [copied(paired.at[a, order[3]], left, left_l.at[0]), copied(kept.at[a, order[3]], right.at[0], right_l.at[0])]
        for n in range(3):
            arrived(crossed.at[a, n], cross_r.at[a, n])
            slot = (n + 1) % 2
            more = copied(crossed.at[a, n], right.at[slot], right_l.at[slot])
            for copy in copies:
                copy.wait()
            add_units(left, [right.at[1 - slot]], 8)
            copies = [more]
        copies[0].wait()
        add_units(left, [right.at[1]], 8)
        for k in range(1, 4):
            z = (s + k) % 4
            sent.append(send(left.at[z], homed.at[a, s], home_s.at[a, k], home_r.at[a, k], (f, z)))
        homes['own', a] = copied(left.at[s], homed.at[a, s], local.at[2 + a])


    def go_home(a):
        homes['own', a].wait()
        for k in range(1, 4):
            arrived(homed.at[a, (s + 4 - k) % 4], home_r.at[a, k])
        for k in range(1, 8):
            j = (f + k) % 8
            sent.append(send(homed.at[a, j // 2, j % 2], results[a].at[f], back_s.at[a, k], back_r.at[a, k], (j, s)))
        homes[a] = copied(homed.at[a, f // 2, core], results[a].at[f], local.at[4 + a])

    def give_vectors():
        for which in range(2):
            gain = norm_ref[2 * which:2 * which + 1, :]
            scaled = jnp.sum(vecs[2 * which], axis=0, keepdims=True) / gain
            plain = jnp.sum(vecs[2 * which + 1], axis=0, keepdims=True)
            for j in range(8):
                part_of = slice(j * span, (j + 1) * span)
                vec_out[j, 2 * which:2 * which + 1, :] = scaled[:, part_of]
                vec_out[j, 2 * which + 1:2 * which + 2, :] = plain[:, part_of]
        for k in range(1, 8):
            j = (f + k) % 8
            sent.append(send(vec_out.at[j], vec_in.at[f], vec_s.at[k], vec_r.at[k], (j, s)))
        homes['vec'] = copied(vec_out.at[f], vec_in.at[f], local.at[6])

    def add_vectors():
        homes['vec'].wait()
        bias_own.wait()
        for k in range(1, 8):
            arrived(vec_in.at[(f + 8 - k) % 8], vec_r.at[k])
        value = vec_in[0]
        for j in range(1, 8):
            value = value + vec_in[j]
        small[0:8, :] = value
        for k in range(1, 4):
            sent.append(send(small, small_in.at[s], small_s.at[k], small_r.at[k], (f, (s + k) % 4)))
        homes['small'] = copied(small, small_in.at[s], local.at[7])

    def add_small():
        homes['small'].wait()
        for k in range(1, 4):
            arrived(small_in.at[(s + 4 - k) % 4], small_r.at[k])
        value = small_in[0]
        for z in range(1, 4):
            value = value + small_in[z]
        o_small[...] = value

    def turn_start():
        for k in range(1, 8):
            j = (f + k) % 8
            sent.append(send(dense_ref.at[j], turned.at[0, :, :, :, columns], turn_s.at[k], turn_r.at[k], (j, s)))

    def turn_done():
        turn_own.wait()
        for k in range(1, 8):
            j = (f + 8 - k) % 8
            there = pl.ds(pl.multiple_of(j * span, span), span)
            arrived(turned.at[0, :, :, :, there], turn_r.at[k])

    def task(name, i):
        if name == 'turn':
            turn_start()
        elif name == 'turned':
            turn_done()
        elif name == 'up':
            up_group(i)
        elif name == 'qkv':
            qkv_group(i)
        elif name == 'out':
            out_tile(i)
        elif name == 'back':
            back_tile(i)
        elif name == 'pair':
            add_pair(i // 3, i % 3)
        elif name == 'chips':
            add_chips(i)
        elif name == 'home':
            go_home(i)
        elif name == 'vectors':
            give_vectors()
        elif name == 'sums':
            add_vectors()
        else:
            add_small()

    @pl.when(is_end)
    def _():
        for k in range(ahead):
            from_end(k).start()

    @pl.when(is_mid)
    def _():
        for k in range(2):
            load_own(k).start()
    for k in range(count + 2):
        for name, first, last in FINISH_STEPS[k] if k in FINISH_STEPS else ():
            for i in range(first, last):
                task(name, i)
        if k + ahead - 1 in groups and groups[k + ahead - 1][0] in ('up', 'qkv'):
            stored(groups[k + ahead - 1][1])

        @pl.when(is_mid)
        def _():
            if k < count:
                mid_in(k)
            if 1 <= k <= count:
                mid_out(k - 1)

        @pl.when(is_end)
        def _():
            if 1 <= k <= count:
                to_end(k - 1).wait_recv()
                if k - 1 + ahead < count:
                    from_end(k - 1 + ahead).start()
    for a in range(2):
        homes[a].wait()
        for k in range(1, 8):
            arrived(results[a].at[(f + 8 - k) % 8], back_r.at[a, k])
    for slot in range(2):
        free(slot)
    for copy in sent:
        copy.wait_send()

    @pl.when(is_end)
    def _():
        for k in range(count):
            from_end(k).wait_send()

    @pl.when(is_mid)
    def _():
        for k in range(count):
            across(k).wait_send()
            to_end(k).wait_send()
            keep(k).wait()


FINISH_STEPS = {
    0: (("turn", 0, 1),),
    1: (("up", 0, 1),),
    2: (("up", 1, 2),),
    3: (("up", 2, 4),),
    4: (("qkv", 0, 3),),
    5: (("out", 0, 6),),
    6: (("out", 6, 8), ("back", 0, 3)),
    7: (("pair", 0, 3), ("turned", 0, 1), ("back", 3, 5)),
    8: (("back", 5, 8), ("vectors", 0, 1)),
    9: (("pair", 3, 6), ("chips", 0, 1)),
    10: (("home", 0, 1), ("sums", 0, 1)),
    12: (("chips", 1, 2),),
    13: (("small", 0, 1),),
    14: (("home", 1, 2),),
}


def finish(down, dense, hidden_grad, normed_mlp, packed_grad, normed, act, context, w_up, w_down, w_qkv, dense_in, norms, h_sums, p_sums, bias):
    width = down.shape[1]
    tokens = hidden_grad.shape[0]
    low = down.dtype
    unit = tokens // 64
    size = 8 * unit
    span = width // 8

    def grouped(rows):
        return (rows // size, 4, 2, unit, width)

    def columns(sums):
        return jnp.broadcast_to(sums[:, None], (sums.shape[0], 128))
    sets = [w.shape[0] // size for w in (down, w_up, w_qkv)]
    number = sum(sets) + 1
    count = sum(sets) + 5
    sums = [jax.ShapeDtypeStruct(grouped(n * size), low) for n in (*sets, 1)]
    token = jax.ShapeDtypeStruct((8, unit, width), low)
    halves = jax.ShapeDtypeStruct((2, 4, 4, 2, unit, width), low)
    others = [jax.ShapeDtypeStruct(grouped((sets[1] + sets[2]) * size), low), halves, halves, jax.ShapeDtypeStruct((2, 3, 4, 2, unit, width), low),
        jax.ShapeDtypeStruct((2, 4, 2, unit, width), low)]
    dma = pltpu.SemaphoreType.DMA
    vmem = pltpu.VMEM
    anywhere = pl.BlockSpec(memory_space=pl.ANY)
    inside = pl.BlockSpec(memory_space=pltpu.VMEM)
    result = pl.pallas_call(finish_kernel, out_shape=(*sums, token, token, *others, jax.ShapeDtypeStruct((16, span), jnp.float32)),
        in_specs=[anywhere] * 12 + [inside] * 3 + [anywhere], out_specs=[anywhere] * 11 + [inside], scratch_shapes=[vmem((number, 4, 2, unit, width),
        low), vmem((number, 4, 2, unit, width), low), vmem((1, 4, 2, unit, width), low), vmem(grouped(tokens), low), vmem(hidden_grad.shape, low),
        vmem(packed_grad.shape, low), vmem(w_up.shape, low), vmem(w_qkv.shape, low), vmem(dense_in.shape, low), vmem(context.shape, low), vmem((2,
        size, act.shape[1]), low), vmem((size, width), jnp.float32), *(vmem((2, 4, 2, unit, width), low) for _ in range(3)), vmem((4, 8, width),
        jnp.float32), vmem((8, 8, span), jnp.float32), vmem((8, 8, span), jnp.float32), vmem((16, span), jnp.float32), vmem((4, 16, span),
        jnp.float32), dma((10,)), dma((2,)), dma((sets[1] + sets[2],)), dma((2, 8)), dma((2, 8)), dma((2, 8)), dma((2,)), dma((2,)), dma((count,)),
        dma((count,)), dma((count,)), dma((count,)), dma((count,)), dma((count,)), dma((2,)), dma((count,)), dma((8,)), dma((8,)), dma((2, 3)),
        dma((2, 3)), dma((2, 4)), dma((2, 4)), dma((2, 8)), dma((2, 8)), dma((8,)), dma((8,)), dma((8,)), dma((4,)), dma((4,))],
        compiler_params=pltpu.CompilerParams(collective_id=2, has_side_effects=True, vmem_limit_bytes=60 * 1024 * 1024),
        name='finish')(down.reshape(grouped(down.shape[0])), dense.reshape(8, 4, 2, unit, span), hidden_grad, normed_mlp.reshape(grouped(tokens)), packed_grad, normed.reshape(grouped(tokens)), act,
        context, w_up, w_down, w_qkv, dense_in, norms, columns(h_sums), columns(p_sums), bias)
    grads = [grad.reshape(-1, width) for grad in result[:4]]
    return (grads, result[4], result[5], result[11])


def own_tokens(hidden_in, cotangent, output, weighted, shift):
    inputs = hidden_in.astype(jnp.float32)
    output = (inputs + (output.astype(jnp.float32) + shift)).astype(jnp.bfloat16)
    scaled, inverse = norm_scaled(inputs)
    weighted = weighted.astype(jnp.float32)
    first_mean = jnp.mean(weighted, axis=-1, keepdims=True)
    second_mean = jnp.mean(weighted * scaled, axis=-1, keepdims=True)
    input_grad = (cotangent.astype(jnp.float32) + inverse * (weighted - first_mean - scaled * second_mean)).astype(jnp.bfloat16)
    return (output, input_grad)


def by_collectives(hidden_in, segments, ln1_gain, ln1_bias, ln2_gain, ln2_bias, w_qkv, b_qkv, w_dense, b_dense, w_up, b_up, w_down, b_down,
    cotangent):
    seq_local, shard_len, width = hidden_in.shape
    seq_len = segments.shape[1]
    nf, ns = (lax.axis_size('fsdp'), lax.axis_size('sp'))
    f_place, s_place = (lax.axis_index('fsdp'), lax.axis_index('sp'))
    seqs = seq_local * nf
    group = seqs // ns
    piece = shard_len // nf
    tokens = group * seq_len
    per_head = max(1, nf // HEADS)
    head_count = max(1, HEADS // nf)
    head_sets = [[head * per_head + k for k in range(per_head)] for head in range(nf // per_head)]

    def gather_tokens(block):
        part = lax.all_to_all(block, 'fsdp', split_axis=1, concat_axis=0, tiled=True)
        part = lax.all_to_all(part, 'sp', split_axis=0, concat_axis=1, tiled=True)
        return in_order(lax.all_gather(part, 'fsdp', axis=0, tiled=True)).reshape(tokens, width)

    def scatter_tokens(partial):
        part = out_of_order(partial).reshape(nf * group, ns * piece, width)
        part = lax.psum_scatter(part, 'fsdp', scatter_dimension=0, tiled=True)
        part = lax.all_to_all(part, 'sp', split_axis=1, concat_axis=0, tiled=True)
        return lax.all_to_all(part, 'fsdp', split_axis=0, concat_axis=1, tiled=True)

    def in_order(array):
        array = array.reshape(nf, group, ns, piece, -1)
        return array.transpose(1, 2, 0, 3, 4).reshape(group, seq_len, -1)

    def out_of_order(array):
        array = array.reshape(group, ns, nf, piece, -1)
        return array.transpose(2, 0, 1, 3, 4).reshape(tokens, -1)

    def over_head(array, axis):
        if per_head == 1:
            return array
        return lax.all_gather(array, 'fsdp', axis=axis, tiled=True, axis_index_groups=head_sets)

    def own_columns(array):
        if per_head == 1:
            return array
        share = array.shape[-1] // per_head
        return lax.dynamic_slice_in_dim(array, f_place % per_head * share, share, array.ndim - 1)

    def own_part(vector):
        share = vector.shape[0] // nf
        return lax.dynamic_slice_in_dim(vector, f_place * share, share, 0)
    gathered, upstream = (gather_tokens(hidden_in), gather_tokens(cotangent))
    rows = lax.all_gather(segments, 'fsdp', axis=0, tiled=True)
    rows = lax.dynamic_slice_in_dim(rows, s_place * group, group, 0)
    dense_in = lax.all_to_all(w_dense, 'fsdp', split_axis=1, concat_axis=0, tiled=True)
    head_qkv = over_head(w_qkv, 0)
    head_dense = over_head(dense_in, 1)
    head_bias = lax.dynamic_slice_in_dim(b_qkv, f_place // per_head * head_qkv.shape[0], head_qkv.shape[0], 0)
    scaled, _ = norm_scaled(gathered.astype(jnp.float32))
    normed = (scaled * ln1_gain + ln1_bias).astype(jnp.bfloat16)
    normed_mlp = (scaled * ln2_gain + ln2_bias).astype(jnp.bfloat16)
    hidden = times_transposed(normed_mlp, w_up) + own_part(b_up)
    activated, slope = gelu_pair(hidden)
    activated = activated.astype(jnp.bfloat16)
    down_term = contract_rows(activated, upstream).astype(jnp.bfloat16)
    grad_down_w = lax.psum(down_term, 'sp').astype(jnp.float32)
    hidden_grad = (times_transposed(upstream, w_down) * slope).astype(jnp.bfloat16)
    up_term = contract_rows(hidden_grad, normed_mlp)
    mlp_norm_grad = times(hidden_grad, w_up)
    packed = (times_transposed(normed, head_qkv) + head_bias).astype(jnp.bfloat16)
    packed = packed.reshape(group, seq_len, head_count, 3 * HEAD_DIM)
    cos_table, sin_table = rotary_tables(rows)
    queries = rotate(packed[..., :HEAD_DIM].astype(jnp.float32), cos_table, sin_table).astype(jnp.bfloat16)
    keys_rot = rotate(packed[..., HEAD_DIM:2 * HEAD_DIM].astype(jnp.float32), cos_table, sin_table).astype(jnp.bfloat16)
    values = packed[..., 2 * HEAD_DIM:]
    mask = build_mask(rows)
    context, log_total = attend_forward(queries, keys_rot, values, mask)
    context = own_columns(context.reshape(tokens, -1))
    partial_out = times_transposed(context, dense_in) + times(activated, w_down)
    context_grad = times(upstream, head_dense).astype(jnp.bfloat16).reshape(group, seq_len, head_count, HEAD_DIM)
    query_grad, key_grad, value_grad = attend_backward(queries, keys_rot, values, mask, log_total, context_grad)
    packed_grad = jnp.concatenate([unrotate(query_grad, cos_table, sin_table), unrotate(key_grad, cos_table, sin_table), value_grad],
        axis=-1).astype(jnp.bfloat16)
    packed_grad = own_columns(packed_grad.reshape(tokens, -1))
    attn_norm_grad = times(packed_grad, w_qkv)
    qkv_term = contract_rows(packed_grad, normed)
    dense_term = contract_rows(upstream, context).astype(jnp.bfloat16)
    partial_back = attn_norm_grad * ln1_gain + mlp_norm_grad * ln2_gain
    vectors = jnp.stack([jnp.sum(attn_norm_grad * scaled, axis=0), jnp.sum(attn_norm_grad, axis=0), jnp.sum(mlp_norm_grad * scaled, axis=0),
        jnp.sum(mlp_norm_grad, axis=0)])
    bias_out = own_part(jnp.sum(upstream.astype(jnp.float32), axis=0))
    bias_qkv = jnp.sum(packed_grad.astype(jnp.float32), axis=0)
    bias_up = jnp.sum(hidden_grad.astype(jnp.float32), axis=0)
    vectors = lax.psum_scatter(vectors, 'fsdp', scatter_dimension=1, tiled=True)
    vectors, bias_out, bias_qkv, bias_up = lax.psum((vectors, bias_out, bias_qkv, bias_up), 'sp')
    output = scatter_tokens(rounded(partial_out))
    weighted = scatter_tokens(rounded(partial_back))
    dense_term = lax.all_to_all(dense_term, 'fsdp', split_axis=0, concat_axis=1, tiled=True)
    grad_up_w, grad_qkv_w, grad_dense_w = (lax.psum(term.astype(jnp.bfloat16), 'sp').astype(jnp.float32) for term in (up_term, qkv_term, dense_term))
    output, input_grad = own_tokens(hidden_in, cotangent, output, weighted, b_dense + b_down)
    return (output, input_grad, vectors[0], vectors[1], vectors[2], vectors[3], grad_qkv_w, bias_qkv, grad_dense_w, bias_out, grad_up_w, bias_up,
        grad_down_w, bias_out)


def by_kernels(hidden_in, segments, ln1_gain, ln1_bias, ln2_gain, ln2_bias, w_qkv, b_qkv, w_dense, b_dense, w_up, b_up, w_down, b_down, cotangent):
    width = hidden_in.shape[2]
    seq_len = segments.shape[1]
    nf, ns = (lax.axis_size('fsdp'), lax.axis_size('sp'))
    group = nf // ns
    tokens = group * seq_len
    share = width // nf
    f_place = lax.axis_index('fsdp')

    def own_part(vector):
        size = vector.shape[0] // nf
        return lax.dynamic_slice_in_dim(vector, f_place * size, size, 0)
    norms = jnp.stack([ln1_gain, ln1_bias, ln2_gain, ln2_bias])
    _, upstream, rows, normed, normed_mlp, packed, activated, slope = gather_both(hidden_in[0], cotangent[0], segments.reshape(8, seq_len // 8),
        w_up, w_qkv, own_part(b_up), own_part(b_qkv), norms)
    upstream = upstream.reshape(tokens, width)
    w_dense, upstream = lax.optimization_barrier((w_dense, upstream))
    dense_in = lax.all_to_all(w_dense, 'fsdp', split_axis=1, concat_axis=0, tiled=True)
    early = activated.shape[1] // 2
    down_term = contract_rows(activated[:, :early], upstream).astype(jnp.bfloat16)
    early_down_w = lax.psum(down_term, 'sp').astype(jnp.float32)
    slope, activated, down_term = lax.optimization_barrier((slope, activated, down_term))
    hidden_grad, context_grad, c_sums, h_sums = upstream_parts(upstream, slope, w_down, dense_in)
    context, packed_grad, p_sums = attend(packed, context_grad, head_tables(rows.reshape(group, seq_len)), seq_len)
    late_down_term = contract_rows(activated[:, early:], upstream).astype(jnp.bfloat16)
    dense_term = contract_rows(upstream, context).astype(jnp.bfloat16)
    bias_up, bias_qkv = (jnp.sum(h_sums, axis=0), jnp.sum(p_sums, axis=0))
    bias_out = own_part(jnp.sum(c_sums, axis=0))
    grads, output, weighted, sums = finish(late_down_term, dense_term, hidden_grad, normed_mlp, packed_grad, normed, activated, context, w_up,
        w_down, w_qkv, dense_in, norms, bias_up, bias_qkv, jnp.concatenate([bias_out, bias_qkv, bias_up]).reshape(8, share))
    late_down_w, grad_up_w, grad_qkv_w, grad_dense_w = (grad.astype(jnp.float32) for grad in grads)
    grad_down_w = jnp.concatenate([early_down_w, late_down_w])
    bias_out = sums[8]
    output, input_grad = own_tokens(hidden_in, cotangent, output.reshape(hidden_in.shape), weighted.reshape(hidden_in.shape), b_dense + b_down)
    return (output, input_grad, sums[0], sums[1], sums[2], sums[3], grad_qkv_w, sums[9:12].reshape(-1), grad_dense_w, bias_out, grad_up_w,
        sums[12:16].reshape(-1), grad_down_w, bias_out)


def per_device(hidden_in, *rest):
    sizes = (lax.axis_size('fsdp'), lax.axis_size('sp'), hidden_in.shape[0])
    shapes = (hidden_in.shape[1] % 256, hidden_in.shape[2] % (8 * HEAD_DIM), rest[9].shape[0] % 256)
    if sizes == (8, 4, 1) and HEADS == 8 and (not any(shapes)):
        return by_kernels(hidden_in, *rest)
    return by_collectives(hidden_in, *rest)


def solution(mesh):
    rows = P('fsdp', 'sp', None)
    first = P('fsdp', None)
    return jax.shard_map(per_device, mesh=mesh, in_specs=(rows, first, P(), P(), P(), P(), first, P(), first, P(), first, P(), first, P(), rows),
        out_specs=(rows, rows, P('fsdp'), P('fsdp'), P('fsdp'), P('fsdp'), first, P('fsdp'), first, P('fsdp'), first, P('fsdp'), first, P('fsdp')),
        check_vma=False)
```

```python
import functools
import math

import jax
import jax.numpy as jnp
from jax import lax
from jax.experimental import pallas as pl
from jax.experimental.pallas import tpu as pltpu
from jax.sharding import PartitionSpec as P

MESH = pl.DeviceIdType.MESH

HEADS = 8
HEAD_DIM = 256
ROT = 64


EPSILON = 1e-05
NEGATIVE = -1e30
ROOT_HALF = 0.7071067811865476
ROOT_TWO_PI = 2.5066282746310002
SCALE = 1.0 / math.sqrt(HEAD_DIM)


def rounded(array):
    return lax.reduce_precision(array.astype(jnp.float32), 8, 7).astype(jnp.bfloat16)


def contract_rows(former, latter):
    return lax.dot_general(former, latter, (((0,), (0,)), ((), ())), preferred_element_type=jnp.float32)


def times_transposed(former, latter):
    return lax.dot_general(former, latter, (((1,), (1,)), ((), ())), preferred_element_type=jnp.float32)


def times(former, latter):
    return jnp.dot(former, latter, preferred_element_type=jnp.float32)


def norm_scaled(inputs):
    average = jnp.mean(inputs, axis=-1, keepdims=True)
    centred = inputs - average
    variance = jnp.mean(centred * centred, axis=-1, keepdims=True)
    inverse = lax.rsqrt(variance + EPSILON)
    return (centred * inverse, inverse)


def gelu_pair(hidden):
    cumulative = 0.5 * (1.0 + lax.erf(hidden * ROOT_HALF))
    return (hidden * cumulative, cumulative + hidden * (jnp.exp(-0.5 * hidden * hidden) * (1.0 / ROOT_TWO_PI)))


def document_starts(segment_rows):
    places = jnp.arange(segment_rows.shape[-1], dtype=jnp.int32)
    changes = jnp.concatenate([jnp.ones_like(segment_rows[..., :1]), (segment_rows[..., 1:] != segment_rows[..., :-1]).astype(jnp.int32)], axis=-1)
    return (places, lax.cummax(changes * places, axis=segment_rows.ndim - 1))


def frequencies():
    return 1.0 / jnp.power(10000.0, jnp.arange(0, ROT, 2).astype(jnp.float32) / ROT)


def rotary_tables(segment_rows):
    places, starts = document_starts(segment_rows)
    angles = (places - starts).astype(jnp.float32)[..., None] * frequencies()
    angles = jnp.concatenate([angles, angles], axis=-1)
    return (jnp.cos(angles), jnp.sin(angles))


def head_tables(segment_rows):
    places, starts = document_starts(segment_rows)
    angles = (places - starts).astype(jnp.float32)[:, None, :] * frequencies()[None, :, None]
    starts = jnp.broadcast_to(starts.astype(jnp.float32)[:, None, :], (starts.shape[0], ROT, starts.shape[1]))
    return jnp.concatenate([jnp.cos(angles), jnp.sin(angles), starts], axis=1)


def rotate(heads_part, cos_table, sin_table):
    half_rot = ROT // 2
    turned = heads_part[..., :ROT]
    swapped = jnp.concatenate([-turned[..., half_rot:], turned[..., :half_rot]], axis=-1)
    turned = turned * cos_table[..., None, :] + swapped * sin_table[..., None, :]
    return jnp.concatenate([turned, heads_part[..., ROT:]], axis=-1)


def unrotate(grads_part, cos_table, sin_table):
    half_rot = ROT // 2
    turned = grads_part[..., :ROT]
    along_sin = turned * sin_table[..., None, :]
    back_turn = jnp.concatenate([along_sin[..., half_rot:], -along_sin[..., :half_rot]], axis=-1)
    turned = turned * cos_table[..., None, :] + back_turn
    return jnp.concatenate([turned, grads_part[..., ROT:]], axis=-1)


def build_mask(segment_rows):
    places = jnp.arange(segment_rows.shape[-1], dtype=jnp.int32)
    return (segment_rows[:, :, None] == segment_rows[:, None, :]) & (places[None, :] <= places[:, None])


def attention_scores(queries, keys_rot):
    return jnp.einsum('bqhd,bkhd->bhqk', queries, keys_rot, preferred_element_type=jnp.float32) * SCALE


def attend_forward(queries, keys_rot, values, mask):
    scores = jnp.where(mask[:, None], attention_scores(queries, keys_rot), NEGATIVE)
    row_top = jnp.max(scores, axis=-1, keepdims=True)
    exponent = jnp.exp(scores - row_top)
    row_total = jnp.sum(exponent, axis=-1, keepdims=True)
    attention = (exponent / row_total).astype(jnp.bfloat16)
    context = jnp.einsum('bhqk,bkhd->bqhd', attention, values, preferred_element_type=jnp.float32)
    return (context.astype(jnp.bfloat16), row_top + jnp.log(row_total))


def attend_backward(queries, keys_rot, values, mask, log_total, context_grad):
    scores = attention_scores(queries, keys_rot)
    attention = jnp.where(mask[:, None], jnp.exp(scores - log_total), 0.0)
    value_grad = jnp.einsum('bhqk,bqhd->bkhd', attention.astype(jnp.bfloat16), context_grad, preferred_element_type=jnp.float32)
    attention_grad = jnp.einsum('bqhd,bkhd->bhqk', context_grad, values, preferred_element_type=jnp.float32)
    row_centre = jnp.sum(attention * attention_grad, axis=-1, keepdims=True)
    score_grad = (attention * (attention_grad - row_centre)).astype(jnp.bfloat16)
    query_grad = jnp.einsum('bhqk,bkhd->bqhd', score_grad, keys_rot, preferred_element_type=jnp.float32) * SCALE
    key_grad = jnp.einsum('bhqk,bqhd->bkhd', score_grad, queries, preferred_element_type=jnp.float32) * SCALE
    return (query_grad, key_grad, value_grad)


def whole_block(array):
    return pl.BlockSpec(array.shape, lambda *_: (0,) * array.ndim, pipeline_mode=pl.Buffered(1))


def eight_rows(array):
    return jnp.sum(array.reshape(array.shape[0] // 8, 8, array.shape[1]), axis=0)


def upstream_kernel(c_ref, slope_ref, down_ref, dense_ref, grad_ref, context_ref, c_sum_ref, h_sum_ref):
    @pl.when(pl.program_id(0) == 0)
    def _():
        c_sum_ref[...] = jnp.zeros_like(c_sum_ref)
        h_sum_ref[...] = jnp.zeros_like(h_sum_ref)
    hidden_grad = (times_transposed(c_ref[...], down_ref[...]) * slope_ref[...]).astype(grad_ref.dtype)
    grad_ref[...] = hidden_grad
    context_ref[...] = times(c_ref[...], dense_ref[...]).astype(context_ref.dtype)
    c_sum_ref[...] += eight_rows(c_ref[...].astype(jnp.float32))
    h_sum_ref[...] += eight_rows(hidden_grad.astype(jnp.float32))


def upstream_parts(c, slope, w_down, dense, rows=256):
    tokens, width = c.shape
    units, columns = (w_down.shape[0], dense.shape[1])

    def tile(size):
        return pl.BlockSpec((rows, size), lambda i: (i, 0))

    def total(size):
        return pl.BlockSpec((8, size), lambda i: (0, 0))
    return pl.pallas_call(upstream_kernel, grid=(tokens // rows,), out_shape=(jax.ShapeDtypeStruct((tokens, units), c.dtype),
        jax.ShapeDtypeStruct((tokens, columns), c.dtype), jax.ShapeDtypeStruct((8, width), jnp.float32), jax.ShapeDtypeStruct((8, units),
        jnp.float32)), in_specs=[tile(width), tile(units), whole_block(w_down), whole_block(dense)], out_specs=[tile(units), tile(columns),
        total(width), total(units)], compiler_params=pltpu.CompilerParams(vmem_limit_bytes=48 * 1024 * 1024),
        cost_estimate=pl.CostEstimate(flops=2 * tokens * width * (units + columns), transcendentals=0,
        bytes_accessed=2 * tokens * (width + 3 * units + columns) + 2 * width * (units + columns)), name='upstream_parts')(c, slope, w_down, dense)


def attention_kernel(packed_ref, grad_ref, table_ref, context_ref, back_ref, sum_ref, q_ref, k_ref, low_ref, score_ref, turned_ref):
    length = packed_ref.shape[0]
    size = 256
    lanes = 128
    lane = lax.broadcasted_iota(jnp.int32, (size, lanes), 1)
    half = ROT // 2

    def tables(rows):
        table = turned_ref[rows, :]
        cosine = jnp.where(lane < half, table, jnp.where(lane < ROT, pltpu.roll(table, half, 1), 1.0))
        sine = jnp.where(lane < half, pltpu.roll(table, lanes - half, 1), jnp.where(lane < ROT, table, 0.0))
        return (cosine, jnp.where(lane < half, -sine, sine))

    def swapped(array):
        return jnp.where(lane < half, pltpu.roll(array, lanes - half, 1), pltpu.roll(array, half, 1))

    def turn(array, cosine, sine):
        front = array[:, :lanes]
        return jnp.concatenate([front * cosine + swapped(front) * sine, array[:, lanes:]], axis=1)
    blocks = length // size
    for i in range(blocks):
        rows = pl.ds(i * size, size)
        turned_ref[rows, :] = jnp.transpose(table_ref[0, :, rows])
        cosine, sine = tables(rows)
        for part, ref in enumerate((q_ref, k_ref)):
            array = packed_ref[rows, part * HEAD_DIM:(part + 1) * HEAD_DIM].astype(jnp.float32)
            ref[rows, :] = turn(array, cosine, sine).astype(ref.dtype)
    values = pl.ds(2 * HEAD_DIM, HEAD_DIM)
    for i in range(blocks):
        rows = pl.ds(i * size, size)
        reach = (i + 1) * size
        keys = pl.ds(0, reach)
        scores = times_transposed(q_ref[rows, :], k_ref[keys, :]) * SCALE
        gradient = times_transposed(grad_ref[rows, :], packed_ref[keys, values])
        place = lax.broadcasted_iota(jnp.int32, (size, reach), 1)
        query = lax.broadcasted_iota(jnp.int32, (size, reach), 0) + i * size
        start = turned_ref[rows, ROT:ROT + 1].astype(jnp.int32)
        allowed = (place >= start) & (place <= query)
        scores = jnp.where(allowed, scores, NEGATIVE)
        exponent = jnp.exp(scores - jnp.max(scores, axis=-1, keepdims=True))
        attention = exponent / jnp.sum(exponent, axis=-1, keepdims=True)
        low = attention.astype(low_ref.dtype)
        low_ref[rows, keys] = low
        context_ref[rows, :] = times(low, packed_ref[keys, values]).astype(context_ref.dtype)
        centre = jnp.sum(attention * gradient, axis=-1, keepdims=True)
        score_grad = (attention * (gradient - centre)).astype(score_ref.dtype)
        score_ref[rows, keys] = score_grad
        query_grad = times(score_grad, k_ref[keys, :]) * SCALE
        cosine, sine = tables(rows)
        back_ref[rows, :HEAD_DIM] = turn(query_grad, cosine, -sine).astype(back_ref.dtype)
    for j in range(blocks):
        keys = pl.ds(j * size, size)
        rows = pl.ds(j * size, length - j * size)
        key_grad = contract_rows(score_ref[rows, keys], q_ref[rows, :]) * SCALE
        cosine, sine = tables(keys)
        back_ref[keys, HEAD_DIM:2 * HEAD_DIM] = turn(key_grad, cosine, -sine).astype(back_ref.dtype)
        value_grad = contract_rows(low_ref[rows, keys], grad_ref[rows, :])
        back_ref[keys, values] = value_grad.astype(back_ref.dtype)

    @pl.when(pl.program_id(0) == 0)
    def _():
        sum_ref[...] = jnp.zeros_like(sum_ref)
    for i in range(blocks):
        sum_ref[...] += eight_rows(back_ref[pl.ds(i * size, size), :].astype(jnp.float32))


def attend(packed, context_grad, table, length):
    tokens, columns = packed.shape
    low = packed.dtype

    def tile(size):
        return pl.BlockSpec((length, size), lambda i: (i, 0))
    pairs = tokens * (length + 256) // 2
    return pl.pallas_call(attention_kernel, grid=(tokens // length,), out_shape=(jax.ShapeDtypeStruct((tokens, HEAD_DIM), low),
        jax.ShapeDtypeStruct((tokens, columns), low), jax.ShapeDtypeStruct((8, columns), jnp.float32)), in_specs=[tile(columns), tile(HEAD_DIM),
        pl.BlockSpec((1, *table.shape[1:]), lambda i: (i, 0, 0))], out_specs=[tile(HEAD_DIM), tile(columns), pl.BlockSpec((8, columns), lambda i: (0,
        0))], scratch_shapes=[pltpu.VMEM((length, HEAD_DIM), low), pltpu.VMEM((length, HEAD_DIM), low), pltpu.VMEM((length, length), low),
        pltpu.VMEM((length, length), low), pltpu.VMEM((length, table.shape[1]), jnp.float32)],
        compiler_params=pltpu.CompilerParams(vmem_limit_bytes=48 * 1024 * 1024), cost_estimate=pl.CostEstimate(flops=14 * pairs * HEAD_DIM,
        transcendentals=pairs, bytes_accessed=tokens * (4 * columns + 4 * HEAD_DIM + 512)), name='attend')(packed, context_grad, table)


def remote(src, dst, send_sem, recv_sem, device):
    return pltpu.make_async_remote_copy(src_ref=src, dst_ref=dst, send_sem=send_sem, recv_sem=recv_sem, device_id=device, device_id_type=MESH)


def copied(src, dst, sem):
    copy = pltpu.make_async_copy(src, dst, sem)
    copy.start()
    return copy


def meet(f, s):
    barrier = pltpu.get_barrier_semaphore()
    for k in range(1, 8):
        pl.semaphore_signal(barrier, inc=1, device_id=((f + k) % 8, s), device_id_type=MESH)
    for k in range(1, 4):
        pl.semaphore_signal(barrier, inc=1, device_id=(f, (s + k) % 4), device_id_type=MESH)
    pl.semaphore_wait(barrier, 10)


def neighbours(f):
    f_x, f_y = (f + 2 - 4 * (f // 2 % 2), f + 4 - 8 * (f // 4))
    return (f_x, f_y, f + 1 - 2 * (f % 2), f_x + f_y - f)


def gather_kernel(x_ref, c_ref, seg_ref, up_ref, qkv_ref, b_up_in, b_qkv_in, norm_in, xg_ref, cg_ref, segs_ref, normed_out, normed_mlp_out,
    packed_out, act_out, slope_out, held, tile, w_up, w_qkv, normed, normed_mlp, packed, act, slope, seg_s, seg_r, seg_l, s1, r1, s2, r2, s3, r3,
    local, w_l, tile_l, keep_l, b_up_ref, b_qkv_ref, norm_ref):
    f, s = (lax.axis_index('fsdp'), lax.axis_index('sp'))
    core = f % 2
    f_x, f_y, f_c, f_d = neighbours(f)
    piece = xg_ref.shape[3]
    meet(f, s)
    pairs = ((x_ref, xg_ref), (c_ref, cg_ref))
    sent = []

    def send(src, dst, send_sem, recv_sem, device):
        copy = remote(src, dst, send_sem, recv_sem, device)
        copy.start()
        sent.append(copy)

    def arrived(ref, recv_sem):
        remote(ref, ref, s1.at[0, 0], recv_sem, (f_c, s)).wait_recv()
    holds = f // 2 == s
    keep_seg = pltpu.make_async_copy(seg_ref, segs_ref.at[core], seg_l.at[0])
    give_seg = [remote(seg_ref, segs_ref.at[core], seg_s.at[k], seg_r.at[core], ((f + k) % 8, s)) for k in range(1, 8)]

    @pl.when(holds)
    def _():
        keep_seg.start()
        for copy in give_seg:
            copy.start()
    weights = [
        pltpu.make_async_copy(ref, held_ref, w_l.at[n])
        for n, (ref, held_ref) in enumerate(
            ((up_ref, w_up), (qkv_ref, w_qkv), (b_up_in, b_up_ref), (b_qkv_in, b_qkv_ref), (norm_in, norm_ref))
        )
    ]
    for copy in weights:
        copy.start()
    kept = []
    for a, (src, _) in enumerate(pairs):
        own = pltpu.make_async_copy(src.at[pl.ds(f * piece, piece)], held.at[a, f], local.at[a, 0])
        own.start()
        kept.append(own)
        for k in range(1, 8):
            j = (f + k) % 8
            send(src.at[pl.ds(j * piece, piece)], held.at[a, f], s1.at[a, k], r1.at[a, k], (j, s))

    def to_planes(a):
        out = pairs[a][1]
        kept[a].wait()
        for k in range(1, 8):
            arrived(held.at[a, (f + 8 - k) % 8], r1.at[a, k])
        for k in range(1, 4):
            plane = (s + k) % 4
            send(held.at[a, pl.ds(2 * plane, 2)], out.at[:, s, f], s2.at[a, k], r2.at[a, k], (f, plane))
        own = pltpu.make_async_copy(held.at[a, pl.ds(2 * s, 2)], out.at[:, s, f], local.at[a, 1])
        own.start()
        return own

    def spread(a, k):
        out = pairs[a][1]
        z = (s + 4 - k) % 4
        if k:
            arrived(out.at[:, z, f], r2.at[a, k])
        ref = out.at[:, z, f]
        send(ref, ref, s3.at[a, 0, k], r3.at[a, 0, k], (f_x, s))
        send(ref, ref, s3.at[a, 1, k], r3.at[a, 1, k], (f_y, s))
        send(ref, ref, s3.at[a, 2, k], r3.at[a, 2, k], (f_c, s))

    def pass_on(a, k):
        out = pairs[a][1]
        z = (s + 4 - k) % 4
        ref = out.at[:, z, f_x]
        arrived(ref, r3.at[a, 0, k])
        send(out.at[0, z, f_x], out.at[0, z, f_x], s3.at[a, 5, k], r3.at[a, 5, k], (f_y, s))
        send(ref, ref, s3.at[a, 3, k], r3.at[a, 3, k], (f_c, s))
        ref = out.at[:, z, f_y]
        arrived(ref, r3.at[a, 1, k])
        send(out.at[1, z, f_y], out.at[1, z, f_y], s3.at[a, 6, k], r3.at[a, 6, k], (f_x, s))
        send(ref, ref, s3.at[a, 4, k], r3.at[a, 4, k], (f_c, s))

    def pass_corner(a, k):
        out = pairs[a][1]
        z = (s + 4 - k) % 4
        for half in range(2):
            ref = out.at[half, z, f_d]
            arrived(ref, r3.at[a, 5 + half, k])
            send(ref, ref, s3.at[a, 7 + half, k], r3.at[a, 7 + half, k], (f_c, s))

    def from_core(a, k):
        out = pairs[a][1]
        z = (s + 4 - k) % 4
        g_x, g_y, _, g_d = neighbours(f_c)
        arrived(out.at[:, z, f_c], r3.at[a, 2, k])
        arrived(out.at[:, z, g_x], r3.at[a, 3, k])
        arrived(out.at[:, z, g_y], r3.at[a, 4, k])
        for half in range(2):
            arrived(out.at[half, z, g_d], r3.at[a, 7 + half, k])
    results = ((normed, normed_out), (normed_mlp, normed_mlp_out), (packed, packed_out), (act, act_out), (slope, slope_out))
    size = 8 * piece

    def keep(b, z, n):
        rows = pl.ds(pl.multiple_of((b * 4 + z) * size, size), size)
        return pltpu.make_async_copy(results[n][0].at[b], results[n][1].at[rows], keep_l.at[b, n])

    tiles = {}

    def work(k, b):
        z = (s + 4 - k) % 4
        if b == 0:
            for half in range(2):
                tiles[half] = copied(xg_ref.at[half, z], tile.at[half], tile_l.at[half])
            if k == 0:
                for copy in weights:
                    copy.wait()
        tiles[b].wait()
        if k:
            for n in range(5):
                keep(b, (s + 5 - k) % 4, n).wait()

        @pl.loop(0, 8)
        def _(i):
            inputs = tile[b, i].astype(jnp.float32)
            centred = inputs - jnp.mean(inputs, axis=-1, keepdims=True)
            variance = jnp.mean(centred * centred, axis=-1, keepdims=True)
            scaled = centred * lax.rsqrt(variance + EPSILON)
            rows = pl.ds(pl.multiple_of(i * piece, piece), piece)
            low = normed.dtype
            normed[b, rows, :] = (scaled * norm_ref[0:1, :] + norm_ref[1:2, :]).astype(low)
            normed_mlp[b, rows, :] = (scaled * norm_ref[2:3, :] + norm_ref[3:4, :]).astype(low)
        hidden = times_transposed(normed_mlp[b], w_up[...]) + b_up_ref[...]
        packed[b] = (times_transposed(normed[b], w_qkv[...]) + b_qkv_ref[...]).astype(packed.dtype)
        activated, grown = gelu_pair(hidden)
        act[b] = activated.astype(act.dtype)
        slope[b] = grown
        for n in range(5):
            keep(b, z, n).start()
    own0 = to_planes(0)
    own1 = to_planes(1)
    steps = [(a, k) for a in range(2) for k in range(4)]
    for i in range(len(steps) + 2):
        if i < len(steps):
            a, k = steps[i]
            if k == 0:
                (own0 if a == 0 else own1).wait()
            spread(a, k)
        if 3 <= i < 7:
            from_core(0, i - 3)
            work(i - 3, 0)
        if 0 <= i - 1 < len(steps):
            pass_on(*steps[i - 1])
        if 0 <= i - 2 < len(steps):
            pass_corner(*steps[i - 2])
        if 3 <= i < 7:
            work(i - 3, 1)
    for k in range(4):
        from_core(1, k)
    for b in range(2):
        for n in range(5):
            keep(b, (s + 1) % 4, n).wait()
    for b in range(2):

        @pl.when(f != 2 * s + b)
        def _():
            arrived(segs_ref.at[b], seg_r.at[b])

    @pl.when(holds)
    def _():
        keep_seg.wait()
        for copy in give_seg:
            copy.wait_send()
    for copy in sent:
        copy.wait_send()


def gather_both(x, c, segments, w_up, w_qkv, b_up, b_qkv, norms):
    rows, width = x.shape
    piece = rows // 8
    tokens = 8 * rows
    units, columns = (w_up.shape[0], w_qkv.shape[0])
    shape = jax.ShapeDtypeStruct((2, 4, 8, piece, width), x.dtype)
    dma = pltpu.SemaphoreType.DMA
    vmem = pltpu.VMEM
    anywhere = pl.BlockSpec(memory_space=pl.ANY)
    sizes = ((width, x.dtype), (width, x.dtype), (columns, x.dtype), (units, x.dtype), (units, jnp.float32))
    return pl.pallas_call(gather_kernel, out_shape=(shape, shape, jax.ShapeDtypeStruct((2, *segments.shape), segments.dtype),
        *(jax.ShapeDtypeStruct((tokens, size), kind) for size, kind in sizes)), in_specs=[anywhere] * 8, out_specs=[anywhere] * 8,
        scratch_shapes=[vmem((2, 8, piece, width), x.dtype), vmem((2, 8, piece, width), x.dtype), vmem(w_up.shape, w_up.dtype), vmem(w_qkv.shape,
        w_qkv.dtype), *(vmem((2, 8 * piece, size), kind) for size, kind in sizes), dma((8,)), dma((2,)), dma((1,)), dma((2, 8)), dma((2, 8)), dma((2,
        4)), dma((2, 4)), dma((2, 9, 4)), dma((2, 9, 4)), dma((2, 2)), dma((5,)), dma((2,)), dma((2, 5)),
        vmem((1, units), jnp.float32), vmem((1, columns), jnp.float32), vmem(norms.shape, jnp.float32)],
        compiler_params=pltpu.CompilerParams(collective_id=1, has_side_effects=True, vmem_limit_bytes=48 * 1024 * 1024), name='gather_tokens')(x, c,
        segments, w_up, w_qkv, b_up.reshape(1, units), b_qkv.reshape(1, columns), norms)


def finish_kernel(down_ref, dense_ref, hidden_ref, normed_mlp_ref, packed_ref, normed_ref, act_ref, context_ref, up_w_ref, down_w_ref, qkv_w_ref,
    dense_w_ref, norm_ref, h_col_ref, p_col_ref, bias_ref, g_down, g_up, g_qkv, g_dense, o_out, o_back, part, paired, kept, crossed, homed, o_small,
    line_a, line_b, turned, big, hidden, packed, weight, qkv_w, dense_w, context, act, total, made, own, right, vecs, vec_out, vec_in, small,
    small_in, load_l, act_l, part_l, tile_s, tile_r, tile_l, left_l, right_l, in_s, in_r, mid_s, mid_r, end_s, end_r, own_l, keep_l, turn_s, turn_r,
    cross_s, cross_r, home_s, home_r, back_s, back_r, local, vec_s, vec_r, small_s, small_r):
    f, s = (lax.axis_index('fsdp'), lax.axis_index('sp'))
    core = f % 2
    f_x, f_y, f_c, f_d = neighbours(f)
    is_end = (s == 0) | (s == 3)
    is_mid = (s == 1) | (s == 2)
    inner, outer, facing = (1 + s // 3, 3 * (s // 2), 3 - s)
    unit = made.shape[3]
    size = 8 * unit
    low = made.dtype
    meet(f, s)
    sent = []

    def send(src, dst, send_sem, recv_sem, device):
        copy = remote(src, dst, send_sem, recv_sem, device)
        copy.start()
        return copy

    def arrived(ref, recv_sem):
        remote(ref, ref, vec_s.at[0], recv_sem, (f_c, s)).wait_recv()
    chunks = []
    at = 0
    groups = {}
    for name, ref, first, result in (('down', down_ref, 0, g_down), ('up', part, 0, g_up), ('qkv', part, g_up.shape[0], g_qkv), ('dense', turned, 0,
        g_dense)):
        for g in range(result.shape[0]):
            cuts = (4,)
            if not chunks:
                cuts = (1, 1, 2)
            if name == 'dense':
                cuts = (2, 1, 1)
            start = 0
            for pairs_of in cuts:
                chunks.append((ref, first + g, result, g, start, pairs_of, at))
                groups[len(chunks) - 1] = (name, first + g)
                start += pairs_of
            at += 1
    count = len(chunks)
    ahead = 4

    def cut(ref, g, k):
        _, _, _, _, start, pairs_of, _ = chunks[k]
        return ref.at[g, pl.ds(start, pairs_of)]

    def source(k):
        return cut(chunks[k][0], chunks[k][1], k)

    def goal(k):
        return cut(chunks[k][2], chunks[k][3], k)

    def from_end(k):
        return remote(source(k), cut(line_a, chunks[k][6], k), in_s.at[k], in_r.at[k], (f, inner))

    def across(k):
        return remote(cut(line_a, chunks[k][6], k), cut(line_b, chunks[k][6], k), mid_s.at[k], mid_r.at[k], (f, facing))

    def to_end(k):
        return remote(cut(line_b, chunks[k][6], k), goal(k), end_s.at[k], end_r.at[k], (f, outer))

    def load_own(k):
        return pltpu.make_async_copy(source(k), cut(own, k % 2, k), own_l.at[k % 2])

    def keep(k):
        return pltpu.make_async_copy(cut(line_b, chunks[k][6], k), goal(k), keep_l.at[k])

    def add_units(target, others, number):
        @pl.loop(0, number)
        def _(i):
            for half in range(2):
                rows = pl.ds(half * (unit // 2), unit // 2)
                value = target[i // 2, i % 2, rows, :].astype(jnp.float32)
                for other in others:
                    value = value + other[i // 2, i % 2, rows, :].astype(jnp.float32)
                target[i // 2, i % 2, rows, :] = value.astype(low)

    def mid_in(k):
        load_own(k).wait()
        from_end(k).wait_recv()
        add_units(cut(line_a, chunks[k][6], k), [cut(own, k % 2, k)], 2 * chunks[k][5])
        across(k).start()
        if k + 2 < count:
            load_own(k + 2).start()

    def mid_out(k):
        across(k).wait_recv()
        add_units(cut(line_b, chunks[k][6], k), [cut(line_a, chunks[k][6], k)], 2 * chunks[k][5])
        to_end(k).start()
        keep(k).start()
    coming = {'big': copied(normed_mlp_ref, big, load_l.at[0]), 'hidden': copied(hidden_ref, hidden, load_l.at[1]), 'weight': copied(up_w_ref,
        weight, load_l.at[2]), 'packed': copied(packed_ref, packed, load_l.at[3]), 'qkv': copied(qkv_w_ref, qkv_w, load_l.at[4]),
        'dense': copied(dense_w_ref, dense_w, load_l.at[5]), 'context': copied(context_ref, context, load_l.at[6])}

    def ready(*names):
        for name in names:
            if coming[name] is not None:
                coming[name].wait()
                coming[name] = None
    span = dense_ref.shape[4]
    columns = pl.ds(pl.multiple_of(f * span, span), span)
    turn_own = copied(dense_ref.at[f], turned.at[0, :, :, :, columns], local.at[0])
    bias_own = copied(bias_ref, small.at[pl.ds(8, 8)], local.at[1])
    vecs[...] = jnp.zeros_like(vecs)
    vec_out[...] = jnp.zeros_like(vec_out)
    busy = {0: [], 1: []}
    turns = [0]

    def next_made():
        slot = turns[0] % 2
        turns[0] += 1
        for wait in busy[slot]:
            wait()
        busy[slot] = []
        return slot
    stores = {}

    def finish_group(g, weights, first, column_ref, which):
        slot = next_made()

        @pl.loop(0, 8)
        def _(i):
            rows = pl.ds(pl.multiple_of(i * unit, unit), unit)
            wide = pl.ds(pl.multiple_of(first + i * unit, unit), unit)
            value = total[rows, :]
            made[slot, i // 2, i % 2] = value.astype(low)
            line = weights[wide, :].astype(jnp.float32)
            sums = column_ref[wide, 0:1]
            scaled = line * (value - sums * norm_ref[2 * which + 1:2 * which + 2, :])
            vecs[2 * which] += eight_rows(scaled)
            vecs[2 * which + 1] += eight_rows(line * sums)
        stores[g] = copied(made.at[slot], part.at[g], part_l.at[g])
        busy[slot] = [functools.partial(stored, g)]

    def stored(g):
        if stores[g] is not None:
            stores[g].wait()
            stores[g] = None

    def up_group(g):
        ready('big', 'hidden', 'weight')
        total[...] = contract_rows(hidden[:, g * size:(g + 1) * size], big[...].reshape(hidden.shape[0], -1))
        finish_group(g, weight, g * size, h_col_ref, 1)
        if g == g_up.shape[0] - 1:
            coming['big'] = copied(normed_ref, big, load_l.at[7])
            coming['weight'] = copied(down_w_ref, weight, load_l.at[8])
            load_act(0)

    def qkv_group(g):
        ready('big', 'packed', 'qkv')
        total[...] = contract_rows(packed[:, g * size:(g + 1) * size], big[...].reshape(hidden.shape[0], -1))
        finish_group(g_up.shape[0] + g, qkv_w, g * size, p_col_ref, 0)

    def load_act(t):
        coming['act', t] = copied(act_ref.at[pl.ds(t * size, size)], act.at[t % 2], act_l.at[t % 2])

    def give_tile(a, t, value):
        b, z = (t // 4, t % 4)
        slot = next_made()
        made[slot] = value.astype(low).reshape(4, 2, unit, value.shape[1])
        give = send(made.at[slot, :, 1 - core], paired.at[a, :, z, b], tile_s.at[a, t], tile_r.at[a, t], (f_c, s))
        hold = copied(made.at[slot, :, core], kept.at[a, :, z, b], tile_l.at[a, t])
        busy[slot] = [give.wait_send, hold.wait]

    def out_tile(t):
        ready('weight', 'context', 'dense', ('act', t))
        if t < 7:
            load_act(t + 1)
        rows = slice(t * size, (t + 1) * size)
        value = times_transposed(context[rows, :], dense_w[...]) + times(act[t % 2], weight[...])
        give_tile(0, t, value)
        if t == 7:
            coming['weight'] = copied(up_w_ref, weight, load_l.at[9])

    def back_tile(t):
        ready('weight', 'packed', 'qkv', 'hidden')
        rows = slice(t * size, (t + 1) * size)
        value = times(packed[rows, :], qkv_w[...]) * norm_ref[0:1, :]
        value = value + times(hidden[rows, :], weight[...]) * norm_ref[2:3, :]
        give_tile(1, t, value)
    results = (o_out, o_back)
    order = (f_d // 2, f_x // 2, f_y // 2, f // 2)
    homes = {}

    def free(slot):
        for wait in busy[slot]:
            wait()
        busy[slot] = []

    def tiles_here(a):
        for slot in range(2):
            free(slot)
        for t in range(8):
            arrived(paired.at[a, :, t % 4, t // 4], tile_r.at[a, t])

    def add_pair(a, n):
        if n == 0:
            tiles_here(a)
        left = big.at[3 * a + n]
        slot = n % 2
        first = copied(paired.at[a, order[n]], left, left_l.at[slot])
        second = copied(kept.at[a, order[n]], right.at[slot], right_l.at[slot])
        first.wait()
        second.wait()
        add_units(left, [right.at[slot]], 8)
        sent.append(send(left, crossed.at[a, n], cross_s.at[a, n], cross_r.at[a, n], ((f_d, f_x, f_y)[n], s)))

    def add_chips(a):
        left = big.at[6 + a]
        copies = [copied(paired.at[a, order[3]], left, left_l.at[0]), copied(kept.at[a, order[3]], right.at[0], right_l.at[0])]
        for n in range(3):
            arrived(crossed.at[a, n], cross_r.at[a, n])
            slot = (n + 1) % 2
            more = copied(crossed.at[a, n], right.at[slot], right_l.at[slot])
            for copy in copies:
                copy.wait()
            add_units(left, [right.at[1 - slot]], 8)
            copies = [more]
        copies[0].wait()
        add_units(left, [right.at[1]], 8)
        for k in range(1, 4):
            z = (s + k) % 4
            sent.append(send(left.at[z], homed.at[a, s], home_s.at[a, k], home_r.at[a, k], (f, z)))
        homes['own', a] = copied(left.at[s], homed.at[a, s], local.at[2 + a])


    def go_home(a):
        homes['own', a].wait()
        for k in range(1, 4):
            arrived(homed.at[a, (s + 4 - k) % 4], home_r.at[a, k])
        for k in range(1, 8):
            j = (f + k) % 8
            sent.append(send(homed.at[a, j // 2, j % 2], results[a].at[f], back_s.at[a, k], back_r.at[a, k], (j, s)))
        homes[a] = copied(homed.at[a, f // 2, core], results[a].at[f], local.at[4 + a])

    def give_vectors():
        for which in range(2):
            gain = norm_ref[2 * which:2 * which + 1, :]
            scaled = jnp.sum(vecs[2 * which], axis=0, keepdims=True) / gain
            plain = jnp.sum(vecs[2 * which + 1], axis=0, keepdims=True)
            for j in range(8):
                part_of = slice(j * span, (j + 1) * span)
                vec_out[j, 2 * which:2 * which + 1, :] = scaled[:, part_of]
                vec_out[j, 2 * which + 1:2 * which + 2, :] = plain[:, part_of]
        for k in range(1, 8):
            j = (f + k) % 8
            sent.append(send(vec_out.at[j], vec_in.at[f], vec_s.at[k], vec_r.at[k], (j, s)))
        homes['vec'] = copied(vec_out.at[f], vec_in.at[f], local.at[6])

    def add_vectors():
        homes['vec'].wait()
        bias_own.wait()
        for k in range(1, 8):
            arrived(vec_in.at[(f + 8 - k) % 8], vec_r.at[k])
        value = vec_in[0]
        for j in range(1, 8):
            value = value + vec_in[j]
        small[0:8, :] = value
        for k in range(1, 4):
            sent.append(send(small, small_in.at[s], small_s.at[k], small_r.at[k], (f, (s + k) % 4)))
        homes['small'] = copied(small, small_in.at[s], local.at[7])

    def add_small():
        homes['small'].wait()
        for k in range(1, 4):
            arrived(small_in.at[(s + 4 - k) % 4], small_r.at[k])
        value = small_in[0]
        for z in range(1, 4):
            value = value + small_in[z]
        o_small[...] = value

    def turn_start():
        for k in range(1, 8):
            j = (f + k) % 8
            sent.append(send(dense_ref.at[j], turned.at[0, :, :, :, columns], turn_s.at[k], turn_r.at[k], (j, s)))

    def turn_done():
        turn_own.wait()
        for k in range(1, 8):
            j = (f + 8 - k) % 8
            there = pl.ds(pl.multiple_of(j * span, span), span)
            arrived(turned.at[0, :, :, :, there], turn_r.at[k])

    def task(name, i):
        if name == 'turn':
            turn_start()
        elif name == 'turned':
            turn_done()
        elif name == 'up':
            up_group(i)
        elif name == 'qkv':
            qkv_group(i)
        elif name == 'out':
            out_tile(i)
        elif name == 'back':
            back_tile(i)
        elif name == 'pair':
            add_pair(i // 3, i % 3)
        elif name == 'chips':
            add_chips(i)
        elif name == 'home':
            go_home(i)
        elif name == 'vectors':
            give_vectors()
        elif name == 'sums':
            add_vectors()
        else:
            add_small()

    @pl.when(is_end)
    def _():
        for k in range(ahead):
            from_end(k).start()

    @pl.when(is_mid)
    def _():
        for k in range(2):
            load_own(k).start()
    for k in range(count + 2):
        for name, first, last in FINISH_STEPS[k] if k in FINISH_STEPS else ():
            for i in range(first, last):
                task(name, i)
        if k + ahead - 1 in groups and groups[k + ahead - 1][0] in ('up', 'qkv'):
            stored(groups[k + ahead - 1][1])

        @pl.when(is_mid)
        def _():
            if k < count:
                mid_in(k)
            if 1 <= k <= count:
                mid_out(k - 1)

        @pl.when(is_end)
        def _():
            if 1 <= k <= count:
                to_end(k - 1).wait_recv()
                if k - 1 + ahead < count:
                    from_end(k - 1 + ahead).start()
    for a in range(2):
        homes[a].wait()
        for k in range(1, 8):
            arrived(results[a].at[(f + 8 - k) % 8], back_r.at[a, k])
    for slot in range(2):
        free(slot)
    for copy in sent:
        copy.wait_send()

    @pl.when(is_end)
    def _():
        for k in range(count):
            from_end(k).wait_send()

    @pl.when(is_mid)
    def _():
        for k in range(count):
            across(k).wait_send()
            to_end(k).wait_send()
            keep(k).wait()


FINISH_STEPS = {
    0: (("turn", 0, 1),),
    1: (("up", 0, 1),),
    2: (("up", 1, 2),),
    3: (("up", 2, 4),),
    4: (("qkv", 0, 3),),
    5: (("out", 0, 8),),
    6: (("pair", 0, 3), ("back", 0, 3)),
    7: (("back", 3, 6), ("turned", 0, 1)),
    8: (("back", 6, 8), ("vectors", 0, 1), ("pair", 3, 6)),
    9: (("chips", 0, 1),),
    10: (("sums", 0, 1),),
    11: (("home", 0, 1), ("chips", 1, 2)),
    12: (("small", 0, 1),),
    14: (("home", 1, 2),),
}


def finish(down, dense, hidden_grad, normed_mlp, packed_grad, normed, act, context, w_up, w_down, w_qkv, dense_in, norms, h_sums, p_sums, bias):
    width = down.shape[1]
    tokens = hidden_grad.shape[0]
    low = down.dtype
    unit = tokens // 64
    size = 8 * unit
    span = width // 8

    def grouped(rows):
        return (rows // size, 4, 2, unit, width)

    def columns(sums):
        return jnp.broadcast_to(sums[:, None], (sums.shape[0], 128))
    sets = [w.shape[0] // size for w in (down, w_up, w_qkv)]
    number = sum(sets) + 1
    count = sum(sets) + 5
    sums = [jax.ShapeDtypeStruct(grouped(n * size), low) for n in (*sets, 1)]
    token = jax.ShapeDtypeStruct((8, unit, width), low)
    halves = jax.ShapeDtypeStruct((2, 4, 4, 2, unit, width), low)
    others = [jax.ShapeDtypeStruct(grouped((sets[1] + sets[2]) * size), low), halves, halves, jax.ShapeDtypeStruct((2, 3, 4, 2, unit, width), low),
        jax.ShapeDtypeStruct((2, 4, 2, unit, width), low)]
    dma = pltpu.SemaphoreType.DMA
    vmem = pltpu.VMEM
    anywhere = pl.BlockSpec(memory_space=pl.ANY)
    inside = pl.BlockSpec(memory_space=pltpu.VMEM)
    result = pl.pallas_call(finish_kernel, out_shape=(*sums, token, token, *others, jax.ShapeDtypeStruct((16, span), jnp.float32)),
        in_specs=[anywhere] * 12 + [inside] * 3 + [anywhere], out_specs=[anywhere] * 11 + [inside], scratch_shapes=[vmem((number, 4, 2, unit, width),
        low), vmem((number, 4, 2, unit, width), low), vmem((1, 4, 2, unit, width), low), vmem(grouped(tokens), low), vmem(hidden_grad.shape, low),
        vmem(packed_grad.shape, low), vmem(w_up.shape, low), vmem(w_qkv.shape, low), vmem(dense_in.shape, low), vmem(context.shape, low), vmem((2,
        size, act.shape[1]), low), vmem((size, width), jnp.float32), *(vmem((2, 4, 2, unit, width), low) for _ in range(3)), vmem((4, 8, width),
        jnp.float32), vmem((8, 8, span), jnp.float32), vmem((8, 8, span), jnp.float32), vmem((16, span), jnp.float32), vmem((4, 16, span),
        jnp.float32), dma((10,)), dma((2,)), dma((sets[1] + sets[2],)), dma((2, 8)), dma((2, 8)), dma((2, 8)), dma((2,)), dma((2,)), dma((count,)),
        dma((count,)), dma((count,)), dma((count,)), dma((count,)), dma((count,)), dma((2,)), dma((count,)), dma((8,)), dma((8,)), dma((2, 3)),
        dma((2, 3)), dma((2, 4)), dma((2, 4)), dma((2, 8)), dma((2, 8)), dma((8,)), dma((8,)), dma((8,)), dma((4,)), dma((4,))],
        compiler_params=pltpu.CompilerParams(collective_id=2, has_side_effects=True, vmem_limit_bytes=60 * 1024 * 1024),
        name='finish')(down.reshape(grouped(down.shape[0])), dense.reshape(8, 4, 2, unit, span), hidden_grad, normed_mlp.reshape(grouped(tokens)), packed_grad, normed.reshape(grouped(tokens)), act,
        context, w_up, w_down, w_qkv, dense_in, norms, columns(h_sums), columns(p_sums), bias)
    grads = [grad.reshape(-1, width) for grad in result[:4]]
    return (grads, result[4], result[5], result[11])


def widen_kernel(early_ref, late_ref, up_ref, qkv_ref, dense_ref, down_out, up_out, qkv_out, dense_out):
    down_out[0] = early_ref[...].astype(jnp.float32)
    down_out[1] = late_ref[...].astype(jnp.float32)
    for ref, out in ((up_ref, up_out), (qkv_ref, qkv_out), (dense_ref, dense_out)):
        out[...] = ref[...].astype(jnp.float32)


def widen(early, late, up, qkv, dense, steps=8):
    width = up.shape[1]

    def tile(array):
        return pl.BlockSpec((array.shape[0] // steps, width), lambda i: (i, 0))

    arrays = (early, late, up, qkv, dense)
    wide = jax.ShapeDtypeStruct((2, early.shape[0], width), jnp.float32)
    number = 2 * early.size + up.size + qkv.size + dense.size
    down, up, qkv, dense = pl.pallas_call(
        widen_kernel,
        grid=(steps,),
        out_shape=(wide, *(jax.ShapeDtypeStruct(array.shape, jnp.float32) for array in arrays[2:])),
        in_specs=[tile(array) for array in arrays],
        out_specs=[pl.BlockSpec((2, early.shape[0] // steps, width), lambda i: (0, i, 0)), *(tile(array) for array in arrays[2:])],
        compiler_params=pltpu.CompilerParams(vmem_limit_bytes=60 * 1024 * 1024),
        cost_estimate=pl.CostEstimate(flops=0, transcendentals=0, bytes_accessed=6 * number),
        name="widen",
    )(*arrays)
    return down.reshape(-1, width), up, qkv, dense


def own_tokens(hidden_in, cotangent, output, weighted, shift):
    inputs = hidden_in.astype(jnp.float32)
    output = (inputs + (output.astype(jnp.float32) + shift)).astype(jnp.bfloat16)
    scaled, inverse = norm_scaled(inputs)
    weighted = weighted.astype(jnp.float32)
    first_mean = jnp.mean(weighted, axis=-1, keepdims=True)
    second_mean = jnp.mean(weighted * scaled, axis=-1, keepdims=True)
    input_grad = (cotangent.astype(jnp.float32) + inverse * (weighted - first_mean - scaled * second_mean)).astype(jnp.bfloat16)
    return (output, input_grad)


def by_collectives(hidden_in, segments, ln1_gain, ln1_bias, ln2_gain, ln2_bias, w_qkv, b_qkv, w_dense, b_dense, w_up, b_up, w_down, b_down,
    cotangent):
    seq_local, shard_len, width = hidden_in.shape
    seq_len = segments.shape[1]
    nf, ns = (lax.axis_size('fsdp'), lax.axis_size('sp'))
    f_place, s_place = (lax.axis_index('fsdp'), lax.axis_index('sp'))
    seqs = seq_local * nf
    group = seqs // ns
    piece = shard_len // nf
    tokens = group * seq_len
    per_head = max(1, nf // HEADS)
    head_count = max(1, HEADS // nf)
    head_sets = [[head * per_head + k for k in range(per_head)] for head in range(nf // per_head)]

    def gather_tokens(block):
        part = lax.all_to_all(block, 'fsdp', split_axis=1, concat_axis=0, tiled=True)
        part = lax.all_to_all(part, 'sp', split_axis=0, concat_axis=1, tiled=True)
        return in_order(lax.all_gather(part, 'fsdp', axis=0, tiled=True)).reshape(tokens, width)

    def scatter_tokens(partial):
        part = out_of_order(partial).reshape(nf * group, ns * piece, width)
        part = lax.psum_scatter(part, 'fsdp', scatter_dimension=0, tiled=True)
        part = lax.all_to_all(part, 'sp', split_axis=1, concat_axis=0, tiled=True)
        return lax.all_to_all(part, 'fsdp', split_axis=0, concat_axis=1, tiled=True)

    def in_order(array):
        array = array.reshape(nf, group, ns, piece, -1)
        return array.transpose(1, 2, 0, 3, 4).reshape(group, seq_len, -1)

    def out_of_order(array):
        array = array.reshape(group, ns, nf, piece, -1)
        return array.transpose(2, 0, 1, 3, 4).reshape(tokens, -1)

    def over_head(array, axis):
        if per_head == 1:
            return array
        return lax.all_gather(array, 'fsdp', axis=axis, tiled=True, axis_index_groups=head_sets)

    def own_columns(array):
        if per_head == 1:
            return array
        share = array.shape[-1] // per_head
        return lax.dynamic_slice_in_dim(array, f_place % per_head * share, share, array.ndim - 1)

    def own_part(vector):
        share = vector.shape[0] // nf
        return lax.dynamic_slice_in_dim(vector, f_place * share, share, 0)
    gathered, upstream = (gather_tokens(hidden_in), gather_tokens(cotangent))
    rows = lax.all_gather(segments, 'fsdp', axis=0, tiled=True)
    rows = lax.dynamic_slice_in_dim(rows, s_place * group, group, 0)
    dense_in = lax.all_to_all(w_dense, 'fsdp', split_axis=1, concat_axis=0, tiled=True)
    head_qkv = over_head(w_qkv, 0)
    head_dense = over_head(dense_in, 1)
    head_bias = lax.dynamic_slice_in_dim(b_qkv, f_place // per_head * head_qkv.shape[0], head_qkv.shape[0], 0)
    scaled, _ = norm_scaled(gathered.astype(jnp.float32))
    normed = (scaled * ln1_gain + ln1_bias).astype(jnp.bfloat16)
    normed_mlp = (scaled * ln2_gain + ln2_bias).astype(jnp.bfloat16)
    hidden = times_transposed(normed_mlp, w_up) + own_part(b_up)
    activated, slope = gelu_pair(hidden)
    activated = activated.astype(jnp.bfloat16)
    down_term = contract_rows(activated, upstream).astype(jnp.bfloat16)
    grad_down_w = lax.psum(down_term, 'sp').astype(jnp.float32)
    hidden_grad = (times_transposed(upstream, w_down) * slope).astype(jnp.bfloat16)
    up_term = contract_rows(hidden_grad, normed_mlp)
    mlp_norm_grad = times(hidden_grad, w_up)
    packed = (times_transposed(normed, head_qkv) + head_bias).astype(jnp.bfloat16)
    packed = packed.reshape(group, seq_len, head_count, 3 * HEAD_DIM)
    cos_table, sin_table = rotary_tables(rows)
    queries = rotate(packed[..., :HEAD_DIM].astype(jnp.float32), cos_table, sin_table).astype(jnp.bfloat16)
    keys_rot = rotate(packed[..., HEAD_DIM:2 * HEAD_DIM].astype(jnp.float32), cos_table, sin_table).astype(jnp.bfloat16)
    values = packed[..., 2 * HEAD_DIM:]
    mask = build_mask(rows)
    context, log_total = attend_forward(queries, keys_rot, values, mask)
    context = own_columns(context.reshape(tokens, -1))
    partial_out = times_transposed(context, dense_in) + times(activated, w_down)
    context_grad = times(upstream, head_dense).astype(jnp.bfloat16).reshape(group, seq_len, head_count, HEAD_DIM)
    query_grad, key_grad, value_grad = attend_backward(queries, keys_rot, values, mask, log_total, context_grad)
    packed_grad = jnp.concatenate([unrotate(query_grad, cos_table, sin_table), unrotate(key_grad, cos_table, sin_table), value_grad],
        axis=-1).astype(jnp.bfloat16)
    packed_grad = own_columns(packed_grad.reshape(tokens, -1))
    attn_norm_grad = times(packed_grad, w_qkv)
    qkv_term = contract_rows(packed_grad, normed)
    dense_term = contract_rows(upstream, context).astype(jnp.bfloat16)
    partial_back = attn_norm_grad * ln1_gain + mlp_norm_grad * ln2_gain
    vectors = jnp.stack([jnp.sum(attn_norm_grad * scaled, axis=0), jnp.sum(attn_norm_grad, axis=0), jnp.sum(mlp_norm_grad * scaled, axis=0),
        jnp.sum(mlp_norm_grad, axis=0)])
    bias_out = own_part(jnp.sum(upstream.astype(jnp.float32), axis=0))
    bias_qkv = jnp.sum(packed_grad.astype(jnp.float32), axis=0)
    bias_up = jnp.sum(hidden_grad.astype(jnp.float32), axis=0)
    vectors = lax.psum_scatter(vectors, 'fsdp', scatter_dimension=1, tiled=True)
    vectors, bias_out, bias_qkv, bias_up = lax.psum((vectors, bias_out, bias_qkv, bias_up), 'sp')
    output = scatter_tokens(rounded(partial_out))
    weighted = scatter_tokens(rounded(partial_back))
    dense_term = lax.all_to_all(dense_term, 'fsdp', split_axis=0, concat_axis=1, tiled=True)
    grad_up_w, grad_qkv_w, grad_dense_w = (lax.psum(term.astype(jnp.bfloat16), 'sp').astype(jnp.float32) for term in (up_term, qkv_term, dense_term))
    output, input_grad = own_tokens(hidden_in, cotangent, output, weighted, b_dense + b_down)
    return (output, input_grad, vectors[0], vectors[1], vectors[2], vectors[3], grad_qkv_w, bias_qkv, grad_dense_w, bias_out, grad_up_w, bias_up,
        grad_down_w, bias_out)


def by_kernels(hidden_in, segments, ln1_gain, ln1_bias, ln2_gain, ln2_bias, w_qkv, b_qkv, w_dense, b_dense, w_up, b_up, w_down, b_down, cotangent):
    width = hidden_in.shape[2]
    seq_len = segments.shape[1]
    nf, ns = (lax.axis_size('fsdp'), lax.axis_size('sp'))
    group = nf // ns
    tokens = group * seq_len
    share = width // nf
    f_place = lax.axis_index('fsdp')

    def own_part(vector):
        size = vector.shape[0] // nf
        return lax.dynamic_slice_in_dim(vector, f_place * size, size, 0)
    norms = jnp.stack([ln1_gain, ln1_bias, ln2_gain, ln2_bias])
    _, upstream, rows, normed, normed_mlp, packed, activated, slope = gather_both(hidden_in[0], cotangent[0], segments.reshape(8, seq_len // 8),
        w_up, w_qkv, own_part(b_up), own_part(b_qkv), norms)
    upstream = upstream.reshape(tokens, width)
    w_dense, upstream = lax.optimization_barrier((w_dense, upstream))
    dense_in = lax.all_to_all(w_dense, 'fsdp', split_axis=1, concat_axis=0, tiled=True)
    early = activated.shape[1] // 2
    down_term = contract_rows(activated[:, :early], upstream).astype(jnp.bfloat16)
    early_down_w = lax.psum(down_term, 'sp')
    slope, activated, down_term = lax.optimization_barrier((slope, activated, down_term))
    hidden_grad, context_grad, c_sums, h_sums = upstream_parts(upstream, slope, w_down, dense_in)
    context, packed_grad, p_sums = attend(packed, context_grad, head_tables(rows.reshape(group, seq_len)), seq_len)
    late_down_term = contract_rows(activated[:, early:], upstream).astype(jnp.bfloat16)
    dense_term = contract_rows(upstream, context).astype(jnp.bfloat16)
    bias_up, bias_qkv = (jnp.sum(h_sums, axis=0), jnp.sum(p_sums, axis=0))
    bias_out = own_part(jnp.sum(c_sums, axis=0))
    grads, output, weighted, sums = finish(late_down_term, dense_term, hidden_grad, normed_mlp, packed_grad, normed, activated, context, w_up,
        w_down, w_qkv, dense_in, norms, bias_up, bias_qkv, jnp.concatenate([bias_out, bias_qkv, bias_up]).reshape(8, share))
    grad_down_w, grad_up_w, grad_qkv_w, grad_dense_w = widen(early_down_w, *grads)
    bias_out = sums[8]
    output, input_grad = own_tokens(hidden_in, cotangent, output.reshape(hidden_in.shape), weighted.reshape(hidden_in.shape), b_dense + b_down)
    return (output, input_grad, sums[0], sums[1], sums[2], sums[3], grad_qkv_w, sums[9:12].reshape(-1), grad_dense_w, bias_out, grad_up_w,
        sums[12:16].reshape(-1), grad_down_w, bias_out)


def per_device(hidden_in, *rest):
    sizes = (lax.axis_size('fsdp'), lax.axis_size('sp'), hidden_in.shape[0])
    shapes = (hidden_in.shape[1] % 256, hidden_in.shape[2] % (8 * HEAD_DIM), rest[9].shape[0] % 256)
    if sizes == (8, 4, 1) and HEADS == 8 and (not any(shapes)):
        return by_kernels(hidden_in, *rest)
    return by_collectives(hidden_in, *rest)


def solution(mesh):
    rows = P('fsdp', 'sp', None)
    first = P('fsdp', None)
    return jax.shard_map(per_device, mesh=mesh, in_specs=(rows, first, P(), P(), P(), P(), first, P(), first, P(), first, P(), first, P(), rows),
        out_specs=(rows, rows, P('fsdp'), P('fsdp'), P('fsdp'), P('fsdp'), first, P('fsdp'), first, P('fsdp'), first, P('fsdp'), first, P('fsdp')),
        check_vma=False)
```

```python
import functools
import math

import jax
import jax.numpy as jnp
from jax import lax
from jax.experimental import pallas as pl
from jax.experimental.pallas import tpu as pltpu
from jax.sharding import PartitionSpec as P

MESH = pl.DeviceIdType.MESH

HEADS = 8
HEAD_DIM = 256
ROT = 64


EPSILON = 1e-05
NEGATIVE = -1e30
ROOT_HALF = 0.7071067811865476
ROOT_TWO_PI = 2.5066282746310002
SCALE = 1.0 / math.sqrt(HEAD_DIM)


def rounded(array):
    return lax.reduce_precision(array.astype(jnp.float32), 8, 7).astype(jnp.bfloat16)


def contract_rows(former, latter):
    return lax.dot_general(former, latter, (((0,), (0,)), ((), ())), preferred_element_type=jnp.float32)


def times_transposed(former, latter):
    return lax.dot_general(former, latter, (((1,), (1,)), ((), ())), preferred_element_type=jnp.float32)


def times(former, latter):
    return jnp.dot(former, latter, preferred_element_type=jnp.float32)


def norm_scaled(inputs):
    average = jnp.mean(inputs, axis=-1, keepdims=True)
    centred = inputs - average
    variance = jnp.mean(centred * centred, axis=-1, keepdims=True)
    inverse = lax.rsqrt(variance + EPSILON)
    return (centred * inverse, inverse)


def gelu_pair(hidden):
    cumulative = 0.5 * (1.0 + lax.erf(hidden * ROOT_HALF))
    return (hidden * cumulative, cumulative + hidden * (jnp.exp(-0.5 * hidden * hidden) * (1.0 / ROOT_TWO_PI)))


def document_starts(segment_rows):
    places = jnp.arange(segment_rows.shape[-1], dtype=jnp.int32)
    changes = jnp.concatenate([jnp.ones_like(segment_rows[..., :1]), (segment_rows[..., 1:] != segment_rows[..., :-1]).astype(jnp.int32)], axis=-1)
    return (places, lax.cummax(changes * places, axis=segment_rows.ndim - 1))


def frequencies():
    return 1.0 / jnp.power(10000.0, jnp.arange(0, ROT, 2).astype(jnp.float32) / ROT)


def rotary_tables(segment_rows):
    places, starts = document_starts(segment_rows)
    angles = (places - starts).astype(jnp.float32)[..., None] * frequencies()
    angles = jnp.concatenate([angles, angles], axis=-1)
    return (jnp.cos(angles), jnp.sin(angles))


def head_tables(segment_rows):
    places, starts = document_starts(segment_rows)
    angles = (places - starts).astype(jnp.float32)[:, None, :] * frequencies()[None, :, None]
    starts = jnp.broadcast_to(starts.astype(jnp.float32)[:, None, :], (starts.shape[0], ROT, starts.shape[1]))
    return jnp.concatenate([jnp.cos(angles), jnp.sin(angles), starts], axis=1)


def rotate(heads_part, cos_table, sin_table):
    half_rot = ROT // 2
    turned = heads_part[..., :ROT]
    swapped = jnp.concatenate([-turned[..., half_rot:], turned[..., :half_rot]], axis=-1)
    turned = turned * cos_table[..., None, :] + swapped * sin_table[..., None, :]
    return jnp.concatenate([turned, heads_part[..., ROT:]], axis=-1)


def unrotate(grads_part, cos_table, sin_table):
    half_rot = ROT // 2
    turned = grads_part[..., :ROT]
    along_sin = turned * sin_table[..., None, :]
    back_turn = jnp.concatenate([along_sin[..., half_rot:], -along_sin[..., :half_rot]], axis=-1)
    turned = turned * cos_table[..., None, :] + back_turn
    return jnp.concatenate([turned, grads_part[..., ROT:]], axis=-1)


def build_mask(segment_rows):
    places = jnp.arange(segment_rows.shape[-1], dtype=jnp.int32)
    return (segment_rows[:, :, None] == segment_rows[:, None, :]) & (places[None, :] <= places[:, None])


def attention_scores(queries, keys_rot):
    return jnp.einsum('bqhd,bkhd->bhqk', queries, keys_rot, preferred_element_type=jnp.float32) * SCALE


def attend_forward(queries, keys_rot, values, mask):
    scores = jnp.where(mask[:, None], attention_scores(queries, keys_rot), NEGATIVE)
    row_top = jnp.max(scores, axis=-1, keepdims=True)
    exponent = jnp.exp(scores - row_top)
    row_total = jnp.sum(exponent, axis=-1, keepdims=True)
    attention = (exponent / row_total).astype(jnp.bfloat16)
    context = jnp.einsum('bhqk,bkhd->bqhd', attention, values, preferred_element_type=jnp.float32)
    return (context.astype(jnp.bfloat16), row_top + jnp.log(row_total))


def attend_backward(queries, keys_rot, values, mask, log_total, context_grad):
    scores = attention_scores(queries, keys_rot)
    attention = jnp.where(mask[:, None], jnp.exp(scores - log_total), 0.0)
    value_grad = jnp.einsum('bhqk,bqhd->bkhd', attention.astype(jnp.bfloat16), context_grad, preferred_element_type=jnp.float32)
    attention_grad = jnp.einsum('bqhd,bkhd->bhqk', context_grad, values, preferred_element_type=jnp.float32)
    row_centre = jnp.sum(attention * attention_grad, axis=-1, keepdims=True)
    score_grad = (attention * (attention_grad - row_centre)).astype(jnp.bfloat16)
    query_grad = jnp.einsum('bhqk,bkhd->bqhd', score_grad, keys_rot, preferred_element_type=jnp.float32) * SCALE
    key_grad = jnp.einsum('bhqk,bqhd->bkhd', score_grad, queries, preferred_element_type=jnp.float32) * SCALE
    return (query_grad, key_grad, value_grad)


def whole_block(array):
    return pl.BlockSpec(array.shape, lambda *_: (0,) * array.ndim, pipeline_mode=pl.Buffered(1))


def eight_rows(array):
    return jnp.sum(array.reshape(array.shape[0] // 8, 8, array.shape[1]), axis=0)


def upstream_kernel(c_ref, slope_ref, down_ref, dense_ref, grad_ref, context_ref, c_sum_ref, h_sum_ref):
    @pl.when(pl.program_id(0) == 0)
    def _():
        c_sum_ref[...] = jnp.zeros_like(c_sum_ref)
        h_sum_ref[...] = jnp.zeros_like(h_sum_ref)
    hidden_grad = (times_transposed(c_ref[...], down_ref[...]) * slope_ref[...]).astype(grad_ref.dtype)
    grad_ref[...] = hidden_grad
    context_ref[...] = times(c_ref[...], dense_ref[...]).astype(context_ref.dtype)
    c_sum_ref[...] += eight_rows(c_ref[...].astype(jnp.float32))
    h_sum_ref[...] += eight_rows(hidden_grad.astype(jnp.float32))


def upstream_parts(c, slope, w_down, dense, rows=256):
    tokens, width = c.shape
    units, columns = (w_down.shape[0], dense.shape[1])

    def tile(size):
        return pl.BlockSpec((rows, size), lambda i: (i, 0))

    def total(size):
        return pl.BlockSpec((8, size), lambda i: (0, 0))
    return pl.pallas_call(upstream_kernel, grid=(tokens // rows,), out_shape=(jax.ShapeDtypeStruct((tokens, units), c.dtype),
        jax.ShapeDtypeStruct((tokens, columns), c.dtype), jax.ShapeDtypeStruct((8, width), jnp.float32), jax.ShapeDtypeStruct((8, units),
        jnp.float32)), in_specs=[tile(width), tile(units), whole_block(w_down), whole_block(dense)], out_specs=[tile(units), tile(columns),
        total(width), total(units)], compiler_params=pltpu.CompilerParams(vmem_limit_bytes=48 * 1024 * 1024),
        cost_estimate=pl.CostEstimate(flops=2 * tokens * width * (units + columns), transcendentals=0,
        bytes_accessed=2 * tokens * (width + 3 * units + columns) + 2 * width * (units + columns)), name='upstream_parts')(c, slope, w_down, dense)


def attention_kernel(packed_ref, grad_ref, table_ref, context_ref, back_ref, sum_ref, q_ref, k_ref, low_ref, score_ref, turned_ref):
    length = packed_ref.shape[0]
    size = 256
    lanes = 128
    lane = lax.broadcasted_iota(jnp.int32, (size, lanes), 1)
    half = ROT // 2

    def tables(rows):
        table = turned_ref[rows, :]
        cosine = jnp.where(lane < half, table, jnp.where(lane < ROT, pltpu.roll(table, half, 1), 1.0))
        sine = jnp.where(lane < half, pltpu.roll(table, lanes - half, 1), jnp.where(lane < ROT, table, 0.0))
        return (cosine, jnp.where(lane < half, -sine, sine))

    def swapped(array):
        return jnp.where(lane < half, pltpu.roll(array, lanes - half, 1), pltpu.roll(array, half, 1))

    def turn(array, cosine, sine):
        front = array[:, :lanes]
        return jnp.concatenate([front * cosine + swapped(front) * sine, array[:, lanes:]], axis=1)
    blocks = length // size
    for i in range(blocks):
        rows = pl.ds(i * size, size)
        turned_ref[rows, :] = jnp.transpose(table_ref[0, :, rows])
        cosine, sine = tables(rows)
        for part, ref in enumerate((q_ref, k_ref)):
            array = packed_ref[rows, part * HEAD_DIM:(part + 1) * HEAD_DIM].astype(jnp.float32)
            ref[rows, :] = turn(array, cosine, sine).astype(ref.dtype)
    values = pl.ds(2 * HEAD_DIM, HEAD_DIM)
    for i in range(blocks):
        rows = pl.ds(i * size, size)
        reach = (i + 1) * size
        keys = pl.ds(0, reach)
        scores = times_transposed(q_ref[rows, :], k_ref[keys, :]) * SCALE
        gradient = times_transposed(grad_ref[rows, :], packed_ref[keys, values])
        place = lax.broadcasted_iota(jnp.int32, (size, reach), 1)
        query = lax.broadcasted_iota(jnp.int32, (size, reach), 0) + i * size
        start = turned_ref[rows, ROT:ROT + 1].astype(jnp.int32)
        allowed = (place >= start) & (place <= query)
        scores = jnp.where(allowed, scores, NEGATIVE)
        exponent = jnp.exp(scores - jnp.max(scores, axis=-1, keepdims=True))
        attention = exponent / jnp.sum(exponent, axis=-1, keepdims=True)
        low = attention.astype(low_ref.dtype)
        low_ref[rows, keys] = low
        context_ref[rows, :] = times(low, packed_ref[keys, values]).astype(context_ref.dtype)
        centre = jnp.sum(attention * gradient, axis=-1, keepdims=True)
        score_grad = (attention * (gradient - centre)).astype(score_ref.dtype)
        score_ref[rows, keys] = score_grad
        query_grad = times(score_grad, k_ref[keys, :]) * SCALE
        cosine, sine = tables(rows)
        back_ref[rows, :HEAD_DIM] = turn(query_grad, cosine, -sine).astype(back_ref.dtype)
    for j in range(blocks):
        keys = pl.ds(j * size, size)
        rows = pl.ds(j * size, length - j * size)
        key_grad = contract_rows(score_ref[rows, keys], q_ref[rows, :]) * SCALE
        cosine, sine = tables(keys)
        back_ref[keys, HEAD_DIM:2 * HEAD_DIM] = turn(key_grad, cosine, -sine).astype(back_ref.dtype)
        value_grad = contract_rows(low_ref[rows, keys], grad_ref[rows, :])
        back_ref[keys, values] = value_grad.astype(back_ref.dtype)

    @pl.when(pl.program_id(0) == 0)
    def _():
        sum_ref[...] = jnp.zeros_like(sum_ref)
    for i in range(blocks):
        sum_ref[...] += eight_rows(back_ref[pl.ds(i * size, size), :].astype(jnp.float32))


def attend(packed, context_grad, table, length):
    tokens, columns = packed.shape
    low = packed.dtype

    def tile(size):
        return pl.BlockSpec((length, size), lambda i: (i, 0))
    pairs = tokens * (length + 256) // 2
    return pl.pallas_call(attention_kernel, grid=(tokens // length,), out_shape=(jax.ShapeDtypeStruct((tokens, HEAD_DIM), low),
        jax.ShapeDtypeStruct((tokens, columns), low), jax.ShapeDtypeStruct((8, columns), jnp.float32)), in_specs=[tile(columns), tile(HEAD_DIM),
        pl.BlockSpec((1, *table.shape[1:]), lambda i: (i, 0, 0))], out_specs=[tile(HEAD_DIM), tile(columns), pl.BlockSpec((8, columns), lambda i: (0,
        0))], scratch_shapes=[pltpu.VMEM((length, HEAD_DIM), low), pltpu.VMEM((length, HEAD_DIM), low), pltpu.VMEM((length, length), low),
        pltpu.VMEM((length, length), low), pltpu.VMEM((length, table.shape[1]), jnp.float32)],
        compiler_params=pltpu.CompilerParams(vmem_limit_bytes=48 * 1024 * 1024), cost_estimate=pl.CostEstimate(flops=14 * pairs * HEAD_DIM,
        transcendentals=pairs, bytes_accessed=tokens * (4 * columns + 4 * HEAD_DIM + 512)), name='attend')(packed, context_grad, table)


def remote(src, dst, send_sem, recv_sem, device):
    return pltpu.make_async_remote_copy(src_ref=src, dst_ref=dst, send_sem=send_sem, recv_sem=recv_sem, device_id=device, device_id_type=MESH)


def copied(src, dst, sem):
    copy = pltpu.make_async_copy(src, dst, sem)
    copy.start()
    return copy


def meet(f, s):
    barrier = pltpu.get_barrier_semaphore()
    for k in range(1, 8):
        pl.semaphore_signal(barrier, inc=1, device_id=((f + k) % 8, s), device_id_type=MESH)
    for k in range(1, 4):
        pl.semaphore_signal(barrier, inc=1, device_id=(f, (s + k) % 4), device_id_type=MESH)
    pl.semaphore_wait(barrier, 10)


def neighbours(f):
    f_x, f_y = (f + 2 - 4 * (f // 2 % 2), f + 4 - 8 * (f // 4))
    return (f_x, f_y, f + 1 - 2 * (f % 2), f_x + f_y - f)


def gather_kernel(x_ref, c_ref, seg_ref, up_ref, qkv_ref, b_up_in, b_qkv_in, norm_in, xg_ref, cg_ref, segs_ref, normed_out, normed_mlp_out,
    packed_out, act_out, slope_out, held, tile, w_up, w_qkv, normed, normed_mlp, packed, act, slope, seg_s, seg_r, seg_l, s1, r1, s2, r2, s3, r3,
    local, w_l, tile_l, keep_l, b_up_ref, b_qkv_ref, norm_ref):
    f, s = (lax.axis_index('fsdp'), lax.axis_index('sp'))
    core = f % 2
    f_x, f_y, f_c, f_d = neighbours(f)
    piece = xg_ref.shape[3]
    meet(f, s)
    pairs = ((x_ref, xg_ref), (c_ref, cg_ref))
    sent = []

    def send(src, dst, send_sem, recv_sem, device):
        copy = remote(src, dst, send_sem, recv_sem, device)
        copy.start()
        sent.append(copy)

    def arrived(ref, recv_sem):
        remote(ref, ref, s1.at[0, 0], recv_sem, (f_c, s)).wait_recv()
    holds = f // 2 == s
    keep_seg = pltpu.make_async_copy(seg_ref, segs_ref.at[core], seg_l.at[0])
    give_seg = [remote(seg_ref, segs_ref.at[core], seg_s.at[k], seg_r.at[core], ((f + k) % 8, s)) for k in range(1, 8)]

    @pl.when(holds)
    def _():
        keep_seg.start()
        for copy in give_seg:
            copy.start()
    weights = [
        pltpu.make_async_copy(ref, held_ref, w_l.at[n])
        for n, (ref, held_ref) in enumerate(
            ((up_ref, w_up), (qkv_ref, w_qkv), (b_up_in, b_up_ref), (b_qkv_in, b_qkv_ref), (norm_in, norm_ref))
        )
    ]
    for copy in weights:
        copy.start()
    kept = []
    for a, (src, _) in enumerate(pairs):
        own = pltpu.make_async_copy(src.at[pl.ds(f * piece, piece)], held.at[a, f], local.at[a, 0])
        own.start()
        kept.append(own)
        for k in range(1, 8):
            j = (f + k) % 8
            send(src.at[pl.ds(j * piece, piece)], held.at[a, f], s1.at[a, k], r1.at[a, k], (j, s))

    def to_planes(a):
        out = pairs[a][1]
        kept[a].wait()
        for k in range(1, 8):
            arrived(held.at[a, (f + 8 - k) % 8], r1.at[a, k])
        for k in range(1, 4):
            plane = (s + k) % 4
            send(held.at[a, pl.ds(2 * plane, 2)], out.at[:, s, f], s2.at[a, k], r2.at[a, k], (f, plane))
        own = pltpu.make_async_copy(held.at[a, pl.ds(2 * s, 2)], out.at[:, s, f], local.at[a, 1])
        own.start()
        return own

    def spread(a, k):
        out = pairs[a][1]
        z = (s + 4 - k) % 4
        if k:
            arrived(out.at[:, z, f], r2.at[a, k])
        ref = out.at[:, z, f]
        send(ref, ref, s3.at[a, 0, k], r3.at[a, 0, k], (f_x, s))
        send(ref, ref, s3.at[a, 1, k], r3.at[a, 1, k], (f_y, s))
        send(ref, ref, s3.at[a, 2, k], r3.at[a, 2, k], (f_c, s))

    def pass_on(a, k):
        out = pairs[a][1]
        z = (s + 4 - k) % 4
        ref = out.at[:, z, f_x]
        arrived(ref, r3.at[a, 0, k])
        send(out.at[0, z, f_x], out.at[0, z, f_x], s3.at[a, 5, k], r3.at[a, 5, k], (f_y, s))
        send(ref, ref, s3.at[a, 3, k], r3.at[a, 3, k], (f_c, s))
        ref = out.at[:, z, f_y]
        arrived(ref, r3.at[a, 1, k])
        send(out.at[1, z, f_y], out.at[1, z, f_y], s3.at[a, 6, k], r3.at[a, 6, k], (f_x, s))
        send(ref, ref, s3.at[a, 4, k], r3.at[a, 4, k], (f_c, s))

    def pass_corner(a, k):
        out = pairs[a][1]
        z = (s + 4 - k) % 4
        for half in range(2):
            ref = out.at[half, z, f_d]
            arrived(ref, r3.at[a, 5 + half, k])
            send(ref, ref, s3.at[a, 7 + half, k], r3.at[a, 7 + half, k], (f_c, s))

    def from_core(a, k):
        out = pairs[a][1]
        z = (s + 4 - k) % 4
        g_x, g_y, _, g_d = neighbours(f_c)
        arrived(out.at[:, z, f_c], r3.at[a, 2, k])
        arrived(out.at[:, z, g_x], r3.at[a, 3, k])
        arrived(out.at[:, z, g_y], r3.at[a, 4, k])
        for half in range(2):
            arrived(out.at[half, z, g_d], r3.at[a, 7 + half, k])
    results = ((normed, normed_out), (normed_mlp, normed_mlp_out), (packed, packed_out), (act, act_out), (slope, slope_out))
    size = 8 * piece

    def keep(b, z, n):
        rows = pl.ds(pl.multiple_of((b * 4 + z) * size, size), size)
        return pltpu.make_async_copy(results[n][0].at[b], results[n][1].at[rows], keep_l.at[b, n])

    tiles = {}

    def work(k, b):
        z = (s + 4 - k) % 4
        if b == 0:
            for half in range(2):
                tiles[half] = copied(xg_ref.at[half, z], tile.at[half], tile_l.at[half])
            if k == 0:
                for copy in weights:
                    copy.wait()
        tiles[b].wait()
        if k:
            for n in range(5):
                keep(b, (s + 5 - k) % 4, n).wait()

        @pl.loop(0, 8)
        def _(i):
            inputs = tile[b, i].astype(jnp.float32)
            centred = inputs - jnp.mean(inputs, axis=-1, keepdims=True)
            variance = jnp.mean(centred * centred, axis=-1, keepdims=True)
            scaled = centred * lax.rsqrt(variance + EPSILON)
            rows = pl.ds(pl.multiple_of(i * piece, piece), piece)
            low = normed.dtype
            normed[b, rows, :] = (scaled * norm_ref[0:1, :] + norm_ref[1:2, :]).astype(low)
            normed_mlp[b, rows, :] = (scaled * norm_ref[2:3, :] + norm_ref[3:4, :]).astype(low)
        hidden = times_transposed(normed_mlp[b], w_up[...]) + b_up_ref[...]
        packed[b] = (times_transposed(normed[b], w_qkv[...]) + b_qkv_ref[...]).astype(packed.dtype)
        activated, grown = gelu_pair(hidden)
        act[b] = activated.astype(act.dtype)
        slope[b] = grown
        for n in range(5):
            keep(b, z, n).start()
    own0 = to_planes(0)
    own1 = to_planes(1)
    steps = [(a, k) for a in range(2) for k in range(4)]
    for i in range(len(steps) + 2):
        if i < len(steps):
            a, k = steps[i]
            if k == 0:
                (own0 if a == 0 else own1).wait()
            spread(a, k)
        if 3 <= i < 7:
            from_core(0, i - 3)
            work(i - 3, 0)
        if 0 <= i - 1 < len(steps):
            pass_on(*steps[i - 1])
        if 0 <= i - 2 < len(steps):
            pass_corner(*steps[i - 2])
        if 3 <= i < 7:
            work(i - 3, 1)
    for k in range(4):
        from_core(1, k)
    for b in range(2):
        for n in range(5):
            keep(b, (s + 1) % 4, n).wait()
    for b in range(2):

        @pl.when(f != 2 * s + b)
        def _():
            arrived(segs_ref.at[b], seg_r.at[b])

    @pl.when(holds)
    def _():
        keep_seg.wait()
        for copy in give_seg:
            copy.wait_send()
    for copy in sent:
        copy.wait_send()


def gather_both(x, c, segments, w_up, w_qkv, b_up, b_qkv, norms):
    rows, width = x.shape
    piece = rows // 8
    tokens = 8 * rows
    units, columns = (w_up.shape[0], w_qkv.shape[0])
    shape = jax.ShapeDtypeStruct((2, 4, 8, piece, width), x.dtype)
    dma = pltpu.SemaphoreType.DMA
    vmem = pltpu.VMEM
    anywhere = pl.BlockSpec(memory_space=pl.ANY)
    sizes = ((width, x.dtype), (width, x.dtype), (columns, x.dtype), (units, x.dtype), (units, jnp.float32))
    return pl.pallas_call(gather_kernel, out_shape=(shape, shape, jax.ShapeDtypeStruct((2, *segments.shape), segments.dtype),
        *(jax.ShapeDtypeStruct((tokens, size), kind) for size, kind in sizes)), in_specs=[anywhere] * 8, out_specs=[anywhere] * 8,
        scratch_shapes=[vmem((2, 8, piece, width), x.dtype), vmem((2, 8, piece, width), x.dtype), vmem(w_up.shape, w_up.dtype), vmem(w_qkv.shape,
        w_qkv.dtype), *(vmem((2, 8 * piece, size), kind) for size, kind in sizes), dma((8,)), dma((2,)), dma((1,)), dma((2, 8)), dma((2, 8)), dma((2,
        4)), dma((2, 4)), dma((2, 9, 4)), dma((2, 9, 4)), dma((2, 2)), dma((5,)), dma((2,)), dma((2, 5)),
        vmem((1, units), jnp.float32), vmem((1, columns), jnp.float32), vmem(norms.shape, jnp.float32)],
        compiler_params=pltpu.CompilerParams(collective_id=1, has_side_effects=True, vmem_limit_bytes=60 * 1024 * 1024), name='gather_tokens')(x, c,
        segments, w_up, w_qkv, b_up.reshape(1, units), b_qkv.reshape(1, columns), norms)


def finish_kernel(down_ref, dense_ref, hidden_ref, normed_mlp_ref, packed_ref, normed_ref, act_ref, context_ref, up_w_ref, down_w_ref, qkv_w_ref,
    dense_w_ref, norm_ref, h_col_ref, p_col_ref, bias_ref, g_down, g_up, g_qkv, g_dense, o_out, o_back, part, paired, kept, crossed, homed, o_small,
    line_a, line_b, turned, big, hidden, packed, weight, qkv_w, dense_w, context, act, total, made, own, right, vecs, vec_out, vec_in, small,
    small_in, load_l, act_l, part_l, tile_s, tile_r, tile_l, left_l, right_l, in_s, in_r, mid_s, mid_r, end_s, end_r, own_l, keep_l, turn_s, turn_r,
    cross_s, cross_r, home_s, home_r, back_s, back_r, local, vec_s, vec_r, small_s, small_r):
    f, s = (lax.axis_index('fsdp'), lax.axis_index('sp'))
    core = f % 2
    f_x, f_y, f_c, f_d = neighbours(f)
    is_end = (s == 0) | (s == 3)
    is_mid = (s == 1) | (s == 2)
    inner, outer, facing = (1 + s // 3, 3 * (s // 2), 3 - s)
    unit = made.shape[3]
    size = 8 * unit
    low = made.dtype
    meet(f, s)
    sent = []

    def send(src, dst, send_sem, recv_sem, device):
        copy = remote(src, dst, send_sem, recv_sem, device)
        copy.start()
        return copy

    def arrived(ref, recv_sem):
        remote(ref, ref, vec_s.at[0], recv_sem, (f_c, s)).wait_recv()
    chunks = []
    at = 0
    groups = {}
    for name, ref, first, result in (('down', down_ref, 0, g_down), ('up', part, 0, g_up), ('qkv', part, g_up.shape[0], g_qkv), ('dense', turned, 0,
        g_dense)):
        for g in range(result.shape[0]):
            cuts = (4,)
            if not chunks:
                cuts = (1, 1, 2)
            if name == 'dense':
                cuts = (2, 1, 1)
            start = 0
            for pairs_of in cuts:
                chunks.append((ref, first + g, result, g, start, pairs_of, at))
                groups[len(chunks) - 1] = (name, first + g)
                start += pairs_of
            at += 1
    count = len(chunks)
    ahead = 4

    def cut(ref, g, k):
        _, _, _, _, start, pairs_of, _ = chunks[k]
        return ref.at[g, pl.ds(start, pairs_of)]

    def source(k):
        return cut(chunks[k][0], chunks[k][1], k)

    def goal(k):
        return cut(chunks[k][2], chunks[k][3], k)

    def from_end(k):
        return remote(source(k), cut(line_a, chunks[k][6], k), in_s.at[k], in_r.at[k], (f, inner))

    def across(k):
        return remote(cut(line_a, chunks[k][6], k), cut(line_b, chunks[k][6], k), mid_s.at[k], mid_r.at[k], (f, facing))

    def to_end(k):
        return remote(cut(line_b, chunks[k][6], k), goal(k), end_s.at[k], end_r.at[k], (f, outer))

    def load_own(k):
        return pltpu.make_async_copy(source(k), cut(own, k % 2, k), own_l.at[k % 2])

    def keep(k):
        return pltpu.make_async_copy(cut(line_b, chunks[k][6], k), goal(k), keep_l.at[k])

    def add_units(target, others, number):
        @pl.loop(0, number)
        def _(i):
            for half in range(2):
                rows = pl.ds(half * (unit // 2), unit // 2)
                value = target[i // 2, i % 2, rows, :].astype(jnp.float32)
                for other in others:
                    value = value + other[i // 2, i % 2, rows, :].astype(jnp.float32)
                target[i // 2, i % 2, rows, :] = value.astype(low)

    def mid_in(k):
        load_own(k).wait()
        from_end(k).wait_recv()
        add_units(cut(line_a, chunks[k][6], k), [cut(own, k % 2, k)], 2 * chunks[k][5])
        across(k).start()
        if k + 2 < count:
            load_own(k + 2).start()

    def mid_out(k):
        across(k).wait_recv()
        add_units(cut(line_b, chunks[k][6], k), [cut(line_a, chunks[k][6], k)], 2 * chunks[k][5])
        to_end(k).start()
        keep(k).start()
    coming = {'big': copied(normed_mlp_ref, big, load_l.at[0]), 'hidden': copied(hidden_ref, hidden, load_l.at[1]), 'weight': copied(up_w_ref,
        weight, load_l.at[2]), 'packed': copied(packed_ref, packed, load_l.at[3]), 'qkv': copied(qkv_w_ref, qkv_w, load_l.at[4]),
        'dense': copied(dense_w_ref, dense_w, load_l.at[5]), 'context': copied(context_ref, context, load_l.at[6])}

    def ready(*names):
        for name in names:
            if coming[name] is not None:
                coming[name].wait()
                coming[name] = None
    span = dense_ref.shape[4]
    columns = pl.ds(pl.multiple_of(f * span, span), span)
    turn_own = copied(dense_ref.at[f], turned.at[0, :, :, :, columns], local.at[0])
    bias_own = copied(bias_ref, small.at[pl.ds(8, 8)], local.at[1])
    vecs[...] = jnp.zeros_like(vecs)
    vec_out[...] = jnp.zeros_like(vec_out)
    busy = {0: [], 1: []}
    turns = [0]

    def next_made():
        slot = turns[0] % 2
        turns[0] += 1
        for wait in busy[slot]:
            wait()
        busy[slot] = []
        return slot
    stores = {}

    def finish_group(g, weights, first, column_ref, which):
        slot = next_made()

        @pl.loop(0, 8)
        def _(i):
            rows = pl.ds(pl.multiple_of(i * unit, unit), unit)
            wide = pl.ds(pl.multiple_of(first + i * unit, unit), unit)
            value = total[rows, :]
            made[slot, i // 2, i % 2] = value.astype(low)
            line = weights[wide, :].astype(jnp.float32)
            sums = column_ref[wide, 0:1]
            scaled = line * (value - sums * norm_ref[2 * which + 1:2 * which + 2, :])
            vecs[2 * which] += eight_rows(scaled)
            vecs[2 * which + 1] += eight_rows(line * sums)
        stores[g] = copied(made.at[slot], part.at[g], part_l.at[g])
        busy[slot] = [functools.partial(stored, g)]

    def stored(g):
        if stores[g] is not None:
            stores[g].wait()
            stores[g] = None

    def up_group(g):
        ready('big', 'hidden', 'weight')
        total[...] = contract_rows(hidden[:, g * size:(g + 1) * size], big[...].reshape(hidden.shape[0], -1))
        finish_group(g, weight, g * size, h_col_ref, 1)
        if g == g_up.shape[0] - 1:
            coming['big'] = copied(normed_ref, big, load_l.at[7])
            coming['weight'] = copied(down_w_ref, weight, load_l.at[8])
            load_act(0)

    def qkv_group(g):
        ready('big', 'packed', 'qkv')
        total[...] = contract_rows(packed[:, g * size:(g + 1) * size], big[...].reshape(hidden.shape[0], -1))
        finish_group(g_up.shape[0] + g, qkv_w, g * size, p_col_ref, 0)

    def load_act(t):
        coming['act', t] = copied(act_ref.at[pl.ds(t * size, size)], act.at[t % 2], act_l.at[t % 2])

    def give_tile(a, t, value):
        b, z = (t // 4, t % 4)
        slot = next_made()
        made[slot] = value.astype(low).reshape(4, 2, unit, value.shape[1])
        give = send(made.at[slot, :, 1 - core], paired.at[a, :, z, b], tile_s.at[a, t], tile_r.at[a, t], (f_c, s))
        hold = copied(made.at[slot, :, core], kept.at[a, :, z, b], tile_l.at[a, t])
        busy[slot] = [give.wait_send, hold.wait]

    def out_tile(t):
        ready('weight', 'context', 'dense', ('act', t))
        if t < 7:
            load_act(t + 1)
        rows = slice(t * size, (t + 1) * size)
        value = times_transposed(context[rows, :], dense_w[...]) + times(act[t % 2], weight[...])
        give_tile(0, t, value)
        if t == 7:
            coming['weight'] = copied(up_w_ref, weight, load_l.at[9])

    def back_tile(t):
        ready('weight', 'packed', 'qkv', 'hidden')
        rows = slice(t * size, (t + 1) * size)
        value = times(packed[rows, :], qkv_w[...]) * norm_ref[0:1, :]
        value = value + times(hidden[rows, :], weight[...]) * norm_ref[2:3, :]
        give_tile(1, t, value)
    results = (o_out, o_back)
    order = (f_d // 2, f_x // 2, f_y // 2, f // 2)
    homes = {}

    def free(slot):
        for wait in busy[slot]:
            wait()
        busy[slot] = []

    def tiles_here(a):
        for slot in range(2):
            free(slot)
        for t in range(8):
            arrived(paired.at[a, :, t % 4, t // 4], tile_r.at[a, t])

    def add_pair(a, n):
        if n == 0:
            tiles_here(a)
        left = big.at[3 * a + n]
        slot = n % 2
        first = copied(paired.at[a, order[n]], left, left_l.at[slot])
        second = copied(kept.at[a, order[n]], right.at[slot], right_l.at[slot])
        first.wait()
        second.wait()
        add_units(left, [right.at[slot]], 8)
        sent.append(send(left, crossed.at[a, n], cross_s.at[a, n], cross_r.at[a, n], ((f_d, f_x, f_y)[n], s)))

    def add_chips(a):
        left = big.at[6 + a]
        copies = [copied(paired.at[a, order[3]], left, left_l.at[0]), copied(kept.at[a, order[3]], right.at[0], right_l.at[0])]
        for n in range(3):
            arrived(crossed.at[a, n], cross_r.at[a, n])
            slot = (n + 1) % 2
            more = copied(crossed.at[a, n], right.at[slot], right_l.at[slot])
            for copy in copies:
                copy.wait()
            add_units(left, [right.at[1 - slot]], 8)
            copies = [more]
        copies[0].wait()
        add_units(left, [right.at[1]], 8)
        for k in range(1, 4):
            z = (s + k) % 4
            sent.append(send(left.at[z], homed.at[a, s], home_s.at[a, k], home_r.at[a, k], (f, z)))
        homes['own', a] = copied(left.at[s], homed.at[a, s], local.at[2 + a])


    def go_home(a):
        homes['own', a].wait()
        for k in range(1, 4):
            arrived(homed.at[a, (s + 4 - k) % 4], home_r.at[a, k])
        for k in range(1, 8):
            j = (f + k) % 8
            sent.append(send(homed.at[a, j // 2, j % 2], results[a].at[f], back_s.at[a, k], back_r.at[a, k], (j, s)))
        homes[a] = copied(homed.at[a, f // 2, core], results[a].at[f], local.at[4 + a])

    def give_vectors():
        for which in range(2):
            gain = norm_ref[2 * which:2 * which + 1, :]
            scaled = jnp.sum(vecs[2 * which], axis=0, keepdims=True) / gain
            plain = jnp.sum(vecs[2 * which + 1], axis=0, keepdims=True)
            for j in range(8):
                part_of = slice(j * span, (j + 1) * span)
                vec_out[j, 2 * which:2 * which + 1, :] = scaled[:, part_of]
                vec_out[j, 2 * which + 1:2 * which + 2, :] = plain[:, part_of]
        for k in range(1, 8):
            j = (f + k) % 8
            sent.append(send(vec_out.at[j], vec_in.at[f], vec_s.at[k], vec_r.at[k], (j, s)))
        homes['vec'] = copied(vec_out.at[f], vec_in.at[f], local.at[6])

    def add_vectors():
        homes['vec'].wait()
        bias_own.wait()
        for k in range(1, 8):
            arrived(vec_in.at[(f + 8 - k) % 8], vec_r.at[k])
        value = vec_in[0]
        for j in range(1, 8):
            value = value + vec_in[j]
        small[0:8, :] = value
        for k in range(1, 4):
            sent.append(send(small, small_in.at[s], small_s.at[k], small_r.at[k], (f, (s + k) % 4)))
        homes['small'] = copied(small, small_in.at[s], local.at[7])

    def add_small():
        homes['small'].wait()
        for k in range(1, 4):
            arrived(small_in.at[(s + 4 - k) % 4], small_r.at[k])
        value = small_in[0]
        for z in range(1, 4):
            value = value + small_in[z]
        o_small[...] = value

    def turn_start():
        for k in range(1, 8):
            j = (f + k) % 8
            sent.append(send(dense_ref.at[j], turned.at[0, :, :, :, columns], turn_s.at[k], turn_r.at[k], (j, s)))

    def turn_done():
        turn_own.wait()
        for k in range(1, 8):
            j = (f + 8 - k) % 8
            there = pl.ds(pl.multiple_of(j * span, span), span)
            arrived(turned.at[0, :, :, :, there], turn_r.at[k])

    def task(name, i):
        if name == 'turn':
            turn_start()
        elif name == 'turned':
            turn_done()
        elif name == 'up':
            up_group(i)
        elif name == 'qkv':
            qkv_group(i)
        elif name == 'out':
            out_tile(i)
        elif name == 'back':
            back_tile(i)
        elif name == 'pair':
            add_pair(i // 3, i % 3)
        elif name == 'chips':
            add_chips(i)
        elif name == 'home':
            go_home(i)
        elif name == 'vectors':
            give_vectors()
        elif name == 'sums':
            add_vectors()
        else:
            add_small()

    @pl.when(is_end)
    def _():
        for k in range(ahead):
            from_end(k).start()

    @pl.when(is_mid)
    def _():
        for k in range(2):
            load_own(k).start()
    for k in range(count + 2):
        for name, first, last in FINISH_STEPS[k] if k in FINISH_STEPS else ():
            for i in range(first, last):
                task(name, i)
        if k + ahead - 1 in groups and groups[k + ahead - 1][0] in ('up', 'qkv'):
            stored(groups[k + ahead - 1][1])

        @pl.when(is_mid)
        def _():
            if k < count:
                mid_in(k)
            if 1 <= k <= count:
                mid_out(k - 1)

        @pl.when(is_end)
        def _():
            if 1 <= k <= count:
                to_end(k - 1).wait_recv()
                if k - 1 + ahead < count:
                    from_end(k - 1 + ahead).start()
    for a in range(2):
        homes[a].wait()
        for k in range(1, 8):
            arrived(results[a].at[(f + 8 - k) % 8], back_r.at[a, k])
    for slot in range(2):
        free(slot)
    for copy in sent:
        copy.wait_send()

    @pl.when(is_end)
    def _():
        for k in range(count):
            from_end(k).wait_send()

    @pl.when(is_mid)
    def _():
        for k in range(count):
            across(k).wait_send()
            to_end(k).wait_send()
            keep(k).wait()


FINISH_STEPS = {
    0: (("turn", 0, 1),),
    1: (("up", 0, 1),),
    2: (("up", 1, 2),),
    3: (("up", 2, 4),),
    4: (("qkv", 0, 3),),
    5: (("out", 0, 8),),
    6: (("pair", 0, 3), ("back", 0, 3)),
    7: (("back", 3, 6), ("turned", 0, 1)),
    8: (("back", 6, 8), ("vectors", 0, 1), ("pair", 3, 6)),
    9: (("chips", 0, 1),),
    10: (("sums", 0, 1),),
    11: (("home", 0, 1), ("chips", 1, 2)),
    12: (("small", 0, 1),),
    14: (("home", 1, 2),),
}


def finish(down, dense, hidden_grad, normed_mlp, packed_grad, normed, act, context, w_up, w_down, w_qkv, dense_in, norms, h_sums, p_sums, bias):
    width = down.shape[1]
    tokens = hidden_grad.shape[0]
    low = down.dtype
    unit = tokens // 64
    size = 8 * unit
    span = width // 8

    def grouped(rows):
        return (rows // size, 4, 2, unit, width)

    def columns(sums):
        return jnp.broadcast_to(sums[:, None], (sums.shape[0], 128))
    sets = [w.shape[0] // size for w in (down, w_up, w_qkv)]
    number = sum(sets) + 1
    count = sum(sets) + 5
    sums = [jax.ShapeDtypeStruct(grouped(n * size), low) for n in (*sets, 1)]
    token = jax.ShapeDtypeStruct((8, unit, width), low)
    halves = jax.ShapeDtypeStruct((2, 4, 4, 2, unit, width), low)
    others = [jax.ShapeDtypeStruct(grouped((sets[1] + sets[2]) * size), low), halves, halves, jax.ShapeDtypeStruct((2, 3, 4, 2, unit, width), low),
        jax.ShapeDtypeStruct((2, 4, 2, unit, width), low)]
    dma = pltpu.SemaphoreType.DMA
    vmem = pltpu.VMEM
    anywhere = pl.BlockSpec(memory_space=pl.ANY)
    inside = pl.BlockSpec(memory_space=pltpu.VMEM)
    result = pl.pallas_call(finish_kernel, out_shape=(*sums, token, token, *others, jax.ShapeDtypeStruct((16, span), jnp.float32)),
        in_specs=[anywhere] * 12 + [inside] * 3 + [anywhere], out_specs=[anywhere] * 11 + [inside], scratch_shapes=[vmem((number, 4, 2, unit, width),
        low), vmem((number, 4, 2, unit, width), low), vmem((1, 4, 2, unit, width), low), vmem(grouped(tokens), low), vmem(hidden_grad.shape, low),
        vmem(packed_grad.shape, low), vmem(w_up.shape, low), vmem(w_qkv.shape, low), vmem(dense_in.shape, low), vmem(context.shape, low), vmem((2,
        size, act.shape[1]), low), vmem((size, width), jnp.float32), *(vmem((2, 4, 2, unit, width), low) for _ in range(3)), vmem((4, 8, width),
        jnp.float32), vmem((8, 8, span), jnp.float32), vmem((8, 8, span), jnp.float32), vmem((16, span), jnp.float32), vmem((4, 16, span),
        jnp.float32), dma((10,)), dma((2,)), dma((sets[1] + sets[2],)), dma((2, 8)), dma((2, 8)), dma((2, 8)), dma((2,)), dma((2,)), dma((count,)),
        dma((count,)), dma((count,)), dma((count,)), dma((count,)), dma((count,)), dma((2,)), dma((count,)), dma((8,)), dma((8,)), dma((2, 3)),
        dma((2, 3)), dma((2, 4)), dma((2, 4)), dma((2, 8)), dma((2, 8)), dma((8,)), dma((8,)), dma((8,)), dma((4,)), dma((4,))],
        compiler_params=pltpu.CompilerParams(collective_id=2, has_side_effects=True, vmem_limit_bytes=60 * 1024 * 1024),
        name='finish')(down.reshape(grouped(down.shape[0])), dense.reshape(8, 4, 2, unit, span), hidden_grad, normed_mlp.reshape(grouped(tokens)), packed_grad, normed.reshape(grouped(tokens)), act,
        context, w_up, w_down, w_qkv, dense_in, norms, columns(h_sums), columns(p_sums), bias)
    grads = [grad.reshape(-1, width) for grad in result[:4]]
    return (grads, result[4], result[5], result[11])


def last_kernel(
    x_ref, c_ref, out_ref, back_ref, shift_ref, early_ref, late_ref, up_ref, qkv_ref, dense_ref,
    output, input_grad, down_out, up_out, qkv_out, dense_out,
):
    inputs = x_ref[...].astype(jnp.float32)
    output[...] = (inputs + (out_ref[...].astype(jnp.float32) + shift_ref[...])).astype(output.dtype)
    centred = inputs - jnp.mean(inputs, axis=-1, keepdims=True)
    inverse = lax.rsqrt(jnp.mean(centred * centred, axis=-1, keepdims=True) + EPSILON)
    scaled = centred * inverse
    weighted = back_ref[...].astype(jnp.float32)
    first_mean = jnp.mean(weighted, axis=-1, keepdims=True)
    second_mean = jnp.mean(weighted * scaled, axis=-1, keepdims=True)
    change = inverse * (weighted - first_mean - scaled * second_mean)
    input_grad[...] = (c_ref[...].astype(jnp.float32) + change).astype(input_grad.dtype)
    down_out[0] = early_ref[...].astype(jnp.float32)
    down_out[1] = late_ref[...].astype(jnp.float32)
    for ref, out in ((up_ref, up_out), (qkv_ref, qkv_out), (dense_ref, dense_out)):
        out[...] = ref[...].astype(jnp.float32)


def last(x, c, out, back, shift, early, late, up, qkv, dense, steps=8):
    width = up.shape[1]

    def tile(array):
        return pl.BlockSpec((array.shape[0] // steps, width), lambda i: (i, 0))

    tokens, sums = (x, c, out, back), (early, late, up, qkv, dense)
    wide = jax.ShapeDtypeStruct((2, early.shape[0], width), jnp.float32)
    number = 2 * early.size + up.size + qkv.size + dense.size
    output, input_grad, down, up, qkv, dense = pl.pallas_call(
        last_kernel,
        grid=(steps,),
        out_shape=(
            jax.ShapeDtypeStruct(x.shape, x.dtype), jax.ShapeDtypeStruct(x.shape, x.dtype), wide,
            *(jax.ShapeDtypeStruct(array.shape, jnp.float32) for array in sums[2:]),
        ),
        in_specs=[tile(array) for array in tokens] + [pl.BlockSpec((1, width), lambda i: (0, 0))] + [tile(array) for array in sums],
        out_specs=[
            tile(x), tile(x), pl.BlockSpec((2, early.shape[0] // steps, width), lambda i: (0, i, 0)),
            *(tile(array) for array in sums[2:]),
        ],
        compiler_params=pltpu.CompilerParams(vmem_limit_bytes=60 * 1024 * 1024),
        cost_estimate=pl.CostEstimate(flops=20 * x.size, transcendentals=0, bytes_accessed=6 * number + 12 * x.size),
        name="last",
    )(*tokens, shift.reshape(1, width), *sums)
    return output, input_grad, down.reshape(-1, width), up, qkv, dense


def own_tokens(hidden_in, cotangent, output, weighted, shift):
    inputs = hidden_in.astype(jnp.float32)
    output = (inputs + (output.astype(jnp.float32) + shift)).astype(jnp.bfloat16)
    scaled, inverse = norm_scaled(inputs)
    weighted = weighted.astype(jnp.float32)
    first_mean = jnp.mean(weighted, axis=-1, keepdims=True)
    second_mean = jnp.mean(weighted * scaled, axis=-1, keepdims=True)
    input_grad = (cotangent.astype(jnp.float32) + inverse * (weighted - first_mean - scaled * second_mean)).astype(jnp.bfloat16)
    return (output, input_grad)


def by_collectives(hidden_in, segments, ln1_gain, ln1_bias, ln2_gain, ln2_bias, w_qkv, b_qkv, w_dense, b_dense, w_up, b_up, w_down, b_down,
    cotangent):
    seq_local, shard_len, width = hidden_in.shape
    seq_len = segments.shape[1]
    nf, ns = (lax.axis_size('fsdp'), lax.axis_size('sp'))
    f_place, s_place = (lax.axis_index('fsdp'), lax.axis_index('sp'))
    seqs = seq_local * nf
    group = seqs // ns
    piece = shard_len // nf
    tokens = group * seq_len
    per_head = max(1, nf // HEADS)
    head_count = max(1, HEADS // nf)
    head_sets = [[head * per_head + k for k in range(per_head)] for head in range(nf // per_head)]

    def gather_tokens(block):
        part = lax.all_to_all(block, 'fsdp', split_axis=1, concat_axis=0, tiled=True)
        part = lax.all_to_all(part, 'sp', split_axis=0, concat_axis=1, tiled=True)
        return in_order(lax.all_gather(part, 'fsdp', axis=0, tiled=True)).reshape(tokens, width)

    def scatter_tokens(partial):
        part = out_of_order(partial).reshape(nf * group, ns * piece, width)
        part = lax.psum_scatter(part, 'fsdp', scatter_dimension=0, tiled=True)
        part = lax.all_to_all(part, 'sp', split_axis=1, concat_axis=0, tiled=True)
        return lax.all_to_all(part, 'fsdp', split_axis=0, concat_axis=1, tiled=True)

    def in_order(array):
        array = array.reshape(nf, group, ns, piece, -1)
        return array.transpose(1, 2, 0, 3, 4).reshape(group, seq_len, -1)

    def out_of_order(array):
        array = array.reshape(group, ns, nf, piece, -1)
        return array.transpose(2, 0, 1, 3, 4).reshape(tokens, -1)

    def over_head(array, axis):
        if per_head == 1:
            return array
        return lax.all_gather(array, 'fsdp', axis=axis, tiled=True, axis_index_groups=head_sets)

    def own_columns(array):
        if per_head == 1:
            return array
        share = array.shape[-1] // per_head
        return lax.dynamic_slice_in_dim(array, f_place % per_head * share, share, array.ndim - 1)

    def own_part(vector):
        share = vector.shape[0] // nf
        return lax.dynamic_slice_in_dim(vector, f_place * share, share, 0)
    gathered, upstream = (gather_tokens(hidden_in), gather_tokens(cotangent))
    rows = lax.all_gather(segments, 'fsdp', axis=0, tiled=True)
    rows = lax.dynamic_slice_in_dim(rows, s_place * group, group, 0)
    dense_in = lax.all_to_all(w_dense, 'fsdp', split_axis=1, concat_axis=0, tiled=True)
    head_qkv = over_head(w_qkv, 0)
    head_dense = over_head(dense_in, 1)
    head_bias = lax.dynamic_slice_in_dim(b_qkv, f_place // per_head * head_qkv.shape[0], head_qkv.shape[0], 0)
    scaled, _ = norm_scaled(gathered.astype(jnp.float32))
    normed = (scaled * ln1_gain + ln1_bias).astype(jnp.bfloat16)
    normed_mlp = (scaled * ln2_gain + ln2_bias).astype(jnp.bfloat16)
    hidden = times_transposed(normed_mlp, w_up) + own_part(b_up)
    activated, slope = gelu_pair(hidden)
    activated = activated.astype(jnp.bfloat16)
    down_term = contract_rows(activated, upstream).astype(jnp.bfloat16)
    grad_down_w = lax.psum(down_term, 'sp').astype(jnp.float32)
    hidden_grad = (times_transposed(upstream, w_down) * slope).astype(jnp.bfloat16)
    up_term = contract_rows(hidden_grad, normed_mlp)
    mlp_norm_grad = times(hidden_grad, w_up)
    packed = (times_transposed(normed, head_qkv) + head_bias).astype(jnp.bfloat16)
    packed = packed.reshape(group, seq_len, head_count, 3 * HEAD_DIM)
    cos_table, sin_table = rotary_tables(rows)
    queries = rotate(packed[..., :HEAD_DIM].astype(jnp.float32), cos_table, sin_table).astype(jnp.bfloat16)
    keys_rot = rotate(packed[..., HEAD_DIM:2 * HEAD_DIM].astype(jnp.float32), cos_table, sin_table).astype(jnp.bfloat16)
    values = packed[..., 2 * HEAD_DIM:]
    mask = build_mask(rows)
    context, log_total = attend_forward(queries, keys_rot, values, mask)
    context = own_columns(context.reshape(tokens, -1))
    partial_out = times_transposed(context, dense_in) + times(activated, w_down)
    context_grad = times(upstream, head_dense).astype(jnp.bfloat16).reshape(group, seq_len, head_count, HEAD_DIM)
    query_grad, key_grad, value_grad = attend_backward(queries, keys_rot, values, mask, log_total, context_grad)
    packed_grad = jnp.concatenate([unrotate(query_grad, cos_table, sin_table), unrotate(key_grad, cos_table, sin_table), value_grad],
        axis=-1).astype(jnp.bfloat16)
    packed_grad = own_columns(packed_grad.reshape(tokens, -1))
    attn_norm_grad = times(packed_grad, w_qkv)
    qkv_term = contract_rows(packed_grad, normed)
    dense_term = contract_rows(upstream, context).astype(jnp.bfloat16)
    partial_back = attn_norm_grad * ln1_gain + mlp_norm_grad * ln2_gain
    vectors = jnp.stack([jnp.sum(attn_norm_grad * scaled, axis=0), jnp.sum(attn_norm_grad, axis=0), jnp.sum(mlp_norm_grad * scaled, axis=0),
        jnp.sum(mlp_norm_grad, axis=0)])
    bias_out = own_part(jnp.sum(upstream.astype(jnp.float32), axis=0))
    bias_qkv = jnp.sum(packed_grad.astype(jnp.float32), axis=0)
    bias_up = jnp.sum(hidden_grad.astype(jnp.float32), axis=0)
    vectors = lax.psum_scatter(vectors, 'fsdp', scatter_dimension=1, tiled=True)
    vectors, bias_out, bias_qkv, bias_up = lax.psum((vectors, bias_out, bias_qkv, bias_up), 'sp')
    output = scatter_tokens(rounded(partial_out))
    weighted = scatter_tokens(rounded(partial_back))
    dense_term = lax.all_to_all(dense_term, 'fsdp', split_axis=0, concat_axis=1, tiled=True)
    grad_up_w, grad_qkv_w, grad_dense_w = (lax.psum(term.astype(jnp.bfloat16), 'sp').astype(jnp.float32) for term in (up_term, qkv_term, dense_term))
    output, input_grad = own_tokens(hidden_in, cotangent, output, weighted, b_dense + b_down)
    return (output, input_grad, vectors[0], vectors[1], vectors[2], vectors[3], grad_qkv_w, bias_qkv, grad_dense_w, bias_out, grad_up_w, bias_up,
        grad_down_w, bias_out)


def by_kernels(hidden_in, segments, ln1_gain, ln1_bias, ln2_gain, ln2_bias, w_qkv, b_qkv, w_dense, b_dense, w_up, b_up, w_down, b_down, cotangent):
    width = hidden_in.shape[2]
    seq_len = segments.shape[1]
    nf, ns = (lax.axis_size('fsdp'), lax.axis_size('sp'))
    group = nf // ns
    tokens = group * seq_len
    share = width // nf
    f_place = lax.axis_index('fsdp')

    def own_part(vector):
        size = vector.shape[0] // nf
        return lax.dynamic_slice_in_dim(vector, f_place * size, size, 0)
    norms = jnp.stack([ln1_gain, ln1_bias, ln2_gain, ln2_bias])
    _, upstream, rows, normed, normed_mlp, packed, activated, slope = gather_both(hidden_in[0], cotangent[0], segments.reshape(8, seq_len // 8),
        w_up, w_qkv, own_part(b_up), own_part(b_qkv), norms)
    upstream = upstream.reshape(tokens, width)
    w_dense, upstream = lax.optimization_barrier((w_dense, upstream))
    dense_in = lax.all_to_all(w_dense, 'fsdp', split_axis=1, concat_axis=0, tiled=True)
    early = activated.shape[1] // 2
    down_term = contract_rows(activated[:, :early], upstream).astype(jnp.bfloat16)
    early_down_w = lax.psum(down_term, 'sp')
    slope, activated, down_term = lax.optimization_barrier((slope, activated, down_term))
    hidden_grad, context_grad, c_sums, h_sums = upstream_parts(upstream, slope, w_down, dense_in)
    context, packed_grad, p_sums = attend(packed, context_grad, head_tables(rows.reshape(group, seq_len)), seq_len)
    late_down_term = contract_rows(activated[:, early:], upstream).astype(jnp.bfloat16)
    dense_term = contract_rows(upstream, context).astype(jnp.bfloat16)
    bias_up, bias_qkv = (jnp.sum(h_sums, axis=0), jnp.sum(p_sums, axis=0))
    bias_out = own_part(jnp.sum(c_sums, axis=0))
    grads, output, weighted, sums = finish(late_down_term, dense_term, hidden_grad, normed_mlp, packed_grad, normed, activated, context, w_up,
        w_down, w_qkv, dense_in, norms, bias_up, bias_qkv, jnp.concatenate([bias_out, bias_qkv, bias_up]).reshape(8, share))
    output, input_grad, grad_down_w, grad_up_w, grad_qkv_w, grad_dense_w = last(
        hidden_in[0], cotangent[0], output.reshape(-1, width), weighted.reshape(-1, width), b_dense + b_down, early_down_w, *grads
    )
    output, input_grad = output[None], input_grad[None]
    bias_out = sums[8]
    return (output, input_grad, sums[0], sums[1], sums[2], sums[3], grad_qkv_w, sums[9:12].reshape(-1), grad_dense_w, bias_out, grad_up_w,
        sums[12:16].reshape(-1), grad_down_w, bias_out)


def per_device(hidden_in, *rest):
    sizes = (lax.axis_size('fsdp'), lax.axis_size('sp'), hidden_in.shape[0])
    shapes = (hidden_in.shape[1] % 256, hidden_in.shape[2] % (8 * HEAD_DIM), rest[9].shape[0] % 256)
    if sizes == (8, 4, 1) and HEADS == 8 and (not any(shapes)):
        return by_kernels(hidden_in, *rest)
    return by_collectives(hidden_in, *rest)


def solution(mesh):
    rows = P('fsdp', 'sp', None)
    first = P('fsdp', None)
    return jax.shard_map(per_device, mesh=mesh, in_specs=(rows, first, P(), P(), P(), P(), first, P(), first, P(), first, P(), first, P(), rows),
        out_specs=(rows, rows, P('fsdp'), P('fsdp'), P('fsdp'), P('fsdp'), first, P('fsdp'), first, P('fsdp'), first, P('fsdp'), first, P('fsdp')),
        check_vma=False)
```

```python
import functools
import math

import jax
import jax.numpy as jnp
from jax import lax
from jax.experimental import pallas as pl
from jax.experimental.pallas import tpu as pltpu
from jax.sharding import PartitionSpec as P

MESH = pl.DeviceIdType.MESH

HEADS = 8
HEAD_DIM = 256
ROT = 64


EPSILON = 1e-05
NEGATIVE = -1e30
ROOT_HALF = 0.7071067811865476
ROOT_TWO_PI = 2.5066282746310002
SCALE = 1.0 / math.sqrt(HEAD_DIM)


def rounded(array):
    return lax.reduce_precision(array.astype(jnp.float32), 8, 7).astype(jnp.bfloat16)


def contract_rows(former, latter):
    return lax.dot_general(former, latter, (((0,), (0,)), ((), ())), preferred_element_type=jnp.float32)


def times_transposed(former, latter):
    return lax.dot_general(former, latter, (((1,), (1,)), ((), ())), preferred_element_type=jnp.float32)


def times(former, latter):
    return jnp.dot(former, latter, preferred_element_type=jnp.float32)


def norm_scaled(inputs):
    average = jnp.mean(inputs, axis=-1, keepdims=True)
    centred = inputs - average
    variance = jnp.mean(centred * centred, axis=-1, keepdims=True)
    inverse = lax.rsqrt(variance + EPSILON)
    return (centred * inverse, inverse)


def gelu_pair(hidden):
    cumulative = 0.5 * (1.0 + lax.erf(hidden * ROOT_HALF))
    return (hidden * cumulative, cumulative + hidden * (jnp.exp(-0.5 * hidden * hidden) * (1.0 / ROOT_TWO_PI)))


def document_starts(segment_rows):
    places = jnp.arange(segment_rows.shape[-1], dtype=jnp.int32)
    changes = jnp.concatenate([jnp.ones_like(segment_rows[..., :1]), (segment_rows[..., 1:] != segment_rows[..., :-1]).astype(jnp.int32)], axis=-1)
    return (places, lax.cummax(changes * places, axis=segment_rows.ndim - 1))


def frequencies():
    return 1.0 / jnp.power(10000.0, jnp.arange(0, ROT, 2).astype(jnp.float32) / ROT)


def rotary_tables(segment_rows):
    places, starts = document_starts(segment_rows)
    angles = (places - starts).astype(jnp.float32)[..., None] * frequencies()
    angles = jnp.concatenate([angles, angles], axis=-1)
    return (jnp.cos(angles), jnp.sin(angles))


def head_tables(segment_rows):
    smaller = segment_rows[:, :, None] < segment_rows[:, None, :]
    starts = jnp.sum(smaller.astype(jnp.float32), axis=1)
    places = jnp.arange(segment_rows.shape[-1], dtype=jnp.float32)
    angles = (places - starts)[:, None, :] * frequencies()[None, :, None]
    starts = jnp.broadcast_to(starts[:, None, :], (starts.shape[0], ROT, starts.shape[1]))
    return jnp.concatenate([jnp.cos(angles), jnp.sin(angles), starts], axis=1)


def rotate(heads_part, cos_table, sin_table):
    half_rot = ROT // 2
    turned = heads_part[..., :ROT]
    swapped = jnp.concatenate([-turned[..., half_rot:], turned[..., :half_rot]], axis=-1)
    turned = turned * cos_table[..., None, :] + swapped * sin_table[..., None, :]
    return jnp.concatenate([turned, heads_part[..., ROT:]], axis=-1)


def unrotate(grads_part, cos_table, sin_table):
    half_rot = ROT // 2
    turned = grads_part[..., :ROT]
    along_sin = turned * sin_table[..., None, :]
    back_turn = jnp.concatenate([along_sin[..., half_rot:], -along_sin[..., :half_rot]], axis=-1)
    turned = turned * cos_table[..., None, :] + back_turn
    return jnp.concatenate([turned, grads_part[..., ROT:]], axis=-1)


def build_mask(segment_rows):
    places = jnp.arange(segment_rows.shape[-1], dtype=jnp.int32)
    return (segment_rows[:, :, None] == segment_rows[:, None, :]) & (places[None, :] <= places[:, None])


def attention_scores(queries, keys_rot):
    return jnp.einsum('bqhd,bkhd->bhqk', queries, keys_rot, preferred_element_type=jnp.float32) * SCALE


def attend_forward(queries, keys_rot, values, mask):
    scores = jnp.where(mask[:, None], attention_scores(queries, keys_rot), NEGATIVE)
    row_top = jnp.max(scores, axis=-1, keepdims=True)
    exponent = jnp.exp(scores - row_top)
    row_total = jnp.sum(exponent, axis=-1, keepdims=True)
    attention = (exponent / row_total).astype(jnp.bfloat16)
    context = jnp.einsum('bhqk,bkhd->bqhd', attention, values, preferred_element_type=jnp.float32)
    return (context.astype(jnp.bfloat16), row_top + jnp.log(row_total))


def attend_backward(queries, keys_rot, values, mask, log_total, context_grad):
    scores = attention_scores(queries, keys_rot)
    attention = jnp.where(mask[:, None], jnp.exp(scores - log_total), 0.0)
    value_grad = jnp.einsum('bhqk,bqhd->bkhd', attention.astype(jnp.bfloat16), context_grad, preferred_element_type=jnp.float32)
    attention_grad = jnp.einsum('bqhd,bkhd->bhqk', context_grad, values, preferred_element_type=jnp.float32)
    row_centre = jnp.sum(attention * attention_grad, axis=-1, keepdims=True)
    score_grad = (attention * (attention_grad - row_centre)).astype(jnp.bfloat16)
    query_grad = jnp.einsum('bhqk,bkhd->bqhd', score_grad, keys_rot, preferred_element_type=jnp.float32) * SCALE
    key_grad = jnp.einsum('bhqk,bqhd->bkhd', score_grad, queries, preferred_element_type=jnp.float32) * SCALE
    return (query_grad, key_grad, value_grad)


def whole_block(array):
    return pl.BlockSpec(array.shape, lambda *_: (0,) * array.ndim, pipeline_mode=pl.Buffered(1))


def eight_rows(array):
    return jnp.sum(array.reshape(array.shape[0] // 8, 8, array.shape[1]), axis=0)


def upstream_kernel(c_ref, slope_ref, down_ref, dense_ref, grad_ref, context_ref, c_sum_ref, h_sum_ref):
    @pl.when(pl.program_id(0) == 0)
    def _():
        c_sum_ref[...] = jnp.zeros_like(c_sum_ref)
        h_sum_ref[...] = jnp.zeros_like(h_sum_ref)
    hidden_grad = (times_transposed(c_ref[...], down_ref[...]) * slope_ref[...]).astype(grad_ref.dtype)
    grad_ref[...] = hidden_grad
    context_ref[...] = times(c_ref[...], dense_ref[...]).astype(context_ref.dtype)
    c_sum_ref[...] += eight_rows(c_ref[...].astype(jnp.float32))
    h_sum_ref[...] += eight_rows(hidden_grad.astype(jnp.float32))


def upstream_parts(c, slope, w_down, dense, rows=256):
    tokens, width = c.shape
    units, columns = (w_down.shape[0], dense.shape[1])

    def tile(size):
        return pl.BlockSpec((rows, size), lambda i: (i, 0))

    def total(size):
        return pl.BlockSpec((8, size), lambda i: (0, 0))
    return pl.pallas_call(upstream_kernel, grid=(tokens // rows,), out_shape=(jax.ShapeDtypeStruct((tokens, units), c.dtype),
        jax.ShapeDtypeStruct((tokens, columns), c.dtype), jax.ShapeDtypeStruct((8, width), jnp.float32), jax.ShapeDtypeStruct((8, units),
        jnp.float32)), in_specs=[tile(width), tile(units), whole_block(w_down), whole_block(dense)], out_specs=[tile(units), tile(columns),
        total(width), total(units)], compiler_params=pltpu.CompilerParams(vmem_limit_bytes=48 * 1024 * 1024),
        cost_estimate=pl.CostEstimate(flops=2 * tokens * width * (units + columns), transcendentals=0,
        bytes_accessed=2 * tokens * (width + 3 * units + columns) + 2 * width * (units + columns)), name='upstream_parts')(c, slope, w_down, dense)


def attention_kernel(packed_ref, grad_ref, table_ref, context_ref, back_ref, sum_ref, q_ref, k_ref, low_ref, score_ref, turned_ref):
    length = packed_ref.shape[0]
    size = 256
    lanes = 128
    lane = lax.broadcasted_iota(jnp.int32, (size, lanes), 1)
    half = ROT // 2

    def tables(rows):
        table = turned_ref[rows, :]
        cosine = jnp.where(lane < half, table, jnp.where(lane < ROT, pltpu.roll(table, half, 1), 1.0))
        sine = jnp.where(lane < half, pltpu.roll(table, lanes - half, 1), jnp.where(lane < ROT, table, 0.0))
        return (cosine, jnp.where(lane < half, -sine, sine))

    def swapped(array):
        return jnp.where(lane < half, pltpu.roll(array, lanes - half, 1), pltpu.roll(array, half, 1))

    def turn(array, cosine, sine):
        front = array[:, :lanes]
        return jnp.concatenate([front * cosine + swapped(front) * sine, array[:, lanes:]], axis=1)
    blocks = length // size
    for i in range(blocks):
        rows = pl.ds(i * size, size)
        turned_ref[rows, :] = jnp.transpose(table_ref[0, :, rows])
        cosine, sine = tables(rows)
        for part, ref in enumerate((q_ref, k_ref)):
            array = packed_ref[rows, part * HEAD_DIM:(part + 1) * HEAD_DIM].astype(jnp.float32)
            ref[rows, :] = turn(array, cosine, sine).astype(ref.dtype)
    values = pl.ds(2 * HEAD_DIM, HEAD_DIM)
    for i in range(blocks):
        rows = pl.ds(i * size, size)
        reach = (i + 1) * size
        keys = pl.ds(0, reach)
        scores = times_transposed(q_ref[rows, :], k_ref[keys, :]) * SCALE
        gradient = times_transposed(grad_ref[rows, :], packed_ref[keys, values])
        place = lax.broadcasted_iota(jnp.int32, (size, reach), 1)
        query = lax.broadcasted_iota(jnp.int32, (size, reach), 0) + i * size
        start = turned_ref[rows, ROT:ROT + 1].astype(jnp.int32)
        allowed = (place >= start) & (place <= query)
        scores = jnp.where(allowed, scores, NEGATIVE)
        exponent = jnp.exp(scores - jnp.max(scores, axis=-1, keepdims=True))
        attention = exponent / jnp.sum(exponent, axis=-1, keepdims=True)
        low = attention.astype(low_ref.dtype)
        low_ref[rows, keys] = low
        context_ref[rows, :] = times(low, packed_ref[keys, values]).astype(context_ref.dtype)
        centre = jnp.sum(attention * gradient, axis=-1, keepdims=True)
        score_grad = (attention * (gradient - centre)).astype(score_ref.dtype)
        score_ref[rows, keys] = score_grad
        query_grad = times(score_grad, k_ref[keys, :]) * SCALE
        cosine, sine = tables(rows)
        back_ref[rows, :HEAD_DIM] = turn(query_grad, cosine, -sine).astype(back_ref.dtype)
    for j in range(blocks):
        keys = pl.ds(j * size, size)
        rows = pl.ds(j * size, length - j * size)
        key_grad = contract_rows(score_ref[rows, keys], q_ref[rows, :]) * SCALE
        cosine, sine = tables(keys)
        back_ref[keys, HEAD_DIM:2 * HEAD_DIM] = turn(key_grad, cosine, -sine).astype(back_ref.dtype)
        value_grad = contract_rows(low_ref[rows, keys], grad_ref[rows, :])
        back_ref[keys, values] = value_grad.astype(back_ref.dtype)

    @pl.when(pl.program_id(0) == 0)
    def _():
        sum_ref[...] = jnp.zeros_like(sum_ref)
    for i in range(blocks):
        sum_ref[...] += eight_rows(back_ref[pl.ds(i * size, size), :].astype(jnp.float32))


def attend(packed, context_grad, table, length):
    tokens, columns = packed.shape
    low = packed.dtype

    def tile(size):
        return pl.BlockSpec((length, size), lambda i: (i, 0))
    pairs = tokens * (length + 256) // 2
    return pl.pallas_call(attention_kernel, grid=(tokens // length,), out_shape=(jax.ShapeDtypeStruct((tokens, HEAD_DIM), low),
        jax.ShapeDtypeStruct((tokens, columns), low), jax.ShapeDtypeStruct((8, columns), jnp.float32)), in_specs=[tile(columns), tile(HEAD_DIM),
        pl.BlockSpec((1, *table.shape[1:]), lambda i: (i, 0, 0))], out_specs=[tile(HEAD_DIM), tile(columns), pl.BlockSpec((8, columns), lambda i: (0,
        0))], scratch_shapes=[pltpu.VMEM((length, HEAD_DIM), low), pltpu.VMEM((length, HEAD_DIM), low), pltpu.VMEM((length, length), low),
        pltpu.VMEM((length, length), low), pltpu.VMEM((length, table.shape[1]), jnp.float32)],
        compiler_params=pltpu.CompilerParams(vmem_limit_bytes=48 * 1024 * 1024), cost_estimate=pl.CostEstimate(flops=14 * pairs * HEAD_DIM,
        transcendentals=pairs, bytes_accessed=tokens * (4 * columns + 4 * HEAD_DIM + 512)), name='attend')(packed, context_grad, table)


def remote(src, dst, send_sem, recv_sem, device):
    return pltpu.make_async_remote_copy(src_ref=src, dst_ref=dst, send_sem=send_sem, recv_sem=recv_sem, device_id=device, device_id_type=MESH)


def copied(src, dst, sem):
    copy = pltpu.make_async_copy(src, dst, sem)
    copy.start()
    return copy


def meet(f, s):
    barrier = pltpu.get_barrier_semaphore()
    for k in range(1, 8):
        pl.semaphore_signal(barrier, inc=1, device_id=((f + k) % 8, s), device_id_type=MESH)
    for k in range(1, 4):
        pl.semaphore_signal(barrier, inc=1, device_id=(f, (s + k) % 4), device_id_type=MESH)
    pl.semaphore_wait(barrier, 10)


def neighbours(f):
    f_x, f_y = (f + 2 - 4 * (f // 2 % 2), f + 4 - 8 * (f // 4))
    return (f_x, f_y, f + 1 - 2 * (f % 2), f_x + f_y - f)


def gather_kernel(x_ref, c_ref, seg_ref, up_ref, qkv_ref, b_up_in, b_qkv_in, norm_in, xg_ref, cg_ref, segs_ref, normed_out, normed_mlp_out,
    packed_out, act_out, slope_out, held, tile, w_up, w_qkv, normed, normed_mlp, packed, act, slope, seg_s, seg_r, seg_l, s1, r1, s2, r2, s3, r3,
    local, w_l, tile_l, keep_l, b_up_ref, b_qkv_ref, norm_ref):
    f, s = (lax.axis_index('fsdp'), lax.axis_index('sp'))
    core = f % 2
    f_x, f_y, f_c, f_d = neighbours(f)
    piece = xg_ref.shape[3]
    meet(f, s)
    pairs = ((x_ref, xg_ref), (c_ref, cg_ref))
    sent = []

    def send(src, dst, send_sem, recv_sem, device):
        copy = remote(src, dst, send_sem, recv_sem, device)
        copy.start()
        sent.append(copy)

    def arrived(ref, recv_sem):
        remote(ref, ref, s1.at[0, 0], recv_sem, (f_c, s)).wait_recv()
    holds = f // 2 == s
    keep_seg = pltpu.make_async_copy(seg_ref, segs_ref.at[core], seg_l.at[0])
    give_seg = [remote(seg_ref, segs_ref.at[core], seg_s.at[k], seg_r.at[core], ((f + k) % 8, s)) for k in range(1, 8)]

    @pl.when(holds)
    def _():
        keep_seg.start()
        for copy in give_seg:
            copy.start()
    weights = [
        pltpu.make_async_copy(ref, held_ref, w_l.at[n])
        for n, (ref, held_ref) in enumerate(
            ((up_ref, w_up), (qkv_ref, w_qkv), (b_up_in, b_up_ref), (b_qkv_in, b_qkv_ref), (norm_in, norm_ref))
        )
    ]
    for copy in weights:
        copy.start()
    kept = []
    for a, (src, _) in enumerate(pairs):
        own = pltpu.make_async_copy(src.at[pl.ds(f * piece, piece)], held.at[a, f], local.at[a, 0])
        own.start()
        kept.append(own)
        for k in range(1, 8):
            j = (f + k) % 8
            send(src.at[pl.ds(j * piece, piece)], held.at[a, f], s1.at[a, k], r1.at[a, k], (j, s))

    def to_planes(a):
        out = pairs[a][1]
        kept[a].wait()
        for k in range(1, 8):
            arrived(held.at[a, (f + 8 - k) % 8], r1.at[a, k])
        for k in range(1, 4):
            plane = (s + k) % 4
            send(held.at[a, pl.ds(2 * plane, 2)], out.at[:, s, f], s2.at[a, k], r2.at[a, k], (f, plane))
        own = pltpu.make_async_copy(held.at[a, pl.ds(2 * s, 2)], out.at[:, s, f], local.at[a, 1])
        own.start()
        return own

    def spread(a, k):
        out = pairs[a][1]
        z = (s + 4 - k) % 4
        if k:
            arrived(out.at[:, z, f], r2.at[a, k])
        ref = out.at[:, z, f]
        send(ref, ref, s3.at[a, 0, k], r3.at[a, 0, k], (f_x, s))
        send(ref, ref, s3.at[a, 1, k], r3.at[a, 1, k], (f_y, s))
        send(ref, ref, s3.at[a, 2, k], r3.at[a, 2, k], (f_c, s))

    def pass_on(a, k):
        out = pairs[a][1]
        z = (s + 4 - k) % 4
        ref = out.at[:, z, f_x]
        arrived(ref, r3.at[a, 0, k])
        send(out.at[0, z, f_x], out.at[0, z, f_x], s3.at[a, 5, k], r3.at[a, 5, k], (f_y, s))
        send(ref, ref, s3.at[a, 3, k], r3.at[a, 3, k], (f_c, s))
        ref = out.at[:, z, f_y]
        arrived(ref, r3.at[a, 1, k])
        send(out.at[1, z, f_y], out.at[1, z, f_y], s3.at[a, 6, k], r3.at[a, 6, k], (f_x, s))
        send(ref, ref, s3.at[a, 4, k], r3.at[a, 4, k], (f_c, s))

    def pass_corner(a, k):
        out = pairs[a][1]
        z = (s + 4 - k) % 4
        for half in range(2):
            ref = out.at[half, z, f_d]
            arrived(ref, r3.at[a, 5 + half, k])
            send(ref, ref, s3.at[a, 7 + half, k], r3.at[a, 7 + half, k], (f_c, s))

    def from_core(a, k):
        out = pairs[a][1]
        z = (s + 4 - k) % 4
        g_x, g_y, _, g_d = neighbours(f_c)
        arrived(out.at[:, z, f_c], r3.at[a, 2, k])
        arrived(out.at[:, z, g_x], r3.at[a, 3, k])
        arrived(out.at[:, z, g_y], r3.at[a, 4, k])
        for half in range(2):
            arrived(out.at[half, z, g_d], r3.at[a, 7 + half, k])
    results = ((normed, normed_out), (normed_mlp, normed_mlp_out), (packed, packed_out), (act, act_out), (slope, slope_out))
    size = 8 * piece

    def keep(b, z, n):
        rows = pl.ds(pl.multiple_of((b * 4 + z) * size, size), size)
        return pltpu.make_async_copy(results[n][0].at[b], results[n][1].at[rows], keep_l.at[b, n])

    tiles = {}

    def work(k, b):
        z = (s + 4 - k) % 4
        if b == 0:
            for half in range(2):
                tiles[half] = copied(xg_ref.at[half, z], tile.at[half], tile_l.at[half])
            if k == 0:
                for copy in weights:
                    copy.wait()
        tiles[b].wait()
        if k:
            for n in range(5):
                keep(b, (s + 5 - k) % 4, n).wait()

        @pl.loop(0, 8)
        def _(i):
            inputs = tile[b, i].astype(jnp.float32)
            centred = inputs - jnp.mean(inputs, axis=-1, keepdims=True)
            variance = jnp.mean(centred * centred, axis=-1, keepdims=True)
            scaled = centred * lax.rsqrt(variance + EPSILON)
            rows = pl.ds(pl.multiple_of(i * piece, piece), piece)
            low = normed.dtype
            normed[b, rows, :] = (scaled * norm_ref[0:1, :] + norm_ref[1:2, :]).astype(low)
            normed_mlp[b, rows, :] = (scaled * norm_ref[2:3, :] + norm_ref[3:4, :]).astype(low)
        hidden = times_transposed(normed_mlp[b], w_up[...]) + b_up_ref[...]
        packed[b] = (times_transposed(normed[b], w_qkv[...]) + b_qkv_ref[...]).astype(packed.dtype)
        activated, grown = gelu_pair(hidden)
        act[b] = activated.astype(act.dtype)
        slope[b] = grown
        for n in range(5):
            keep(b, z, n).start()
    own0 = to_planes(0)
    own1 = to_planes(1)
    steps = [(a, k) for a in range(2) for k in range(4)]
    for i in range(len(steps) + 2):
        if i < len(steps):
            a, k = steps[i]
            if k == 0:
                (own0 if a == 0 else own1).wait()
            spread(a, k)
        if 3 <= i < 7:
            from_core(0, i - 3)
            work(i - 3, 0)
        if 0 <= i - 1 < len(steps):
            pass_on(*steps[i - 1])
        if 0 <= i - 2 < len(steps):
            pass_corner(*steps[i - 2])
        if 3 <= i < 7:
            work(i - 3, 1)
    for k in range(4):
        from_core(1, k)
    for b in range(2):
        for n in range(5):
            keep(b, (s + 1) % 4, n).wait()
    for b in range(2):

        @pl.when(f != 2 * s + b)
        def _():
            arrived(segs_ref.at[b], seg_r.at[b])

    @pl.when(holds)
    def _():
        keep_seg.wait()
        for copy in give_seg:
            copy.wait_send()
    for copy in sent:
        copy.wait_send()


def gather_both(x, c, segments, w_up, w_qkv, b_up, b_qkv, norms):
    rows, width = x.shape
    piece = rows // 8
    tokens = 8 * rows
    units, columns = (w_up.shape[0], w_qkv.shape[0])
    shape = jax.ShapeDtypeStruct((2, 4, 8, piece, width), x.dtype)
    dma = pltpu.SemaphoreType.DMA
    vmem = pltpu.VMEM
    anywhere = pl.BlockSpec(memory_space=pl.ANY)
    sizes = ((width, x.dtype), (width, x.dtype), (columns, x.dtype), (units, x.dtype), (units, jnp.float32))
    return pl.pallas_call(gather_kernel, out_shape=(shape, shape, jax.ShapeDtypeStruct((2, *segments.shape), segments.dtype),
        *(jax.ShapeDtypeStruct((tokens, size), kind) for size, kind in sizes)), in_specs=[anywhere] * 8, out_specs=[anywhere] * 8,
        scratch_shapes=[vmem((2, 8, piece, width), x.dtype), vmem((2, 8, piece, width), x.dtype), vmem(w_up.shape, w_up.dtype), vmem(w_qkv.shape,
        w_qkv.dtype), *(vmem((2, 8 * piece, size), kind) for size, kind in sizes), dma((8,)), dma((2,)), dma((1,)), dma((2, 8)), dma((2, 8)), dma((2,
        4)), dma((2, 4)), dma((2, 9, 4)), dma((2, 9, 4)), dma((2, 2)), dma((5,)), dma((2,)), dma((2, 5)),
        vmem((1, units), jnp.float32), vmem((1, columns), jnp.float32), vmem(norms.shape, jnp.float32)],
        compiler_params=pltpu.CompilerParams(collective_id=1, has_side_effects=True, vmem_limit_bytes=60 * 1024 * 1024), name='gather_tokens')(x, c,
        segments, w_up, w_qkv, b_up.reshape(1, units), b_qkv.reshape(1, columns), norms)


def finish_kernel(down_ref, dense_ref, hidden_ref, normed_mlp_ref, packed_ref, normed_ref, act_ref, context_ref, up_w_ref, down_w_ref, qkv_w_ref,
    dense_w_ref, norm_ref, h_col_ref, p_col_ref, bias_ref, g_down, g_up, g_qkv, g_dense, o_out, o_back, part, paired, kept, crossed, homed, o_small,
    line_a, line_b, turned, big, hidden, packed, weight, qkv_w, dense_w, context, act, total, made, own, right, vecs, vec_out, vec_in, small,
    small_in, load_l, act_l, part_l, tile_s, tile_r, tile_l, left_l, right_l, in_s, in_r, mid_s, mid_r, end_s, end_r, own_l, keep_l, turn_s, turn_r,
    cross_s, cross_r, home_s, home_r, back_s, back_r, local, vec_s, vec_r, small_s, small_r):
    f, s = (lax.axis_index('fsdp'), lax.axis_index('sp'))
    core = f % 2
    f_x, f_y, f_c, f_d = neighbours(f)
    is_end = (s == 0) | (s == 3)
    is_mid = (s == 1) | (s == 2)
    inner, outer, facing = (1 + s // 3, 3 * (s // 2), 3 - s)
    unit = made.shape[3]
    size = 8 * unit
    low = made.dtype
    meet(f, s)
    sent = []

    def send(src, dst, send_sem, recv_sem, device):
        copy = remote(src, dst, send_sem, recv_sem, device)
        copy.start()
        return copy

    def arrived(ref, recv_sem):
        remote(ref, ref, vec_s.at[0], recv_sem, (f_c, s)).wait_recv()
    chunks = []
    at = 0
    groups = {}
    for name, ref, first, result in (('down', down_ref, 0, g_down), ('up', part, 0, g_up), ('qkv', part, g_up.shape[0], g_qkv), ('dense', turned, 0,
        g_dense)):
        for g in range(result.shape[0]):
            cuts = (4,)
            if not chunks:
                cuts = (1, 1, 2)
            if name == 'dense':
                cuts = (2, 1, 1)
            start = 0
            for pairs_of in cuts:
                chunks.append((ref, first + g, result, g, start, pairs_of, at))
                groups[len(chunks) - 1] = (name, first + g)
                start += pairs_of
            at += 1
    count = len(chunks)
    ahead = 4

    def cut(ref, g, k):
        _, _, _, _, start, pairs_of, _ = chunks[k]
        return ref.at[g, pl.ds(start, pairs_of)]

    def source(k):
        return cut(chunks[k][0], chunks[k][1], k)

    def goal(k):
        return cut(chunks[k][2], chunks[k][3], k)

    def from_end(k):
        return remote(source(k), cut(line_a, chunks[k][6], k), in_s.at[k], in_r.at[k], (f, inner))

    def across(k):
        return remote(cut(line_a, chunks[k][6], k), cut(line_b, chunks[k][6], k), mid_s.at[k], mid_r.at[k], (f, facing))

    def to_end(k):
        return remote(cut(line_b, chunks[k][6], k), goal(k), end_s.at[k], end_r.at[k], (f, outer))

    def load_own(k):
        return pltpu.make_async_copy(source(k), cut(own, k % 2, k), own_l.at[k % 2])

    def keep(k):
        return pltpu.make_async_copy(cut(line_b, chunks[k][6], k), goal(k), keep_l.at[k])

    def add_units(target, others, number):
        @pl.loop(0, number)
        def _(i):
            for half in range(2):
                rows = pl.ds(half * (unit // 2), unit // 2)
                value = target[i // 2, i % 2, rows, :].astype(jnp.float32)
                for other in others:
                    value = value + other[i // 2, i % 2, rows, :].astype(jnp.float32)
                target[i // 2, i % 2, rows, :] = value.astype(low)

    def mid_in(k):
        load_own(k).wait()
        from_end(k).wait_recv()
        add_units(cut(line_a, chunks[k][6], k), [cut(own, k % 2, k)], 2 * chunks[k][5])
        across(k).start()
        if k + 2 < count:
            load_own(k + 2).start()

    def mid_out(k):
        across(k).wait_recv()
        add_units(cut(line_b, chunks[k][6], k), [cut(line_a, chunks[k][6], k)], 2 * chunks[k][5])
        to_end(k).start()
        keep(k).start()
    coming = {'big': copied(normed_mlp_ref, big, load_l.at[0]), 'hidden': copied(hidden_ref, hidden, load_l.at[1]), 'weight': copied(up_w_ref,
        weight, load_l.at[2]), 'packed': copied(packed_ref, packed, load_l.at[3]), 'qkv': copied(qkv_w_ref, qkv_w, load_l.at[4]),
        'dense': copied(dense_w_ref, dense_w, load_l.at[5]), 'context': copied(context_ref, context, load_l.at[6])}

    def ready(*names):
        for name in names:
            if coming[name] is not None:
                coming[name].wait()
                coming[name] = None
    span = dense_ref.shape[4]
    columns = pl.ds(pl.multiple_of(f * span, span), span)
    turn_own = copied(dense_ref.at[f], turned.at[0, :, :, :, columns], local.at[0])
    bias_own = copied(bias_ref, small.at[pl.ds(8, 8)], local.at[1])
    vecs[...] = jnp.zeros_like(vecs)
    vec_out[...] = jnp.zeros_like(vec_out)
    busy = {0: [], 1: []}
    turns = [0]

    def next_made():
        slot = turns[0] % 2
        turns[0] += 1
        for wait in busy[slot]:
            wait()
        busy[slot] = []
        return slot
    stores = {}

    def finish_group(g, weights, first, column_ref, which):
        slot = next_made()

        @pl.loop(0, 8)
        def _(i):
            rows = pl.ds(pl.multiple_of(i * unit, unit), unit)
            wide = pl.ds(pl.multiple_of(first + i * unit, unit), unit)
            value = total[rows, :]
            made[slot, i // 2, i % 2] = value.astype(low)
            line = weights[wide, :].astype(jnp.float32)
            sums = column_ref[wide, 0:1]
            scaled = line * (value - sums * norm_ref[2 * which + 1:2 * which + 2, :])
            vecs[2 * which] += eight_rows(scaled)
            vecs[2 * which + 1] += eight_rows(line * sums)
        stores[g] = copied(made.at[slot], part.at[g], part_l.at[g])
        busy[slot] = [functools.partial(stored, g)]

    def stored(g):
        if stores[g] is not None:
            stores[g].wait()
            stores[g] = None

    def up_group(g):
        ready('big', 'hidden', 'weight')
        total[...] = contract_rows(hidden[:, g * size:(g + 1) * size], big[...].reshape(hidden.shape[0], -1))
        finish_group(g, weight, g * size, h_col_ref, 1)
        if g == g_up.shape[0] - 1:
            coming['big'] = copied(normed_ref, big, load_l.at[7])
            coming['weight'] = copied(down_w_ref, weight, load_l.at[8])
            load_act(0)

    def qkv_group(g):
        ready('big', 'packed', 'qkv')
        total[...] = contract_rows(packed[:, g * size:(g + 1) * size], big[...].reshape(hidden.shape[0], -1))
        finish_group(g_up.shape[0] + g, qkv_w, g * size, p_col_ref, 0)

    def load_act(t):
        coming['act', t] = copied(act_ref.at[pl.ds(t * size, size)], act.at[t % 2], act_l.at[t % 2])

    def give_tile(a, t, value):
        b, z = (t // 4, t % 4)
        slot = next_made()
        made[slot] = value.astype(low).reshape(4, 2, unit, value.shape[1])
        give = send(made.at[slot, :, 1 - core], paired.at[a, :, z, b], tile_s.at[a, t], tile_r.at[a, t], (f_c, s))
        hold = copied(made.at[slot, :, core], kept.at[a, :, z, b], tile_l.at[a, t])
        busy[slot] = [give.wait_send, hold.wait]

    def out_tile(t):
        ready('weight', 'context', 'dense', ('act', t))
        if t < 7:
            load_act(t + 1)
        rows = slice(t * size, (t + 1) * size)
        value = times_transposed(context[rows, :], dense_w[...]) + times(act[t % 2], weight[...])
        give_tile(0, t, value)
        if t == 7:
            coming['weight'] = copied(up_w_ref, weight, load_l.at[9])

    def back_tile(t):
        ready('weight', 'packed', 'qkv', 'hidden')
        rows = slice(t * size, (t + 1) * size)
        value = times(packed[rows, :], qkv_w[...]) * norm_ref[0:1, :]
        value = value + times(hidden[rows, :], weight[...]) * norm_ref[2:3, :]
        give_tile(1, t, value)
    results = (o_out, o_back)
    order = (f_d // 2, f_x // 2, f_y // 2, f // 2)
    homes = {}

    def free(slot):
        for wait in busy[slot]:
            wait()
        busy[slot] = []

    def tiles_here(a):
        for slot in range(2):
            free(slot)
        for t in range(8):
            arrived(paired.at[a, :, t % 4, t // 4], tile_r.at[a, t])

    def add_pair(a, n):
        if n == 0:
            tiles_here(a)
        left = big.at[3 * a + n]
        slot = n % 2
        first = copied(paired.at[a, order[n]], left, left_l.at[slot])
        second = copied(kept.at[a, order[n]], right.at[slot], right_l.at[slot])
        first.wait()
        second.wait()
        add_units(left, [right.at[slot]], 8)
        sent.append(send(left, crossed.at[a, n], cross_s.at[a, n], cross_r.at[a, n], ((f_d, f_x, f_y)[n], s)))

    def add_chips(a):
        left = big.at[6 + a]
        copies = [copied(paired.at[a, order[3]], left, left_l.at[0]), copied(kept.at[a, order[3]], right.at[0], right_l.at[0])]
        for n in range(3):
            arrived(crossed.at[a, n], cross_r.at[a, n])
            slot = (n + 1) % 2
            more = copied(crossed.at[a, n], right.at[slot], right_l.at[slot])
            for copy in copies:
                copy.wait()
            add_units(left, [right.at[1 - slot]], 8)
            copies = [more]
        copies[0].wait()
        add_units(left, [right.at[1]], 8)
        for k in range(1, 4):
            z = (s + k) % 4
            sent.append(send(left.at[z], homed.at[a, s], home_s.at[a, k], home_r.at[a, k], (f, z)))
        homes['own', a] = copied(left.at[s], homed.at[a, s], local.at[2 + a])


    def go_home(a):
        homes['own', a].wait()
        for k in range(1, 4):
            arrived(homed.at[a, (s + 4 - k) % 4], home_r.at[a, k])
        for k in range(1, 8):
            j = (f + k) % 8
            sent.append(send(homed.at[a, j // 2, j % 2], results[a].at[f], back_s.at[a, k], back_r.at[a, k], (j, s)))
        homes[a] = copied(homed.at[a, f // 2, core], results[a].at[f], local.at[4 + a])

    def give_vectors():
        for which in range(2):
            gain = norm_ref[2 * which:2 * which + 1, :]
            scaled = jnp.sum(vecs[2 * which], axis=0, keepdims=True) / gain
            plain = jnp.sum(vecs[2 * which + 1], axis=0, keepdims=True)
            for j in range(8):
                part_of = slice(j * span, (j + 1) * span)
                vec_out[j, 2 * which:2 * which + 1, :] = scaled[:, part_of]
                vec_out[j, 2 * which + 1:2 * which + 2, :] = plain[:, part_of]
        for k in range(1, 8):
            j = (f + k) % 8
            sent.append(send(vec_out.at[j], vec_in.at[f], vec_s.at[k], vec_r.at[k], (j, s)))
        homes['vec'] = copied(vec_out.at[f], vec_in.at[f], local.at[6])

    def add_vectors():
        homes['vec'].wait()
        bias_own.wait()
        for k in range(1, 8):
            arrived(vec_in.at[(f + 8 - k) % 8], vec_r.at[k])
        value = vec_in[0]
        for j in range(1, 8):
            value = value + vec_in[j]
        small[0:8, :] = value
        for k in range(1, 4):
            sent.append(send(small, small_in.at[s], small_s.at[k], small_r.at[k], (f, (s + k) % 4)))
        homes['small'] = copied(small, small_in.at[s], local.at[7])

    def add_small():
        homes['small'].wait()
        for k in range(1, 4):
            arrived(small_in.at[(s + 4 - k) % 4], small_r.at[k])
        value = small_in[0]
        for z in range(1, 4):
            value = value + small_in[z]
        o_small[...] = value

    def turn_start():
        for k in range(1, 8):
            j = (f + k) % 8
            sent.append(send(dense_ref.at[j], turned.at[0, :, :, :, columns], turn_s.at[k], turn_r.at[k], (j, s)))

    def turn_done():
        turn_own.wait()
        for k in range(1, 8):
            j = (f + 8 - k) % 8
            there = pl.ds(pl.multiple_of(j * span, span), span)
            arrived(turned.at[0, :, :, :, there], turn_r.at[k])

    def task(name, i):
        if name == 'turn':
            turn_start()
        elif name == 'turned':
            turn_done()
        elif name == 'up':
            up_group(i)
        elif name == 'qkv':
            qkv_group(i)
        elif name == 'out':
            out_tile(i)
        elif name == 'back':
            back_tile(i)
        elif name == 'pair':
            add_pair(i // 3, i % 3)
        elif name == 'chips':
            add_chips(i)
        elif name == 'home':
            go_home(i)
        elif name == 'vectors':
            give_vectors()
        elif name == 'sums':
            add_vectors()
        else:
            add_small()

    @pl.when(is_end)
    def _():
        for k in range(ahead):
            from_end(k).start()

    @pl.when(is_mid)
    def _():
        for k in range(2):
            load_own(k).start()
    for k in range(count + 2):
        for name, first, last in FINISH_STEPS[k] if k in FINISH_STEPS else ():
            for i in range(first, last):
                task(name, i)
        if k + ahead - 1 in groups and groups[k + ahead - 1][0] in ('up', 'qkv'):
            stored(groups[k + ahead - 1][1])

        @pl.when(is_mid)
        def _():
            if k < count:
                mid_in(k)
            if 1 <= k <= count:
                mid_out(k - 1)

        @pl.when(is_end)
        def _():
            if 1 <= k <= count:
                to_end(k - 1).wait_recv()
                if k - 1 + ahead < count:
                    from_end(k - 1 + ahead).start()
    for a in range(2):
        homes[a].wait()
        for k in range(1, 8):
            arrived(results[a].at[(f + 8 - k) % 8], back_r.at[a, k])
    for slot in range(2):
        free(slot)
    for copy in sent:
        copy.wait_send()

    @pl.when(is_end)
    def _():
        for k in range(count):
            from_end(k).wait_send()

    @pl.when(is_mid)
    def _():
        for k in range(count):
            across(k).wait_send()
            to_end(k).wait_send()
            keep(k).wait()


FINISH_STEPS = {
    0: (("turn", 0, 1),),
    1: (("up", 0, 1),),
    2: (("up", 1, 2),),
    3: (("up", 2, 4),),
    4: (("qkv", 0, 3),),
    5: (("out", 0, 8),),
    6: (("pair", 0, 3), ("back", 0, 3)),
    7: (("back", 3, 6), ("turned", 0, 1)),
    8: (("back", 6, 8), ("vectors", 0, 1), ("pair", 3, 6)),
    9: (("chips", 0, 1),),
    10: (("sums", 0, 1),),
    11: (("home", 0, 1), ("chips", 1, 2)),
    12: (("small", 0, 1),),
    14: (("home", 1, 2),),
}


def finish(down, dense, hidden_grad, normed_mlp, packed_grad, normed, act, context, w_up, w_down, w_qkv, dense_in, norms, h_sums, p_sums, bias):
    width = down.shape[1]
    tokens = hidden_grad.shape[0]
    low = down.dtype
    unit = tokens // 64
    size = 8 * unit
    span = width // 8

    def grouped(rows):
        return (rows // size, 4, 2, unit, width)

    def columns(sums):
        return jnp.broadcast_to(sums[:, None], (sums.shape[0], 128))
    sets = [w.shape[0] // size for w in (down, w_up, w_qkv)]
    number = sum(sets) + 1
    count = sum(sets) + 5
    sums = [jax.ShapeDtypeStruct(grouped(n * size), low) for n in (*sets, 1)]
    token = jax.ShapeDtypeStruct((8, unit, width), low)
    halves = jax.ShapeDtypeStruct((2, 4, 4, 2, unit, width), low)
    others = [jax.ShapeDtypeStruct(grouped((sets[1] + sets[2]) * size), low), halves, halves, jax.ShapeDtypeStruct((2, 3, 4, 2, unit, width), low),
        jax.ShapeDtypeStruct((2, 4, 2, unit, width), low)]
    dma = pltpu.SemaphoreType.DMA
    vmem = pltpu.VMEM
    anywhere = pl.BlockSpec(memory_space=pl.ANY)
    inside = pl.BlockSpec(memory_space=pltpu.VMEM)
    result = pl.pallas_call(finish_kernel, out_shape=(*sums, token, token, *others, jax.ShapeDtypeStruct((16, span), jnp.float32)),
        in_specs=[anywhere] * 12 + [inside] * 3 + [anywhere], out_specs=[anywhere] * 11 + [inside], scratch_shapes=[vmem((number, 4, 2, unit, width),
        low), vmem((number, 4, 2, unit, width), low), vmem((1, 4, 2, unit, width), low), vmem(grouped(tokens), low), vmem(hidden_grad.shape, low),
        vmem(packed_grad.shape, low), vmem(w_up.shape, low), vmem(w_qkv.shape, low), vmem(dense_in.shape, low), vmem(context.shape, low), vmem((2,
        size, act.shape[1]), low), vmem((size, width), jnp.float32), *(vmem((2, 4, 2, unit, width), low) for _ in range(3)), vmem((4, 8, width),
        jnp.float32), vmem((8, 8, span), jnp.float32), vmem((8, 8, span), jnp.float32), vmem((16, span), jnp.float32), vmem((4, 16, span),
        jnp.float32), dma((10,)), dma((2,)), dma((sets[1] + sets[2],)), dma((2, 8)), dma((2, 8)), dma((2, 8)), dma((2,)), dma((2,)), dma((count,)),
        dma((count,)), dma((count,)), dma((count,)), dma((count,)), dma((count,)), dma((2,)), dma((count,)), dma((8,)), dma((8,)), dma((2, 3)),
        dma((2, 3)), dma((2, 4)), dma((2, 4)), dma((2, 8)), dma((2, 8)), dma((8,)), dma((8,)), dma((8,)), dma((4,)), dma((4,))],
        compiler_params=pltpu.CompilerParams(collective_id=2, has_side_effects=True, vmem_limit_bytes=60 * 1024 * 1024),
        name='finish')(down.reshape(grouped(down.shape[0])), dense.reshape(8, 4, 2, unit, span), hidden_grad, normed_mlp.reshape(grouped(tokens)), packed_grad, normed.reshape(grouped(tokens)), act,
        context, w_up, w_down, w_qkv, dense_in, norms, columns(h_sums), columns(p_sums), bias)
    grads = [grad.reshape(-1, width) for grad in result[:4]]
    return (grads, result[4], result[5], result[11])


def last_kernel(
    x_ref, c_ref, out_ref, back_ref, shift_ref, early_ref, late_ref, up_ref, qkv_ref, dense_ref,
    output, input_grad, down_out, up_out, qkv_out, dense_out,
):
    inputs = x_ref[...].astype(jnp.float32)
    output[...] = (inputs + (out_ref[...].astype(jnp.float32) + shift_ref[...])).astype(output.dtype)
    centred = inputs - jnp.mean(inputs, axis=-1, keepdims=True)
    inverse = lax.rsqrt(jnp.mean(centred * centred, axis=-1, keepdims=True) + EPSILON)
    scaled = centred * inverse
    weighted = back_ref[...].astype(jnp.float32)
    first_mean = jnp.mean(weighted, axis=-1, keepdims=True)
    second_mean = jnp.mean(weighted * scaled, axis=-1, keepdims=True)
    change = inverse * (weighted - first_mean - scaled * second_mean)
    input_grad[...] = (c_ref[...].astype(jnp.float32) + change).astype(input_grad.dtype)
    down_out[0] = early_ref[...].astype(jnp.float32)
    down_out[1] = late_ref[...].astype(jnp.float32)
    for ref, out in ((up_ref, up_out), (qkv_ref, qkv_out), (dense_ref, dense_out)):
        out[...] = ref[...].astype(jnp.float32)


def last(x, c, out, back, shift, early, late, up, qkv, dense, steps=8):
    width = up.shape[1]

    def tile(array):
        return pl.BlockSpec((array.shape[0] // steps, width), lambda i: (i, 0))

    tokens, sums = (x, c, out, back), (early, late, up, qkv, dense)
    wide = jax.ShapeDtypeStruct((2, early.shape[0], width), jnp.float32)
    number = 2 * early.size + up.size + qkv.size + dense.size
    output, input_grad, down, up, qkv, dense = pl.pallas_call(
        last_kernel,
        grid=(steps,),
        out_shape=(
            jax.ShapeDtypeStruct(x.shape, x.dtype), jax.ShapeDtypeStruct(x.shape, x.dtype), wide,
            *(jax.ShapeDtypeStruct(array.shape, jnp.float32) for array in sums[2:]),
        ),
        in_specs=[tile(array) for array in tokens] + [pl.BlockSpec((1, width), lambda i: (0, 0))] + [tile(array) for array in sums],
        out_specs=[
            tile(x), tile(x), pl.BlockSpec((2, early.shape[0] // steps, width), lambda i: (0, i, 0)),
            *(tile(array) for array in sums[2:]),
        ],
        compiler_params=pltpu.CompilerParams(vmem_limit_bytes=60 * 1024 * 1024),
        cost_estimate=pl.CostEstimate(flops=20 * x.size, transcendentals=0, bytes_accessed=6 * number + 12 * x.size),
        name="last",
    )(*tokens, shift.reshape(1, width), *sums)
    return output, input_grad, down.reshape(-1, width), up, qkv, dense


def own_tokens(hidden_in, cotangent, output, weighted, shift):
    inputs = hidden_in.astype(jnp.float32)
    output = (inputs + (output.astype(jnp.float32) + shift)).astype(jnp.bfloat16)
    scaled, inverse = norm_scaled(inputs)
    weighted = weighted.astype(jnp.float32)
    first_mean = jnp.mean(weighted, axis=-1, keepdims=True)
    second_mean = jnp.mean(weighted * scaled, axis=-1, keepdims=True)
    input_grad = (cotangent.astype(jnp.float32) + inverse * (weighted - first_mean - scaled * second_mean)).astype(jnp.bfloat16)
    return (output, input_grad)


def by_collectives(hidden_in, segments, ln1_gain, ln1_bias, ln2_gain, ln2_bias, w_qkv, b_qkv, w_dense, b_dense, w_up, b_up, w_down, b_down,
    cotangent):
    seq_local, shard_len, width = hidden_in.shape
    seq_len = segments.shape[1]
    nf, ns = (lax.axis_size('fsdp'), lax.axis_size('sp'))
    f_place, s_place = (lax.axis_index('fsdp'), lax.axis_index('sp'))
    seqs = seq_local * nf
    group = seqs // ns
    piece = shard_len // nf
    tokens = group * seq_len
    per_head = max(1, nf // HEADS)
    head_count = max(1, HEADS // nf)
    head_sets = [[head * per_head + k for k in range(per_head)] for head in range(nf // per_head)]

    def gather_tokens(block):
        part = lax.all_to_all(block, 'fsdp', split_axis=1, concat_axis=0, tiled=True)
        part = lax.all_to_all(part, 'sp', split_axis=0, concat_axis=1, tiled=True)
        return in_order(lax.all_gather(part, 'fsdp', axis=0, tiled=True)).reshape(tokens, width)

    def scatter_tokens(partial):
        part = out_of_order(partial).reshape(nf * group, ns * piece, width)
        part = lax.psum_scatter(part, 'fsdp', scatter_dimension=0, tiled=True)
        part = lax.all_to_all(part, 'sp', split_axis=1, concat_axis=0, tiled=True)
        return lax.all_to_all(part, 'fsdp', split_axis=0, concat_axis=1, tiled=True)

    def in_order(array):
        array = array.reshape(nf, group, ns, piece, -1)
        return array.transpose(1, 2, 0, 3, 4).reshape(group, seq_len, -1)

    def out_of_order(array):
        array = array.reshape(group, ns, nf, piece, -1)
        return array.transpose(2, 0, 1, 3, 4).reshape(tokens, -1)

    def over_head(array, axis):
        if per_head == 1:
            return array
        return lax.all_gather(array, 'fsdp', axis=axis, tiled=True, axis_index_groups=head_sets)

    def own_columns(array):
        if per_head == 1:
            return array
        share = array.shape[-1] // per_head
        return lax.dynamic_slice_in_dim(array, f_place % per_head * share, share, array.ndim - 1)

    def own_part(vector):
        share = vector.shape[0] // nf
        return lax.dynamic_slice_in_dim(vector, f_place * share, share, 0)
    gathered, upstream = (gather_tokens(hidden_in), gather_tokens(cotangent))
    rows = lax.all_gather(segments, 'fsdp', axis=0, tiled=True)
    rows = lax.dynamic_slice_in_dim(rows, s_place * group, group, 0)
    dense_in = lax.all_to_all(w_dense, 'fsdp', split_axis=1, concat_axis=0, tiled=True)
    head_qkv = over_head(w_qkv, 0)
    head_dense = over_head(dense_in, 1)
    head_bias = lax.dynamic_slice_in_dim(b_qkv, f_place // per_head * head_qkv.shape[0], head_qkv.shape[0], 0)
    scaled, _ = norm_scaled(gathered.astype(jnp.float32))
    normed = (scaled * ln1_gain + ln1_bias).astype(jnp.bfloat16)
    normed_mlp = (scaled * ln2_gain + ln2_bias).astype(jnp.bfloat16)
    hidden = times_transposed(normed_mlp, w_up) + own_part(b_up)
    activated, slope = gelu_pair(hidden)
    activated = activated.astype(jnp.bfloat16)
    down_term = contract_rows(activated, upstream).astype(jnp.bfloat16)
    grad_down_w = lax.psum(down_term, 'sp').astype(jnp.float32)
    hidden_grad = (times_transposed(upstream, w_down) * slope).astype(jnp.bfloat16)
    up_term = contract_rows(hidden_grad, normed_mlp)
    mlp_norm_grad = times(hidden_grad, w_up)
    packed = (times_transposed(normed, head_qkv) + head_bias).astype(jnp.bfloat16)
    packed = packed.reshape(group, seq_len, head_count, 3 * HEAD_DIM)
    cos_table, sin_table = rotary_tables(rows)
    queries = rotate(packed[..., :HEAD_DIM].astype(jnp.float32), cos_table, sin_table).astype(jnp.bfloat16)
    keys_rot = rotate(packed[..., HEAD_DIM:2 * HEAD_DIM].astype(jnp.float32), cos_table, sin_table).astype(jnp.bfloat16)
    values = packed[..., 2 * HEAD_DIM:]
    mask = build_mask(rows)
    context, log_total = attend_forward(queries, keys_rot, values, mask)
    context = own_columns(context.reshape(tokens, -1))
    partial_out = times_transposed(context, dense_in) + times(activated, w_down)
    context_grad = times(upstream, head_dense).astype(jnp.bfloat16).reshape(group, seq_len, head_count, HEAD_DIM)
    query_grad, key_grad, value_grad = attend_backward(queries, keys_rot, values, mask, log_total, context_grad)
    packed_grad = jnp.concatenate([unrotate(query_grad, cos_table, sin_table), unrotate(key_grad, cos_table, sin_table), value_grad],
        axis=-1).astype(jnp.bfloat16)
    packed_grad = own_columns(packed_grad.reshape(tokens, -1))
    attn_norm_grad = times(packed_grad, w_qkv)
    qkv_term = contract_rows(packed_grad, normed)
    dense_term = contract_rows(upstream, context).astype(jnp.bfloat16)
    partial_back = attn_norm_grad * ln1_gain + mlp_norm_grad * ln2_gain
    vectors = jnp.stack([jnp.sum(attn_norm_grad * scaled, axis=0), jnp.sum(attn_norm_grad, axis=0), jnp.sum(mlp_norm_grad * scaled, axis=0),
        jnp.sum(mlp_norm_grad, axis=0)])
    bias_out = own_part(jnp.sum(upstream.astype(jnp.float32), axis=0))
    bias_qkv = jnp.sum(packed_grad.astype(jnp.float32), axis=0)
    bias_up = jnp.sum(hidden_grad.astype(jnp.float32), axis=0)
    vectors = lax.psum_scatter(vectors, 'fsdp', scatter_dimension=1, tiled=True)
    vectors, bias_out, bias_qkv, bias_up = lax.psum((vectors, bias_out, bias_qkv, bias_up), 'sp')
    output = scatter_tokens(rounded(partial_out))
    weighted = scatter_tokens(rounded(partial_back))
    dense_term = lax.all_to_all(dense_term, 'fsdp', split_axis=0, concat_axis=1, tiled=True)
    grad_up_w, grad_qkv_w, grad_dense_w = (lax.psum(term.astype(jnp.bfloat16), 'sp').astype(jnp.float32) for term in (up_term, qkv_term, dense_term))
    output, input_grad = own_tokens(hidden_in, cotangent, output, weighted, b_dense + b_down)
    return (output, input_grad, vectors[0], vectors[1], vectors[2], vectors[3], grad_qkv_w, bias_qkv, grad_dense_w, bias_out, grad_up_w, bias_up,
        grad_down_w, bias_out)


def by_kernels(hidden_in, segments, ln1_gain, ln1_bias, ln2_gain, ln2_bias, w_qkv, b_qkv, w_dense, b_dense, w_up, b_up, w_down, b_down, cotangent):
    width = hidden_in.shape[2]
    seq_len = segments.shape[1]
    nf, ns = (lax.axis_size('fsdp'), lax.axis_size('sp'))
    group = nf // ns
    tokens = group * seq_len
    share = width // nf
    f_place = lax.axis_index('fsdp')

    def own_part(vector):
        size = vector.shape[0] // nf
        return lax.dynamic_slice_in_dim(vector, f_place * size, size, 0)
    norms = jnp.stack([ln1_gain, ln1_bias, ln2_gain, ln2_bias])
    _, upstream, rows, normed, normed_mlp, packed, activated, slope = gather_both(hidden_in[0], cotangent[0], segments.reshape(8, seq_len // 8),
        w_up, w_qkv, own_part(b_up), own_part(b_qkv), norms)
    upstream = upstream.reshape(tokens, width)
    w_dense, upstream = lax.optimization_barrier((w_dense, upstream))
    dense_in = lax.all_to_all(w_dense, 'fsdp', split_axis=1, concat_axis=0, tiled=True)
    early = activated.shape[1] // 2
    down_term = contract_rows(activated[:, :early], upstream).astype(jnp.bfloat16)
    early_down_w = lax.psum(down_term, 'sp')
    slope, activated, down_term = lax.optimization_barrier((slope, activated, down_term))
    hidden_grad, context_grad, c_sums, h_sums = upstream_parts(upstream, slope, w_down, dense_in)
    context, packed_grad, p_sums = attend(packed, context_grad, head_tables(rows.reshape(group, seq_len)), seq_len)
    late_down_term = contract_rows(activated[:, early:], upstream).astype(jnp.bfloat16)
    dense_term = contract_rows(upstream, context).astype(jnp.bfloat16)
    bias_up, bias_qkv = (jnp.sum(h_sums, axis=0), jnp.sum(p_sums, axis=0))
    bias_out = own_part(jnp.sum(c_sums, axis=0))
    grads, output, weighted, sums = finish(late_down_term, dense_term, hidden_grad, normed_mlp, packed_grad, normed, activated, context, w_up,
        w_down, w_qkv, dense_in, norms, bias_up, bias_qkv, jnp.concatenate([bias_out, bias_qkv, bias_up]).reshape(8, share))
    output, input_grad, grad_down_w, grad_up_w, grad_qkv_w, grad_dense_w = last(
        hidden_in[0], cotangent[0], output.reshape(-1, width), weighted.reshape(-1, width), b_dense + b_down, early_down_w, *grads
    )
    output, input_grad = output[None], input_grad[None]
    bias_out = sums[8]
    return (output, input_grad, sums[0], sums[1], sums[2], sums[3], grad_qkv_w, sums[9:12].reshape(-1), grad_dense_w, bias_out, grad_up_w,
        sums[12:16].reshape(-1), grad_down_w, bias_out)


def per_device(hidden_in, *rest):
    sizes = (lax.axis_size('fsdp'), lax.axis_size('sp'), hidden_in.shape[0])
    shapes = (hidden_in.shape[1] % 256, hidden_in.shape[2] % (8 * HEAD_DIM), rest[9].shape[0] % 256)
    if sizes == (8, 4, 1) and HEADS == 8 and (not any(shapes)):
        return by_kernels(hidden_in, *rest)
    return by_collectives(hidden_in, *rest)


def solution(mesh):
    rows = P('fsdp', 'sp', None)
    first = P('fsdp', None)
    return jax.shard_map(per_device, mesh=mesh, in_specs=(rows, first, P(), P(), P(), P(), first, P(), first, P(), first, P(), first, P(), rows),
        out_specs=(rows, rows, P('fsdp'), P('fsdp'), P('fsdp'), P('fsdp'), first, P('fsdp'), first, P('fsdp'), first, P('fsdp'), first, P('fsdp')),
        check_vma=False)
```

```python
import functools
import math

import jax
import jax.numpy as jnp
from jax import lax
from jax.experimental import pallas as pl
from jax.experimental.pallas import tpu as pltpu
from jax.sharding import PartitionSpec as P

MESH = pl.DeviceIdType.MESH

HEADS = 8
HEAD_DIM = 256
ROT = 64


EPSILON = 1e-05
NEGATIVE = -1e30
ROOT_HALF = 0.7071067811865476
ROOT_TWO_PI = 2.5066282746310002
SCALE = 1.0 / math.sqrt(HEAD_DIM)


def rounded(array):
    return lax.reduce_precision(array.astype(jnp.float32), 8, 7).astype(jnp.bfloat16)


def contract_rows(former, latter):
    return lax.dot_general(former, latter, (((0,), (0,)), ((), ())), preferred_element_type=jnp.float32)


def times_transposed(former, latter):
    return lax.dot_general(former, latter, (((1,), (1,)), ((), ())), preferred_element_type=jnp.float32)


def times(former, latter):
    return jnp.dot(former, latter, preferred_element_type=jnp.float32)


def norm_scaled(inputs):
    average = jnp.mean(inputs, axis=-1, keepdims=True)
    centred = inputs - average
    variance = jnp.mean(centred * centred, axis=-1, keepdims=True)
    inverse = lax.rsqrt(variance + EPSILON)
    return (centred * inverse, inverse)


def gelu_pair(hidden):
    cumulative = 0.5 * (1.0 + lax.erf(hidden * ROOT_HALF))
    return (hidden * cumulative, cumulative + hidden * (jnp.exp(-0.5 * hidden * hidden) * (1.0 / ROOT_TWO_PI)))


def document_starts(segment_rows):
    places = jnp.arange(segment_rows.shape[-1], dtype=jnp.int32)
    changes = jnp.concatenate([jnp.ones_like(segment_rows[..., :1]), (segment_rows[..., 1:] != segment_rows[..., :-1]).astype(jnp.int32)], axis=-1)
    return (places, lax.cummax(changes * places, axis=segment_rows.ndim - 1))


def frequencies():
    return 1.0 / jnp.power(10000.0, jnp.arange(0, ROT, 2).astype(jnp.float32) / ROT)


def rotary_tables(segment_rows):
    places, starts = document_starts(segment_rows)
    angles = (places - starts).astype(jnp.float32)[..., None] * frequencies()
    angles = jnp.concatenate([angles, angles], axis=-1)
    return (jnp.cos(angles), jnp.sin(angles))


def head_tables(segment_rows):
    smaller = segment_rows[:, :, None] < segment_rows[:, None, :]
    starts = jnp.sum(smaller.astype(jnp.float32), axis=1)
    places = jnp.arange(segment_rows.shape[-1], dtype=jnp.float32)
    angles = (places - starts)[:, None, :] * frequencies()[None, :, None]
    starts = jnp.broadcast_to(starts[:, None, :], (starts.shape[0], ROT, starts.shape[1]))
    return jnp.concatenate([jnp.cos(angles), jnp.sin(angles), starts], axis=1)


def rotate(heads_part, cos_table, sin_table):
    half_rot = ROT // 2
    turned = heads_part[..., :ROT]
    swapped = jnp.concatenate([-turned[..., half_rot:], turned[..., :half_rot]], axis=-1)
    turned = turned * cos_table[..., None, :] + swapped * sin_table[..., None, :]
    return jnp.concatenate([turned, heads_part[..., ROT:]], axis=-1)


def unrotate(grads_part, cos_table, sin_table):
    half_rot = ROT // 2
    turned = grads_part[..., :ROT]
    along_sin = turned * sin_table[..., None, :]
    back_turn = jnp.concatenate([along_sin[..., half_rot:], -along_sin[..., :half_rot]], axis=-1)
    turned = turned * cos_table[..., None, :] + back_turn
    return jnp.concatenate([turned, grads_part[..., ROT:]], axis=-1)


def build_mask(segment_rows):
    places = jnp.arange(segment_rows.shape[-1], dtype=jnp.int32)
    return (segment_rows[:, :, None] == segment_rows[:, None, :]) & (places[None, :] <= places[:, None])


def attention_scores(queries, keys_rot):
    return jnp.einsum('bqhd,bkhd->bhqk', queries, keys_rot, preferred_element_type=jnp.float32) * SCALE


def attend_forward(queries, keys_rot, values, mask):
    scores = jnp.where(mask[:, None], attention_scores(queries, keys_rot), NEGATIVE)
    row_top = jnp.max(scores, axis=-1, keepdims=True)
    exponent = jnp.exp(scores - row_top)
    row_total = jnp.sum(exponent, axis=-1, keepdims=True)
    attention = (exponent / row_total).astype(jnp.bfloat16)
    context = jnp.einsum('bhqk,bkhd->bqhd', attention, values, preferred_element_type=jnp.float32)
    return (context.astype(jnp.bfloat16), row_top + jnp.log(row_total))


def attend_backward(queries, keys_rot, values, mask, log_total, context_grad):
    scores = attention_scores(queries, keys_rot)
    attention = jnp.where(mask[:, None], jnp.exp(scores - log_total), 0.0)
    value_grad = jnp.einsum('bhqk,bqhd->bkhd', attention.astype(jnp.bfloat16), context_grad, preferred_element_type=jnp.float32)
    attention_grad = jnp.einsum('bqhd,bkhd->bhqk', context_grad, values, preferred_element_type=jnp.float32)
    row_centre = jnp.sum(attention * attention_grad, axis=-1, keepdims=True)
    score_grad = (attention * (attention_grad - row_centre)).astype(jnp.bfloat16)
    query_grad = jnp.einsum('bhqk,bkhd->bqhd', score_grad, keys_rot, preferred_element_type=jnp.float32) * SCALE
    key_grad = jnp.einsum('bhqk,bqhd->bkhd', score_grad, queries, preferred_element_type=jnp.float32) * SCALE
    return (query_grad, key_grad, value_grad)


def whole_block(array):
    return pl.BlockSpec(array.shape, lambda *_: (0,) * array.ndim, pipeline_mode=pl.Buffered(1))


def eight_rows(array):
    return jnp.sum(array.reshape(array.shape[0] // 8, 8, array.shape[1]), axis=0)


def upstream_kernel(c_ref, slope_ref, down_ref, dense_ref, grad_ref, context_ref, c_sum_ref, h_sum_ref):
    @pl.when(pl.program_id(0) == 0)
    def _():
        c_sum_ref[...] = jnp.zeros_like(c_sum_ref)
        h_sum_ref[...] = jnp.zeros_like(h_sum_ref)
    hidden_grad = (times_transposed(c_ref[...], down_ref[...]) * slope_ref[...]).astype(grad_ref.dtype)
    grad_ref[...] = hidden_grad
    context_ref[...] = times(c_ref[...], dense_ref[...]).astype(context_ref.dtype)
    c_sum_ref[...] += eight_rows(c_ref[...].astype(jnp.float32))
    h_sum_ref[...] += eight_rows(hidden_grad.astype(jnp.float32))


def upstream_parts(c, slope, w_down, dense, rows=256):
    tokens, width = c.shape
    units, columns = (w_down.shape[0], dense.shape[1])

    def tile(size):
        return pl.BlockSpec((rows, size), lambda i: (i, 0))

    def total(size):
        return pl.BlockSpec((8, size), lambda i: (0, 0))
    return pl.pallas_call(upstream_kernel, grid=(tokens // rows,), out_shape=(jax.ShapeDtypeStruct((tokens, units), c.dtype),
        jax.ShapeDtypeStruct((tokens, columns), c.dtype), jax.ShapeDtypeStruct((8, width), jnp.float32), jax.ShapeDtypeStruct((8, units),
        jnp.float32)), in_specs=[tile(width), tile(units), whole_block(w_down), whole_block(dense)], out_specs=[tile(units), tile(columns),
        total(width), total(units)], compiler_params=pltpu.CompilerParams(vmem_limit_bytes=48 * 1024 * 1024),
        cost_estimate=pl.CostEstimate(flops=2 * tokens * width * (units + columns), transcendentals=0,
        bytes_accessed=2 * tokens * (width + 3 * units + columns) + 2 * width * (units + columns)), name='upstream_parts')(c, slope, w_down, dense)


def attention_kernel(packed_ref, grad_ref, table_ref, context_ref, back_ref, sum_ref, q_ref, k_ref, low_ref, score_ref, turned_ref):
    length = packed_ref.shape[0]
    size = 256
    lanes = 128
    lane = lax.broadcasted_iota(jnp.int32, (size, lanes), 1)
    half = ROT // 2

    def tables(rows):
        table = turned_ref[rows, :]
        cosine = jnp.where(lane < half, table, jnp.where(lane < ROT, pltpu.roll(table, half, 1), 1.0))
        sine = jnp.where(lane < half, pltpu.roll(table, lanes - half, 1), jnp.where(lane < ROT, table, 0.0))
        return (cosine, jnp.where(lane < half, -sine, sine))

    def swapped(array):
        return jnp.where(lane < half, pltpu.roll(array, lanes - half, 1), pltpu.roll(array, half, 1))

    def turn(array, cosine, sine):
        front = array[:, :lanes]
        return jnp.concatenate([front * cosine + swapped(front) * sine, array[:, lanes:]], axis=1)
    blocks = length // size
    for i in range(blocks):
        rows = pl.ds(i * size, size)
        turned_ref[rows, :] = jnp.transpose(table_ref[0, :, rows])
        cosine, sine = tables(rows)
        for part, ref in enumerate((q_ref, k_ref)):
            array = packed_ref[rows, part * HEAD_DIM:(part + 1) * HEAD_DIM].astype(jnp.float32)
            ref[rows, :] = turn(array, cosine, sine).astype(ref.dtype)
    values = pl.ds(2 * HEAD_DIM, HEAD_DIM)
    for i in range(blocks):
        rows = pl.ds(i * size, size)
        reach = (i + 1) * size
        keys = pl.ds(0, reach)
        scores = times_transposed(q_ref[rows, :], k_ref[keys, :]) * SCALE
        gradient = times_transposed(grad_ref[rows, :], packed_ref[keys, values])
        place = lax.broadcasted_iota(jnp.int32, (size, reach), 1)
        query = lax.broadcasted_iota(jnp.int32, (size, reach), 0) + i * size
        start = turned_ref[rows, ROT:ROT + 1].astype(jnp.int32)
        allowed = (place >= start) & (place <= query)
        scores = jnp.where(allowed, scores, NEGATIVE)
        exponent = jnp.exp(scores - jnp.max(scores, axis=-1, keepdims=True))
        attention = exponent / jnp.sum(exponent, axis=-1, keepdims=True)
        low = attention.astype(low_ref.dtype)
        low_ref[rows, keys] = low
        context_ref[rows, :] = times(low, packed_ref[keys, values]).astype(context_ref.dtype)
        centre = jnp.sum(attention * gradient, axis=-1, keepdims=True)
        score_grad = (attention * (gradient - centre)).astype(score_ref.dtype)
        score_ref[rows, keys] = score_grad
        query_grad = times(score_grad, k_ref[keys, :]) * SCALE
        cosine, sine = tables(rows)
        back_ref[rows, :HEAD_DIM] = turn(query_grad, cosine, -sine).astype(back_ref.dtype)
    for j in range(blocks):
        keys = pl.ds(j * size, size)
        rows = pl.ds(j * size, length - j * size)
        key_grad = contract_rows(score_ref[rows, keys], q_ref[rows, :]) * SCALE
        cosine, sine = tables(keys)
        back_ref[keys, HEAD_DIM:2 * HEAD_DIM] = turn(key_grad, cosine, -sine).astype(back_ref.dtype)
        value_grad = contract_rows(low_ref[rows, keys], grad_ref[rows, :])
        back_ref[keys, values] = value_grad.astype(back_ref.dtype)

    @pl.when(pl.program_id(0) == 0)
    def _():
        sum_ref[...] = jnp.zeros_like(sum_ref)
    for i in range(blocks):
        sum_ref[...] += eight_rows(back_ref[pl.ds(i * size, size), :].astype(jnp.float32))


def attend(packed, context_grad, table, length):
    tokens, columns = packed.shape
    low = packed.dtype

    def tile(size):
        return pl.BlockSpec((length, size), lambda i: (i, 0))
    pairs = tokens * (length + 256) // 2
    return pl.pallas_call(attention_kernel, grid=(tokens // length,), out_shape=(jax.ShapeDtypeStruct((tokens, HEAD_DIM), low),
        jax.ShapeDtypeStruct((tokens, columns), low), jax.ShapeDtypeStruct((8, columns), jnp.float32)), in_specs=[tile(columns), tile(HEAD_DIM),
        pl.BlockSpec((1, *table.shape[1:]), lambda i: (i, 0, 0))], out_specs=[tile(HEAD_DIM), tile(columns), pl.BlockSpec((8, columns), lambda i: (0,
        0))], scratch_shapes=[pltpu.VMEM((length, HEAD_DIM), low), pltpu.VMEM((length, HEAD_DIM), low), pltpu.VMEM((length, length), low),
        pltpu.VMEM((length, length), low), pltpu.VMEM((length, table.shape[1]), jnp.float32)],
        compiler_params=pltpu.CompilerParams(vmem_limit_bytes=48 * 1024 * 1024), cost_estimate=pl.CostEstimate(flops=14 * pairs * HEAD_DIM,
        transcendentals=pairs, bytes_accessed=tokens * (4 * columns + 4 * HEAD_DIM + 512)), name='attend')(packed, context_grad, table)


def remote(src, dst, send_sem, recv_sem, device):
    return pltpu.make_async_remote_copy(src_ref=src, dst_ref=dst, send_sem=send_sem, recv_sem=recv_sem, device_id=device, device_id_type=MESH)


def copied(src, dst, sem):
    copy = pltpu.make_async_copy(src, dst, sem)
    copy.start()
    return copy


def meet(f, s):
    barrier = pltpu.get_barrier_semaphore()
    for k in range(1, 8):
        pl.semaphore_signal(barrier, inc=1, device_id=((f + k) % 8, s), device_id_type=MESH)
    for k in range(1, 4):
        pl.semaphore_signal(barrier, inc=1, device_id=(f, (s + k) % 4), device_id_type=MESH)
    pl.semaphore_wait(barrier, 10)


def neighbours(f):
    f_x, f_y = (f + 2 - 4 * (f // 2 % 2), f + 4 - 8 * (f // 4))
    return (f_x, f_y, f + 1 - 2 * (f % 2), f_x + f_y - f)


def gather_kernel(x_ref, c_ref, seg_ref, up_ref, qkv_ref, b_up_in, b_qkv_in, norm_in, xg_ref, cg_ref, segs_ref, normed_out, normed_mlp_out,
    packed_out, act_out, slope_out, held, tile, w_up, w_qkv, normed, normed_mlp, packed, act, slope, seg_s, seg_r, seg_l, s1, r1, s2, r2, s3, r3,
    local, w_l, tile_l, keep_l, b_up_ref, b_qkv_ref, norm_ref):
    f, s = (lax.axis_index('fsdp'), lax.axis_index('sp'))
    core = f % 2
    f_x, f_y, f_c, f_d = neighbours(f)
    piece = xg_ref.shape[3]
    meet(f, s)
    pairs = ((x_ref, xg_ref), (c_ref, cg_ref))
    sent = []

    def send(src, dst, send_sem, recv_sem, device):
        copy = remote(src, dst, send_sem, recv_sem, device)
        copy.start()
        sent.append(copy)

    def arrived(ref, recv_sem):
        remote(ref, ref, s1.at[0, 0], recv_sem, (f_c, s)).wait_recv()
    holds = f // 2 == s
    keep_seg = pltpu.make_async_copy(seg_ref, segs_ref.at[core], seg_l.at[0])
    give_seg = [remote(seg_ref, segs_ref.at[core], seg_s.at[k], seg_r.at[core], ((f + k) % 8, s)) for k in range(1, 8)]

    @pl.when(holds)
    def _():
        keep_seg.start()
        for copy in give_seg:
            copy.start()
    weights = [
        pltpu.make_async_copy(ref, held_ref, w_l.at[n])
        for n, (ref, held_ref) in enumerate(
            ((up_ref, w_up), (qkv_ref, w_qkv), (b_up_in, b_up_ref), (b_qkv_in, b_qkv_ref), (norm_in, norm_ref))
        )
    ]
    for copy in weights:
        copy.start()
    kept = []
    for a, (src, _) in enumerate(pairs):
        own = pltpu.make_async_copy(src.at[pl.ds(f * piece, piece)], held.at[a, f], local.at[a, 0])
        own.start()
        kept.append(own)
        for k in range(1, 8):
            j = (f + k) % 8
            send(src.at[pl.ds(j * piece, piece)], held.at[a, f], s1.at[a, k], r1.at[a, k], (j, s))

    def to_planes(a):
        out = pairs[a][1]
        kept[a].wait()
        for k in range(1, 8):
            arrived(held.at[a, (f + 8 - k) % 8], r1.at[a, k])
        for k in range(1, 4):
            plane = (s + k) % 4
            send(held.at[a, pl.ds(2 * plane, 2)], out.at[:, s, f], s2.at[a, k], r2.at[a, k], (f, plane))
        own = pltpu.make_async_copy(held.at[a, pl.ds(2 * s, 2)], out.at[:, s, f], local.at[a, 1])
        own.start()
        return own

    def spread(a, k):
        out = pairs[a][1]
        z = (s + 4 - k) % 4
        if k:
            arrived(out.at[:, z, f], r2.at[a, k])
        ref = out.at[:, z, f]
        send(ref, ref, s3.at[a, 0, k], r3.at[a, 0, k], (f_x, s))
        send(ref, ref, s3.at[a, 1, k], r3.at[a, 1, k], (f_y, s))
        send(ref, ref, s3.at[a, 2, k], r3.at[a, 2, k], (f_c, s))

    def pass_on(a, k):
        out = pairs[a][1]
        z = (s + 4 - k) % 4
        ref = out.at[:, z, f_x]
        arrived(ref, r3.at[a, 0, k])
        send(out.at[0, z, f_x], out.at[0, z, f_x], s3.at[a, 5, k], r3.at[a, 5, k], (f_y, s))
        send(ref, ref, s3.at[a, 3, k], r3.at[a, 3, k], (f_c, s))
        ref = out.at[:, z, f_y]
        arrived(ref, r3.at[a, 1, k])
        send(out.at[1, z, f_y], out.at[1, z, f_y], s3.at[a, 6, k], r3.at[a, 6, k], (f_x, s))
        send(ref, ref, s3.at[a, 4, k], r3.at[a, 4, k], (f_c, s))

    def pass_corner(a, k):
        out = pairs[a][1]
        z = (s + 4 - k) % 4
        for half in range(2):
            ref = out.at[half, z, f_d]
            arrived(ref, r3.at[a, 5 + half, k])
            send(ref, ref, s3.at[a, 7 + half, k], r3.at[a, 7 + half, k], (f_c, s))

    def from_core(a, k):
        out = pairs[a][1]
        z = (s + 4 - k) % 4
        g_x, g_y, _, g_d = neighbours(f_c)
        arrived(out.at[:, z, f_c], r3.at[a, 2, k])
        arrived(out.at[:, z, g_x], r3.at[a, 3, k])
        arrived(out.at[:, z, g_y], r3.at[a, 4, k])
        for half in range(2):
            arrived(out.at[half, z, g_d], r3.at[a, 7 + half, k])
    results = ((normed, normed_out), (normed_mlp, normed_mlp_out), (packed, packed_out), (act, act_out), (slope, slope_out))
    size = 8 * piece

    def keep(b, z, n):
        rows = pl.ds(pl.multiple_of((b * 4 + z) * size, size), size)
        return pltpu.make_async_copy(results[n][0].at[b], results[n][1].at[rows], keep_l.at[b, n])

    tiles = {}

    def work(k, b):
        z = (s + 4 - k) % 4
        if b == 0:
            for half in range(2):
                tiles[half] = copied(xg_ref.at[half, z], tile.at[half], tile_l.at[half])
            if k == 0:
                for copy in weights:
                    copy.wait()
        tiles[b].wait()
        if k:
            for n in range(5):
                keep(b, (s + 5 - k) % 4, n).wait()

        @pl.loop(0, 8)
        def _(i):
            inputs = tile[b, i].astype(jnp.float32)
            centred = inputs - jnp.mean(inputs, axis=-1, keepdims=True)
            variance = jnp.mean(centred * centred, axis=-1, keepdims=True)
            scaled = centred * lax.rsqrt(variance + EPSILON)
            rows = pl.ds(pl.multiple_of(i * piece, piece), piece)
            low = normed.dtype
            normed[b, rows, :] = (scaled * norm_ref[0:1, :] + norm_ref[1:2, :]).astype(low)
            normed_mlp[b, rows, :] = (scaled * norm_ref[2:3, :] + norm_ref[3:4, :]).astype(low)
        hidden = times_transposed(normed_mlp[b], w_up[...]) + b_up_ref[...]
        packed[b] = (times_transposed(normed[b], w_qkv[...]) + b_qkv_ref[...]).astype(packed.dtype)
        activated, grown = gelu_pair(hidden)
        act[b] = activated.astype(act.dtype)
        slope[b] = grown
        for n in range(5):
            keep(b, z, n).start()
    own0 = to_planes(0)
    own1 = to_planes(1)
    steps = [(a, k) for a in range(2) for k in range(4)]
    for i in range(len(steps) + 2):
        if i < len(steps):
            a, k = steps[i]
            if k == 0:
                (own0 if a == 0 else own1).wait()
            spread(a, k)
        if 3 <= i < 7:
            from_core(0, i - 3)
            work(i - 3, 0)
        if 0 <= i - 1 < len(steps):
            pass_on(*steps[i - 1])
        if 0 <= i - 2 < len(steps):
            pass_corner(*steps[i - 2])
        if 3 <= i < 7:
            work(i - 3, 1)
    for k in range(4):
        from_core(1, k)
    for b in range(2):
        for n in range(5):
            keep(b, (s + 1) % 4, n).wait()
    for b in range(2):

        @pl.when(f != 2 * s + b)
        def _():
            arrived(segs_ref.at[b], seg_r.at[b])

    @pl.when(holds)
    def _():
        keep_seg.wait()
        for copy in give_seg:
            copy.wait_send()
    for copy in sent:
        copy.wait_send()


def gather_both(x, c, segments, w_up, w_qkv, b_up, b_qkv, norms):
    rows, width = x.shape
    piece = rows // 8
    tokens = 8 * rows
    units, columns = (w_up.shape[0], w_qkv.shape[0])
    shape = jax.ShapeDtypeStruct((2, 4, 8, piece, width), x.dtype)
    dma = pltpu.SemaphoreType.DMA
    vmem = pltpu.VMEM
    anywhere = pl.BlockSpec(memory_space=pl.ANY)
    sizes = ((width, x.dtype), (width, x.dtype), (columns, x.dtype), (units, x.dtype), (units, jnp.float32))
    return pl.pallas_call(gather_kernel, out_shape=(shape, shape, jax.ShapeDtypeStruct((2, *segments.shape), segments.dtype),
        *(jax.ShapeDtypeStruct((tokens, size), kind) for size, kind in sizes)), in_specs=[anywhere] * 8, out_specs=[anywhere] * 8,
        scratch_shapes=[vmem((2, 8, piece, width), x.dtype), vmem((2, 8, piece, width), x.dtype), vmem(w_up.shape, w_up.dtype), vmem(w_qkv.shape,
        w_qkv.dtype), *(vmem((2, 8 * piece, size), kind) for size, kind in sizes), dma((8,)), dma((2,)), dma((1,)), dma((2, 8)), dma((2, 8)), dma((2,
        4)), dma((2, 4)), dma((2, 9, 4)), dma((2, 9, 4)), dma((2, 2)), dma((5,)), dma((2,)), dma((2, 5)),
        vmem((1, units), jnp.float32), vmem((1, columns), jnp.float32), vmem(norms.shape, jnp.float32)],
        compiler_params=pltpu.CompilerParams(collective_id=1, has_side_effects=True, vmem_limit_bytes=60 * 1024 * 1024), name='gather_tokens')(x, c,
        segments, w_up, w_qkv, b_up.reshape(1, units), b_qkv.reshape(1, columns), norms)


def finish_kernel(down_ref, dense_ref, hidden_ref, normed_mlp_ref, packed_ref, normed_ref, act_ref, context_ref, up_w_ref, down_w_ref, qkv_w_ref,
    dense_w_ref, norm_ref, h_col_ref, p_col_ref, bias_ref, g_down, g_up, g_qkv, g_dense, o_out, o_back, part, paired, kept, crossed, homed, o_small,
    line_a, line_b, turned, big, hidden, packed, weight, qkv_w, dense_w, context, act, total, made, own, right, vecs, vec_out, vec_in, small,
    small_in, load_l, act_l, part_l, tile_s, tile_r, tile_l, left_l, right_l, in_s, in_r, mid_s, mid_r, end_s, end_r, own_l, keep_l, turn_s, turn_r,
    cross_s, cross_r, home_s, home_r, back_s, back_r, local, vec_s, vec_r, small_s, small_r):
    f, s = (lax.axis_index('fsdp'), lax.axis_index('sp'))
    core = f % 2
    f_x, f_y, f_c, f_d = neighbours(f)
    is_end = (s == 0) | (s == 3)
    is_mid = (s == 1) | (s == 2)
    inner, outer, facing = (1 + s // 3, 3 * (s // 2), 3 - s)
    unit = made.shape[3]
    size = 8 * unit
    low = made.dtype
    meet(f, s)
    sent = []

    def send(src, dst, send_sem, recv_sem, device):
        copy = remote(src, dst, send_sem, recv_sem, device)
        copy.start()
        return copy

    def arrived(ref, recv_sem):
        remote(ref, ref, vec_s.at[0], recv_sem, (f_c, s)).wait_recv()
    chunks = []
    at = 0
    groups = {}
    for name, ref, first, result in (('down', down_ref, 0, g_down), ('up', part, 0, g_up), ('qkv', part, g_up.shape[0], g_qkv), ('dense', turned, 0,
        g_dense)):
        for g in range(result.shape[0]):
            cuts = (4,)
            if not chunks:
                cuts = (1, 1, 2)
            if name == 'dense':
                cuts = (2, 1, 1)
            start = 0
            for pairs_of in cuts:
                chunks.append((ref, first + g, result, g, start, pairs_of, at))
                groups[len(chunks) - 1] = (name, first + g)
                start += pairs_of
            at += 1
    count = len(chunks)
    ahead = 3

    def cut(ref, g, k):
        _, _, _, _, start, pairs_of, _ = chunks[k]
        return ref.at[g, pl.ds(start, pairs_of)]

    def source(k):
        return cut(chunks[k][0], chunks[k][1], k)

    def goal(k):
        return cut(chunks[k][2], chunks[k][3], k)

    def from_end(k):
        return remote(source(k), cut(line_a, chunks[k][6], k), in_s.at[k], in_r.at[k], (f, inner))

    def across(k):
        return remote(cut(line_a, chunks[k][6], k), cut(line_b, chunks[k][6], k), mid_s.at[k], mid_r.at[k], (f, facing))

    def to_end(k):
        return remote(cut(line_b, chunks[k][6], k), goal(k), end_s.at[k], end_r.at[k], (f, outer))

    def load_own(k):
        return pltpu.make_async_copy(source(k), cut(own, k % 2, k), own_l.at[k % 2])

    def keep(k):
        return pltpu.make_async_copy(cut(line_b, chunks[k][6], k), goal(k), keep_l.at[k])

    def add_units(target, others, number):
        @pl.loop(0, number)
        def _(i):
            for half in range(2):
                rows = pl.ds(half * (unit // 2), unit // 2)
                value = target[i // 2, i % 2, rows, :].astype(jnp.float32)
                for other in others:
                    value = value + other[i // 2, i % 2, rows, :].astype(jnp.float32)
                target[i // 2, i % 2, rows, :] = value.astype(low)

    def mid_in(k):
        load_own(k).wait()
        from_end(k).wait_recv()
        add_units(cut(line_a, chunks[k][6], k), [cut(own, k % 2, k)], 2 * chunks[k][5])
        across(k).start()
        if k + 2 < count:
            load_own(k + 2).start()

    def mid_out(k):
        across(k).wait_recv()
        add_units(cut(line_b, chunks[k][6], k), [cut(line_a, chunks[k][6], k)], 2 * chunks[k][5])
        to_end(k).start()
        keep(k).start()
    coming = {'big': copied(normed_mlp_ref, big, load_l.at[0]), 'hidden': copied(hidden_ref, hidden, load_l.at[1]), 'weight': copied(up_w_ref,
        weight, load_l.at[2]), 'packed': copied(packed_ref, packed, load_l.at[3]), 'qkv': copied(qkv_w_ref, qkv_w, load_l.at[4]),
        'dense': copied(dense_w_ref, dense_w, load_l.at[5]), 'context': copied(context_ref, context, load_l.at[6])}

    def ready(*names):
        for name in names:
            if coming[name] is not None:
                coming[name].wait()
                coming[name] = None
    span = dense_ref.shape[4]
    columns = pl.ds(pl.multiple_of(f * span, span), span)
    turn_own = copied(dense_ref.at[f], turned.at[0, :, :, :, columns], local.at[0])
    bias_own = copied(bias_ref, small.at[pl.ds(8, 8)], local.at[1])
    vecs[...] = jnp.zeros_like(vecs)
    vec_out[...] = jnp.zeros_like(vec_out)
    busy = {0: [], 1: []}
    turns = [0]

    def next_made():
        slot = turns[0] % 2
        turns[0] += 1
        for wait in busy[slot]:
            wait()
        busy[slot] = []
        return slot
    stores = {}

    def finish_group(g, weights, first, column_ref, which):
        slot = next_made()

        @pl.loop(0, 8)
        def _(i):
            rows = pl.ds(pl.multiple_of(i * unit, unit), unit)
            wide = pl.ds(pl.multiple_of(first + i * unit, unit), unit)
            value = total[rows, :]
            made[slot, i // 2, i % 2] = value.astype(low)
            line = weights[wide, :].astype(jnp.float32)
            sums = column_ref[wide, 0:1]
            scaled = line * (value - sums * norm_ref[2 * which + 1:2 * which + 2, :])
            vecs[2 * which] += eight_rows(scaled)
            vecs[2 * which + 1] += eight_rows(line * sums)
        stores[g] = copied(made.at[slot], part.at[g], part_l.at[g])
        busy[slot] = [functools.partial(stored, g)]

    def stored(g):
        if stores[g] is not None:
            stores[g].wait()
            stores[g] = None

    def up_group(g):
        ready('big', 'hidden', 'weight')
        total[...] = contract_rows(hidden[:, g * size:(g + 1) * size], big[...].reshape(hidden.shape[0], -1))
        finish_group(g, weight, g * size, h_col_ref, 1)
        if g == g_up.shape[0] - 1:
            coming['big'] = copied(normed_ref, big, load_l.at[7])
            coming['weight'] = copied(down_w_ref, weight, load_l.at[8])
            load_act(0)

    def qkv_group(g):
        ready('big', 'packed', 'qkv')
        total[...] = contract_rows(packed[:, g * size:(g + 1) * size], big[...].reshape(hidden.shape[0], -1))
        finish_group(g_up.shape[0] + g, qkv_w, g * size, p_col_ref, 0)

    def load_act(t):
        coming['act', t] = copied(act_ref.at[pl.ds(t * size, size)], act.at[t % 2], act_l.at[t % 2])

    def give_tile(a, t, value):
        b, z = (t // 4, t % 4)
        slot = next_made()
        made[slot] = value.astype(low).reshape(4, 2, unit, value.shape[1])
        give = send(made.at[slot, :, 1 - core], paired.at[a, :, z, b], tile_s.at[a, t], tile_r.at[a, t], (f_c, s))
        hold = copied(made.at[slot, :, core], kept.at[a, :, z, b], tile_l.at[a, t])
        busy[slot] = [give.wait_send, hold.wait]

    def out_tile(t):
        ready('weight', 'context', 'dense', ('act', t))
        if t < 7:
            load_act(t + 1)
        rows = slice(t * size, (t + 1) * size)
        value = times_transposed(context[rows, :], dense_w[...]) + times(act[t % 2], weight[...])
        give_tile(0, t, value)
        if t == 7:
            coming['weight'] = copied(up_w_ref, weight, load_l.at[9])

    def back_tile(t):
        ready('weight', 'packed', 'qkv', 'hidden')
        rows = slice(t * size, (t + 1) * size)
        value = times(packed[rows, :], qkv_w[...]) * norm_ref[0:1, :]
        value = value + times(hidden[rows, :], weight[...]) * norm_ref[2:3, :]
        give_tile(1, t, value)
    results = (o_out, o_back)
    order = (f_d // 2, f_x // 2, f_y // 2, f // 2)
    homes = {}

    def free(slot):
        for wait in busy[slot]:
            wait()
        busy[slot] = []

    def tiles_here(a):
        for slot in range(2):
            free(slot)
        for t in range(8):
            arrived(paired.at[a, :, t % 4, t // 4], tile_r.at[a, t])

    def add_pair(a, n):
        if n == 0:
            tiles_here(a)
        left = big.at[3 * a + n]
        slot = n % 2
        first = copied(paired.at[a, order[n]], left, left_l.at[slot])
        second = copied(kept.at[a, order[n]], right.at[slot], right_l.at[slot])
        first.wait()
        second.wait()
        add_units(left, [right.at[slot]], 8)
        sent.append(send(left, crossed.at[a, n], cross_s.at[a, n], cross_r.at[a, n], ((f_d, f_x, f_y)[n], s)))

    def add_chips(a):
        left = big.at[6 + a]
        copies = [copied(paired.at[a, order[3]], left, left_l.at[0]), copied(kept.at[a, order[3]], right.at[0], right_l.at[0])]
        for n in range(3):
            arrived(crossed.at[a, n], cross_r.at[a, n])
            slot = (n + 1) % 2
            more = copied(crossed.at[a, n], right.at[slot], right_l.at[slot])
            for copy in copies:
                copy.wait()
            add_units(left, [right.at[1 - slot]], 8)
            copies = [more]
        copies[0].wait()
        add_units(left, [right.at[1]], 8)
        for k in range(1, 4):
            z = (s + k) % 4
            sent.append(send(left.at[z], homed.at[a, s], home_s.at[a, k], home_r.at[a, k], (f, z)))
        homes['own', a] = copied(left.at[s], homed.at[a, s], local.at[2 + a])


    def go_home(a):
        homes['own', a].wait()
        for k in range(1, 4):
            arrived(homed.at[a, (s + 4 - k) % 4], home_r.at[a, k])
        for k in range(1, 8):
            j = (f + k) % 8
            sent.append(send(homed.at[a, j // 2, j % 2], results[a].at[f], back_s.at[a, k], back_r.at[a, k], (j, s)))
        homes[a] = copied(homed.at[a, f // 2, core], results[a].at[f], local.at[4 + a])

    def give_vectors():
        for which in range(2):
            gain = norm_ref[2 * which:2 * which + 1, :]
            scaled = jnp.sum(vecs[2 * which], axis=0, keepdims=True) / gain
            plain = jnp.sum(vecs[2 * which + 1], axis=0, keepdims=True)
            for j in range(8):
                part_of = slice(j * span, (j + 1) * span)
                vec_out[j, 2 * which:2 * which + 1, :] = scaled[:, part_of]
                vec_out[j, 2 * which + 1:2 * which + 2, :] = plain[:, part_of]
        for k in range(1, 8):
            j = (f + k) % 8
            sent.append(send(vec_out.at[j], vec_in.at[f], vec_s.at[k], vec_r.at[k], (j, s)))
        homes['vec'] = copied(vec_out.at[f], vec_in.at[f], local.at[6])

    def add_vectors():
        homes['vec'].wait()
        bias_own.wait()
        for k in range(1, 8):
            arrived(vec_in.at[(f + 8 - k) % 8], vec_r.at[k])
        value = vec_in[0]
        for j in range(1, 8):
            value = value + vec_in[j]
        small[0:8, :] = value
        for k in range(1, 4):
            sent.append(send(small, small_in.at[s], small_s.at[k], small_r.at[k], (f, (s + k) % 4)))
        homes['small'] = copied(small, small_in.at[s], local.at[7])

    def add_small():
        homes['small'].wait()
        for k in range(1, 4):
            arrived(small_in.at[(s + 4 - k) % 4], small_r.at[k])
        value = small_in[0]
        for z in range(1, 4):
            value = value + small_in[z]
        o_small[...] = value

    def turn_start():
        for k in range(1, 8):
            j = (f + k) % 8
            sent.append(send(dense_ref.at[j], turned.at[0, :, :, :, columns], turn_s.at[k], turn_r.at[k], (j, s)))

    def turn_done():
        turn_own.wait()
        for k in range(1, 8):
            j = (f + 8 - k) % 8
            there = pl.ds(pl.multiple_of(j * span, span), span)
            arrived(turned.at[0, :, :, :, there], turn_r.at[k])

    def task(name, i):
        if name == 'turn':
            turn_start()
        elif name == 'turned':
            turn_done()
        elif name == 'up':
            up_group(i)
        elif name == 'qkv':
            qkv_group(i)
        elif name == 'out':
            out_tile(i)
        elif name == 'back':
            back_tile(i)
        elif name == 'pair':
            add_pair(i // 3, i % 3)
        elif name == 'chips':
            add_chips(i)
        elif name == 'home':
            go_home(i)
        elif name == 'vectors':
            give_vectors()
        elif name == 'sums':
            add_vectors()
        else:
            add_small()

    @pl.when(is_end)
    def _():
        for k in range(ahead):
            from_end(k).start()

    @pl.when(is_mid)
    def _():
        for k in range(2):
            load_own(k).start()
    for k in range(count + 2):
        for name, first, last in FINISH_STEPS[k] if k in FINISH_STEPS else ():
            for i in range(first, last):
                task(name, i)
        if k + ahead - 1 in groups and groups[k + ahead - 1][0] in ('up', 'qkv'):
            stored(groups[k + ahead - 1][1])

        @pl.when(is_mid)
        def _():
            if k < count:
                mid_in(k)
            if 1 <= k <= count:
                mid_out(k - 1)

        @pl.when(is_end)
        def _():
            if 1 <= k <= count:
                to_end(k - 1).wait_recv()
                if k - 1 + ahead < count:
                    from_end(k - 1 + ahead).start()
    for a in range(2):
        homes[a].wait()
        for k in range(1, 8):
            arrived(results[a].at[(f + 8 - k) % 8], back_r.at[a, k])
    for slot in range(2):
        free(slot)
    for copy in sent:
        copy.wait_send()

    @pl.when(is_end)
    def _():
        for k in range(count):
            from_end(k).wait_send()

    @pl.when(is_mid)
    def _():
        for k in range(count):
            across(k).wait_send()
            to_end(k).wait_send()
            keep(k).wait()


FINISH_STEPS = {
    0: (("turn", 0, 1),),
    1: (("up", 0, 1),),
    2: (("up", 1, 2),),
    3: (("up", 2, 4),),
    4: (("qkv", 0, 3),),
    5: (("out", 0, 8),),
    6: (("pair", 0, 3), ("back", 0, 3)),
    7: (("back", 3, 6), ("turned", 0, 1)),
    8: (("back", 6, 8), ("vectors", 0, 1), ("pair", 3, 6)),
    9: (("chips", 0, 1),),
    10: (("sums", 0, 1),),
    11: (("home", 0, 1), ("chips", 1, 2)),
    12: (("small", 0, 1),),
    14: (("home", 1, 2),),
}


def finish(down, dense, hidden_grad, normed_mlp, packed_grad, normed, act, context, w_up, w_down, w_qkv, dense_in, norms, h_sums, p_sums, bias):
    width = down.shape[1]
    tokens = hidden_grad.shape[0]
    low = down.dtype
    unit = tokens // 64
    size = 8 * unit
    span = width // 8

    def grouped(rows):
        return (rows // size, 4, 2, unit, width)

    def columns(sums):
        return jnp.broadcast_to(sums[:, None], (sums.shape[0], 128))
    sets = [w.shape[0] // size for w in (down, w_up, w_qkv)]
    number = sum(sets) + 1
    count = sum(sets) + 5
    sums = [jax.ShapeDtypeStruct(grouped(n * size), low) for n in (*sets, 1)]
    token = jax.ShapeDtypeStruct((8, unit, width), low)
    halves = jax.ShapeDtypeStruct((2, 4, 4, 2, unit, width), low)
    others = [jax.ShapeDtypeStruct(grouped((sets[1] + sets[2]) * size), low), halves, halves, jax.ShapeDtypeStruct((2, 3, 4, 2, unit, width), low),
        jax.ShapeDtypeStruct((2, 4, 2, unit, width), low)]
    dma = pltpu.SemaphoreType.DMA
    vmem = pltpu.VMEM
    anywhere = pl.BlockSpec(memory_space=pl.ANY)
    inside = pl.BlockSpec(memory_space=pltpu.VMEM)
    result = pl.pallas_call(finish_kernel, out_shape=(*sums, token, token, *others, jax.ShapeDtypeStruct((16, span), jnp.float32)),
        in_specs=[anywhere] * 12 + [inside] * 3 + [anywhere], out_specs=[anywhere] * 11 + [inside], scratch_shapes=[vmem((number, 4, 2, unit, width),
        low), vmem((number, 4, 2, unit, width), low), vmem((1, 4, 2, unit, width), low), vmem(grouped(tokens), low), vmem(hidden_grad.shape, low),
        vmem(packed_grad.shape, low), vmem(w_up.shape, low), vmem(w_qkv.shape, low), vmem(dense_in.shape, low), vmem(context.shape, low), vmem((2,
        size, act.shape[1]), low), vmem((size, width), jnp.float32), *(vmem((2, 4, 2, unit, width), low) for _ in range(3)), vmem((4, 8, width),
        jnp.float32), vmem((8, 8, span), jnp.float32), vmem((8, 8, span), jnp.float32), vmem((16, span), jnp.float32), vmem((4, 16, span),
        jnp.float32), dma((10,)), dma((2,)), dma((sets[1] + sets[2],)), dma((2, 8)), dma((2, 8)), dma((2, 8)), dma((2,)), dma((2,)), dma((count,)),
        dma((count,)), dma((count,)), dma((count,)), dma((count,)), dma((count,)), dma((2,)), dma((count,)), dma((8,)), dma((8,)), dma((2, 3)),
        dma((2, 3)), dma((2, 4)), dma((2, 4)), dma((2, 8)), dma((2, 8)), dma((8,)), dma((8,)), dma((8,)), dma((4,)), dma((4,))],
        compiler_params=pltpu.CompilerParams(collective_id=2, has_side_effects=True, vmem_limit_bytes=60 * 1024 * 1024),
        name='finish')(down.reshape(grouped(down.shape[0])), dense.reshape(8, 4, 2, unit, span), hidden_grad, normed_mlp.reshape(grouped(tokens)), packed_grad, normed.reshape(grouped(tokens)), act,
        context, w_up, w_down, w_qkv, dense_in, norms, columns(h_sums), columns(p_sums), bias)
    grads = [grad.reshape(-1, width) for grad in result[:4]]
    return (grads, result[4], result[5], result[11])


def last_kernel(
    x_ref, c_ref, out_ref, back_ref, shift_ref, early_ref, late_ref, up_ref, qkv_ref, dense_ref,
    output, input_grad, down_out, up_out, qkv_out, dense_out,
):
    inputs = x_ref[...].astype(jnp.float32)
    output[...] = (inputs + (out_ref[...].astype(jnp.float32) + shift_ref[...])).astype(output.dtype)
    centred = inputs - jnp.mean(inputs, axis=-1, keepdims=True)
    inverse = lax.rsqrt(jnp.mean(centred * centred, axis=-1, keepdims=True) + EPSILON)
    scaled = centred * inverse
    weighted = back_ref[...].astype(jnp.float32)
    first_mean = jnp.mean(weighted, axis=-1, keepdims=True)
    second_mean = jnp.mean(weighted * scaled, axis=-1, keepdims=True)
    change = inverse * (weighted - first_mean - scaled * second_mean)
    input_grad[...] = (c_ref[...].astype(jnp.float32) + change).astype(input_grad.dtype)
    down_out[0] = early_ref[...].astype(jnp.float32)
    down_out[1] = late_ref[...].astype(jnp.float32)
    for ref, out in ((up_ref, up_out), (qkv_ref, qkv_out), (dense_ref, dense_out)):
        out[...] = ref[...].astype(jnp.float32)


def last(x, c, out, back, shift, early, late, up, qkv, dense, steps=8):
    width = up.shape[1]

    def tile(array):
        return pl.BlockSpec((array.shape[0] // steps, width), lambda i: (i, 0))

    tokens, sums = (x, c, out, back), (early, late, up, qkv, dense)
    wide = jax.ShapeDtypeStruct((2, early.shape[0], width), jnp.float32)
    number = 2 * early.size + up.size + qkv.size + dense.size
    output, input_grad, down, up, qkv, dense = pl.pallas_call(
        last_kernel,
        grid=(steps,),
        out_shape=(
            jax.ShapeDtypeStruct(x.shape, x.dtype), jax.ShapeDtypeStruct(x.shape, x.dtype), wide,
            *(jax.ShapeDtypeStruct(array.shape, jnp.float32) for array in sums[2:]),
        ),
        in_specs=[tile(array) for array in tokens] + [pl.BlockSpec((1, width), lambda i: (0, 0))] + [tile(array) for array in sums],
        out_specs=[
            tile(x), tile(x), pl.BlockSpec((2, early.shape[0] // steps, width), lambda i: (0, i, 0)),
            *(tile(array) for array in sums[2:]),
        ],
        compiler_params=pltpu.CompilerParams(vmem_limit_bytes=60 * 1024 * 1024),
        cost_estimate=pl.CostEstimate(flops=20 * x.size, transcendentals=0, bytes_accessed=6 * number + 12 * x.size),
        name="last",
    )(*tokens, shift.reshape(1, width), *sums)
    return output, input_grad, down.reshape(-1, width), up, qkv, dense


def own_tokens(hidden_in, cotangent, output, weighted, shift):
    inputs = hidden_in.astype(jnp.float32)
    output = (inputs + (output.astype(jnp.float32) + shift)).astype(jnp.bfloat16)
    scaled, inverse = norm_scaled(inputs)
    weighted = weighted.astype(jnp.float32)
    first_mean = jnp.mean(weighted, axis=-1, keepdims=True)
    second_mean = jnp.mean(weighted * scaled, axis=-1, keepdims=True)
    input_grad = (cotangent.astype(jnp.float32) + inverse * (weighted - first_mean - scaled * second_mean)).astype(jnp.bfloat16)
    return (output, input_grad)


def by_collectives(hidden_in, segments, ln1_gain, ln1_bias, ln2_gain, ln2_bias, w_qkv, b_qkv, w_dense, b_dense, w_up, b_up, w_down, b_down,
    cotangent):
    seq_local, shard_len, width = hidden_in.shape
    seq_len = segments.shape[1]
    nf, ns = (lax.axis_size('fsdp'), lax.axis_size('sp'))
    f_place, s_place = (lax.axis_index('fsdp'), lax.axis_index('sp'))
    seqs = seq_local * nf
    group = seqs // ns
    piece = shard_len // nf
    tokens = group * seq_len
    per_head = max(1, nf // HEADS)
    head_count = max(1, HEADS // nf)
    head_sets = [[head * per_head + k for k in range(per_head)] for head in range(nf // per_head)]

    def gather_tokens(block):
        part = lax.all_to_all(block, 'fsdp', split_axis=1, concat_axis=0, tiled=True)
        part = lax.all_to_all(part, 'sp', split_axis=0, concat_axis=1, tiled=True)
        return in_order(lax.all_gather(part, 'fsdp', axis=0, tiled=True)).reshape(tokens, width)

    def scatter_tokens(partial):
        part = out_of_order(partial).reshape(nf * group, ns * piece, width)
        part = lax.psum_scatter(part, 'fsdp', scatter_dimension=0, tiled=True)
        part = lax.all_to_all(part, 'sp', split_axis=1, concat_axis=0, tiled=True)
        return lax.all_to_all(part, 'fsdp', split_axis=0, concat_axis=1, tiled=True)

    def in_order(array):
        array = array.reshape(nf, group, ns, piece, -1)
        return array.transpose(1, 2, 0, 3, 4).reshape(group, seq_len, -1)

    def out_of_order(array):
        array = array.reshape(group, ns, nf, piece, -1)
        return array.transpose(2, 0, 1, 3, 4).reshape(tokens, -1)

    def over_head(array, axis):
        if per_head == 1:
            return array
        return lax.all_gather(array, 'fsdp', axis=axis, tiled=True, axis_index_groups=head_sets)

    def own_columns(array):
        if per_head == 1:
            return array
        share = array.shape[-1] // per_head
        return lax.dynamic_slice_in_dim(array, f_place % per_head * share, share, array.ndim - 1)

    def own_part(vector):
        share = vector.shape[0] // nf
        return lax.dynamic_slice_in_dim(vector, f_place * share, share, 0)
    gathered, upstream = (gather_tokens(hidden_in), gather_tokens(cotangent))
    rows = lax.all_gather(segments, 'fsdp', axis=0, tiled=True)
    rows = lax.dynamic_slice_in_dim(rows, s_place * group, group, 0)
    dense_in = lax.all_to_all(w_dense, 'fsdp', split_axis=1, concat_axis=0, tiled=True)
    head_qkv = over_head(w_qkv, 0)
    head_dense = over_head(dense_in, 1)
    head_bias = lax.dynamic_slice_in_dim(b_qkv, f_place // per_head * head_qkv.shape[0], head_qkv.shape[0], 0)
    scaled, _ = norm_scaled(gathered.astype(jnp.float32))
    normed = (scaled * ln1_gain + ln1_bias).astype(jnp.bfloat16)
    normed_mlp = (scaled * ln2_gain + ln2_bias).astype(jnp.bfloat16)
    hidden = times_transposed(normed_mlp, w_up) + own_part(b_up)
    activated, slope = gelu_pair(hidden)
    activated = activated.astype(jnp.bfloat16)
    down_term = contract_rows(activated, upstream).astype(jnp.bfloat16)
    grad_down_w = lax.psum(down_term, 'sp').astype(jnp.float32)
    hidden_grad = (times_transposed(upstream, w_down) * slope).astype(jnp.bfloat16)
    up_term = contract_rows(hidden_grad, normed_mlp)
    mlp_norm_grad = times(hidden_grad, w_up)
    packed = (times_transposed(normed, head_qkv) + head_bias).astype(jnp.bfloat16)
    packed = packed.reshape(group, seq_len, head_count, 3 * HEAD_DIM)
    cos_table, sin_table = rotary_tables(rows)
    queries = rotate(packed[..., :HEAD_DIM].astype(jnp.float32), cos_table, sin_table).astype(jnp.bfloat16)
    keys_rot = rotate(packed[..., HEAD_DIM:2 * HEAD_DIM].astype(jnp.float32), cos_table, sin_table).astype(jnp.bfloat16)
    values = packed[..., 2 * HEAD_DIM:]
    mask = build_mask(rows)
    context, log_total = attend_forward(queries, keys_rot, values, mask)
    context = own_columns(context.reshape(tokens, -1))
    partial_out = times_transposed(context, dense_in) + times(activated, w_down)
    context_grad = times(upstream, head_dense).astype(jnp.bfloat16).reshape(group, seq_len, head_count, HEAD_DIM)
    query_grad, key_grad, value_grad = attend_backward(queries, keys_rot, values, mask, log_total, context_grad)
    packed_grad = jnp.concatenate([unrotate(query_grad, cos_table, sin_table), unrotate(key_grad, cos_table, sin_table), value_grad],
        axis=-1).astype(jnp.bfloat16)
    packed_grad = own_columns(packed_grad.reshape(tokens, -1))
    attn_norm_grad = times(packed_grad, w_qkv)
    qkv_term = contract_rows(packed_grad, normed)
    dense_term = contract_rows(upstream, context).astype(jnp.bfloat16)
    partial_back = attn_norm_grad * ln1_gain + mlp_norm_grad * ln2_gain
    vectors = jnp.stack([jnp.sum(attn_norm_grad * scaled, axis=0), jnp.sum(attn_norm_grad, axis=0), jnp.sum(mlp_norm_grad * scaled, axis=0),
        jnp.sum(mlp_norm_grad, axis=0)])
    bias_out = own_part(jnp.sum(upstream.astype(jnp.float32), axis=0))
    bias_qkv = jnp.sum(packed_grad.astype(jnp.float32), axis=0)
    bias_up = jnp.sum(hidden_grad.astype(jnp.float32), axis=0)
    vectors = lax.psum_scatter(vectors, 'fsdp', scatter_dimension=1, tiled=True)
    vectors, bias_out, bias_qkv, bias_up = lax.psum((vectors, bias_out, bias_qkv, bias_up), 'sp')
    output = scatter_tokens(rounded(partial_out))
    weighted = scatter_tokens(rounded(partial_back))
    dense_term = lax.all_to_all(dense_term, 'fsdp', split_axis=0, concat_axis=1, tiled=True)
    grad_up_w, grad_qkv_w, grad_dense_w = (lax.psum(term.astype(jnp.bfloat16), 'sp').astype(jnp.float32) for term in (up_term, qkv_term, dense_term))
    output, input_grad = own_tokens(hidden_in, cotangent, output, weighted, b_dense + b_down)
    return (output, input_grad, vectors[0], vectors[1], vectors[2], vectors[3], grad_qkv_w, bias_qkv, grad_dense_w, bias_out, grad_up_w, bias_up,
        grad_down_w, bias_out)


def by_kernels(hidden_in, segments, ln1_gain, ln1_bias, ln2_gain, ln2_bias, w_qkv, b_qkv, w_dense, b_dense, w_up, b_up, w_down, b_down, cotangent):
    width = hidden_in.shape[2]
    seq_len = segments.shape[1]
    nf, ns = (lax.axis_size('fsdp'), lax.axis_size('sp'))
    group = nf // ns
    tokens = group * seq_len
    share = width // nf
    f_place = lax.axis_index('fsdp')

    def own_part(vector):
        size = vector.shape[0] // nf
        return lax.dynamic_slice_in_dim(vector, f_place * size, size, 0)
    norms = jnp.stack([ln1_gain, ln1_bias, ln2_gain, ln2_bias])
    _, upstream, rows, normed, normed_mlp, packed, activated, slope = gather_both(hidden_in[0], cotangent[0], segments.reshape(8, seq_len // 8),
        w_up, w_qkv, own_part(b_up), own_part(b_qkv), norms)
    upstream = upstream.reshape(tokens, width)
    w_dense, upstream = lax.optimization_barrier((w_dense, upstream))
    dense_in = lax.all_to_all(w_dense, 'fsdp', split_axis=1, concat_axis=0, tiled=True)
    early = activated.shape[1] // 2
    down_term = contract_rows(activated[:, :early], upstream).astype(jnp.bfloat16)
    early_down_w = lax.psum(down_term, 'sp')
    slope, activated, down_term = lax.optimization_barrier((slope, activated, down_term))
    hidden_grad, context_grad, c_sums, h_sums = upstream_parts(upstream, slope, w_down, dense_in)
    context, packed_grad, p_sums = attend(packed, context_grad, head_tables(rows.reshape(group, seq_len)), seq_len)
    late_down_term = contract_rows(activated[:, early:], upstream).astype(jnp.bfloat16)
    dense_term = contract_rows(upstream, context).astype(jnp.bfloat16)
    bias_up, bias_qkv = (jnp.sum(h_sums, axis=0), jnp.sum(p_sums, axis=0))
    bias_out = own_part(jnp.sum(c_sums, axis=0))
    grads, output, weighted, sums = finish(late_down_term, dense_term, hidden_grad, normed_mlp, packed_grad, normed, activated, context, w_up,
        w_down, w_qkv, dense_in, norms, bias_up, bias_qkv, jnp.concatenate([bias_out, bias_qkv, bias_up]).reshape(8, share))
    output, input_grad, grad_down_w, grad_up_w, grad_qkv_w, grad_dense_w = last(
        hidden_in[0], cotangent[0], output.reshape(-1, width), weighted.reshape(-1, width), b_dense + b_down, early_down_w, *grads
    )
    output, input_grad = output[None], input_grad[None]
    bias_out = sums[8]
    return (output, input_grad, sums[0], sums[1], sums[2], sums[3], grad_qkv_w, sums[9:12].reshape(-1), grad_dense_w, bias_out, grad_up_w,
        sums[12:16].reshape(-1), grad_down_w, bias_out)


def per_device(hidden_in, *rest):
    sizes = (lax.axis_size('fsdp'), lax.axis_size('sp'), hidden_in.shape[0])
    shapes = (hidden_in.shape[1] % 256, hidden_in.shape[2] % (8 * HEAD_DIM), rest[9].shape[0] % 256)
    if sizes == (8, 4, 1) and HEADS == 8 and (not any(shapes)):
        return by_kernels(hidden_in, *rest)
    return by_collectives(hidden_in, *rest)


def solution(mesh):
    rows = P('fsdp', 'sp', None)
    first = P('fsdp', None)
    return jax.shard_map(per_device, mesh=mesh, in_specs=(rows, first, P(), P(), P(), P(), first, P(), first, P(), first, P(), first, P(), rows),
        out_specs=(rows, rows, P('fsdp'), P('fsdp'), P('fsdp'), P('fsdp'), first, P('fsdp'), first, P('fsdp'), first, P('fsdp'), first, P('fsdp')),
        check_vma=False)
```
